32 devices in a mesh: seq: 4 (over x, core), ctx: 8 (over z, y).
Axes of the slice: x: 2, y: 2, z: 4, core: 2. Of those that a mesh axis runs over, the one named last changes fastest.
Arguments:
- tokens: bfloat16 [1024, 8, 768], P('ctx', 'seq'), may hold values from -6 to 6
- segment_ids: int32 [8, 1024], P('seq', 'ctx'), may hold values from 0 to 15, never falling along the last dimension, each value on 1 to 512 neighbouring positions
- w_query: bfloat16 [768, 768], P('seq'), may hold values from -0.21875 to 0.21875
- w_key: bfloat16 [768, 768], P('seq'), may hold values from -0.21875 to 0.21875
- w_value: bfloat16 [768, 768], P('seq'), may hold values from -0.21875 to 0.21875
- w_output: bfloat16 [768, 768], P('seq'), may hold values from -0.875 to 0.875
- w_inner: bfloat16 [768, 3072], P('seq'), may hold values from -0.21875 to 0.21875
- w_outer: bfloat16 [3072, 768], P('seq'), may hold values from -0.109375 to 0.109375
- b_query: bfloat16 [768], P('seq'), may hold values from -3 to 3
- b_value: bfloat16 [768], P('seq'), may hold values from -3 to 3
- b_output: bfloat16 [768], P('seq'), may hold values from -3 to 3
- b_inner: bfloat16 [3072], P('seq'), may hold values from -3 to 3
- b_outer: bfloat16 [768], P('seq'), may hold values from -3 to 3
- gain_first: bfloat16 [768], P('seq'), may hold values from 0.099609375 to 1.8984375
- shift_first: bfloat16 [768], P('seq'), may hold values from -3 to 3
- gain_second: bfloat16 [768], P('seq'), may hold values from 0.099609375 to 1.8984375
- shift_second: bfloat16 [768], P('seq'), may hold values from -3 to 3
- cotangent: bfloat16 [1024, 8, 768], P('ctx', 'seq'), may hold values from -6 to 6
Outputs:
- layer_out: bfloat16 [1024, 8, 768], P('ctx', 'seq')
- grad_tokens: float32 [1024, 8, 768], P('ctx', 'seq')
- dweight_query: float32 [768, 768], P('seq')
- dweight_key: float32 [768, 768], P('seq')
- dweight_value: float32 [768, 768], P('seq')
- dweight_output: float32 [768, 768], P('seq')
- dweight_inner: float32 [768, 3072], P('seq')
- dweight_outer: float32 [3072, 768], P('seq')
- dbias_query: float32 [768], P('seq')
- dbias_value: float32 [768], P('seq')
- dbias_output: float32 [768], P('seq')
- dbias_inner: float32 [3072], P('seq')
- dbias_outer: float32 [768], P('seq')
- dgain_first: float32 [768], P('seq')
- dshift_first: float32 [768], P('seq')
- dgain_second: float32 [768], P('seq')
- dshift_second: float32 [768], P('seq')
The draws below stay inside these ranges and needn't reach their ends.
Inputs may be any that keep to these rules, and one draw needn't show every extreme that they name: `segment_ids`: along each sequence the segment numbers never fall; a segment holds at most 512 tokens, and that bound is reached.
All inputs are finite; a program needn't handle non-finite values.
Results may differ from the reference program's by a relative error of at most 0.02.
Values may be sent and summed in bfloat16 or wider, within the bound.
A program may use at most 384 MiB of HBM per device.

```python
import math
import jax
import jax.numpy as jnp
import numpy as np
from jax import lax

D = 768
H = 12
DH = 64
FF = 3072
LENGTH = 1024
SEQS = 8


def block_levels(own_key, shape, cuts, low, largest):
    loudness, own = 1.0, jax.random.fold_in(own_key, 6)
    for dim, parts in cuts:
        draws = jnp.exp(jax.random.uniform(jax.random.fold_in(own, dim), (parts,), jnp.float32, low / len(cuts), largest / len(cuts)))
        loudness = loudness * jnp.repeat(draws, shape[dim] // parts).reshape([-1 if axis == dim else 1 for axis in range(len(shape))])
    return loudness


def profile(amount, total, reach, slope):
    loads = [(1 << 20) // math.isqrt(rank ** slope) + 1 for rank in range(2, amount + 1)]
    surplus, counts = total - reach - (amount - 1), [1] * (amount - 1)
    while surplus > 0:
        candidates = [i for i in range(amount - 1) if counts[i] < reach]
        whole, remaining = sum([loads[i] for i in candidates]), surplus
        for i in candidates:
            extra = min(reach - counts[i], max(1, remaining * loads[i] // whole), surplus)
            counts[i] = counts[i] + extra
            surplus = surplus - extra
    return np.array([reach] + counts)


def uneven_parts(key, amount, total, reach, lean):
    if amount == 2:
        one = jax.random.randint(key, (), max(1, total - reach), min(reach, total - 1) + 1)
        return jnp.stack([one, total - one])
    tallies = jnp.asarray(profile(amount, total, reach, lean), jnp.int32)
    couples = (amount - 1) // 2
    donor, sink = tallies[1:1 + 2 * couples:2], tallies[2:2 + 2 * couples:2]
    slack = jnp.minimum(donor - 1, reach - sink)
    passed = jax.random.randint(jax.random.fold_in(key, 1), (couples,), 0, 1 << 20) % (slack + 1)
    tallies = tallies.at[1:1 + 2 * couples:2].set(donor - passed).at[2:2 + 2 * couples:2].set(sink + passed)
    return tallies[jax.random.permutation(jax.random.fold_in(key, 2), amount)]


def centred(key, dims, width, reach, cuts=(), kind=jnp.bfloat16):
    array = width * jax.random.normal(key, dims, jnp.float32)
    if cuts:
        array = array * block_levels(key, dims, cuts, -0.22, 0.18)
    return jnp.clip(array, -reach, reach).astype(kind)


def setup_inputs(seed: int = 0) -> dict:
    streams_of = jax.random.split(jax.random.key(seed), 19)
    return {
        "tokens": centred(streams_of[0], (LENGTH, SEQS, D), 1.0, 6.0, ((0, 8), (1, 4))),
        "segment_ids": jax.vmap(lambda own: jnp.searchsorted(jnp.cumsum(uneven_parts(own, max(LENGTH // 64, 4), LENGTH, LENGTH // 2, 2)), jnp.arange(LENGTH), side="right"))(jax.random.split(streams_of[1], SEQS)).reshape((SEQS, LENGTH)).astype(jnp.int32),
        "w_query": centred(streams_of[2], (D, D), D ** -0.5, 0.21875, ((0, 4),)),
        "w_key": centred(streams_of[3], (D, D), D ** -0.5, 0.21875, ((0, 4),)),
        "w_value": centred(streams_of[4], (D, D), D ** -0.5, 0.21875, ((0, 4),)),
        "w_output": centred(streams_of[5], (D, D), (D // 16) ** -0.5, 0.875, ((0, 4),)),
        "w_inner": centred(streams_of[6], (D, FF), D ** -0.5, 0.21875, ((0, 4),)),
        "w_outer": centred(streams_of[7], (FF, D), FF ** -0.5, 0.109375, ((0, 4),)),
        "b_query": centred(streams_of[8], (D,), 0.5, 3.0, ((0, 4),)),
        "b_value": centred(streams_of[9], (D,), 0.5, 3.0, ((0, 4),)),
        "b_output": centred(streams_of[10], (D,), 0.5, 3.0, ((0, 4),)),
        "b_inner": centred(streams_of[11], (FF,), 0.5, 3.0, ((0, 4),)),
        "b_outer": centred(streams_of[12], (D,), 0.5, 3.0, ((0, 4),)),
        "gain_first": jnp.clip(1.0 + 0.18 * jax.random.normal(streams_of[13], (D,), jnp.float32), 0.099609375, 1.8984375).astype(jnp.bfloat16),
        "shift_first": centred(streams_of[14], (D,), 0.5, 3.0, ((0, 4),)),
        "gain_second": jnp.clip(1.0 + 0.18 * jax.random.normal(streams_of[15], (D,), jnp.float32), 0.099609375, 1.8984375).astype(jnp.bfloat16),
        "shift_second": centred(streams_of[16], (D,), 0.5, 3.0, ((0, 4),)),
        "cotangent": centred(streams_of[17], (LENGTH, SEQS, D), 1.0, 6.0, ((0, 8), (1, 4))),
    }


@jax.custom_vjp
def low(v):
    return lax.optimization_barrier(v.astype(jnp.bfloat16)).astype(jnp.float32)

@jax.custom_vjp
def low_back(v):
    return v

def low_keep(v):
    return (low(v), None)

def low_pass(kept, grad):
    return (grad,)

def back_keep(v):
    return (v, None)

def back_low(kept, grad):
    return (low(grad),)
low.defvjp(low_keep, low_pass)
low_back.defvjp(back_keep, back_low)
HIGHEST = lax.Precision.HIGHEST
EPSILON = 1e-12
SCORE_SCALE = 0.125

def layer_norm(values, gain_vec, shift_vec):
    center = values - lax.optimization_barrier(jnp.mean(values, axis=-1, keepdims=True))
    var_rows = lax.optimization_barrier(jnp.mean(center * center, axis=-1, keepdims=True))
    return center * lax.rsqrt(var_rows + EPSILON) * gain_vec + shift_vec

def gelu_exact(values):
    return values * (0.5 * (1.0 + lax.erf(values * 0.7071067811865476)))

def attend_block(key_rows, value_rows, seg_keys, queries, seg_query):
    scores = low_back(jnp.einsum('ihd,jhd->hij', queries, key_rows, precision=HIGHEST) * SCORE_SCALE)
    allowed = (seg_query[:, None] == seg_keys[None, :])[None]
    unnorm = jnp.where(allowed, jnp.exp(scores), 0.0)
    totals = lax.optimization_barrier(jnp.sum(unnorm, axis=-1))
    mixture = jnp.einsum('hij,jhd->ihd', low(unnorm), value_rows, precision=HIGHEST)
    return low_back(mixture) / jnp.transpose(totals)[:, :, None]

def attend_sequence(pieces):
    queries, key_rows, value_rows, segments = pieces
    length = queries.shape[0]
    qblock = math.gcd(length, 512)
    checked = jax.checkpoint(attend_block)

    def visit_block(element):
        return checked(key_rows, value_rows, segments, element[0], element[1])
    blocks = lax.map(visit_block, (queries.reshape(length // qblock, qblock, H, DH), segments.reshape(length // qblock, qblock)))
    return blocks.reshape(length, H, DH)

def forward(tokens, segment_ids, w_query, w_key, w_value, w_output, w_inner, w_outer, b_query, b_value, b_output, b_inner, b_outer, gain_first, shift_first, gain_second, shift_second):
    length, seq_count, feature_count = tokens.shape
    flat_rows = tokens.reshape(length * seq_count, feature_count)
    queries = low_back(low(jnp.dot(flat_rows, w_query, precision=HIGHEST) + b_query))
    key_rows = low_back(low(jnp.dot(flat_rows, w_key, precision=HIGHEST)))
    value_rows = low_back(low(jnp.dot(flat_rows, w_value, precision=HIGHEST) + b_value))

    def heads_first(values):
        return jnp.transpose(values.reshape(length, seq_count, H, DH), (1, 0, 2, 3))
    attended = lax.map(attend_sequence, (heads_first(queries), heads_first(key_rows), heads_first(value_rows), segment_ids))
    context = low_back(low(jnp.transpose(attended, (1, 0, 2, 3)).reshape(length * seq_count, feature_count)))
    branch = low_back(jnp.dot(context, w_output, precision=HIGHEST) + b_output)
    hidden = layer_norm(branch + flat_rows, gain_first, shift_first)
    inner_pre = low_back(jnp.dot(low(hidden), w_inner, precision=HIGHEST) + b_inner)
    activated = low(gelu_exact(inner_pre))
    outer_pre = low_back(jnp.dot(activated, w_outer, precision=HIGHEST) + b_outer)
    result = layer_norm(outer_pre + hidden, gain_second, shift_second)
    return result.reshape(length, seq_count, feature_count)

def reference(tokens, segment_ids, w_query, w_key, w_value, w_output, w_inner, w_outer, b_query, b_value, b_output, b_inner, b_outer, gain_first, shift_first, gain_second, shift_second, cotangent):
    params = tuple((member.astype(jnp.float32) for member in (tokens, w_query, w_key, w_value, w_output, w_inner, w_outer, b_query, b_value, b_output, b_inner, b_outer, gain_first, shift_first, gain_second, shift_second)))

    def wrapped(inputs):
        return forward(inputs[0], segment_ids, inputs[1], inputs[2], inputs[3], inputs[4], inputs[5], inputs[6], inputs[7], inputs[8], inputs[9], inputs[10], inputs[11], inputs[12], inputs[13], inputs[14], inputs[15])
    result, pullback = jax.vjp(wrapped, params)
    gradients = pullback(cotangent.astype(jnp.float32))[0]
    return (result.astype(jnp.bfloat16), gradients[0], gradients[1], gradients[2], gradients[3], gradients[4], gradients[5], gradients[6], gradients[7], gradients[8], gradients[9], gradients[10], gradients[11], gradients[12], gradients[13], gradients[14], gradients[15])
```

```python
import math

import jax
import jax.numpy as jnp
from jax import lax
from jax.experimental import pallas as pl
from jax.experimental.pallas import tpu as pltpu
from jax.sharding import PartitionSpec as P

H = 12
DH = 64


EPSILON = 1e-12
SCORE_SCALE = 0.125


def matmul(first_op, second_op):
    return jnp.dot(first_op, second_op, preferred_element_type=jnp.float32)


def matmul_tn(first_op, second_op):
    return lax.dot_general(
        first_op, second_op, (((0,), (0,)), ((), ())), preferred_element_type=jnp.float32
    )


def matmul_nt(first_op, second_op):
    return lax.dot_general(
        first_op, second_op, (((1,), (1,)), ((), ())), preferred_element_type=jnp.float32
    )


def norm_forward(values, gain_vec, shift_vec):
    center = values - jnp.mean(values, axis=-1, keepdims=True)
    inverse = lax.rsqrt(jnp.mean(center * center, axis=-1, keepdims=True) + EPSILON)
    normed = center * inverse
    return (normed * gain_vec + shift_vec, normed, inverse)


def norm_backward(upstream, normed, inverse, gain_vec):
    scaled = upstream * gain_vec
    back_grad = inverse * (
        scaled
        - jnp.mean(scaled, axis=-1, keepdims=True)
        - normed * jnp.mean(scaled * normed, axis=-1, keepdims=True)
    )
    return (back_grad, jnp.sum(upstream * normed, axis=0), jnp.sum(upstream, axis=0))


def gelu_parts(values):
    cumulative = 0.5 * (1.0 + lax.erf(values * 0.7071067811865476))
    return (
        values * cumulative,
        cumulative + values * jnp.exp(-0.5 * values * values) * 0.3989422804014327,
    )


def block_scores(query_heads, key_heads, seg_query, seg_key):
    raw_scores = (
        jnp.einsum("ishd,jshd->shij", query_heads, key_heads, preferred_element_type=jnp.float32)
        * SCORE_SCALE
    )
    allowed = (jnp.transpose(seg_query)[:, :, None] == jnp.transpose(seg_key)[:, None, :])[:, None]
    return jnp.where(allowed, jnp.exp(raw_scores), 0.0)


def attend_keys(query_heads, seg_query, carry_in, piece_rows):
    key_piece, value_piece, seg_piece = piece_rows
    row_count, seq_count, feature_count = key_piece.shape
    heads, head_size = (query_heads.shape[2], query_heads.shape[3])
    step_rows = math.gcd(row_count, 1024)
    block_count = row_count // step_rows
    key_blocks = key_piece.reshape(block_count, step_rows, seq_count, heads, head_size)
    value_blocks = value_piece.reshape(block_count, step_rows, seq_count, heads, head_size)
    seg_blocks = seg_piece.reshape(block_count, step_rows, seq_count)

    def attend_visit_block(running, element):
        key_block, value_block, seg_block = element
        unnorm = block_scores(query_heads, key_block, seg_query, seg_block)
        totals = running[0] + jnp.sum(unnorm, axis=-1)
        mixture = running[1] + jnp.einsum(
            "shij,jshd->ishd",
            unnorm.astype(jnp.bfloat16),
            value_block,
            preferred_element_type=jnp.float32,
        )
        return ((totals, mixture), None)

    result, unused = lax.scan(attend_visit_block, carry_in, (key_blocks, value_blocks, seg_blocks))
    return result


def key_side(query_heads, d_mixture, correction, seg_query, key_all, value_all, seg_all):
    row_count, seq_count, feature_count = key_all.shape
    heads, head_size = (query_heads.shape[2], query_heads.shape[3])
    step_rows = math.gcd(row_count, 1024)
    block_count = row_count // step_rows
    corr_cols = jnp.transpose(correction, (1, 2, 0))[..., None]
    key_blocks = key_all.reshape(block_count, step_rows, seq_count, heads, head_size)
    value_blocks = value_all.reshape(block_count, step_rows, seq_count, heads, head_size)
    seg_blocks = seg_all.reshape(block_count, step_rows, seq_count)

    def key_visit_block(dq_acc, element):
        key_block, value_block, seg_block = element
        unnorm = block_scores(query_heads, key_block, seg_query, seg_block)
        d_prob = jnp.einsum(
            "ishd,jshd->shij", d_mixture, value_block, preferred_element_type=jnp.float32
        )
        d_score = (unnorm * (d_prob - corr_cols)).astype(jnp.bfloat16)
        dq_acc = dq_acc + jnp.einsum(
            "shij,jshd->ishd", d_score, key_block, preferred_element_type=jnp.float32
        )
        d_key = (
            jnp.einsum("shij,ishd->jshd", d_score, query_heads, preferred_element_type=jnp.float32)
            * SCORE_SCALE
        )
        d_value = jnp.einsum(
            "shij,ishd->jshd",
            unnorm.astype(jnp.bfloat16),
            d_mixture,
            preferred_element_type=jnp.float32,
        )
        stacked = jnp.concatenate(
            [
                d_key.reshape(step_rows, seq_count, feature_count),
                d_value.reshape(step_rows, seq_count, feature_count),
            ],
            axis=-1,
        )
        return (dq_acc, stacked)

    dq_sum, stacked_all = lax.scan(
        key_visit_block,
        jnp.zeros(query_heads.shape, jnp.float32),
        (key_blocks, value_blocks, seg_blocks),
    )
    return (dq_sum, stacked_all.reshape(row_count, seq_count, 2 * feature_count))


def body(
    tokens,
    segment_ids,
    w_query,
    w_key,
    w_value,
    w_output,
    w_inner,
    w_outer,
    b_query,
    b_value,
    b_output,
    b_inner,
    b_outer,
    gain_first,
    shift_first,
    gain_second,
    shift_second,
    cotangent,
):
    tok_rows, seq_count, feature_count = tokens.shape
    rows_total = tok_rows * seq_count
    gathered = (
        lax.all_gather(w_query, "seq", axis=0, tiled=True),
        lax.all_gather(w_key, "seq", axis=0, tiled=True),
        lax.all_gather(w_value, "seq", axis=0, tiled=True),
        lax.all_gather(w_output, "seq", axis=0, tiled=True),
        lax.all_gather(w_inner, "seq", axis=0, tiled=True),
        lax.all_gather(w_outer, "seq", axis=0, tiled=True),
        lax.all_gather(b_query, "seq", axis=0, tiled=True),
        lax.all_gather(b_value, "seq", axis=0, tiled=True),
        lax.all_gather(b_output, "seq", axis=0, tiled=True),
        lax.all_gather(b_inner, "seq", axis=0, tiled=True),
        lax.all_gather(b_outer, "seq", axis=0, tiled=True),
        lax.all_gather(gain_first, "seq", axis=0, tiled=True),
        lax.all_gather(shift_first, "seq", axis=0, tiled=True),
        lax.all_gather(gain_second, "seq", axis=0, tiled=True),
        lax.all_gather(shift_second, "seq", axis=0, tiled=True),
    )
    query_weight, key_weight, value_weight, output_weight, inner_weight, outer_weight = gathered[:6]
    (
        query_bias,
        value_bias,
        output_bias,
        inner_bias,
        outer_bias,
        gain_one,
        shift_one,
        gain_two,
        shift_two,
    ) = [vector.astype(jnp.float32) for vector in gathered[6:]]
    flat_rows = tokens.reshape(rows_total, feature_count)
    flat_float = flat_rows.astype(jnp.float32)
    seg_local = jnp.transpose(segment_ids)
    queries = (matmul(flat_rows, query_weight) + query_bias).astype(jnp.bfloat16)
    key_rows = matmul(flat_rows, key_weight).astype(jnp.bfloat16)
    value_rows = (matmul(flat_rows, value_weight) + value_bias).astype(jnp.bfloat16)
    query_heads = queries.reshape(tok_rows, seq_count, H, DH)
    key_block_rows = key_rows.reshape(tok_rows, seq_count, feature_count)
    value_block_rows = value_rows.reshape(tok_rows, seq_count, feature_count)
    initial = (
        jnp.zeros((seq_count, H, tok_rows), jnp.float32),
        jnp.zeros((tok_rows, seq_count, H, DH), jnp.float32),
    )
    totals, mixture = attend_keys(
        query_heads,
        seg_local,
        initial,
        (
            lax.all_gather(key_block_rows, "ctx", axis=0, tiled=True),
            lax.all_gather(value_block_rows, "ctx", axis=0, tiled=True),
            lax.all_gather(seg_local, "ctx", axis=0, tiled=True),
        ),
    )
    denominator = jnp.transpose(totals, (2, 0, 1))[..., None]
    attended = mixture / denominator
    context = attended.astype(jnp.bfloat16).reshape(rows_total, feature_count)
    first_in = matmul(context, output_weight) + output_bias + flat_float
    hidden, normed_one, inverse_one = norm_forward(first_in, gain_one, shift_one)
    hidden_low = hidden.astype(jnp.bfloat16)
    inner_pre = matmul(hidden_low, inner_weight) + inner_bias
    activated, gelu_slope = gelu_parts(inner_pre)
    act_low = activated.astype(jnp.bfloat16)
    second_in = matmul(act_low, outer_weight) + outer_bias + hidden
    result, normed_two, inverse_two = norm_forward(second_in, gain_two, shift_two)
    layer_out = result.astype(jnp.bfloat16).reshape(tok_rows, seq_count, feature_count)
    upstream = cotangent.astype(jnp.float32).reshape(rows_total, feature_count)
    d_second, dgain_second, dshift_second = norm_backward(
        upstream, normed_two, inverse_two, gain_two
    )
    d_outer = d_second.astype(jnp.bfloat16)
    dbias_outer = jnp.sum(d_outer.astype(jnp.float32), axis=0)
    dweight_outer = matmul_tn(act_low, d_outer)
    d_inner = (matmul_nt(d_outer, outer_weight) * gelu_slope).astype(jnp.bfloat16)
    dbias_inner = jnp.sum(d_inner.astype(jnp.float32), axis=0)
    dweight_inner = matmul_tn(hidden_low, d_inner)
    d_hidden = matmul_nt(d_inner, inner_weight) + d_second
    d_first, dgain_first, dshift_first = norm_backward(d_hidden, normed_one, inverse_one, gain_one)
    d_branch = d_first.astype(jnp.bfloat16)
    dbias_output = jnp.sum(d_branch.astype(jnp.float32), axis=0)
    dweight_output = matmul_tn(context, d_branch)
    d_context = (
        matmul_nt(d_branch, output_weight).astype(jnp.bfloat16).reshape(tok_rows, seq_count, H, DH)
    )
    d_float = d_context.astype(jnp.float32)
    d_mixture = (d_float / denominator).astype(jnp.bfloat16)
    correction = jnp.sum(d_float * attended, axis=-1) / denominator[..., 0]
    key_all, value_all, seg_all = (
        lax.all_gather(key_block_rows, "ctx", axis=0, tiled=True),
        lax.all_gather(value_block_rows, "ctx", axis=0, tiled=True),
        lax.all_gather(seg_local, "ctx", axis=0, tiled=True),
    )
    dq_sum, term_rows = key_side(
        query_heads, d_mixture, correction, seg_local, key_all, value_all, seg_all
    )
    summed = lax.psum_scatter(term_rows, "ctx", scatter_dimension=0, tiled=True)
    d_query = (dq_sum * SCORE_SCALE).astype(jnp.bfloat16)
    d_key = summed[..., :feature_count].astype(jnp.bfloat16)
    d_value = summed[..., feature_count:].astype(jnp.bfloat16)
    dq_flat = d_query.reshape(rows_total, feature_count)
    dk_flat = d_key.reshape(rows_total, feature_count)
    dv_flat = d_value.reshape(rows_total, feature_count)
    dweight_query = matmul_tn(flat_rows, dq_flat)
    dweight_key = matmul_tn(flat_rows, dk_flat)
    dweight_value = matmul_tn(flat_rows, dv_flat)
    dbias_query = jnp.sum(dq_flat.astype(jnp.float32), axis=0)
    dbias_value = jnp.sum(dv_flat.astype(jnp.float32), axis=0)
    grad_tokens = (
        matmul_nt(dq_flat, query_weight)
        + matmul_nt(dk_flat, key_weight)
        + matmul_nt(dv_flat, value_weight)
        + d_first
    )
    shards = (
        lax.psum_scatter(
            dweight_query.astype(jnp.bfloat16), "seq", scatter_dimension=0, tiled=True
        ).astype(jnp.float32),
        lax.psum_scatter(
            dweight_key.astype(jnp.bfloat16), "seq", scatter_dimension=0, tiled=True
        ).astype(jnp.float32),
        lax.psum_scatter(
            dweight_value.astype(jnp.bfloat16), "seq", scatter_dimension=0, tiled=True
        ).astype(jnp.float32),
        lax.psum_scatter(
            dweight_output.astype(jnp.bfloat16), "seq", scatter_dimension=0, tiled=True
        ).astype(jnp.float32),
        lax.psum_scatter(
            dweight_inner.astype(jnp.bfloat16), "seq", scatter_dimension=0, tiled=True
        ).astype(jnp.float32),
        lax.psum_scatter(
            dweight_outer.astype(jnp.bfloat16), "seq", scatter_dimension=0, tiled=True
        ).astype(jnp.float32),
        lax.psum_scatter(
            dbias_query.astype(jnp.bfloat16), "seq", scatter_dimension=0, tiled=True
        ).astype(jnp.float32),
        lax.psum_scatter(
            dbias_value.astype(jnp.bfloat16), "seq", scatter_dimension=0, tiled=True
        ).astype(jnp.float32),
        lax.psum_scatter(
            dbias_output.astype(jnp.bfloat16), "seq", scatter_dimension=0, tiled=True
        ).astype(jnp.float32),
        lax.psum_scatter(
            dbias_inner.astype(jnp.bfloat16), "seq", scatter_dimension=0, tiled=True
        ).astype(jnp.float32),
        lax.psum_scatter(
            dbias_outer.astype(jnp.bfloat16), "seq", scatter_dimension=0, tiled=True
        ).astype(jnp.float32),
        lax.psum_scatter(
            dgain_first.astype(jnp.bfloat16), "seq", scatter_dimension=0, tiled=True
        ).astype(jnp.float32),
        lax.psum_scatter(
            dshift_first.astype(jnp.bfloat16), "seq", scatter_dimension=0, tiled=True
        ).astype(jnp.float32),
        lax.psum_scatter(
            dgain_second.astype(jnp.bfloat16), "seq", scatter_dimension=0, tiled=True
        ).astype(jnp.float32),
        lax.psum_scatter(
            dshift_second.astype(jnp.bfloat16), "seq", scatter_dimension=0, tiled=True
        ).astype(jnp.float32),
    )
    finals = lax.psum(
        (
            shards[0],
            shards[1],
            shards[2],
            shards[3],
            shards[4],
            shards[5],
            shards[6],
            shards[7],
            shards[8],
            shards[9],
            shards[10],
            shards[11],
            shards[12],
            shards[13],
            shards[14],
        ),
        "ctx",
    )
    return (
        layer_out,
        grad_tokens.reshape(tok_rows, seq_count, feature_count),
        finals[0],
        finals[1],
        finals[2],
        finals[3],
        finals[4],
        finals[5],
        finals[6],
        finals[7],
        finals[8],
        finals[9],
        finals[10],
        finals[11],
        finals[12],
        finals[13],
        finals[14],
    )


MESH = pl.DeviceIdType.MESH
BIG = 1e30
SEND, LAND = 0, 1


def place():
    seq, ctx = lax.axis_index("seq"), lax.axis_index("ctx")
    return seq, ctx


def remote(src, dst, send_sem, recv_sem, seq, ctx):
    return pltpu.make_async_remote_copy(
        src_ref=src,
        dst_ref=dst,
        send_sem=send_sem,
        recv_sem=recv_sem,
        device_id=(seq, ctx),
        device_id_type=MESH,
    )


def greet(seq, ctx):
    barrier = pltpu.get_barrier_semaphore()
    for hop in range(1, 8):
        pl.semaphore_signal(
            barrier, inc=1, device_id=(seq, lax.rem(ctx + hop, 8)), device_id_type=MESH
        )
    for hop in range(1, 4):
        pl.semaphore_signal(
            barrier, inc=1, device_id=(lax.rem(seq + hop, 4), ctx), device_id_type=MESH
        )
    pl.semaphore_wait(barrier, 10)


def flip(index, bit):
    low = lax.rem(index // bit, 2)
    return index + bit - 2 * bit * low


def head_window(group):
    start = group * 192
    inside = lax.rem(group, 2) * 64
    return pl.multiple_of(start - inside, 128), pl.multiple_of(inside, 64)


def stage_forward(
    x_ref,
    seg_ref,
    pack_ref,
    wq_ref,
    wk_ref,
    wv_ref,
    wo_ref,
    wi_ref,
    wu_ref,
    ctx_out,
    qa_out,
    ka_out,
    vt_out,
    ot_out,
    sum_out,
    xs_out,
    wg_out,
    vec_out,
    inner_bias_out,
    wo_out,
    wi_out,
    wu_out,
    seg_own,
    seg_all,
    pack_all,
    wo_full,
    wi_full,
    wu_full,
    key_rows,
    o_send,
    loc_sem,
    w_send,
    w_recv,
    x_send,
    x_recv,
    s_send,
    s_recv,
    p_send,
    p_recv,
    g_send,
    g_recv,
    o_ssem,
    o_rsem,
    out_sem,
):
    seq, ctx = place()
    mate, across = flip(seq, 1), flip(seq, 2)
    across_mate = flip(mate, 2)
    row = lax.rem(ctx, 2)
    beside = flip(ctx, 1)
    mirror = flip(ctx, 4)
    side, group = ctx // 4, lax.rem(ctx, 4)
    window, inside = head_window(group)

    chunks = [
        (wo_ref, lambda ref: ref, lambda owner: wo_full.at[owner], 96),
        (
            wi_ref,
            lambda ref: ref.at[:, 0:1536],
            lambda owner: wi_full.at[owner, :, 0:1536],
            96,
        ),
        (
            wi_ref,
            lambda ref: ref.at[:, 1536:3072],
            lambda owner: wi_full.at[owner, :, 1536:3072],
            96,
        ),
        (
            wu_ref,
            lambda ref: ref.at[0:384],
            lambda owner: wu_full.at[owner, 0:384],
            192,
        ),
        (
            wu_ref,
            lambda ref: ref.at[384:768],
            lambda owner: wu_full.at[owner, 384:768],
            192,
        ),
    ]

    def half(view, rows, which):
        return view.at[pl.ds(pl.multiple_of(which * rows, 32), rows)]

    def w_copy(k, leg):
        ref, cut, full, rows = chunks[k]
        if leg == 0:
            return remote(
                cut(ref), full(seq), w_send.at[k, 0], w_recv.at[k, 0], mate, ctx
            )
        if leg == 1:
            return remote(
                half(cut(ref), rows, row),
                half(full(seq), rows, row),
                w_send.at[k, 1],
                w_recv.at[k, 1],
                across,
                ctx,
            )
        which = row if leg in (2, 3) else 1 - row
        came = half(full(across), rows, which)
        target = (seq, beside) if leg == 2 else (mate, ctx)
        return remote(came, came, w_send.at[k, leg], w_recv.at[k, leg], *target)

    def w_landing(k, leg):
        ref, cut, full, rows = chunks[k]
        if leg == 0:
            spot = full(mate)
        elif leg == 1:
            spot = half(full(across), rows, row)
        elif leg == 2:
            spot = half(full(across), rows, 1 - row)
        elif leg == 3:
            spot = half(full(across_mate), rows, row)
        else:
            spot = half(full(across_mate), rows, 1 - row)
        return remote(spot, spot, w_send.at[k, leg], w_recv.at[k, leg], mate, ctx)

    group_refs = (wq_ref, wk_ref, wv_ref)

    def group_view(which):
        return group_refs[which].at[:, pl.ds(window, 256)]

    local = []
    for which in range(3):
        local.append(
            pltpu.make_async_copy(
                group_view(which), wg_out.at[which, seq], loc_sem.at[which]
            )
        )
    for k, (ref, cut, full, rows) in enumerate(chunks):
        local.append(pltpu.make_async_copy(cut(ref), full(seq), loc_sem.at[3 + k]))
    for which in range(2):
        seg_own[which] = jnp.broadcast_to(seg_ref[which : which + 1], (8, 128))
    own_block = pltpu.make_async_copy(
        x_ref.at[side], xs_out.at[ctx], loc_sem.at[8]
    )
    own_seg = pltpu.make_async_copy(seg_own.at[side], seg_all.at[ctx], loc_sem.at[9])
    own_pack = pltpu.make_async_copy(pack_ref, pack_all.at[seq], loc_sem.at[10])
    local += [own_block, own_seg, own_pack]
    for copy in local:
        copy.start()

    greet(seq, ctx)

    far = remote(
        x_ref.at[1 - side], xs_out.at[ctx], x_send.at[0], x_recv.at[0], seq, mirror
    )
    far.start()
    near = []
    square = []
    for hop in range(1, 4):
        other = side * 4 + lax.rem(group + hop, 4)
        square.append(other)
        near.append(
            remote(
                x_ref.at[side],
                xs_out.at[ctx],
                x_send.at[hop],
                x_recv.at[hop],
                seq,
                other,
            )
        )
        near[-1].start()
    segs = []
    for hop in range(1, 8):
        other = lax.rem(ctx + hop, 8)
        segs.append(
            remote(
                seg_own.at[other // 4],
                seg_all.at[ctx],
                s_send.at[hop],
                s_recv.at[hop],
                seq,
                other,
            )
        )
        segs[-1].start()
    packs, groups = [], []
    for hop in range(1, 4):
        other = lax.rem(seq + hop, 4)
        packs.append(
            remote(
                pack_ref, pack_all.at[seq], p_send.at[hop], p_recv.at[hop], other, ctx
            )
        )
        packs[-1].start()
    for which in range(3):
        for n, other in enumerate((mate, across)):
            groups.append(
                remote(
                    group_view(which),
                    wg_out.at[which, seq],
                    g_send.at[which, n],
                    g_recv.at[which, n],
                    other,
                    ctx,
                )
            )
            groups[-1].start()
    for k in range(len(chunks)):
        w_copy(k, 0).start()
        w_copy(k, 1).start()

    remote(
        x_ref.at[0], xs_out.at[mirror], x_send.at[0], x_recv.at[0], seq, mirror
    ).wait_recv()
    passed = []
    for n, other in enumerate(square):
        passed.append(
            remote(
                xs_out.at[mirror],
                xs_out.at[mirror],
                x_send.at[4 + n],
                x_recv.at[4 + n],
                seq,
                other,
            )
        )
        passed[-1].start()

    on = []
    for which in range(3):
        spot = wg_out.at[which, across]
        remote(
            spot, spot, g_send.at[which, 1], g_recv.at[which, 1], mate, ctx
        ).wait_recv()
        on.append(
            remote(spot, spot, g_send.at[which, 2], g_recv.at[which, 2], mate, ctx)
        )
        on[-1].start()

    def pass_across(k):
        w_landing(k, 1).wait_recv()
        w_copy(k, 2).start()
        w_copy(k, 3).start()

    def pass_beside(k):
        w_landing(k, 2).wait_recv()
        w_copy(k, 4).start()

    for which in range(3):
        local[which].wait()
        for n, owner in ((0, mate), (2, across_mate)):
            spot = wg_out.at[which, owner]
            remote(
                spot, spot, g_send.at[which, n], g_recv.at[which, n], mate, ctx
            ).wait_recv()
    own_pack.wait()
    for hop in range(1, 4):
        spot = pack_all.at[lax.rem(seq + 4 - hop, 4)]
        remote(spot, spot, p_send.at[hop], p_recv.at[hop], mate, ctx).wait_recv()
    own_seg.wait()
    for hop in range(1, 8):
        spot = seg_all.at[lax.rem(ctx + 8 - hop, 8)]
        remote(spot, spot, s_send.at[hop], s_recv.at[hop], seq, beside).wait_recv()

    lane = lax.broadcasted_iota(jnp.int32, (256, 768), 1)
    at = lax.broadcasted_iota(jnp.int32, (256, 768), 0)
    rows = jnp.zeros((8, 768), jnp.float32)
    for owner in range(4):
        chosen = ((lane == at + 192 * owner) & (at < 192)).astype(jnp.bfloat16)
        rows += matmul(pack_all[owner, 0:8, 0:256], chosen)
        inner_bias_out[owner : owner + 1] = pack_all[owner, 8:9].astype(jnp.float32)
    vec_out[...] = rows

    pass_across(0)

    own_block.wait()
    for hop in range(1, 4):
        spot = xs_out.at[side * 4 + lax.rem(group + 4 - hop, 4)]
        remote(spot, spot, x_send.at[hop], x_recv.at[hop], seq, beside).wait_recv()
    for n in range(3):
        other = lax.rem(side * 4 + 4, 8) + lax.rem(group + 3 - n, 4)
        spot = xs_out.at[other]
        remote(spot, spot, x_send.at[4 + n], x_recv.at[4 + n], seq, beside).wait_recv()
    pass_beside(0)
    pass_across(1)

    tokens = xs_out[...].reshape(1024, 768)
    own_rows = pack_all[group]
    qkv = []
    for which in range(3):
        weight = wg_out[which].reshape(768, 256)
        product = matmul_nt(weight.T, tokens)
        if which != 1:
            bias = own_rows[which // 2 : which // 2 + 1, 0:256].astype(jnp.float32)
            column = jnp.broadcast_to(bias, (128, 256)).T
            shifted = jnp.where(inside == 0, column, pltpu.roll(column, 64, 0))
            product = product + jnp.concatenate([shifted] * 8, axis=1)
        low = product.astype(jnp.bfloat16)
        if which == 0:
            low = low * jnp.bfloat16(SCORE_SCALE)
        qkv.append(low)

    number = jnp.concatenate([seg_all[block, 0:1] for block in range(8)], axis=1)
    hot = lax.broadcasted_iota(jnp.int32, (16, 1024), 0) == number
    query_marks = jnp.where(hot, 1.0, 0.0).astype(jnp.bfloat16)
    key_marks = jnp.where(hot, 0.0, -BIG).astype(jnp.bfloat16)
    blank = jnp.zeros((48, 1024), jnp.bfloat16)
    odd = inside != 0
    for head in range(3):
        spans = [
            jnp.where(
                odd, part[64 * head + 64 : 64 * head + 128], part[64 * head : 64 * head + 64]
            )
            for part in qkv
        ]
        qa_out[head] = jnp.concatenate([spans[0], query_marks, blank], axis=0)
        ka_out[head] = jnp.concatenate([spans[1], key_marks, blank], axis=0)
        vt_out[head] = spans[2]
    pass_beside(1)
    pass_across(2)

    for head in range(3):
        key_rows[...] = ka_out[head].T

        def attend(block, unused, head=head):
            lanes = pl.ds(pl.multiple_of(block * 256, 256), 256)
            scores = matmul(key_rows[...], qa_out[head, :, lanes])
            unnorm = jnp.exp(scores)
            total = jnp.sum(unnorm, axis=0, keepdims=True)
            mixture = matmul(vt_out[head], unnorm.astype(jnp.bfloat16))
            attended = mixture / total
            ot_out[head, :, lanes] = attended
            sum_out[head, :, lanes] = jnp.broadcast_to(total, (8, 256))
            o_send[64 * head : 64 * head + 64, lanes] = attended.astype(jnp.bfloat16)
            return unused

        lax.fori_loop(0, 4, attend, 0)
        if head == 0:
            pass_beside(2)
        if head == 1:
            pass_across(3)

    back = []
    my_rows = pl.ds(pl.multiple_of(group * 192, 64), 192)
    my_lanes = pl.ds(pl.multiple_of(side * 128, 128), 128)
    own_o = pltpu.make_async_copy(
        o_send.at[:, pl.ds(pl.multiple_of(ctx * 128, 128), 128)],
        ctx_out.at[my_rows, my_lanes],
        loc_sem.at[11],
    )
    own_o.start()
    for hop in range(1, 8):
        other = lax.rem(ctx + hop, 8)
        back.append(
            remote(
                o_send.at[:, pl.ds(pl.multiple_of(other * 128, 128), 128)],
                ctx_out.at[my_rows, my_lanes],
                o_ssem.at[hop],
                o_rsem.at[hop],
                seq,
                other,
            )
        )
        back[-1].start()
    pass_beside(3)
    pass_across(4)
    pass_beside(4)
    for k, (ref, cut, full, rows) in enumerate(chunks):
        local[3 + k].wait()
        for leg in (0, 3, 4):
            w_landing(k, leg).wait_recv()
        if k in (0, 2, 4):
            n = k // 2
            pltpu.make_async_copy(
                (wo_full, wi_full, wu_full)[n],
                (wo_out, wi_out, wu_out)[n],
                out_sem.at[n],
            ).start()
    own_o.wait()
    for hop in range(1, 8):
        other = lax.rem(ctx + 8 - hop, 8)
        spot = ctx_out.at[
            pl.ds(pl.multiple_of(lax.rem(other, 4) * 192, 64), 192),
            pl.ds(pl.multiple_of((other // 4) * 128, 128), 128),
        ]
        remote(spot, spot, o_ssem.at[hop], o_rsem.at[hop], seq, beside).wait_recv()
    far.wait_send()
    for copy in near + segs + packs + groups + passed + on + back:
        copy.wait_send()
    for k in range(len(chunks)):
        for leg in range(5):
            w_copy(k, leg).wait_send()
    for n in range(3):
        pltpu.make_async_copy(
            (wo_full, wi_full, wu_full)[n], (wo_out, wi_out, wu_out)[n], out_sem.at[n]
        ).wait()


def run_forward(x_rows, seg_rows, pack, wq, wk, wv, wo, wi, wu):
    f32, bf16 = jnp.float32, jnp.bfloat16
    vmem, anywhere = (
        pl.BlockSpec(memory_space=pltpu.VMEM),
        pl.BlockSpec(memory_space=pl.ANY),
    )
    shape = jax.ShapeDtypeStruct
    dma = pltpu.SemaphoreType.DMA
    return pl.pallas_call(
        stage_forward,
        name="stage_forward",
        out_shape=(
            shape((768, 256), bf16),
            shape((3, 128, 1024), bf16),
            shape((3, 128, 1024), bf16),
            shape((3, 64, 1024), bf16),
            shape((3, 64, 1024), f32),
            shape((3, 8, 1024), f32),
            shape((8, 128, 768), bf16),
            shape((3, 4, 192, 256), bf16),
            shape((8, 768), f32),
            shape((4, 768), f32),
            shape((4, 192, 768), bf16),
            shape((4, 192, 3072), bf16),
            shape((4, 768, 768), bf16),
        ),
        in_specs=[vmem] * 3 + [anywhere] * 6,
        out_specs=(vmem,) * 10 + (anywhere,) * 3,
        scratch_shapes=[
            pltpu.VMEM((2, 8, 128), jnp.int32),
            pltpu.VMEM((8, 8, 128), jnp.int32),
            pltpu.VMEM((4, 16, 768), bf16),
            pltpu.VMEM((4, 192, 768), bf16),
            pltpu.VMEM((4, 192, 3072), bf16),
            pltpu.VMEM((4, 768, 768), bf16),
            pltpu.VMEM((1024, 128), bf16),
            pltpu.VMEM((192, 1024), bf16),
            dma((12,)),
            dma((5, 5)),
            dma((5, 5)),
            dma((7,)),
            dma((7,)),
            dma((8,)),
            dma((8,)),
            dma((4,)),
            dma((4,)),
            dma((3, 3)),
            dma((3, 3)),
            dma((8,)),
            dma((8,)),
            dma((3,)),
        ],
        compiler_params=pltpu.CompilerParams(
            collective_id=1, has_side_effects=True, vmem_limit_bytes=60 * 2**20
        ),
    )(x_rows, seg_rows, pack, wq, wk, wv, wo, wi, wu)


def stage_backward(
    do_ref,
    qa_ref,
    ka_ref,
    vt_ref,
    ot_ref,
    sum_ref,
    xs_ref,
    wg_ref,
    vec_ref,
    gu_ref,
    gi_ref,
    go_ref,
    fu_out,
    fi_out,
    fo_out,
    fg_out,
    vec_out,
    bias_out,
    dx_out,
    own_u,
    own_i,
    own_o,
    core_u,
    core_i,
    core_o,
    xs_u,
    xs_i,
    xs_o,
    xr_u,
    xr_i,
    xr_o,
    sum_u,
    sum_i,
    sum_o,
    snd_u,
    snd_i,
    snd_o,
    rcv_u,
    rcv_i,
    rcv_o,
    fin_u,
    fin_i,
    fin_o,
    do_all,
    du_all,
    c_all,
    key_rows,
    value_rows,
    dk_acc,
    dv_acc,
    d_all,
    g_all,
    g_core,
    g_xs,
    g_xr,
    g_half,
    g_mir,
    dx_send,
    dx_recv,
    v_recv,
    v_sum,
    v_all,
    b_send,
    b_recv,
    loc_sem,
    r_send,
    r_recv,
    do_ssem,
    do_rsem,
    dx_ssem,
    dx_rsem,
    v_ssem,
    v_rsem,
    b_ssem,
    b_rsem,
    g_ssem,
    g_rsem,
):
    seq, ctx = place()
    mate, across = flip(seq, 1), flip(seq, 2)
    across_mate = flip(mate, 2)
    beside, paired, mirror = flip(ctx, 1), flip(ctx, 2), flip(ctx, 4)
    bit_y, bit_l, bit_h = lax.rem(ctx, 2), lax.rem(ctx // 2, 2), ctx // 4
    side, group = ctx // 4, lax.rem(ctx, 4)
    window, inside = head_window(group)
    f32, bf16 = jnp.float32, jnp.bfloat16

    buffers_u = (own_u, core_u, xs_u, xr_u, sum_u, snd_u, rcv_u, fin_u)
    buffers_i = (own_i, core_i, xs_i, xr_i, sum_i, snd_i, rcv_i, fin_i)
    buffers_o = (own_o, core_o, xs_o, xr_o, sum_o, snd_o, rcv_o, fin_o)
    chunks = [
        (gu_ref, fu_out, buffers_u, 0, 384, 0, 768),
        (gu_ref, fu_out, buffers_u, 384, 384, 0, 768),
        (gi_ref, fi_out, buffers_i, 0, 192, 0, 1536),
        (gi_ref, fi_out, buffers_i, 0, 192, 1536, 1536),
        (go_ref, fo_out, buffers_o, 0, 192, 0, 768),
    ]

    def reduce_steps(k):
        grad, out, bufs, row, rows, col, cols = chunks[k]
        own, core, xsend, xrecv, total, snd, rcv, fin = bufs
        rr, cc = pl.ds(row, rows), pl.ds(col, cols)
        half = cols // 2
        mine = pl.ds(pl.multiple_of(col + bit_y * half, 128), half)
        other = pl.ds(pl.multiple_of(col + (1 - bit_y) * half, 128), half)

        def cut(r, n, bit):
            return pl.ds(pl.multiple_of(r + bit * n, 16), n)

        r_l = row + bit_l * (rows // 2)
        keep_l, give_l = cut(row, rows // 2, bit_l), cut(row, rows // 2, 1 - bit_l)
        keep_h = cut(r_l, rows // 4, bit_h)
        give_h = cut(r_l, rows // 4, 1 - bit_h)
        sems = lambda leg: (r_send.at[k, leg], r_recv.at[k, leg])
        to_core = [
            remote(
                grad.at[mate, rr, cc], core.at[0, rr, cc], *sems(0), mate, ctx
            ),
            remote(
                grad.at[across_mate, rr, cc], core.at[1, rr, cc], *sems(1), mate, ctx
            ),
        ]
        loads = [
            pltpu.make_async_copy(
                grad.at[seq, rr, cc], own.at[0, rr, cc], loc_sem.at[k, 0]
            ),
            pltpu.make_async_copy(
                grad.at[across, rr, cc], own.at[1, rr, cc], loc_sem.at[k, 1]
            ),
        ]
        to_x = remote(xsend.at[rr, cc], xrecv.at[rr, cc], *sems(2), across, ctx)
        to_y = remote(snd.at[rr, other], rcv.at[rr, other], *sems(3), seq, beside)
        at_y = remote(snd.at[rr, mine], rcv.at[rr, mine], *sems(3), seq, beside)
        spot_h = cut(row, rows // 2, 1 - bit_l)
        spot_h = pl.ds(spot_h.start, rows // 4)
        to_l = remote(snd.at[give_l, mine], rcv.at[give_l, other], *sems(4), seq, paired)
        at_l = remote(snd.at[keep_l, mine], rcv.at[keep_l, other], *sems(4), seq, paired)
        to_h = remote(snd.at[give_h, mine], rcv.at[spot_h, other], *sems(5), seq, mirror)

        def spread(span, lanes, leg, target):
            spot = fin.at[span, lanes]
            return remote(spot, spot, *sems(leg), seq, target)

        def begin():
            for copy in to_core + loads:
                copy.start()

        def cores():
            for copy in to_core:
                copy.wait_recv()
            for copy in loads:
                copy.wait()
            xsend[rr, cc] = (
                own[1, rr, cc].astype(f32) + core[1, rr, cc].astype(f32)
            ).astype(bf16)
            to_x.start()

        def planes():
            to_x.wait_recv()
            summed = (
                own[0, rr, cc].astype(f32)
                + core[0, rr, cc].astype(f32)
                + xrecv[rr, cc].astype(f32)
            )
            total[rr, cc] = summed
            snd[rr, cc] = summed.astype(bf16)
            to_y.start()

        def besides():
            at_y.wait_recv()
            to_y.wait_send()
            for span, copy in ((give_l, to_l), (keep_l, None)):
                summed = total[span, mine] + rcv[span, mine].astype(f32)
                if copy is None:
                    total[span, mine] = summed
                else:
                    snd[span, mine] = summed.astype(bf16)
                    copy.start()

        def pairs():
            at_l.wait_recv()
            for span, copy in ((give_h, to_h), (keep_h, None)):
                summed = total[span, mine] + rcv[span, other].astype(f32)
                if copy is None:
                    total[span, mine] = summed
                else:
                    snd[span, mine] = summed.astype(bf16)
                    copy.start()

        def mirrors():
            to_h.wait_recv()
            fin[keep_h, mine] = (
                total[keep_h, mine] + rcv[spot_h, other].astype(f32)
            ).astype(bf16)
            spread(keep_h, mine, 6, mirror).start()

        def back_h():
            spread(give_h, mine, 6, mirror).wait_recv()
            spread(keep_l, mine, 7, paired).start()

        def back_l():
            spread(give_l, mine, 7, paired).wait_recv()
            spread(rr, mine, 8, beside).start()

        def back_y():
            spread(rr, other, 8, beside).wait_recv()
            pltpu.make_async_copy(
                fin.at[rr, cc], out.at[rr, cc], loc_sem.at[k, 2]
            ).start()

        def end():
            for copy in to_core:
                copy.wait_send()
            to_x.wait_send()
            to_l.wait_send()
            to_h.wait_send()
            spread(keep_h, mine, 6, mirror).wait_send()
            spread(keep_l, mine, 7, paired).wait_send()
            spread(rr, mine, 8, beside).wait_send()
            pltpu.make_async_copy(
                fin.at[rr, cc], out.at[rr, cc], loc_sem.at[k, 2]
            ).wait()

        return [
            begin,
            cores,
            planes,
            besides,
            pairs,
            mirrors,
            back_h,
            back_l,
            back_y,
            end,
        ]

    steps = [reduce_steps(k) for k in range(5)]

    def run(*pairs):
        for k, n in pairs:
            steps[k][n]()

    for head_row in range(3):
        d_all[head_row] = jnp.zeros((256, 1024), bf16)

    greet(seq, ctx)

    my_rows = pl.ds(pl.multiple_of(group * 192, 64), 192)
    sent = []
    own_do = pltpu.make_async_copy(
        do_ref.at[my_rows, pl.ds(pl.multiple_of(side * 128, 128), 128)],
        do_all.at[:, pl.ds(pl.multiple_of(ctx * 128, 128), 128)],
        loc_sem.at[5, 0],
    )
    own_do.start()
    for hop in range(1, 8):
        target = lax.rem(ctx + hop, 8)
        sent.append(
            remote(
                do_ref.at[
                    pl.ds(pl.multiple_of(lax.rem(target, 4) * 192, 64), 192),
                    pl.ds(pl.multiple_of((target // 4) * 128, 128), 128),
                ],
                do_all.at[:, pl.ds(pl.multiple_of(ctx * 128, 128), 128)],
                do_ssem.at[hop],
                do_rsem.at[hop],
                seq,
                target,
            )
        )
        sent[-1].start()
    own_vec = pltpu.make_async_copy(vec_ref.at[seq], v_recv.at[seq], loc_sem.at[5, 1])
    own_vec.start()
    for hop in range(1, 4):
        target = lax.rem(seq + hop, 4)
        sent.append(
            remote(
                vec_ref.at[target],
                v_recv.at[seq],
                v_ssem.at[0, hop],
                v_rsem.at[0, hop],
                target,
                ctx,
            )
        )
        sent[-1].start()
    run(*((k, 0) for k in range(5)))
    run(*((k, 1) for k in range(5)))

    own_vec.wait()
    for hop in range(1, 4):
        spot = v_recv.at[lax.rem(seq + 4 - hop, 4)]
        remote(
            spot, spot, v_ssem.at[0, hop], v_rsem.at[0, hop], mate, ctx
        ).wait_recv()
    v_sum[...] = v_recv[0] + v_recv[1] + v_recv[2] + v_recv[3]
    for hop in range(1, 8):
        target = lax.rem(ctx + hop, 8)
        sent.append(
            remote(
                v_sum,
                v_all.at[ctx],
                v_ssem.at[1, hop],
                v_rsem.at[1, hop],
                seq,
                target,
            )
        )
        sent[-1].start()

    own_do.wait()
    for hop in range(1, 8):
        source = lax.rem(ctx + 8 - hop, 8)
        spot = do_all.at[:, pl.ds(pl.multiple_of(source * 128, 128), 128)]
        remote(spot, spot, do_ssem.at[hop], do_rsem.at[hop], seq, beside).wait_recv()

    for head in range(3):
        span = slice(64 * head, 64 * head + 64)
        total = sum_ref[head, 0:1]
        d_out = do_all[span].astype(f32)
        du_all[...] = (d_out / total).astype(bf16)
        c_all[...] = jnp.sum(d_out * ot_ref[head], axis=0, keepdims=True) / total
        key_rows[...] = ka_ref[head].T
        value_rows[...] = vt_ref[head].T
        dk_acc[...] = jnp.zeros((64, 1024), f32)
        dv_acc[...] = jnp.zeros((64, 1024), f32)
        at = pl.ds(pl.multiple_of(inside + 64 * head, 64), 64)

        def attend(block, unused, head=head, at=at):
            lanes = pl.ds(pl.multiple_of(block * 256, 256), 256)
            scores = matmul(key_rows[...], qa_ref[head, :, lanes])
            unnorm = jnp.exp(scores)
            d_prob = matmul(value_rows[...], du_all[:, lanes])
            d_score = (unnorm * (d_prob - c_all[:, lanes])).astype(bf16)
            d_query = matmul(ka_ref[head, 0:64], d_score) * SCORE_SCALE
            d_all[0, at, lanes] = d_query.astype(bf16)
            dk_acc[...] += matmul_nt(qa_ref[head, 0:64, lanes], d_score)
            dv_acc[...] += matmul_nt(du_all[:, lanes], unnorm.astype(bf16))
            return unused

        lax.fori_loop(0, 4, attend, 0)
        d_all[1, at] = dk_acc[...].astype(bf16)
        d_all[2, at] = dv_acc[...].astype(bf16)
        if head == 0:
            run((0, 2))
        if head == 1:
            run((0, 3))

    tokens = xs_ref[...].reshape(1024, 768)
    ones = jnp.ones((16, 1024), bf16)
    for which in range(3):
        product = matmul(d_all[which], tokens).astype(bf16)
        g_all[which] = product.T.reshape(4, 192, 256)
        if which != 1:
            b_send[which // 2] = matmul_nt(ones, d_all[which])[0:8]
    to_core = [
        remote(
            g_all.at[which, owner],
            g_core.at[which, n],
            g_ssem.at[which, n],
            g_rsem.at[which, n],
            mate,
            ctx,
        )
        for which in range(3)
        for n, owner in ((0, mate), (1, across_mate))
    ]
    for copy in to_core:
        copy.start()
    own_bias = pltpu.make_async_copy(
        b_send, b_recv.at[seq * 2 + side], loc_sem.at[5, 2]
    )

    for hop in range(8):
        target = lax.rem(ctx + hop, 8)
        copy = remote(
            b_send,
            b_recv.at[seq * 2 + side],
            b_ssem.at[hop],
            b_rsem.at[seq * 2 + side],
            group,
            target,
        )
        if hop == 0:

            @pl.when(group == seq)
            def _():
                own_bias.start()

            @pl.when(group != seq)
            def _(copy=copy):
                copy.start()
        else:
            copy.start()

    run((1, 2), (0, 4))
    for part in range(4):
        lanes = slice(256 * part, 256 * part + 256)
        share = matmul(wg_ref[0].reshape(768, 256), d_all[0, :, lanes])
        for which in (1, 2):
            share += matmul(wg_ref[which].reshape(768, 256), d_all[which, :, lanes])
        dx_send[:, lanes] = share.astype(bf16)
    own_dx = pltpu.make_async_copy(
        dx_send.at[:, pl.ds(pl.multiple_of(ctx * 128, 128), 128)],
        dx_recv.at[side, group],
        loc_sem.at[6, 0],
    )
    own_dx.start()
    for hop in range(1, 8):
        target = lax.rem(ctx + hop, 8)
        sent.append(
            remote(
                dx_send.at[:, pl.ds(pl.multiple_of(target * 128, 128), 128)],
                dx_recv.at[side, group],
                dx_ssem.at[hop],
                dx_rsem.at[hop],
                seq,
                target,
            )
        )
        sent[-1].start()

    for copy in to_core:
        copy.wait_recv()
    for which in range(3):
        g_xs[which] = (
            g_all[which, across].astype(f32) + g_core[which, 1].astype(f32)
        ).astype(bf16)
    to_x = remote(g_xs, g_xr, g_ssem.at[3, 0], g_rsem.at[3, 0], across, ctx)
    to_x.start()

    run((1, 3), (0, 5), (2, 2), (1, 4), (0, 6))

    to_x.wait_recv()
    for which in range(3):
        summed = (
            g_all[which, seq].astype(f32)
            + g_core[which, 0].astype(f32)
            + g_xr[which].astype(f32)
        )
        g_half[which] = summed.astype(bf16)
    keep = pl.ds(pl.multiple_of(side * 96, 32), 96)
    give = pl.ds(pl.multiple_of((1 - side) * 96, 32), 96)
    to_m = remote(
        g_half.at[:, give], g_mir, g_ssem.at[3, 1], g_rsem.at[3, 1], seq, mirror
    )
    to_m.start()

    run((1, 5), (2, 3), (0, 7), (1, 6), (2, 4))

    to_m.wait_recv()
    for which in range(3):
        fg_out[group, which, keep] = (
            g_half[which, keep].astype(f32) + g_mir[which].astype(f32)
        ).astype(bf16)
    spot = fg_out.at[group, :, keep]
    square = [side * 4 + lax.rem(group + hop, 4) for hop in range(1, 4)]
    ups = [remote(spot, spot, g_ssem.at[4, 0], g_rsem.at[4, 0], seq, mirror)]
    for n, target in enumerate(square):
        ups.append(
            remote(spot, spot, g_ssem.at[5, n], g_rsem.at[5, n], seq, target)
        )
    for copy in ups:
        copy.start()

    run((1, 7), (3, 2), (2, 5), (0, 8))

    theirs = fg_out.at[group, :, give]
    remote(
        theirs, theirs, g_ssem.at[4, 0], g_rsem.at[4, 0], seq, mirror
    ).wait_recv()
    for n, target in enumerate(square):
        ups.append(
            remote(theirs, theirs, g_ssem.at[6, n], g_rsem.at[6, n], seq, target)
        )
        ups[-1].start()

    run((2, 6), (3, 3), (4, 2), (1, 8), (2, 7), (3, 4), (4, 3))

    own_dx.wait()
    for hop in range(1, 8):
        source = lax.rem(ctx + 8 - hop, 8)
        spot = dx_recv.at[source // 4, lax.rem(source, 4)]
        remote(spot, spot, dx_ssem.at[hop], dx_rsem.at[hop], seq, beside).wait_recv()
    for which in range(2):
        share = dx_recv[which, 0].astype(f32)
        for n in range(1, 4):
            share += dx_recv[which, n].astype(f32)
        dx_out[which] = share.T
    for hop in range(1, 8):
        source = lax.rem(ctx + 8 - hop, 8)
        spot = v_all.at[source]
        remote(
            spot, spot, v_ssem.at[1, hop], v_rsem.at[1, hop], seq, beside
        ).wait_recv()
    v_all[ctx] = v_sum[...]
    gathered = v_all[0]
    for n in range(1, 8):
        gathered += v_all[n]
    vec_out[...] = gathered

    run((3, 5), (4, 4), (3, 6), (4, 5), (2, 8), (3, 7), (4, 6), (4, 7), (3, 8), (4, 8))

    for n in range(8):
        sender = n // 2
        spot = b_recv.at[n]
        arrival = remote(
            spot, spot, b_ssem.at[0], b_rsem.at[n], lax.rem(seq + 1, 4), ctx
        )
        here = (sender == seq) & (lax.rem(n, 2) == side) & (group == seq)

        @pl.when(here)
        def _():
            own_bias.wait()

        @pl.when(jnp.logical_not(here))
        def _(arrival=arrival):
            arrival.wait_recv()

    row_sum = b_recv[0]
    for n in range(1, 8):
        row_sum += b_recv[n]
    bias_out[...] = row_sum
    for n in range(3):
        spot = fg_out.at[lax.rem(group + 3 - n, 4), :, keep]
        remote(spot, spot, g_ssem.at[5, n], g_rsem.at[5, n], seq, beside).wait_recv()
        spot = fg_out.at[lax.rem(group + 3 - n, 4), :, give]
        remote(spot, spot, g_ssem.at[6, n], g_rsem.at[6, n], seq, beside).wait_recv()

    run(*((k, 9) for k in range(5)))
    for copy in sent + to_core + [to_x, to_m] + ups:
        copy.wait_send()
    for hop in range(8):
        target = lax.rem(ctx + hop, 8)
        copy = remote(
            b_send,
            b_recv.at[seq * 2 + side],
            b_ssem.at[hop],
            b_rsem.at[seq * 2 + side],
            group,
            target,
        )
        if hop == 0:

            @pl.when(group != seq)
            def _(copy=copy):
                copy.wait_send()
        else:
            copy.wait_send()


def run_backward(do_t, qa, ka, vt, ot, sums, xs, wg, vec, gu, gi, go):
    f32, bf16 = jnp.float32, jnp.bfloat16
    vmem, anywhere = (
        pl.BlockSpec(memory_space=pltpu.VMEM),
        pl.BlockSpec(memory_space=pl.ANY),
    )
    shape = jax.ShapeDtypeStruct
    dma = pltpu.SemaphoreType.DMA
    sizes = ((768, 768), (192, 3072), (192, 768))

    def each(kind, lead=()):
        return [pltpu.VMEM(lead + size, kind) for size in sizes]

    return pl.pallas_call(
        stage_backward,
        name="stage_backward",
        out_shape=(
            shape((768, 768), bf16),
            shape((192, 3072), bf16),
            shape((192, 768), bf16),
            shape((4, 3, 192, 256), bf16),
            shape((16, 128), f32),
            shape((2, 8, 256), f32),
            shape((2, 128, 768), f32),
        ),
        in_specs=[vmem] * 9 + [anywhere] * 3,
        out_specs=(anywhere,) * 3 + (vmem,) * 4,
        scratch_shapes=each(bf16, (2,))
        + each(bf16, (2,))
        + each(bf16)
        + each(bf16)
        + each(f32)
        + each(bf16)
        + each(bf16)
        + each(bf16)
        + [
            pltpu.VMEM((192, 1024), bf16),
            pltpu.VMEM((64, 1024), bf16),
            pltpu.VMEM((1, 1024), f32),
            pltpu.VMEM((1024, 128), bf16),
            pltpu.VMEM((1024, 64), bf16),
            pltpu.VMEM((64, 1024), f32),
            pltpu.VMEM((64, 1024), f32),
            pltpu.VMEM((3, 256, 1024), bf16),
            pltpu.VMEM((3, 4, 192, 256), bf16),
            pltpu.VMEM((3, 2, 192, 256), bf16),
            pltpu.VMEM((3, 192, 256), bf16),
            pltpu.VMEM((3, 192, 256), bf16),
            pltpu.VMEM((3, 192, 256), bf16),
            pltpu.VMEM((3, 96, 256), bf16),
            pltpu.VMEM((768, 1024), bf16),
            pltpu.VMEM((2, 4, 768, 128), bf16),
            pltpu.VMEM((4, 16, 128), f32),
            pltpu.VMEM((16, 128), f32),
            pltpu.VMEM((8, 16, 128), f32),
            pltpu.VMEM((2, 8, 256), f32),
            pltpu.VMEM((8, 2, 8, 256), f32),
            dma((7, 3)),
            dma((5, 9)),
            dma((5, 9)),
            dma((8,)),
            dma((8,)),
            dma((8,)),
            dma((8,)),
            dma((2, 8)),
            dma((2, 8)),
            dma((8,)),
            dma((8,)),
            dma((7, 3)),
            dma((7, 3)),
        ],
        compiler_params=pltpu.CompilerParams(
            collective_id=2, has_side_effects=True, vmem_limit_bytes=62 * 2**20
        ),
    )(do_t, qa, ka, vt, ot, sums, xs, wg, vec, gu, gi, go)


def fast_body(
    tokens,
    segment_ids,
    w_query,
    w_key,
    w_value,
    w_output,
    w_inner,
    w_outer,
    b_query,
    b_value,
    b_output,
    b_inner,
    b_outer,
    gain_first,
    shift_first,
    gain_second,
    shift_second,
    cotangent,
):
    x_rows = jnp.transpose(tokens, (1, 0, 2))
    gap = jnp.zeros((576,), jnp.bfloat16)
    flat = []
    for vector in (
        b_query,
        b_value,
        b_output,
        b_outer,
        gain_first,
        shift_first,
        gain_second,
        shift_second,
    ):
        flat += [vector, gap]
    flat += [b_inner, jnp.zeros((7 * 768,), jnp.bfloat16)]
    pack = jnp.concatenate(flat).reshape(16, 768)
    (
        context_t,
        qa,
        ka,
        vt,
        ot,
        sums,
        xs,
        wg,
        vec,
        inner_bias,
        output_weight,
        inner_weight,
        outer_weight,
    ) = run_forward(
        x_rows, segment_ids, pack, w_query, w_key, w_value, w_output, w_inner, w_outer
    )
    output_weight = output_weight.reshape(768, 768)
    inner_weight = inner_weight.reshape(768, 3072)
    outer_weight = outer_weight.reshape(3072, 768)
    output_bias, outer_bias, gain_one, shift_one, gain_two, shift_two = [
        vec[n] for n in range(2, 8)
    ]
    inner_bias = inner_bias.reshape(3072)
    flat_float = x_rows.reshape(256, 768).astype(jnp.float32)
    context = context_t.T
    first_in = matmul(context, output_weight) + output_bias + flat_float
    hidden, normed_one, inverse_one = norm_forward(first_in, gain_one, shift_one)
    hidden_low = hidden.astype(jnp.bfloat16)
    inner_pre = matmul(hidden_low, inner_weight) + inner_bias
    activated, gelu_slope = gelu_parts(inner_pre)
    act_low = activated.astype(jnp.bfloat16)
    second_in = matmul(act_low, outer_weight) + outer_bias + hidden
    result, normed_two, inverse_two = norm_forward(second_in, gain_two, shift_two)
    layer_out = jnp.transpose(result.astype(jnp.bfloat16).reshape(2, 128, 768), (1, 0, 2))
    upstream = jnp.transpose(cotangent, (1, 0, 2)).astype(jnp.float32).reshape(256, 768)
    d_second, dgain_second, dshift_second = norm_backward(
        upstream, normed_two, inverse_two, gain_two
    )
    d_outer = d_second.astype(jnp.bfloat16)
    dbias_outer = jnp.sum(d_outer.astype(jnp.float32), axis=0)
    dweight_outer = matmul_tn(act_low, d_outer).astype(jnp.bfloat16)
    d_inner = (matmul_nt(d_outer, outer_weight) * gelu_slope).astype(jnp.bfloat16)
    dbias_inner = jnp.sum(d_inner.astype(jnp.float32), axis=0)
    dweight_inner = matmul_tn(hidden_low, d_inner).astype(jnp.bfloat16)
    d_hidden = matmul_nt(d_inner, inner_weight) + d_second
    d_first, dgain_first, dshift_first = norm_backward(
        d_hidden, normed_one, inverse_one, gain_one
    )
    d_branch = d_first.astype(jnp.bfloat16)
    dbias_output = jnp.sum(d_branch.astype(jnp.float32), axis=0)
    dweight_output = matmul_tn(context, d_branch).astype(jnp.bfloat16)
    do_t = matmul_nt(output_weight, d_branch).astype(jnp.bfloat16)
    vectors = jnp.concatenate(
        [
            vector.reshape(4, 192)
            for vector in (
                dbias_output,
                dbias_outer,
                dgain_first,
                dshift_first,
                dgain_second,
                dshift_second,
            )
        ]
        + [dbias_inner.reshape(4, 768), jnp.zeros((4, 128), jnp.float32)],
        axis=1,
    ).reshape(4, 16, 128)
    fu, fi, fo, fg, vec_sum, bias_sum, dx = run_backward(
        do_t,
        qa,
        ka,
        vt,
        ot,
        sums,
        xs,
        wg,
        vectors,
        dweight_outer.reshape(4, 768, 768),
        dweight_inner.reshape(4, 192, 3072),
        dweight_output.reshape(4, 192, 768),
    )
    grad_tokens = jnp.transpose(dx + d_first.reshape(2, 128, 768), (1, 0, 2))

    def widen(part):
        tiles = part.astype(jnp.float32)
        return jnp.concatenate(
            [
                tiles[0, :, 0:128],
                tiles[0, :, 128:256] + tiles[1, :, 0:128],
                tiles[1, :, 128:256],
                tiles[2, :, 0:128],
                tiles[2, :, 128:256] + tiles[3, :, 0:128],
                tiles[3, :, 128:256],
            ],
            axis=1,
        )

    line = vec_sum.reshape(2048)
    odd = lax.rem(lax.axis_index("seq"), 2) == 1

    def bias_row(n):
        return jnp.where(odd, bias_sum[n, 0, 64:256], bias_sum[n, 0, 0:192])

    return (
        layer_out,
        grad_tokens,
        widen(fg[:, 0]),
        widen(fg[:, 1]),
        widen(fg[:, 2]),
        fo.astype(jnp.float32),
        fi.astype(jnp.float32),
        fu.astype(jnp.float32),
        bias_row(0),
        bias_row(1),
        line[0:192],
        line[1152:1920],
        line[192:384],
        line[384:576],
        line[576:768],
        line[768:960],
        line[960:1152],
    )


def solution(mesh):
    in_specs = (
        P("ctx", "seq", None),
        P("seq", "ctx"),
        P("seq", None),
        P("seq", None),
        P("seq", None),
        P("seq", None),
        P("seq", None),
        P("seq", None),
        P("seq"),
        P("seq"),
        P("seq"),
        P("seq"),
        P("seq"),
        P("seq"),
        P("seq"),
        P("seq"),
        P("seq"),
        P("ctx", "seq", None),
    )
    out_specs = (
        P("ctx", "seq", None),
        P("ctx", "seq", None),
        P("seq", None),
        P("seq", None),
        P("seq", None),
        P("seq", None),
        P("seq", None),
        P("seq", None),
        P("seq"),
        P("seq"),
        P("seq"),
        P("seq"),
        P("seq"),
        P("seq"),
        P("seq"),
        P("seq"),
        P("seq"),
    )
    small = mesh.shape["seq"] == 4 and mesh.shape["ctx"] == 8
    step = fast_body if small else body
    return jax.shard_map(step, mesh=mesh, in_specs=in_specs, out_specs=out_specs, check_vma=False)
```

```python
import contextlib
import math
import types

import jax
import jax.numpy as jnp
from jax import lax
from jax.experimental import pallas as pl
from jax.experimental.pallas import tpu as pltpu
from jax.sharding import PartitionSpec as P

H = 12
DH = 64


EPSILON = 1e-12
SCORE_SCALE = 0.125


def matmul(first_op, second_op):
    return jnp.dot(first_op, second_op, preferred_element_type=jnp.float32)


def matmul_tn(first_op, second_op):
    return lax.dot_general(
        first_op, second_op, (((0,), (0,)), ((), ())), preferred_element_type=jnp.float32
    )


def matmul_nt(first_op, second_op):
    return lax.dot_general(
        first_op, second_op, (((1,), (1,)), ((), ())), preferred_element_type=jnp.float32
    )


def norm_forward(values, gain_vec, shift_vec):
    center = values - jnp.mean(values, axis=-1, keepdims=True)
    inverse = lax.rsqrt(jnp.mean(center * center, axis=-1, keepdims=True) + EPSILON)
    normed = center * inverse
    return (normed * gain_vec + shift_vec, normed, inverse)


def norm_backward(upstream, normed, inverse, gain_vec):
    scaled = upstream * gain_vec
    back_grad = inverse * (
        scaled
        - jnp.mean(scaled, axis=-1, keepdims=True)
        - normed * jnp.mean(scaled * normed, axis=-1, keepdims=True)
    )
    return (back_grad, jnp.sum(upstream * normed, axis=0), jnp.sum(upstream, axis=0))


def gelu_parts(values):
    cumulative = 0.5 * (1.0 + lax.erf(values * 0.7071067811865476))
    return (
        values * cumulative,
        cumulative + values * jnp.exp(-0.5 * values * values) * 0.3989422804014327,
    )


def block_scores(query_heads, key_heads, seg_query, seg_key):
    raw_scores = (
        jnp.einsum("ishd,jshd->shij", query_heads, key_heads, preferred_element_type=jnp.float32)
        * SCORE_SCALE
    )
    allowed = (jnp.transpose(seg_query)[:, :, None] == jnp.transpose(seg_key)[:, None, :])[:, None]
    return jnp.where(allowed, jnp.exp(raw_scores), 0.0)


def attend_keys(query_heads, seg_query, carry_in, piece_rows):
    key_piece, value_piece, seg_piece = piece_rows
    row_count, seq_count, feature_count = key_piece.shape
    heads, head_size = (query_heads.shape[2], query_heads.shape[3])
    step_rows = math.gcd(row_count, 1024)
    block_count = row_count // step_rows
    key_blocks = key_piece.reshape(block_count, step_rows, seq_count, heads, head_size)
    value_blocks = value_piece.reshape(block_count, step_rows, seq_count, heads, head_size)
    seg_blocks = seg_piece.reshape(block_count, step_rows, seq_count)

    def attend_visit_block(running, element):
        key_block, value_block, seg_block = element
        unnorm = block_scores(query_heads, key_block, seg_query, seg_block)
        totals = running[0] + jnp.sum(unnorm, axis=-1)
        mixture = running[1] + jnp.einsum(
            "shij,jshd->ishd",
            unnorm.astype(jnp.bfloat16),
            value_block,
            preferred_element_type=jnp.float32,
        )
        return ((totals, mixture), None)

    result, unused = lax.scan(attend_visit_block, carry_in, (key_blocks, value_blocks, seg_blocks))
    return result


def key_side(query_heads, d_mixture, correction, seg_query, key_all, value_all, seg_all):
    row_count, seq_count, feature_count = key_all.shape
    heads, head_size = (query_heads.shape[2], query_heads.shape[3])
    step_rows = math.gcd(row_count, 1024)
    block_count = row_count // step_rows
    corr_cols = jnp.transpose(correction, (1, 2, 0))[..., None]
    key_blocks = key_all.reshape(block_count, step_rows, seq_count, heads, head_size)
    value_blocks = value_all.reshape(block_count, step_rows, seq_count, heads, head_size)
    seg_blocks = seg_all.reshape(block_count, step_rows, seq_count)

    def key_visit_block(dq_acc, element):
        key_block, value_block, seg_block = element
        unnorm = block_scores(query_heads, key_block, seg_query, seg_block)
        d_prob = jnp.einsum(
            "ishd,jshd->shij", d_mixture, value_block, preferred_element_type=jnp.float32
        )
        d_score = (unnorm * (d_prob - corr_cols)).astype(jnp.bfloat16)
        dq_acc = dq_acc + jnp.einsum(
            "shij,jshd->ishd", d_score, key_block, preferred_element_type=jnp.float32
        )
        d_key = (
            jnp.einsum("shij,ishd->jshd", d_score, query_heads, preferred_element_type=jnp.float32)
            * SCORE_SCALE
        )
        d_value = jnp.einsum(
            "shij,ishd->jshd",
            unnorm.astype(jnp.bfloat16),
            d_mixture,
            preferred_element_type=jnp.float32,
        )
        stacked = jnp.concatenate(
            [
                d_key.reshape(step_rows, seq_count, feature_count),
                d_value.reshape(step_rows, seq_count, feature_count),
            ],
            axis=-1,
        )
        return (dq_acc, stacked)

    dq_sum, stacked_all = lax.scan(
        key_visit_block,
        jnp.zeros(query_heads.shape, jnp.float32),
        (key_blocks, value_blocks, seg_blocks),
    )
    return (dq_sum, stacked_all.reshape(row_count, seq_count, 2 * feature_count))


def body(
    tokens,
    segment_ids,
    w_query,
    w_key,
    w_value,
    w_output,
    w_inner,
    w_outer,
    b_query,
    b_value,
    b_output,
    b_inner,
    b_outer,
    gain_first,
    shift_first,
    gain_second,
    shift_second,
    cotangent,
):
    tok_rows, seq_count, feature_count = tokens.shape
    rows_total = tok_rows * seq_count
    gathered = (
        lax.all_gather(w_query, "seq", axis=0, tiled=True),
        lax.all_gather(w_key, "seq", axis=0, tiled=True),
        lax.all_gather(w_value, "seq", axis=0, tiled=True),
        lax.all_gather(w_output, "seq", axis=0, tiled=True),
        lax.all_gather(w_inner, "seq", axis=0, tiled=True),
        lax.all_gather(w_outer, "seq", axis=0, tiled=True),
        lax.all_gather(b_query, "seq", axis=0, tiled=True),
        lax.all_gather(b_value, "seq", axis=0, tiled=True),
        lax.all_gather(b_output, "seq", axis=0, tiled=True),
        lax.all_gather(b_inner, "seq", axis=0, tiled=True),
        lax.all_gather(b_outer, "seq", axis=0, tiled=True),
        lax.all_gather(gain_first, "seq", axis=0, tiled=True),
        lax.all_gather(shift_first, "seq", axis=0, tiled=True),
        lax.all_gather(gain_second, "seq", axis=0, tiled=True),
        lax.all_gather(shift_second, "seq", axis=0, tiled=True),
    )
    query_weight, key_weight, value_weight, output_weight, inner_weight, outer_weight = gathered[:6]
    (
        query_bias,
        value_bias,
        output_bias,
        inner_bias,
        outer_bias,
        gain_one,
        shift_one,
        gain_two,
        shift_two,
    ) = [vector.astype(jnp.float32) for vector in gathered[6:]]
    flat_rows = tokens.reshape(rows_total, feature_count)
    flat_float = flat_rows.astype(jnp.float32)
    seg_local = jnp.transpose(segment_ids)
    queries = (matmul(flat_rows, query_weight) + query_bias).astype(jnp.bfloat16)
    key_rows = matmul(flat_rows, key_weight).astype(jnp.bfloat16)
    value_rows = (matmul(flat_rows, value_weight) + value_bias).astype(jnp.bfloat16)
    query_heads = queries.reshape(tok_rows, seq_count, H, DH)
    key_block_rows = key_rows.reshape(tok_rows, seq_count, feature_count)
    value_block_rows = value_rows.reshape(tok_rows, seq_count, feature_count)
    initial = (
        jnp.zeros((seq_count, H, tok_rows), jnp.float32),
        jnp.zeros((tok_rows, seq_count, H, DH), jnp.float32),
    )
    totals, mixture = attend_keys(
        query_heads,
        seg_local,
        initial,
        (
            lax.all_gather(key_block_rows, "ctx", axis=0, tiled=True),
            lax.all_gather(value_block_rows, "ctx", axis=0, tiled=True),
            lax.all_gather(seg_local, "ctx", axis=0, tiled=True),
        ),
    )
    denominator = jnp.transpose(totals, (2, 0, 1))[..., None]
    attended = mixture / denominator
    context = attended.astype(jnp.bfloat16).reshape(rows_total, feature_count)
    first_in = matmul(context, output_weight) + output_bias + flat_float
    hidden, normed_one, inverse_one = norm_forward(first_in, gain_one, shift_one)
    hidden_low = hidden.astype(jnp.bfloat16)
    inner_pre = matmul(hidden_low, inner_weight) + inner_bias
    activated, gelu_slope = gelu_parts(inner_pre)
    act_low = activated.astype(jnp.bfloat16)
    second_in = matmul(act_low, outer_weight) + outer_bias + hidden
    result, normed_two, inverse_two = norm_forward(second_in, gain_two, shift_two)
    layer_out = result.astype(jnp.bfloat16).reshape(tok_rows, seq_count, feature_count)
    upstream = cotangent.astype(jnp.float32).reshape(rows_total, feature_count)
    d_second, dgain_second, dshift_second = norm_backward(
        upstream, normed_two, inverse_two, gain_two
    )
    d_outer = d_second.astype(jnp.bfloat16)
    dbias_outer = jnp.sum(d_outer.astype(jnp.float32), axis=0)
    dweight_outer = matmul_tn(act_low, d_outer)
    d_inner = (matmul_nt(d_outer, outer_weight) * gelu_slope).astype(jnp.bfloat16)
    dbias_inner = jnp.sum(d_inner.astype(jnp.float32), axis=0)
    dweight_inner = matmul_tn(hidden_low, d_inner)
    d_hidden = matmul_nt(d_inner, inner_weight) + d_second
    d_first, dgain_first, dshift_first = norm_backward(d_hidden, normed_one, inverse_one, gain_one)
    d_branch = d_first.astype(jnp.bfloat16)
    dbias_output = jnp.sum(d_branch.astype(jnp.float32), axis=0)
    dweight_output = matmul_tn(context, d_branch)
    d_context = (
        matmul_nt(d_branch, output_weight).astype(jnp.bfloat16).reshape(tok_rows, seq_count, H, DH)
    )
    d_float = d_context.astype(jnp.float32)
    d_mixture = (d_float / denominator).astype(jnp.bfloat16)
    correction = jnp.sum(d_float * attended, axis=-1) / denominator[..., 0]
    key_all, value_all, seg_all = (
        lax.all_gather(key_block_rows, "ctx", axis=0, tiled=True),
        lax.all_gather(value_block_rows, "ctx", axis=0, tiled=True),
        lax.all_gather(seg_local, "ctx", axis=0, tiled=True),
    )
    dq_sum, term_rows = key_side(
        query_heads, d_mixture, correction, seg_local, key_all, value_all, seg_all
    )
    summed = lax.psum_scatter(term_rows, "ctx", scatter_dimension=0, tiled=True)
    d_query = (dq_sum * SCORE_SCALE).astype(jnp.bfloat16)
    d_key = summed[..., :feature_count].astype(jnp.bfloat16)
    d_value = summed[..., feature_count:].astype(jnp.bfloat16)
    dq_flat = d_query.reshape(rows_total, feature_count)
    dk_flat = d_key.reshape(rows_total, feature_count)
    dv_flat = d_value.reshape(rows_total, feature_count)
    dweight_query = matmul_tn(flat_rows, dq_flat)
    dweight_key = matmul_tn(flat_rows, dk_flat)
    dweight_value = matmul_tn(flat_rows, dv_flat)
    dbias_query = jnp.sum(dq_flat.astype(jnp.float32), axis=0)
    dbias_value = jnp.sum(dv_flat.astype(jnp.float32), axis=0)
    grad_tokens = (
        matmul_nt(dq_flat, query_weight)
        + matmul_nt(dk_flat, key_weight)
        + matmul_nt(dv_flat, value_weight)
        + d_first
    )
    shards = (
        lax.psum_scatter(
            dweight_query.astype(jnp.bfloat16), "seq", scatter_dimension=0, tiled=True
        ).astype(jnp.float32),
        lax.psum_scatter(
            dweight_key.astype(jnp.bfloat16), "seq", scatter_dimension=0, tiled=True
        ).astype(jnp.float32),
        lax.psum_scatter(
            dweight_value.astype(jnp.bfloat16), "seq", scatter_dimension=0, tiled=True
        ).astype(jnp.float32),
        lax.psum_scatter(
            dweight_output.astype(jnp.bfloat16), "seq", scatter_dimension=0, tiled=True
        ).astype(jnp.float32),
        lax.psum_scatter(
            dweight_inner.astype(jnp.bfloat16), "seq", scatter_dimension=0, tiled=True
        ).astype(jnp.float32),
        lax.psum_scatter(
            dweight_outer.astype(jnp.bfloat16), "seq", scatter_dimension=0, tiled=True
        ).astype(jnp.float32),
        lax.psum_scatter(
            dbias_query.astype(jnp.bfloat16), "seq", scatter_dimension=0, tiled=True
        ).astype(jnp.float32),
        lax.psum_scatter(
            dbias_value.astype(jnp.bfloat16), "seq", scatter_dimension=0, tiled=True
        ).astype(jnp.float32),
        lax.psum_scatter(
            dbias_output.astype(jnp.bfloat16), "seq", scatter_dimension=0, tiled=True
        ).astype(jnp.float32),
        lax.psum_scatter(
            dbias_inner.astype(jnp.bfloat16), "seq", scatter_dimension=0, tiled=True
        ).astype(jnp.float32),
        lax.psum_scatter(
            dbias_outer.astype(jnp.bfloat16), "seq", scatter_dimension=0, tiled=True
        ).astype(jnp.float32),
        lax.psum_scatter(
            dgain_first.astype(jnp.bfloat16), "seq", scatter_dimension=0, tiled=True
        ).astype(jnp.float32),
        lax.psum_scatter(
            dshift_first.astype(jnp.bfloat16), "seq", scatter_dimension=0, tiled=True
        ).astype(jnp.float32),
        lax.psum_scatter(
            dgain_second.astype(jnp.bfloat16), "seq", scatter_dimension=0, tiled=True
        ).astype(jnp.float32),
        lax.psum_scatter(
            dshift_second.astype(jnp.bfloat16), "seq", scatter_dimension=0, tiled=True
        ).astype(jnp.float32),
    )
    finals = lax.psum(
        (
            shards[0],
            shards[1],
            shards[2],
            shards[3],
            shards[4],
            shards[5],
            shards[6],
            shards[7],
            shards[8],
            shards[9],
            shards[10],
            shards[11],
            shards[12],
            shards[13],
            shards[14],
        ),
        "ctx",
    )
    return (
        layer_out,
        grad_tokens.reshape(tok_rows, seq_count, feature_count),
        finals[0],
        finals[1],
        finals[2],
        finals[3],
        finals[4],
        finals[5],
        finals[6],
        finals[7],
        finals[8],
        finals[9],
        finals[10],
        finals[11],
        finals[12],
        finals[13],
        finals[14],
    )


def mark(name):
    return contextlib.nullcontext()


MESH = pl.DeviceIdType.MESH
BIG = 1e30
F32, BF16 = jnp.float32, jnp.bfloat16


def remote(src, dst, send_sem, recv_sem, seq, ctx):
    return pltpu.make_async_remote_copy(
        src_ref=src,
        dst_ref=dst,
        send_sem=send_sem,
        recv_sem=recv_sem,
        device_id=(seq, ctx),
        device_id_type=MESH,
    )


def greet(seq, ctx):
    barrier = pltpu.get_barrier_semaphore()
    for hop in range(1, 8):
        pl.semaphore_signal(
            barrier, inc=1, device_id=(seq, lax.rem(ctx + hop, 8)), device_id_type=MESH
        )
    for hop in range(1, 4):
        pl.semaphore_signal(
            barrier, inc=1, device_id=(lax.rem(seq + hop, 4), ctx), device_id_type=MESH
        )
    pl.semaphore_wait(barrier, 10)


def flip(index, bit):
    low = lax.rem(index // bit, 2)
    return index + bit - 2 * bit * low


def head_window(group):
    start = group * 192
    inside = lax.rem(group, 2) * 64
    return pl.multiple_of(start - inside, 128), pl.multiple_of(inside, 64)


def span(start, size, unit=16):
    return pl.ds(pl.multiple_of(start, unit), size)


INPUTS = (
    "x cot seg b_query b_value b_output b_outer gain_one shift_one gain_two shift_two "
    "b_inner wq wk wv wo wi wu"
).split()
OUTPUTS = "layer grad fu fi fo fg vec_sum bias_sum".split()
SCRATCH = {
    "seg_own": ((2, 8, 128), jnp.int32),
    "seg_all": ((8, 8, 128), jnp.int32),
    "pack_own": ((16, 768), BF16),
    "pack_all": ((4, 16, 768), BF16),
    "rows": ((8, 768), F32),
    "wo_full": ((4, 192, 768), BF16),
    "wi_full": ((4, 192, 3072), BF16),
    "wu_full": ((4, 768, 768), BF16),
    "xs": ((8, 128, 768), BF16),
    "wg": ((3, 4, 192, 256), BF16),
    "qa": ((3, 128, 1024), BF16),
    "ka": ((3, 128, 1024), BF16),
    "vt": ((3, 64, 1024), BF16),
    "ot": ((3, 64, 1024), F32),
    "sums": ((3, 1, 1024), F32),
    "key_rows": ((1024, 128), BF16),
    "o_send": ((192, 1024), BF16),
    "ctx_t": ((768, 256), BF16),
    "normed": ((256, 768), F32),
    "inverse": ((256, 1), F32),
    "low": ((256, 768), BF16),
    "low_t": ((768, 256), BF16),
    "act_t": ((4, 768, 256), BF16),
    "slope": ((4, 256, 768), F32),
    "work": ((256, 768), F32),
    "d_rows": ((256, 768), BF16),
    "dz": ((256, 768), BF16),
    "v_rows": ((16, 768), F32),
    "gu": ((4, 768, 768), BF16),
    "gi": ((4, 192, 3072), BF16),
    "go": ((4, 192, 768), BF16),
    "core_u": ((2, 768, 768), BF16),
    "core_i": ((2, 192, 3072), BF16),
    "core_o": ((2, 192, 768), BF16),
    "xr_u": ((768, 768), BF16),
    "xr_i": ((192, 3072), BF16),
    "xr_o": ((192, 768), BF16),
    "rcv_u": ((768, 768), BF16),
    "rcv_i": ((192, 3072), BF16),
    "rcv_o": ((192, 768), BF16),
    "fin_u": ((768, 768), BF16),
    "fin_i": ((192, 3072), BF16),
    "fin_o": ((192, 768), BF16),
    "tot_0": ((192, 384), F32),
    "tot_1": ((192, 384), F32),
    "tot_2": ((96, 768), F32),
    "tot_3": ((96, 768), F32),
    "tot_4": ((96, 384), F32),
    "do_send": ((768, 256), BF16),
    "do_all": ((192, 1024), BF16),
    "du": ((64, 1024), BF16),
    "c_row": ((1, 1024), F32),
    "value_rows": ((1024, 64), BF16),
    "dk_acc": ((64, 1024), F32),
    "dv_acc": ((64, 1024), F32),
    "d_all": ((3, 256, 1024), BF16),
    "g_all": ((3, 4, 192, 256), BF16),
    "g_core": ((3, 2, 192, 256), BF16),
    "g_xs": ((3, 192, 256), BF16),
    "g_xr": ((3, 192, 256), BF16),
    "g_half": ((3, 192, 256), BF16),
    "g_mir": ((3, 96, 256), BF16),
    "dx_recv": ((2, 4, 768, 128), BF16),
    "v_own": ((4, 16, 256), F32),
    "v_recv": ((4, 16, 256), F32),
    "v_all": ((8, 16, 256), F32),
    "b_send": ((2, 8, 256), F32),
    "b_recv": ((8, 2, 8, 256), F32),
}
SEMAPHORES = {
    "loc": (24,),
    "w_ss": (5, 5),
    "w_rs": (5, 5),
    "x_ss": (7,),
    "x_rs": (7,),
    "s_ss": (8,),
    "s_rs": (8,),
    "p_ss": (4,),
    "p_rs": (4,),
    "g_ss": (3, 3),
    "g_rs": (3, 3),
    "o_ss": (8,),
    "o_rs": (8,),
    "r_ss": (5, 9),
    "r_rs": (5, 9),
    "do_ss": (8,),
    "do_rs": (8,),
    "dx_ss": (8,),
    "dx_rs": (8,),
    "v_ss": (2, 8),
    "v_rs": (2, 8),
    "b_ss": (8,),
    "b_rs": (8,),
    "h_ss": (7, 3),
    "h_rs": (7, 3),
}


def layer_kernel(*refs):
    r = types.SimpleNamespace(
        **dict(zip(INPUTS + OUTPUTS + list(SCRATCH) + list(SEMAPHORES), refs))
    )
    seq, ctx = lax.axis_index("seq"), lax.axis_index("ctx")
    plane = seq // 2
    mate, across = flip(seq, 1), flip(seq, 2)
    across_mate = flip(mate, 2)
    beside, paired, mirror = flip(ctx, 1), flip(ctx, 2), flip(ctx, 4)
    bit_y, bit_l, bit_h = lax.rem(ctx, 2), lax.rem(ctx // 2, 2), ctx // 4
    side, group = ctx // 4, lax.rem(ctx, 4)
    window, inside = head_window(group)
    own_lanes = span(ctx * 128, 128, 128)
    sent = []

    def wi_cut(k, where):
        which = where if k == 1 else 1 - where
        return span(which * 1536, 1536, 128)

    def w_views(k, where):
        if k == 0:
            return r.wo, lambda owner: r.wo_full.at[owner], 96
        if k in (1, 2):
            cols = wi_cut(k, where)
            return r.wi.at[:, cols], lambda owner: r.wi_full.at[owner, :, cols], 96
        part = slice(384 * (k - 3), 384 * (k - 2))
        return r.wu.at[part], lambda owner: r.wu_full.at[owner, part], 192

    beside_of = {k: (beside, bit_y) if k in (0, 1, 3) else (paired, bit_l) for k in range(5)}

    def half(view, rows, which):
        return view.at[span(which * rows, rows, 32)]

    def w_copy(k, leg):
        sems = r.w_ss.at[k, leg], r.w_rs.at[k, leg]
        shard, full, rows = w_views(k, 1 - plane if leg == 1 else plane)
        partner, bit = beside_of[k]
        if leg == 0:
            return remote(shard, full(seq), *sems, mate, ctx)
        if leg == 1:
            return remote(
                half(shard, rows, bit), half(full(seq), rows, bit), *sems, across, ctx
            )
        which = bit if leg in (2, 3) else 1 - bit
        came = half(full(across), rows, which)
        return remote(came, came, *sems, *((seq, partner) if leg == 2 else (mate, ctx)))

    def w_wait(k, leg):
        shard, full, rows = w_views(k, plane)
        bit = beside_of[k][1]
        spots = (
            lambda: full(mate),
            lambda: half(full(across), rows, bit),
            lambda: half(full(across), rows, 1 - bit),
            lambda: half(full(across_mate), rows, bit),
            lambda: half(full(across_mate), rows, 1 - bit),
        )
        spot = spots[leg]()
        remote(spot, spot, r.w_ss.at[k, leg], r.w_rs.at[k, leg], mate, ctx).wait_recv()

    def pass_across(k):
        w_wait(k, 1)
        w_copy(k, 2).start()
        w_copy(k, 3).start()

    def pass_beside(k):
        w_wait(k, 2)
        w_copy(k, 4).start()

    def w_done(k):
        for leg in (0, 3, 4):
            w_wait(k, leg)

    group_refs = (r.wq, r.wk, r.wv)
    g_local, w_local = [], []
    for which in range(3):
        g_local.append(
            pltpu.make_async_copy(
                group_refs[which].at[:, pl.ds(window, 256)],
                r.wg.at[which, seq],
                r.loc.at[which],
            )
        )
    for n, (ref, full) in enumerate(
        ((r.wo, r.wo_full), (r.wi, r.wi_full), (r.wu, r.wu_full))
    ):
        w_local.append(pltpu.make_async_copy(ref, full.at[seq], r.loc.at[3 + n]))
    own_block = pltpu.make_async_copy(r.x.at[side], r.xs.at[ctx], r.loc.at[6])
    for which in range(2):
        r.seg_own[which] = jnp.broadcast_to(r.seg[which : which + 1], (8, 128))
    r.pack_own[...] = jnp.zeros((16, 768), BF16)
    for n, ref in enumerate(
        (
            r.b_query,
            r.b_value,
            r.b_output,
            r.b_outer,
            r.gain_one,
            r.shift_one,
            r.gain_two,
            r.shift_two,
        )
    ):
        r.pack_own[n : n + 1, 0:192] = ref[...].reshape(1, 192)
    r.pack_own[8:9] = r.b_inner[...].reshape(1, 768)
    own_seg = pltpu.make_async_copy(r.seg_own.at[side], r.seg_all.at[ctx], r.loc.at[7])
    own_pack = pltpu.make_async_copy(r.pack_own, r.pack_all.at[seq], r.loc.at[8])
    for copy in g_local + [own_block, own_seg, own_pack] + w_local:
        copy.start()
    r.v_rows[...] = jnp.zeros((16, 768), F32)
    for which in range(3):
        r.d_all[which] = jnp.zeros((256, 1024), BF16)

    with mark("greet"):
        greet(seq, ctx)

    def send(*args):
        copy = remote(*args)
        copy.start()
        sent.append(copy)

    def landed(spot, send_sem, recv_sem):
        remote(spot, spot, send_sem, recv_sem, seq, beside).wait_recv()

    for hop in range(1, 8):
        other = lax.rem(ctx + hop, 8)
        send(
            r.seg_own.at[other // 4],
            r.seg_all.at[ctx],
            r.s_ss.at[hop],
            r.s_rs.at[hop],
            seq,
            other,
        )
    for hop in range(1, 4):
        other = lax.rem(seq + hop, 4)
        send(r.pack_own, r.pack_all.at[seq], r.p_ss.at[hop], r.p_rs.at[hop], other, ctx)
    send(r.x.at[1 - side], r.xs.at[ctx], r.x_ss.at[0], r.x_rs.at[0], seq, mirror)
    square = [side * 4 + lax.rem(group + hop, 4) for hop in range(1, 4)]
    for hop in range(1, 4):
        send(
            r.x.at[side],
            r.xs.at[ctx],
            r.x_ss.at[hop],
            r.x_rs.at[hop],
            seq,
            square[hop - 1],
        )
    for which in range(3):
        for n, other in enumerate((mate, across)):
            send(
                group_refs[which].at[:, pl.ds(window, 256)],
                r.wg.at[which, seq],
                r.g_ss.at[which, n],
                r.g_rs.at[which, n],
                other,
                ctx,
            )
    for k in range(5):
        w_copy(k, 0).start()
        w_copy(k, 1).start()

    with mark("w_group"):
        for which in range(3):
            spot = r.wg.at[which, across]
            landed(spot, r.g_ss.at[which, 1], r.g_rs.at[which, 1])
            send(spot, spot, r.g_ss.at[which, 2], r.g_rs.at[which, 2], mate, ctx)
    with mark("x_far"):
        landed(r.xs.at[mirror], r.x_ss.at[0], r.x_rs.at[0])
    for n, other in enumerate(square):
        send(
            r.xs.at[mirror],
            r.xs.at[mirror],
            r.x_ss.at[4 + n],
            r.x_rs.at[4 + n],
            seq,
            other,
        )
    with mark("w_pass0"):
        pass_across(0)
    with mark("small"):
        for which in range(3):
            g_local[which].wait()
            for n, owner in ((0, mate), (2, across_mate)):
                landed(
                    r.wg.at[which, owner], r.g_ss.at[which, n], r.g_rs.at[which, n]
                )
        own_pack.wait()
        for hop in range(1, 4):
            landed(
                r.pack_all.at[lax.rem(seq + 4 - hop, 4)], r.p_ss.at[hop], r.p_rs.at[hop]
            )
        own_seg.wait()
        for hop in range(1, 8):
            landed(
                r.seg_all.at[lax.rem(ctx + 8 - hop, 8)], r.s_ss.at[hop], r.s_rs.at[hop]
            )

    lane = lax.broadcasted_iota(jnp.int32, (256, 768), 1)
    at = lax.broadcasted_iota(jnp.int32, (256, 768), 0)
    rows = jnp.zeros((8, 768), F32)
    for owner in range(4):
        chosen = ((lane == at + 192 * owner) & (at < 192)).astype(BF16)
        rows += matmul(r.pack_all[owner, 0:8, 0:256], chosen)
    r.rows[...] = rows
    with mark("w_pass1"):
        pass_across(1)
        pass_beside(0)
    with mark("x_near"):
        own_block.wait()
        for hop in range(1, 4):
            spot = r.xs.at[side * 4 + lax.rem(group + 4 - hop, 4)]
            landed(spot, r.x_ss.at[hop], r.x_rs.at[hop])
        for n in range(3):
            spot = r.xs.at[(1 - side) * 4 + lax.rem(group + 3 - n, 4)]
            landed(spot, r.x_ss.at[4 + n], r.x_rs.at[4 + n])
    with mark("qkv"):
        tokens = r.xs[...].reshape(1024, 768)
        own_rows = r.pack_all[group]
        qkv = []
        for which in range(3):
            weight = r.wg[which].reshape(768, 256)
            product = matmul_nt(weight.T, tokens)
            if which != 1:
                bias = own_rows[which // 2 : which // 2 + 1, 0:256].astype(F32)
                column = jnp.broadcast_to(bias, (128, 256)).T
                shifted = jnp.where(inside == 0, column, pltpu.roll(column, 64, 0))
                product = product + jnp.concatenate([shifted] * 8, axis=1)
            part = product.astype(BF16)
            if which == 0:
                part = part * jnp.bfloat16(SCORE_SCALE)
            qkv.append(part)
        number = jnp.concatenate(
            [r.seg_all[block, 0:1] for block in range(8)], axis=1
        )
        hot = lax.broadcasted_iota(jnp.int32, (16, 1024), 0) == number
        query_marks = jnp.where(hot, 1.0, 0.0).astype(BF16)
        key_marks = jnp.where(hot, 0.0, -BIG).astype(BF16)
        blank = jnp.zeros((48, 1024), BF16)
        for head in range(3):
            parts = [
                jnp.where(
                    inside != 0,
                    part[64 * head + 64 : 64 * head + 128],
                    part[64 * head : 64 * head + 64],
                )
                for part in qkv
            ]
            r.qa[head] = jnp.concatenate([parts[0], query_marks, blank], axis=0)
            r.ka[head] = jnp.concatenate([parts[1], key_marks, blank], axis=0)
            r.vt[head] = parts[2]
    with mark("w_pass2"):
        pass_beside(1)

    for head in range(3):
        r.key_rows[...] = r.ka[head].T

        def attend(block, unused, head=head):
            lanes = span(block * 256, 256, 256)
            scores = matmul(r.key_rows[...], r.qa[head, :, lanes])
            unnorm = jnp.exp(scores)
            total = jnp.sum(unnorm, axis=0, keepdims=True)
            attended = matmul(r.vt[head], unnorm.astype(BF16)) / total
            r.ot[head, :, lanes] = attended
            r.sums[head, :, lanes] = total
            r.o_send[64 * head : 64 * head + 64, lanes] = attended.astype(BF16)
            return unused

        with mark(f"attend{head}"):
            lax.fori_loop(0, 4, attend, 0)
        with mark(f"w_pass{3 + head}"):
            if head == 0:
                pass_across(2)
            if head == 1:
                pass_across(3)

    my_rows = span(group * 192, 192, 64)
    my_lanes = span(side * 128, 128, 128)
    own_o = pltpu.make_async_copy(
        r.o_send.at[:, own_lanes], r.ctx_t.at[my_rows, my_lanes], r.loc.at[9]
    )
    own_o.start()
    for hop in range(1, 8):
        other = lax.rem(ctx + hop, 8)
        send(
            r.o_send.at[:, span(other * 128, 128, 128)],
            r.ctx_t.at[my_rows, my_lanes],
            r.o_ss.at[hop],
            r.o_rs.at[hop],
            seq,
            other,
        )
    with mark("w_pass6"):
        pass_beside(2)
        pass_across(4)
        pass_beside(3)
    with mark("o_wait"):
        own_o.wait()
        for hop in range(1, 8):
            other = lax.rem(ctx + 8 - hop, 8)
            spot = r.ctx_t.at[
                span(lax.rem(other, 4) * 192, 192, 64), span((other // 4) * 128, 128, 128)
            ]
            landed(spot, r.o_ss.at[hop], r.o_rs.at[hop])
    with mark("wo_wait"):
        w_local[0].wait()
        w_done(0)

    def row_vec(n):
        return r.rows[n : n + 1]

    def first_norm(which, unused):
        at, lanes = span(which * 128, 128, 128), span(which * 128, 128, 128)
        value = (
            matmul(r.ctx_t[:, lanes].T, r.wo_full[...].reshape(768, 768))
            + row_vec(2)
            + r.x[which].astype(F32)
        )
        hidden, normed, inverse = norm_forward(value, row_vec(4), row_vec(5))
        r.normed[at] = normed
        r.inverse[at] = inverse
        part = hidden.astype(BF16)
        r.low[at] = part
        r.low_t[:, lanes] = part.T
        r.work[at] = hidden + row_vec(3)
        return unused

    with mark("first_norm"):
        lax.fori_loop(0, 2, first_norm, 0)
    with mark("wi0_wait"):
        w_local[1].wait()
        w_local[2].wait()
        w_done(1)
        w_wait(3, 0)
        w_wait(4, 0)

    def inner_weight(n):
        return r.wi_full[:, :, span(n * 768, 768, 128)].reshape(768, 768)

    def feed(where):
        def visit(step, unused):
            n, which = where * 2 + step // 2, lax.rem(step, 2)
            at = span(which * 128, 128, 128)
            value = matmul(r.low[at], inner_weight(n)) + r.pack_all[n, 8:9].astype(F32)
            act, slope = gelu_parts(value)
            part = act.astype(BF16)
            r.slope[n, at] = slope
            r.act_t[n, :, at] = part.T
            r.work[at] += matmul(part, r.wu_full[n])
            return unused

        lax.fori_loop(0, 4, visit, 0)

    with mark("feed0"):
        feed(plane)
    with mark("w_pass7"):
        pass_beside(4)
    with mark("wi1_wait"):
        w_done(2)
        for k in (3, 4):
            w_wait(k, 3)
            w_wait(k, 4)
    with mark("feed1"):
        feed(1 - plane)

    def tally(n, value):
        r.v_rows[n : n + 1] += jnp.sum(value, axis=0, keepdims=True)

    def second_norm(which, unused):
        at = span(which * 128, 128, 128)
        result, normed, inverse = norm_forward(r.work[at], row_vec(6), row_vec(7))
        r.layer[which] = result.astype(BF16)
        upstream = r.cot[which].astype(F32)
        scaled = upstream * row_vec(6)
        back = inverse * (
            scaled
            - jnp.mean(scaled, axis=-1, keepdims=True)
            - normed * jnp.mean(scaled * normed, axis=-1, keepdims=True)
        )
        tally(4, upstream * normed)
        tally(5, upstream)
        r.work[at] = back
        part = back.astype(BF16)
        r.d_rows[at] = part
        tally(1, part.astype(F32))
        return unused

    with mark("second_norm"):
        lax.fori_loop(0, 2, second_norm, 0)

    chunks = [
        (r.gu, r.fu, r.core_u, r.xr_u, r.rcv_u, r.fin_u, r.tot_0, 0, 384, 0, 768),
        (r.gu, r.fu, r.core_u, r.xr_u, r.rcv_u, r.fin_u, r.tot_1, 384, 384, 0, 768),
        (r.gi, r.fi, r.core_i, r.xr_i, r.rcv_i, r.fin_i, r.tot_2, 0, 192, 0, 1536),
        (r.gi, r.fi, r.core_i, r.xr_i, r.rcv_i, r.fin_i, r.tot_3, 0, 192, 1536, 1536),
        (r.go, r.fo, r.core_o, r.xr_o, r.rcv_o, r.fin_o, r.tot_4, 0, 192, 0, 768),
    ]

    def reduce_steps(k):
        grad, out, core, arrived, rcv, fin, total, row, rows, col, cols = chunks[k]
        rr, cc = pl.ds(row, rows), pl.ds(col, cols)
        wide = cols // 2
        mine = span(col + bit_y * wide, wide, 128)
        other = span(col + (1 - bit_y) * wide, wide, 128)
        keep_l = span(row + bit_l * (rows // 2), rows // 2)
        give_l = span(row + (1 - bit_l) * (rows // 2), rows // 2)
        keep_h = span(row + bit_l * (rows // 2) + bit_h * (rows // 4), rows // 4)
        give_h = span(row + bit_l * (rows // 2) + (1 - bit_h) * (rows // 4), rows // 4)
        spot_h = span(row + (1 - bit_l) * (rows // 2), rows // 4)
        tot_keep, tot_give = (
            span(bit_h * (rows // 4), rows // 4),
            span((1 - bit_h) * (rows // 4), rows // 4),
        )

        def sems(leg):
            return r.r_ss.at[k, leg], r.r_rs.at[k, leg]

        to_core = [
            remote(grad.at[mate, rr, cc], core.at[0, rr, cc], *sems(0), mate, ctx),
            remote(
                grad.at[across_mate, rr, cc], core.at[1, rr, cc], *sems(1), mate, ctx
            ),
        ]
        to_x = remote(core.at[1, rr, cc], arrived.at[rr, cc], *sems(2), across, ctx)
        to_y = remote(arrived.at[rr, other], rcv.at[rr, other], *sems(3), seq, beside)
        at_y = remote(arrived.at[rr, mine], rcv.at[rr, mine], *sems(3), seq, beside)
        to_l = remote(
            arrived.at[give_l, mine], rcv.at[give_l, other], *sems(4), seq, paired
        )
        at_l = remote(
            arrived.at[keep_l, mine], rcv.at[keep_l, other], *sems(4), seq, paired
        )
        to_h = remote(
            arrived.at[give_h, mine], rcv.at[spot_h, other], *sems(5), seq, mirror
        )

        def spread(at, lanes, leg, target):
            spot = fin.at[at, lanes]
            return remote(spot, spot, *sems(leg), seq, target)

        def begin():
            for copy in to_core:
                copy.start()

        def cores():
            for copy in to_core:
                copy.wait_recv()
            core[1, rr, cc] = (
                grad[across, rr, cc].astype(F32) + core[1, rr, cc].astype(F32)
            ).astype(BF16)
            to_x.start()

        def three(at, lanes):
            return (
                grad[seq, at, lanes].astype(F32)
                + core[0, at, lanes].astype(F32)
                + arrived[at, lanes].astype(F32)
            )

        def planes():
            to_x.wait_recv()
            arrived[rr, other] = three(rr, other).astype(BF16)
            to_y.start()

        def besides():
            at_y.wait_recv()
            arrived[give_l, mine] = (
                three(give_l, mine) + rcv[give_l, mine].astype(F32)
            ).astype(BF16)
            to_l.start()
            total[...] = three(keep_l, mine) + rcv[keep_l, mine].astype(F32)

        def pairs():
            at_l.wait_recv()
            arrived[give_h, mine] = (
                total[tot_give] + rcv[give_h, other].astype(F32)
            ).astype(BF16)
            to_h.start()
            total[tot_keep] += rcv[keep_h, other].astype(F32)

        def mirrors():
            to_h.wait_recv()
            fin[keep_h, mine] = (
                total[tot_keep] + rcv[spot_h, other].astype(F32)
            ).astype(BF16)
            spread(keep_h, mine, 6, mirror).start()

        def back_h():
            spread(give_h, mine, 6, mirror).wait_recv()
            spread(keep_l, mine, 7, paired).start()

        def back_l():
            spread(give_l, mine, 7, paired).wait_recv()
            spread(rr, mine, 8, beside).start()

        to_out = pltpu.make_async_copy(fin.at[rr, cc], out.at[rr, cc], r.loc.at[10 + k])

        def back_y():
            spread(rr, other, 8, beside).wait_recv()
            to_out.start()

        def end():
            for copy in to_core + [
                to_x,
                to_y,
                to_l,
                to_h,
                spread(keep_h, mine, 6, mirror),
                spread(keep_l, mine, 7, paired),
                spread(rr, mine, 8, beside),
            ]:
                copy.wait_send()
            to_out.wait()

        return [
            begin,
            cores,
            planes,
            besides,
            pairs,
            mirrors,
            back_h,
            back_l,
            back_y,
            end,
        ]

    steps = [reduce_steps(k) for k in range(5)]

    def run(*pairs):
        for k, n in pairs:
            with mark(f"s{k}_{n}"):
                steps[k][n]()

    def make_outer(n, row):
        part = slice(row, row + 384)
        r.gu[n, part] = matmul(r.act_t[n, part], r.d_rows[...]).astype(BF16)

    with mark("dw_outer"):
        for row in (0, 384):
            make_outer(mate, row)
            make_outer(across_mate, row)
            run((row // 384, 0))
        for row in (0, 384):
            make_outer(across, row)
            make_outer(seq, row)
    run((0, 1), (1, 1))

    for n in range(4):

        def inner_back(which, unused, n=n):
            at = span(which * 128, 128, 128)
            part = (matmul_nt(r.d_rows[at], r.wu_full[n]) * r.slope[n, at]).astype(BF16)
            r.dz[at] = part
            tally(8 + n, part.astype(F32))
            r.work[at] += matmul_nt(part, inner_weight(n))
            return unused

        with mark(f"inner_back{n}"):
            lax.fori_loop(0, 2, inner_back, 0)
            r.gi[:, :, 768 * n : 768 * n + 768] = (
                matmul(r.low_t[...], r.dz[...]).astype(BF16).reshape(4, 192, 768)
            )
        if n == 1:
            run((2, 0))
        if n == 3:
            run((3, 0), (2, 1))

    def first_back(which, unused):
        at = span(which * 128, 128, 128)
        upstream, normed = r.work[at], r.normed[at]
        scaled = upstream * row_vec(4)
        back = r.inverse[at] * (
            scaled
            - jnp.mean(scaled, axis=-1, keepdims=True)
            - normed * jnp.mean(scaled * normed, axis=-1, keepdims=True)
        )
        tally(2, upstream * normed)
        tally(3, upstream)
        r.work[at] = back
        part = back.astype(BF16)
        r.dz[at] = part
        tally(0, part.astype(F32))
        return unused

    with mark("first_back"):
        lax.fori_loop(0, 2, first_back, 0)
        r.do_send[...] = matmul_nt(
            r.wo_full[...].reshape(768, 768), r.dz[...]
        ).astype(BF16)
    own_do = pltpu.make_async_copy(
        r.do_send.at[my_rows, my_lanes], r.do_all.at[:, own_lanes], r.loc.at[15]
    )
    own_do.start()
    for hop in range(1, 8):
        other = lax.rem(ctx + hop, 8)
        send(
            r.do_send.at[
                span(lax.rem(other, 4) * 192, 192, 64), span((other // 4) * 128, 128, 128)
            ],
            r.do_all.at[:, own_lanes],
            r.do_ss.at[hop],
            r.do_rs.at[hop],
            seq,
            other,
        )
    with mark("dw_output"):
        r.go[...] = matmul(r.ctx_t[...], r.dz[...]).astype(BF16).reshape(4, 192, 768)
    run((4, 0), (3, 1), (4, 1))

    for owner in range(4):
        start = 192 * owner - 64 * (owner % 2)
        r.v_own[owner, 0:8] = r.v_rows[0:8, start : start + 256]
        for part in range(3):
            r.v_own[owner, 8 + part : 9 + part] = r.v_rows[
                8 + owner : 9 + owner, 256 * part : 256 * part + 256
            ]
        r.v_own[owner, 11:16] = jnp.zeros((5, 256), F32)
    for hop in range(1, 4):
        other = lax.rem(seq + hop, 4)
        send(
            r.v_own.at[other],
            r.v_recv.at[seq],
            r.v_ss.at[0, hop],
            r.v_rs.at[0, hop],
            other,
            ctx,
        )
    run((0, 2))
    with mark("do_wait"):
        own_do.wait()
        for hop in range(1, 8):
            spot = r.do_all.at[:, span(lax.rem(ctx + 8 - hop, 8) * 128, 128, 128)]
            landed(spot, r.do_ss.at[hop], r.do_rs.at[hop])
    for head in range(3):
        at = span(inside + 64 * head, 64, 64)
        total = r.sums[head]
        d_out = r.do_all[64 * head : 64 * head + 64].astype(F32)
        r.du[...] = (d_out / total).astype(BF16)
        r.c_row[...] = jnp.sum(d_out * r.ot[head], axis=0, keepdims=True) / total
        r.key_rows[...] = r.ka[head].T
        r.value_rows[...] = r.vt[head].T
        r.dk_acc[...] = jnp.zeros((64, 1024), F32)
        r.dv_acc[...] = jnp.zeros((64, 1024), F32)

        def attend_back(block, unused, head=head, at=at):
            lanes = span(block * 256, 256, 256)
            scores = matmul(r.key_rows[...], r.qa[head, :, lanes])
            unnorm = jnp.exp(scores)
            d_prob = matmul(r.value_rows[...], r.du[:, lanes])
            d_score = (unnorm * (d_prob - r.c_row[:, lanes])).astype(BF16)
            d_query = matmul(r.ka[head, 0:64], d_score) * SCORE_SCALE
            r.d_all[0, at, lanes] = d_query.astype(BF16)
            r.dk_acc[...] += matmul_nt(r.qa[head, 0:64, lanes], d_score)
            r.dv_acc[...] += matmul_nt(r.du[:, lanes], unnorm.astype(BF16))
            return unused

        with mark(f"attend_back{head}"):
            lax.fori_loop(0, 4, attend_back, 0)
            r.d_all[1, at] = r.dk_acc[...].astype(BF16)
            r.d_all[2, at] = r.dv_acc[...].astype(BF16)
        if head == 0:
            run((0, 3))
        if head == 1:
            run((0, 4))
        if head == 2:
            run((1, 2), (0, 5))

    with mark("dw_qkv"):
        ones = jnp.ones((16, 1024), BF16)
        for which in range(3):
            product = matmul(r.d_all[which], r.xs[...].reshape(1024, 768)).astype(BF16)
            r.g_all[which] = product.T.reshape(4, 192, 256)
            if which != 1:
                r.b_send[which // 2] = matmul_nt(ones, r.d_all[which])[0:8]
    g_cores = [
        remote(
            r.g_all.at[which, owner],
            r.g_core.at[which, n],
            r.h_ss.at[which, n],
            r.h_rs.at[which, n],
            mate,
            ctx,
        )
        for which in range(3)
        for n, owner in ((0, mate), (1, across_mate))
    ]
    for copy in g_cores:
        copy.start()
    own_bias = pltpu.make_async_copy(
        r.b_send, r.b_recv.at[seq * 2 + side], r.loc.at[16]
    )
    to_owners = [
        remote(
            r.b_send,
            r.b_recv.at[seq * 2 + side],
            r.b_ss.at[hop],
            r.b_rs.at[seq * 2 + side],
            group,
            lax.rem(ctx + hop, 8),
        )
        for hop in range(8)
    ]

    @pl.when(group == seq)
    def _():
        own_bias.start()

    @pl.when(group != seq)
    def _():
        to_owners[0].start()

    for copy in to_owners[1:]:
        copy.start()

    run((1, 3))
    with mark("dx"):
        for part in range(4):
            lanes = slice(256 * part, 256 * part + 256)
            share = matmul(r.wg[0].reshape(768, 256), r.d_all[0, :, lanes])
            for which in (1, 2):
                share += matmul(r.wg[which].reshape(768, 256), r.d_all[which, :, lanes])
            r.act_t[part] = share.astype(BF16)

    def dx_block(block):
        return r.act_t.at[block // 2, :, span(lax.rem(block, 2) * 128, 128, 128)]

    with mark("g_core"):
        for copy in g_cores:
            copy.wait_recv()
        for which in range(3):
            r.g_xs[which] = (
                r.g_all[which, across].astype(F32) + r.g_core[which, 1].astype(F32)
            ).astype(BF16)
        g_x = remote(r.g_xs, r.g_xr, r.h_ss.at[3, 0], r.h_rs.at[3, 0], across, ctx)
        g_x.start()
    own_dx = pltpu.make_async_copy(
        dx_block(ctx), r.dx_recv.at[side, group], r.loc.at[17]
    )
    own_dx.start()
    for hop in range(1, 8):
        other = lax.rem(ctx + hop, 8)
        send(
            dx_block(other),
            r.dx_recv.at[side, group],
            r.dx_ss.at[hop],
            r.dx_rs.at[hop],
            seq,
            other,
        )

    run((0, 6), (1, 4), (2, 2), (0, 7), (1, 5), (2, 3), (1, 6), (0, 8), (3, 2), (2, 4))
    run((1, 7), (2, 5), (4, 2), (3, 3), (2, 6), (1, 8), (4, 3), (3, 4))
    keep, give = span(side * 96, 96, 32), span((1 - side) * 96, 96, 32)
    with mark("g_x"):
        g_x.wait_recv()
        for which in range(3):
            r.g_half[which] = (
                r.g_all[which, seq].astype(F32)
                + r.g_core[which, 0].astype(F32)
                + r.g_xr[which].astype(F32)
            ).astype(BF16)
        g_m = remote(
            r.g_half.at[:, give], r.g_mir, r.h_ss.at[3, 1], r.h_rs.at[3, 1], seq, mirror
        )
        g_m.start()

    with mark("v_wait"):
        for hop in range(1, 4):
            spot = r.v_recv.at[lax.rem(seq + 4 - hop, 4)]
            landed(spot, r.v_ss.at[0, hop], r.v_rs.at[0, hop])
        r.v_recv[seq] = r.v_own[seq]
        r.v_all[ctx] = r.v_recv[0] + r.v_recv[1] + r.v_recv[2] + r.v_recv[3]
        for hop in range(1, 8):
            send(
                r.v_all.at[ctx],
                r.v_all.at[ctx],
                r.v_ss.at[1, hop],
                r.v_rs.at[1, hop],
                seq,
                lax.rem(ctx + hop, 8),
            )
    run((2, 7), (4, 4), (3, 5), (4, 5))
    with mark("g_m"):
        g_m.wait_recv()
        for which in range(3):
            r.fg[group, which, keep] = (
                r.g_half[which, keep].astype(F32) + r.g_mir[which].astype(F32)
            ).astype(BF16)
        spot = r.fg.at[group, :, keep]
        send(spot, spot, r.h_ss.at[4, 0], r.h_rs.at[4, 0], seq, mirror)
        for n, other in enumerate(square):
            send(spot, spot, r.h_ss.at[5, n], r.h_rs.at[5, n], seq, other)

    run((3, 6), (2, 8), (4, 6))
    with mark("g_back"):
        theirs = r.fg.at[group, :, give]
        landed(theirs, r.h_ss.at[4, 0], r.h_rs.at[4, 0])
        for n, other in enumerate(square):
            send(theirs, theirs, r.h_ss.at[6, n], r.h_rs.at[6, n], seq, other)

    with mark("dx_wait"):
        own_dx.wait()
        for hop in range(1, 8):
            source = lax.rem(ctx + 8 - hop, 8)
            spot = r.dx_recv.at[source // 4, lax.rem(source, 4)]
            landed(spot, r.dx_ss.at[hop], r.dx_rs.at[hop])
        for which in range(2):
            share = r.dx_recv[which, 0].astype(F32)
            for n in range(1, 4):
                share += r.dx_recv[which, n].astype(F32)
            r.grad[which] = share.T + r.work[128 * which : 128 * which + 128]
    with mark("v_end"):
        for hop in range(1, 8):
            spot = r.v_all.at[lax.rem(ctx + 8 - hop, 8)]
            landed(spot, r.v_ss.at[1, hop], r.v_rs.at[1, hop])
        gathered = r.v_all[0]
        for n in range(1, 8):
            gathered += r.v_all[n]
        r.vec_sum[...] = gathered
        for n in range(8):
            spot = r.b_recv.at[n]
            arrival = remote(
                spot, spot, r.b_ss.at[0], r.b_rs.at[n], lax.rem(seq + 1, 4), ctx
            )
            here = (n // 2 == seq) & (n % 2 == side) & (group == seq)

            @pl.when(here)
            def _():
                own_bias.wait()

            @pl.when(jnp.logical_not(here))
            def _(arrival=arrival):
                arrival.wait_recv()

        row_sum = r.b_recv[0]
        for n in range(1, 8):
            row_sum += r.b_recv[n]
        r.bias_sum[...] = row_sum

    run((3, 7), (4, 7), (4, 8), (3, 8))
    with mark("g_end"):
        for n in range(3):
            source = lax.rem(group + 3 - n, 4)
            landed(r.fg.at[source, :, keep], r.h_ss.at[5, n], r.h_rs.at[5, n])
            landed(r.fg.at[source, :, give], r.h_ss.at[6, n], r.h_rs.at[6, n])

    with mark("ends"):
        run(*((k, 9) for k in range(5)))
        for copy in sent + g_cores + [g_x, g_m] + to_owners[1:]:
            copy.wait_send()

        @pl.when(group != seq)
        def _():
            to_owners[0].wait_send()

        for k in range(5):
            for leg in range(5):
                w_copy(k, leg).wait_send()


def run_layer(*operands):
    vmem = pl.BlockSpec(memory_space=pltpu.VMEM)
    anywhere = pl.BlockSpec(memory_space=pl.ANY)
    shape = jax.ShapeDtypeStruct
    return pl.pallas_call(
        layer_kernel,
        name="layer_kernel",
        out_shape=(
            shape((2, 128, 768), BF16),
            shape((2, 128, 768), F32),
            shape((768, 768), BF16),
            shape((192, 3072), BF16),
            shape((192, 768), BF16),
            shape((4, 3, 192, 256), BF16),
            shape((16, 256), F32),
            shape((2, 8, 256), F32),
        ),
        in_specs=[vmem] * 12 + [anywhere] * 6,
        out_specs=(vmem,) * 2 + (anywhere,) * 3 + (vmem,) * 3,
        scratch_shapes=[pltpu.VMEM(*spec) for spec in SCRATCH.values()]
        + [pltpu.SemaphoreType.DMA(count) for count in SEMAPHORES.values()],
        compiler_params=pltpu.CompilerParams(
            collective_id=1, has_side_effects=True, vmem_limit_bytes=67043328
        ),
    )(*operands)


def fast_body(
    tokens,
    segment_ids,
    w_query,
    w_key,
    w_value,
    w_output,
    w_inner,
    w_outer,
    b_query,
    b_value,
    b_output,
    b_inner,
    b_outer,
    gain_first,
    shift_first,
    gain_second,
    shift_second,
    cotangent,
):
    layer, grad, fu, fi, fo, fg, vec_sum, bias_sum = run_layer(
        jnp.transpose(tokens, (1, 0, 2)),
        jnp.transpose(cotangent, (1, 0, 2)),
        segment_ids,
        b_query,
        b_value,
        b_output,
        b_outer,
        gain_first,
        shift_first,
        gain_second,
        shift_second,
        b_inner,
        w_query,
        w_key,
        w_value,
        w_output,
        w_inner,
        w_outer,
    )

    def widen(part):
        tiles = part.astype(F32)
        return jnp.concatenate(
            [
                tiles[0, :, 0:128],
                tiles[0, :, 128:256] + tiles[1, :, 0:128],
                tiles[1, :, 128:256],
                tiles[2, :, 0:128],
                tiles[2, :, 128:256] + tiles[3, :, 0:128],
                tiles[3, :, 128:256],
            ],
            axis=1,
        )

    odd = lax.rem(lax.axis_index("seq"), 2) == 1

    def owned(row):
        return jnp.where(odd, row[64:256], row[0:192])

    return (
        jnp.transpose(layer, (1, 0, 2)),
        jnp.transpose(grad, (1, 0, 2)),
        widen(fg[:, 0]),
        widen(fg[:, 1]),
        widen(fg[:, 2]),
        fo.astype(F32),
        fi.astype(F32),
        fu.astype(F32),
        owned(bias_sum[0, 0]),
        owned(bias_sum[1, 0]),
        owned(vec_sum[0]),
        vec_sum[8:11].reshape(768),
        owned(vec_sum[1]),
        owned(vec_sum[2]),
        owned(vec_sum[3]),
        owned(vec_sum[4]),
        owned(vec_sum[5]),
    )


def solution(mesh):
    in_specs = (
        P("ctx", "seq", None),
        P("seq", "ctx"),
        P("seq", None),
        P("seq", None),
        P("seq", None),
        P("seq", None),
        P("seq", None),
        P("seq", None),
        P("seq"),
        P("seq"),
        P("seq"),
        P("seq"),
        P("seq"),
        P("seq"),
        P("seq"),
        P("seq"),
        P("seq"),
        P("ctx", "seq", None),
    )
    out_specs = (
        P("ctx", "seq", None),
        P("ctx", "seq", None),
        P("seq", None),
        P("seq", None),
        P("seq", None),
        P("seq", None),
        P("seq", None),
        P("seq", None),
        P("seq"),
        P("seq"),
        P("seq"),
        P("seq"),
        P("seq"),
        P("seq"),
        P("seq"),
        P("seq"),
        P("seq"),
    )
    small = mesh.shape["seq"] == 4 and mesh.shape["ctx"] == 8
    step = fast_body if small else body
    return jax.shard_map(step, mesh=mesh, in_specs=in_specs, out_specs=out_specs, check_vma=False)
```

```python
import contextlib
import functools
import math
import types

import jax
import jax.numpy as jnp
from jax import lax
from jax.experimental import pallas as pl
from jax.experimental.pallas import tpu as pltpu
from jax.sharding import PartitionSpec as P

H = 12
DH = 64


EPSILON = 1e-12
SCORE_SCALE = 0.125


def matmul(first_op, second_op):
    return jnp.dot(first_op, second_op, preferred_element_type=jnp.float32)


def matmul_tn(first_op, second_op):
    return lax.dot_general(
        first_op, second_op, (((0,), (0,)), ((), ())), preferred_element_type=jnp.float32
    )


def matmul_nt(first_op, second_op):
    return lax.dot_general(
        first_op, second_op, (((1,), (1,)), ((), ())), preferred_element_type=jnp.float32
    )


def norm_forward(values, gain_vec, shift_vec):
    center = values - jnp.mean(values, axis=-1, keepdims=True)
    inverse = lax.rsqrt(jnp.mean(center * center, axis=-1, keepdims=True) + EPSILON)
    normed = center * inverse
    return (normed * gain_vec + shift_vec, normed, inverse)


def norm_backward(upstream, normed, inverse, gain_vec):
    scaled = upstream * gain_vec
    back_grad = inverse * (
        scaled
        - jnp.mean(scaled, axis=-1, keepdims=True)
        - normed * jnp.mean(scaled * normed, axis=-1, keepdims=True)
    )
    return (back_grad, jnp.sum(upstream * normed, axis=0), jnp.sum(upstream, axis=0))


def gelu_parts(values):
    cumulative = 0.5 * (1.0 + lax.erf(values * 0.7071067811865476))
    return (
        values * cumulative,
        cumulative + values * jnp.exp(-0.5 * values * values) * 0.3989422804014327,
    )


def block_scores(query_heads, key_heads, seg_query, seg_key):
    raw_scores = (
        jnp.einsum("ishd,jshd->shij", query_heads, key_heads, preferred_element_type=jnp.float32)
        * SCORE_SCALE
    )
    allowed = (jnp.transpose(seg_query)[:, :, None] == jnp.transpose(seg_key)[:, None, :])[:, None]
    return jnp.where(allowed, jnp.exp(raw_scores), 0.0)


def attend_keys(query_heads, seg_query, carry_in, piece_rows):
    key_piece, value_piece, seg_piece = piece_rows
    row_count, seq_count, feature_count = key_piece.shape
    heads, head_size = (query_heads.shape[2], query_heads.shape[3])
    step_rows = math.gcd(row_count, 1024)
    block_count = row_count // step_rows
    key_blocks = key_piece.reshape(block_count, step_rows, seq_count, heads, head_size)
    value_blocks = value_piece.reshape(block_count, step_rows, seq_count, heads, head_size)
    seg_blocks = seg_piece.reshape(block_count, step_rows, seq_count)

    def attend_visit_block(running, element):
        key_block, value_block, seg_block = element
        unnorm = block_scores(query_heads, key_block, seg_query, seg_block)
        totals = running[0] + jnp.sum(unnorm, axis=-1)
        mixture = running[1] + jnp.einsum(
            "shij,jshd->ishd",
            unnorm.astype(jnp.bfloat16),
            value_block,
            preferred_element_type=jnp.float32,
        )
        return ((totals, mixture), None)

    result, unused = lax.scan(attend_visit_block, carry_in, (key_blocks, value_blocks, seg_blocks))
    return result


def key_side(query_heads, d_mixture, correction, seg_query, key_all, value_all, seg_all):
    row_count, seq_count, feature_count = key_all.shape
    heads, head_size = (query_heads.shape[2], query_heads.shape[3])
    step_rows = math.gcd(row_count, 1024)
    block_count = row_count // step_rows
    corr_cols = jnp.transpose(correction, (1, 2, 0))[..., None]
    key_blocks = key_all.reshape(block_count, step_rows, seq_count, heads, head_size)
    value_blocks = value_all.reshape(block_count, step_rows, seq_count, heads, head_size)
    seg_blocks = seg_all.reshape(block_count, step_rows, seq_count)

    def key_visit_block(dq_acc, element):
        key_block, value_block, seg_block = element
        unnorm = block_scores(query_heads, key_block, seg_query, seg_block)
        d_prob = jnp.einsum(
            "ishd,jshd->shij", d_mixture, value_block, preferred_element_type=jnp.float32
        )
        d_score = (unnorm * (d_prob - corr_cols)).astype(jnp.bfloat16)
        dq_acc = dq_acc + jnp.einsum(
            "shij,jshd->ishd", d_score, key_block, preferred_element_type=jnp.float32
        )
        d_key = (
            jnp.einsum("shij,ishd->jshd", d_score, query_heads, preferred_element_type=jnp.float32)
            * SCORE_SCALE
        )
        d_value = jnp.einsum(
            "shij,ishd->jshd",
            unnorm.astype(jnp.bfloat16),
            d_mixture,
            preferred_element_type=jnp.float32,
        )
        stacked = jnp.concatenate(
            [
                d_key.reshape(step_rows, seq_count, feature_count),
                d_value.reshape(step_rows, seq_count, feature_count),
            ],
            axis=-1,
        )
        return (dq_acc, stacked)

    dq_sum, stacked_all = lax.scan(
        key_visit_block,
        jnp.zeros(query_heads.shape, jnp.float32),
        (key_blocks, value_blocks, seg_blocks),
    )
    return (dq_sum, stacked_all.reshape(row_count, seq_count, 2 * feature_count))


def body(
    tokens,
    segment_ids,
    w_query,
    w_key,
    w_value,
    w_output,
    w_inner,
    w_outer,
    b_query,
    b_value,
    b_output,
    b_inner,
    b_outer,
    gain_first,
    shift_first,
    gain_second,
    shift_second,
    cotangent,
):
    tok_rows, seq_count, feature_count = tokens.shape
    rows_total = tok_rows * seq_count
    gathered = (
        lax.all_gather(w_query, "seq", axis=0, tiled=True),
        lax.all_gather(w_key, "seq", axis=0, tiled=True),
        lax.all_gather(w_value, "seq", axis=0, tiled=True),
        lax.all_gather(w_output, "seq", axis=0, tiled=True),
        lax.all_gather(w_inner, "seq", axis=0, tiled=True),
        lax.all_gather(w_outer, "seq", axis=0, tiled=True),
        lax.all_gather(b_query, "seq", axis=0, tiled=True),
        lax.all_gather(b_value, "seq", axis=0, tiled=True),
        lax.all_gather(b_output, "seq", axis=0, tiled=True),
        lax.all_gather(b_inner, "seq", axis=0, tiled=True),
        lax.all_gather(b_outer, "seq", axis=0, tiled=True),
        lax.all_gather(gain_first, "seq", axis=0, tiled=True),
        lax.all_gather(shift_first, "seq", axis=0, tiled=True),
        lax.all_gather(gain_second, "seq", axis=0, tiled=True),
        lax.all_gather(shift_second, "seq", axis=0, tiled=True),
    )
    query_weight, key_weight, value_weight, output_weight, inner_weight, outer_weight = gathered[:6]
    (
        query_bias,
        value_bias,
        output_bias,
        inner_bias,
        outer_bias,
        gain_one,
        shift_one,
        gain_two,
        shift_two,
    ) = [vector.astype(jnp.float32) for vector in gathered[6:]]
    flat_rows = tokens.reshape(rows_total, feature_count)
    flat_float = flat_rows.astype(jnp.float32)
    seg_local = jnp.transpose(segment_ids)
    queries = (matmul(flat_rows, query_weight) + query_bias).astype(jnp.bfloat16)
    key_rows = matmul(flat_rows, key_weight).astype(jnp.bfloat16)
    value_rows = (matmul(flat_rows, value_weight) + value_bias).astype(jnp.bfloat16)
    query_heads = queries.reshape(tok_rows, seq_count, H, DH)
    key_block_rows = key_rows.reshape(tok_rows, seq_count, feature_count)
    value_block_rows = value_rows.reshape(tok_rows, seq_count, feature_count)
    initial = (
        jnp.zeros((seq_count, H, tok_rows), jnp.float32),
        jnp.zeros((tok_rows, seq_count, H, DH), jnp.float32),
    )
    totals, mixture = attend_keys(
        query_heads,
        seg_local,
        initial,
        (
            lax.all_gather(key_block_rows, "ctx", axis=0, tiled=True),
            lax.all_gather(value_block_rows, "ctx", axis=0, tiled=True),
            lax.all_gather(seg_local, "ctx", axis=0, tiled=True),
        ),
    )
    denominator = jnp.transpose(totals, (2, 0, 1))[..., None]
    attended = mixture / denominator
    context = attended.astype(jnp.bfloat16).reshape(rows_total, feature_count)
    first_in = matmul(context, output_weight) + output_bias + flat_float
    hidden, normed_one, inverse_one = norm_forward(first_in, gain_one, shift_one)
    hidden_low = hidden.astype(jnp.bfloat16)
    inner_pre = matmul(hidden_low, inner_weight) + inner_bias
    activated, gelu_slope = gelu_parts(inner_pre)
    act_low = activated.astype(jnp.bfloat16)
    second_in = matmul(act_low, outer_weight) + outer_bias + hidden
    result, normed_two, inverse_two = norm_forward(second_in, gain_two, shift_two)
    layer_out = result.astype(jnp.bfloat16).reshape(tok_rows, seq_count, feature_count)
    upstream = cotangent.astype(jnp.float32).reshape(rows_total, feature_count)
    d_second, dgain_second, dshift_second = norm_backward(
        upstream, normed_two, inverse_two, gain_two
    )
    d_outer = d_second.astype(jnp.bfloat16)
    dbias_outer = jnp.sum(d_outer.astype(jnp.float32), axis=0)
    dweight_outer = matmul_tn(act_low, d_outer)
    d_inner = (matmul_nt(d_outer, outer_weight) * gelu_slope).astype(jnp.bfloat16)
    dbias_inner = jnp.sum(d_inner.astype(jnp.float32), axis=0)
    dweight_inner = matmul_tn(hidden_low, d_inner)
    d_hidden = matmul_nt(d_inner, inner_weight) + d_second
    d_first, dgain_first, dshift_first = norm_backward(d_hidden, normed_one, inverse_one, gain_one)
    d_branch = d_first.astype(jnp.bfloat16)
    dbias_output = jnp.sum(d_branch.astype(jnp.float32), axis=0)
    dweight_output = matmul_tn(context, d_branch)
    d_context = (
        matmul_nt(d_branch, output_weight).astype(jnp.bfloat16).reshape(tok_rows, seq_count, H, DH)
    )
    d_float = d_context.astype(jnp.float32)
    d_mixture = (d_float / denominator).astype(jnp.bfloat16)
    correction = jnp.sum(d_float * attended, axis=-1) / denominator[..., 0]
    key_all, value_all, seg_all = (
        lax.all_gather(key_block_rows, "ctx", axis=0, tiled=True),
        lax.all_gather(value_block_rows, "ctx", axis=0, tiled=True),
        lax.all_gather(seg_local, "ctx", axis=0, tiled=True),
    )
    dq_sum, term_rows = key_side(
        query_heads, d_mixture, correction, seg_local, key_all, value_all, seg_all
    )
    summed = lax.psum_scatter(term_rows, "ctx", scatter_dimension=0, tiled=True)
    d_query = (dq_sum * SCORE_SCALE).astype(jnp.bfloat16)
    d_key = summed[..., :feature_count].astype(jnp.bfloat16)
    d_value = summed[..., feature_count:].astype(jnp.bfloat16)
    dq_flat = d_query.reshape(rows_total, feature_count)
    dk_flat = d_key.reshape(rows_total, feature_count)
    dv_flat = d_value.reshape(rows_total, feature_count)
    dweight_query = matmul_tn(flat_rows, dq_flat)
    dweight_key = matmul_tn(flat_rows, dk_flat)
    dweight_value = matmul_tn(flat_rows, dv_flat)
    dbias_query = jnp.sum(dq_flat.astype(jnp.float32), axis=0)
    dbias_value = jnp.sum(dv_flat.astype(jnp.float32), axis=0)
    grad_tokens = (
        matmul_nt(dq_flat, query_weight)
        + matmul_nt(dk_flat, key_weight)
        + matmul_nt(dv_flat, value_weight)
        + d_first
    )
    shards = (
        lax.psum_scatter(
            dweight_query.astype(jnp.bfloat16), "seq", scatter_dimension=0, tiled=True
        ).astype(jnp.float32),
        lax.psum_scatter(
            dweight_key.astype(jnp.bfloat16), "seq", scatter_dimension=0, tiled=True
        ).astype(jnp.float32),
        lax.psum_scatter(
            dweight_value.astype(jnp.bfloat16), "seq", scatter_dimension=0, tiled=True
        ).astype(jnp.float32),
        lax.psum_scatter(
            dweight_output.astype(jnp.bfloat16), "seq", scatter_dimension=0, tiled=True
        ).astype(jnp.float32),
        lax.psum_scatter(
            dweight_inner.astype(jnp.bfloat16), "seq", scatter_dimension=0, tiled=True
        ).astype(jnp.float32),
        lax.psum_scatter(
            dweight_outer.astype(jnp.bfloat16), "seq", scatter_dimension=0, tiled=True
        ).astype(jnp.float32),
        lax.psum_scatter(
            dbias_query.astype(jnp.bfloat16), "seq", scatter_dimension=0, tiled=True
        ).astype(jnp.float32),
        lax.psum_scatter(
            dbias_value.astype(jnp.bfloat16), "seq", scatter_dimension=0, tiled=True
        ).astype(jnp.float32),
        lax.psum_scatter(
            dbias_output.astype(jnp.bfloat16), "seq", scatter_dimension=0, tiled=True
        ).astype(jnp.float32),
        lax.psum_scatter(
            dbias_inner.astype(jnp.bfloat16), "seq", scatter_dimension=0, tiled=True
        ).astype(jnp.float32),
        lax.psum_scatter(
            dbias_outer.astype(jnp.bfloat16), "seq", scatter_dimension=0, tiled=True
        ).astype(jnp.float32),
        lax.psum_scatter(
            dgain_first.astype(jnp.bfloat16), "seq", scatter_dimension=0, tiled=True
        ).astype(jnp.float32),
        lax.psum_scatter(
            dshift_first.astype(jnp.bfloat16), "seq", scatter_dimension=0, tiled=True
        ).astype(jnp.float32),
        lax.psum_scatter(
            dgain_second.astype(jnp.bfloat16), "seq", scatter_dimension=0, tiled=True
        ).astype(jnp.float32),
        lax.psum_scatter(
            dshift_second.astype(jnp.bfloat16), "seq", scatter_dimension=0, tiled=True
        ).astype(jnp.float32),
    )
    finals = lax.psum(
        (
            shards[0],
            shards[1],
            shards[2],
            shards[3],
            shards[4],
            shards[5],
            shards[6],
            shards[7],
            shards[8],
            shards[9],
            shards[10],
            shards[11],
            shards[12],
            shards[13],
            shards[14],
        ),
        "ctx",
    )
    return (
        layer_out,
        grad_tokens.reshape(tok_rows, seq_count, feature_count),
        finals[0],
        finals[1],
        finals[2],
        finals[3],
        finals[4],
        finals[5],
        finals[6],
        finals[7],
        finals[8],
        finals[9],
        finals[10],
        finals[11],
        finals[12],
        finals[13],
        finals[14],
    )


def mark(name):
    return contextlib.nullcontext()


MESH = pl.DeviceIdType.MESH
BIG = 1e30
F32, BF16 = jnp.float32, jnp.bfloat16


def remote(src, dst, send_sem, recv_sem, seq, ctx):
    return pltpu.make_async_remote_copy(
        src_ref=src,
        dst_ref=dst,
        send_sem=send_sem,
        recv_sem=recv_sem,
        device_id=(seq, ctx),
        device_id_type=MESH,
    )


def greet(seq, ctx):
    barrier = pltpu.get_barrier_semaphore()
    for hop in range(1, 8):
        pl.semaphore_signal(
            barrier, inc=1, device_id=(seq, lax.rem(ctx + hop, 8)), device_id_type=MESH
        )
    for hop in range(1, 4):
        pl.semaphore_signal(
            barrier, inc=1, device_id=(lax.rem(seq + hop, 4), ctx), device_id_type=MESH
        )
    pl.semaphore_wait(barrier, 10)


def flip(index, bit):
    low = lax.rem(index // bit, 2)
    return index + bit - 2 * bit * low


def head_window(group):
    start = group * 192
    inside = lax.rem(group, 2) * 64
    return pl.multiple_of(start - inside, 128), pl.multiple_of(inside, 64)


def span(start, size, unit=16):
    return pl.ds(pl.multiple_of(start, unit), size)


VECTORS = [
    "b_query",
    "b_value",
    "b_output",
    "b_outer",
    "gain_one",
    "shift_one",
    "gain_two",
    "shift_two",
]
INPUTS = ["x", "cot", "seg", *VECTORS, "b_inner", "wq", "wk", "wv", "wo", "wi", "wu"]
OUTPUTS = ["layer", "grad", "fu", "fi", "fo", "fg", "vec_sum", "bias_sum"]
SCRATCH = {
    "seg_own": ((2, 8, 128), jnp.int32),
    "seg_all": ((8, 8, 128), jnp.int32),
    "pack_own": ((16, 768), BF16),
    "pack_all": ((4, 16, 768), BF16),
    "rows": ((8, 768), F32),
    "wo_full": ((4, 192, 768), BF16),
    "wi_full": ((4, 192, 3072), BF16),
    "wu_full": ((4, 768, 768), BF16),
    "xs": ((8, 128, 768), BF16),
    "wg": ((3, 4, 192, 256), BF16),
    "qa": ((3, 128, 1024), BF16),
    "ka": ((3, 128, 1024), BF16),
    "vt": ((3, 64, 1024), BF16),
    "ot": ((3, 64, 1024), F32),
    "sums": ((3, 1, 1024), F32),
    "key_rows": ((1024, 128), BF16),
    "o_send": ((192, 1024), BF16),
    "ctx_t": ((768, 256), BF16),
    "normed": ((256, 768), F32),
    "inverse": ((256, 1), F32),
    "low": ((256, 768), BF16),
    "low_t": ((768, 256), BF16),
    "act_t": ((4, 768, 256), BF16),
    "slope": ((4, 256, 768), F32),
    "work": ((256, 768), F32),
    "d_rows": ((256, 768), BF16),
    "v_rows": ((16, 768), F32),
    "gu": ((4, 768, 768), BF16),
    "gi": ((4, 192, 3072), BF16),
    "go": ((4, 192, 768), BF16),
    "core_u": ((2, 768, 768), BF16),
    "core_i": ((2, 192, 3072), BF16),
    "core_o": ((2, 192, 768), BF16),
    "xr_u": ((768, 768), BF16),
    "xr_i": ((192, 3072), BF16),
    "xr_o": ((192, 768), BF16),
    "rcv_u": ((768, 768), BF16),
    "rcv_i": ((192, 3072), BF16),
    "rcv_o": ((192, 768), BF16),
    "fin_u": ((768, 768), BF16),
    "fin_i": ((192, 3072), BF16),
    "fin_o": ((192, 768), BF16),
    "tot_0": ((192, 384), F32),
    "tot_1": ((192, 384), F32),
    "tot_2": ((96, 768), F32),
    "tot_3": ((96, 768), F32),
    "tot_4": ((96, 384), F32),
    "do_send": ((768, 256), BF16),
    "do_all": ((192, 1024), BF16),
    "du": ((64, 1024), BF16),
    "c_row": ((1, 1024), F32),
    "value_rows": ((1024, 64), BF16),
    "dk_acc": ((64, 1024), F32),
    "dv_acc": ((64, 1024), F32),
    "d_all": ((3, 256, 1024), BF16),
    "g_all": ((3, 4, 192, 256), BF16),
    "g_core": ((3, 2, 192, 256), BF16),
    "g_xs": ((3, 192, 256), BF16),
    "g_xr": ((3, 192, 256), BF16),
    "g_half": ((3, 192, 256), BF16),
    "g_mir": ((3, 96, 256), BF16),
    "dx_y": ((4, 768, 128), BF16),
    "dx_l": ((2, 768, 128), BF16),
    "dx_h": ((768, 128), BF16),
    "two_u": ((384, 384), BF16),
    "two_i": ((96, 1536), BF16),
    "v_own": ((4, 16, 256), F32),
    "v_recv": ((4, 16, 256), F32),
    "v_all": ((8, 16, 256), F32),
    "b_send": ((2, 8, 256), F32),
    "b_recv": ((8, 2, 8, 256), F32),
}
SEMAPHORES = {
    "loc": (24,),
    "w_ss": (5, 5),
    "w_rs": (5, 5),
    "x_ss": (7,),
    "x_rs": (7,),
    "s_ss": (8,),
    "s_rs": (8,),
    "p_ss": (4,),
    "p_rs": (4,),
    "g_ss": (3, 3),
    "g_rs": (3, 3),
    "o_ss": (8,),
    "o_rs": (8,),
    "r_ss": (5, 10),
    "r_rs": (5, 10),
    "do_ss": (8,),
    "do_rs": (8,),
    "dx_ss": (7,),
    "dx_rs": (7,),
    "v_ss": (2, 8),
    "v_rs": (2, 8),
    "b_ss": (8,),
    "b_rs": (8,),
    "h_ss": (7, 3),
    "h_rs": (7, 3),
}


def layer_kernel(*refs):
    r = types.SimpleNamespace(
        **dict(zip(INPUTS + OUTPUTS + list(SCRATCH) + list(SEMAPHORES), refs))
    )
    seq, ctx = lax.axis_index("seq"), lax.axis_index("ctx")
    plane = seq // 2
    mate, across = flip(seq, 1), flip(seq, 2)
    across_mate = flip(mate, 2)
    beside, paired, mirror = flip(ctx, 1), flip(ctx, 2), flip(ctx, 4)
    bit_y, bit_l, bit_h = lax.rem(ctx, 2), lax.rem(ctx // 2, 2), ctx // 4
    side, group = ctx // 4, lax.rem(ctx, 4)
    window, inside = head_window(group)
    own_lanes = span(ctx * 128, 128, 128)
    sent = []

    def wi_cut(k, where):
        which = where if k == 1 else 1 - where
        return span(which * 1536, 1536, 128)

    def w_views(k, where):
        if k == 0:
            return r.wo, lambda owner: r.wo_full.at[owner], 96
        if k in (1, 2):
            cols = wi_cut(k, where)
            return r.wi.at[:, cols], lambda owner: r.wi_full.at[owner, :, cols], 96
        part = slice(384 * (k - 3), 384 * (k - 2))
        return r.wu.at[part], lambda owner: r.wu_full.at[owner, part], 192

    beside_of = {k: (beside, bit_y) if k in (0, 2, 4) else (paired, bit_l) for k in range(5)}

    def half(view, rows, which):
        return view.at[span(which * rows, rows, 32)]

    def w_copy(k, leg):
        sems = r.w_ss.at[k, leg], r.w_rs.at[k, leg]
        shard, full, rows = w_views(k, 1 - plane if leg == 1 else plane)
        partner, bit = beside_of[k]
        if leg == 0:
            return remote(shard, full(seq), *sems, mate, ctx)
        if leg == 1:
            return remote(
                half(shard, rows, bit), half(full(seq), rows, bit), *sems, across, ctx
            )
        which = bit if leg in (2, 3) else 1 - bit
        came = half(full(across), rows, which)
        return remote(came, came, *sems, *((seq, partner) if leg == 2 else (mate, ctx)))

    def w_wait(k, leg):
        shard, full, rows = w_views(k, plane)
        bit = beside_of[k][1]
        spots = (
            lambda: full(mate),
            lambda: half(full(across), rows, bit),
            lambda: half(full(across), rows, 1 - bit),
            lambda: half(full(across_mate), rows, bit),
            lambda: half(full(across_mate), rows, 1 - bit),
        )
        spot = spots[leg]()
        remote(spot, spot, r.w_ss.at[k, leg], r.w_rs.at[k, leg], mate, ctx).wait_recv()

    def pass_across(k):
        w_wait(k, 1)
        w_copy(k, 2).start()
        w_copy(k, 3).start()

    def pass_beside(k):
        w_wait(k, 2)
        w_copy(k, 4).start()

    def w_done(k):
        for leg in (0, 3, 4):
            w_wait(k, leg)

    group_refs = (r.wq, r.wk, r.wv)
    g_local, w_local = [], []
    for which in range(3):
        g_local.append(
            pltpu.make_async_copy(
                group_refs[which].at[:, pl.ds(window, 256)],
                r.wg.at[which, seq],
                r.loc.at[which],
            )
        )
    for n, (ref, full) in enumerate(
        ((r.wo, r.wo_full), (r.wi, r.wi_full), (r.wu, r.wu_full))
    ):
        w_local.append(pltpu.make_async_copy(ref, full.at[seq], r.loc.at[3 + n]))
    own_block = pltpu.make_async_copy(r.x.at[side], r.xs.at[ctx], r.loc.at[6])
    for which in range(2):
        r.seg_own[which] = jnp.broadcast_to(r.seg[which : which + 1], (8, 128))
    r.pack_own[...] = jnp.zeros((16, 768), BF16)
    for n, name in enumerate(VECTORS):
        r.pack_own[n : n + 1, 0:192] = getattr(r, name)[...].reshape(1, 192)
    r.pack_own[8:9] = r.b_inner[...].reshape(1, 768)
    own_seg = pltpu.make_async_copy(r.seg_own.at[side], r.seg_all.at[ctx], r.loc.at[7])
    own_pack = pltpu.make_async_copy(r.pack_own, r.pack_all.at[seq], r.loc.at[8])
    for copy in g_local + [own_block, own_seg, own_pack] + w_local:
        copy.start()
    r.v_rows[...] = jnp.zeros((16, 768), F32)
    for which in range(3):
        r.d_all[which] = jnp.zeros((256, 1024), BF16)

    with mark("greet"):
        greet(seq, ctx)

    def send(*args):
        copy = remote(*args)
        copy.start()
        sent.append(copy)

    def landed(spot, send_sem, recv_sem):
        remote(spot, spot, send_sem, recv_sem, seq, beside).wait_recv()

    for hop in range(1, 8):
        other = lax.rem(ctx + hop, 8)
        send(
            r.seg_own.at[other // 4],
            r.seg_all.at[ctx],
            r.s_ss.at[hop],
            r.s_rs.at[hop],
            seq,
            other,
        )
    for hop in range(1, 4):
        other = lax.rem(seq + hop, 4)
        send(r.pack_own, r.pack_all.at[seq], r.p_ss.at[hop], r.p_rs.at[hop], other, ctx)
    send(r.x.at[1 - side], r.xs.at[ctx], r.x_ss.at[0], r.x_rs.at[0], seq, mirror)
    square = [side * 4 + lax.rem(group + hop, 4) for hop in range(1, 4)]
    for hop in range(1, 4):
        send(
            r.x.at[side],
            r.xs.at[ctx],
            r.x_ss.at[hop],
            r.x_rs.at[hop],
            seq,
            square[hop - 1],
        )
    for which in range(3):
        for n, other in enumerate((mate, across)):
            send(
                group_refs[which].at[:, pl.ds(window, 256)],
                r.wg.at[which, seq],
                r.g_ss.at[which, n],
                r.g_rs.at[which, n],
                other,
                ctx,
            )
    for k in range(5):
        w_copy(k, 0).start()
        w_copy(k, 1).start()

    tasks = {}

    def task(name):
        def keep_it(run):
            tasks[name] = run
            return run

        return keep_it

    for k in range(5):
        tasks[f"pa{k}"] = functools.partial(pass_across, k)
        tasks[f"pb{k}"] = functools.partial(pass_beside, k)

    @task("grp")
    def _():
        for which in range(3):
            spot = r.wg.at[which, across]
            landed(spot, r.g_ss.at[which, 1], r.g_rs.at[which, 1])
            send(spot, spot, r.g_ss.at[which, 2], r.g_rs.at[which, 2], mate, ctx)

    @task("far")
    def _():
        landed(r.xs.at[mirror], r.x_ss.at[0], r.x_rs.at[0])
        for n, other in enumerate(square):
            send(
                r.xs.at[mirror],
                r.xs.at[mirror],
                r.x_ss.at[4 + n],
                r.x_rs.at[4 + n],
                seq,
                other,
            )

    @task("small")
    def _():
        for which in range(3):
            g_local[which].wait()
            for n, owner in ((0, mate), (2, across_mate)):
                landed(
                    r.wg.at[which, owner], r.g_ss.at[which, n], r.g_rs.at[which, n]
                )
        own_pack.wait()
        for hop in range(1, 4):
            landed(
                r.pack_all.at[lax.rem(seq + 4 - hop, 4)], r.p_ss.at[hop], r.p_rs.at[hop]
            )
        own_seg.wait()
        for hop in range(1, 8):
            landed(
                r.seg_all.at[lax.rem(ctx + 8 - hop, 8)], r.s_ss.at[hop], r.s_rs.at[hop]
            )
        lane = lax.broadcasted_iota(jnp.int32, (256, 768), 1)
        at = lax.broadcasted_iota(jnp.int32, (256, 768), 0)
        rows = jnp.zeros((8, 768), F32)
        for owner in range(4):
            chosen = ((lane == at + 192 * owner) & (at < 192)).astype(BF16)
            rows += matmul(r.pack_all[owner, 0:8, 0:256], chosen)
        r.rows[...] = rows

    @task("qkv")
    def _():
        own_block.wait()
        for hop in range(1, 4):
            spot = r.xs.at[side * 4 + lax.rem(group + 4 - hop, 4)]
            landed(spot, r.x_ss.at[hop], r.x_rs.at[hop])
        for n in range(3):
            spot = r.xs.at[(1 - side) * 4 + lax.rem(group + 3 - n, 4)]
            landed(spot, r.x_ss.at[4 + n], r.x_rs.at[4 + n])
        tokens = r.xs[...].reshape(1024, 768)
        own_rows = r.pack_all[group]
        qkv = []
        for which in range(3):
            weight = r.wg[which].reshape(768, 256)
            product = matmul_nt(weight.T, tokens)
            if which != 1:
                bias = own_rows[which // 2 : which // 2 + 1, 0:256].astype(F32)
                column = jnp.broadcast_to(bias, (128, 256)).T
                shifted = jnp.where(inside == 0, column, pltpu.roll(column, 64, 0))
                product = product + jnp.concatenate([shifted] * 8, axis=1)
            part = product.astype(BF16)
            if which == 0:
                part = part * jnp.bfloat16(SCORE_SCALE)
            qkv.append(part)
        number = jnp.concatenate(
            [r.seg_all[block, 0:1] for block in range(8)], axis=1
        )
        hot = lax.broadcasted_iota(jnp.int32, (16, 1024), 0) == number
        query_marks = jnp.where(hot, 1.0, 0.0).astype(BF16)
        key_marks = jnp.where(hot, 0.0, -BIG).astype(BF16)
        blank = jnp.zeros((48, 1024), BF16)
        for head in range(3):
            parts = [
                jnp.where(
                    inside != 0,
                    part[64 * head + 64 : 64 * head + 128],
                    part[64 * head : 64 * head + 64],
                )
                for part in qkv
            ]
            r.qa[head] = jnp.concatenate([parts[0], query_marks, blank], axis=0)
            r.ka[head] = jnp.concatenate([parts[1], key_marks, blank], axis=0)
            r.vt[head] = parts[2]

    my_rows = span(group * 192, 192, 64)
    my_lanes = span(side * 128, 128, 128)
    own_o = pltpu.make_async_copy(
        r.o_send.at[:, own_lanes], r.ctx_t.at[my_rows, my_lanes], r.loc.at[9]
    )

    def attend_head(head):
        r.key_rows[...] = r.ka[head].T

        def attend(block, unused):
            lanes = span(block * 256, 256, 256)
            scores = matmul(r.key_rows[...], r.qa[head, :, lanes])
            unnorm = jnp.exp(scores)
            total = jnp.sum(unnorm, axis=0, keepdims=True)
            attended = matmul(r.vt[head], unnorm.astype(BF16)) / total
            r.ot[head, :, lanes] = attended
            r.sums[head, :, lanes] = total
            r.o_send[64 * head : 64 * head + 64, lanes] = attended.astype(BF16)
            return unused

        lax.fori_loop(0, 4, attend, 0)
        if head == 2:
            own_o.start()
            for hop in range(1, 8):
                other = lax.rem(ctx + hop, 8)
                send(
                    r.o_send.at[:, span(other * 128, 128, 128)],
                    r.ctx_t.at[my_rows, my_lanes],
                    r.o_ss.at[hop],
                    r.o_rs.at[hop],
                    seq,
                    other,
                )

    for head in range(3):
        tasks[f"at{head}"] = functools.partial(attend_head, head)

    def row_vec(n):
        return r.rows[n : n + 1]

    @task("fn")
    def _():
        own_o.wait()
        for hop in range(1, 8):
            other = lax.rem(ctx + 8 - hop, 8)
            spot = r.ctx_t.at[
                span(lax.rem(other, 4) * 192, 192, 64), span((other // 4) * 128, 128, 128)
            ]
            landed(spot, r.o_ss.at[hop], r.o_rs.at[hop])
        w_local[0].wait()
        w_done(0)

        def first_norm(which, unused):
            at, lanes = span(which * 128, 128, 128), span(which * 128, 128, 128)
            value = (
                matmul(r.ctx_t[:, lanes].T, r.wo_full[...].reshape(768, 768))
                + row_vec(2)
                + r.x[which].astype(F32)
            )
            hidden, normed, inverse = norm_forward(value, row_vec(4), row_vec(5))
            r.normed[at] = normed
            r.inverse[at] = inverse
            part = hidden.astype(BF16)
            r.low[at] = part
            r.low_t[:, lanes] = part.T
            r.work[at] = hidden + row_vec(3)
            return unused

        lax.fori_loop(0, 2, first_norm, 0)

    def inner_weight(n):
        return r.wi_full[:, :, span(n * 768, 768, 128)].reshape(768, 768)

    def feed(where):
        def visit(step, unused):
            n, which = where * 2 + step // 2, lax.rem(step, 2)
            at = span(which * 128, 128, 128)
            value = matmul(r.low[at], inner_weight(n)) + r.pack_all[n, 8:9].astype(F32)
            act, slope = gelu_parts(value)
            part = act.astype(BF16)
            r.slope[n, at] = slope
            r.act_t[n, :, at] = part.T
            r.work[at] += matmul(part, r.wu_full[n])
            return unused

        lax.fori_loop(0, 4, visit, 0)

    @task("fe0")
    def _():
        w_local[1].wait()
        w_local[2].wait()
        w_done(1)
        w_wait(3, 0)
        w_wait(4, 0)
        feed(plane)

    @task("fe1")
    def _():
        w_done(2)
        for k in (3, 4):
            w_wait(k, 3)
            w_wait(k, 4)
        feed(1 - plane)

    def tally(n, value):
        r.v_rows[n : n + 1] += jnp.sum(value, axis=0, keepdims=True)

    @task("sn")
    def _():
        def second_norm(which, unused):
            at = span(which * 128, 128, 128)
            result, normed, inverse = norm_forward(r.work[at], row_vec(6), row_vec(7))
            r.layer[which] = result.astype(BF16)
            upstream = r.cot[which].astype(F32)
            scaled = upstream * row_vec(6)
            back = inverse * (
                scaled
                - jnp.mean(scaled, axis=-1, keepdims=True)
                - normed * jnp.mean(scaled * normed, axis=-1, keepdims=True)
            )
            tally(4, upstream * normed)
            tally(5, upstream)
            r.work[at] = back
            part = back.astype(BF16)
            r.d_rows[at] = part
            tally(1, part.astype(F32))
            return unused

        lax.fori_loop(0, 2, second_norm, 0)

    chunks = [
        (r.gu, r.fu, r.core_u, r.xr_u, r.rcv_u, r.fin_u, r.tot_0, 0, 384, 0, 768),
        (r.gu, r.fu, r.core_u, r.xr_u, r.rcv_u, r.fin_u, r.tot_1, 384, 384, 0, 768),
        (r.gi, r.fi, r.core_i, r.xr_i, r.rcv_i, r.fin_i, r.tot_2, 0, 192, 0, 1536),
        (r.gi, r.fi, r.core_i, r.xr_i, r.rcv_i, r.fin_i, r.tot_3, 0, 192, 1536, 1536),
        (r.go, r.fo, r.core_o, r.xr_o, r.rcv_o, r.fin_o, r.tot_4, 0, 192, 0, 768),
    ]

    def reduce_steps(k, first):
        grad, out, core, arrived, rcv, fin, total, row, rows, col, cols = chunks[k]
        rr, cc = pl.ds(row, rows), pl.ds(col, cols)
        wide = cols // 2
        mine = span(col + bit_y * wide, wide, 128)
        other = span(col + (1 - bit_y) * wide, wide, 128)
        keep_l = span(row + bit_l * (rows // 2), rows // 2)
        give_l = span(row + (1 - bit_l) * (rows // 2), rows // 2)
        keep_h = span(row + bit_l * (rows // 2) + bit_h * (rows // 4), rows // 4)
        give_h = span(row + bit_l * (rows // 2) + (1 - bit_h) * (rows // 4), rows // 4)
        spot_h = span(row + (1 - bit_l) * (rows // 2), rows // 4)
        tot_keep, tot_give = (
            span(bit_h * (rows // 4), rows // 4),
            span((1 - bit_h) * (rows // 4), rows // 4),
        )
        owner = (seq, across)

        def sems(leg):
            return r.r_ss.at[k, leg], r.r_rs.at[k, leg]

        to_core = [
            remote(grad.at[mate, rr, cc], core.at[0, rr, cc], *sems(0), mate, ctx),
            remote(
                grad.at[across_mate, rr, cc], core.at[1, rr, cc], *sems(1), mate, ctx
            ),
        ]

        def add(at, lanes, slot, *more):
            value = grad[owner[slot], at, lanes].astype(F32) + core[
                slot, at, lanes
            ].astype(F32)
            for ref in more:
                value += ref[at, lanes].astype(F32)
            return value

        def put(at, lanes, slot, *more):
            core[slot, at, lanes] = add(at, lanes, slot, *more).astype(BF16)

        def spread(at, lanes, leg, target):
            spot = fin.at[at, lanes]
            return remote(spot, spot, *sems(leg), seq, target)

        to_h = remote(
            arrived.at[give_h, mine], rcv.at[spot_h, other], *sems(5), seq, mirror
        )

        def begin():
            for copy in to_core:
                copy.start()

        def cores_in():
            for copy in to_core:
                copy.wait_recv()

        if first == "x":
            to_x = remote(core.at[1, rr, cc], arrived.at[rr, cc], *sems(2), across, ctx)
            to_y = remote(arrived.at[rr, other], rcv.at[rr, other], *sems(3), seq, beside)
            at_y = remote(arrived.at[rr, mine], rcv.at[rr, mine], *sems(3), seq, beside)
            firsts = [to_x, to_y]

            def one():
                put(rr, cc, 1)
                to_x.start()

            def two():
                arrived[rr, other] = add(rr, other, 0, arrived).astype(BF16)
                to_y.start()

        elif first == "y":
            extra = r.two_u
            to_y = [
                remote(
                    core.at[0, rr, other], rcv.at[rr, other], *sems(3), seq, beside
                ),
                remote(core.at[1, rr, other], extra, *sems(9), seq, beside),
            ]
            at_y = [
                remote(core.at[0, rr, mine], rcv.at[rr, mine], *sems(3), seq, beside),
                remote(core.at[1, rr, mine], extra, *sems(9), seq, beside),
            ]
            to_x = remote(
                core.at[1, rr, mine], arrived.at[rr, mine], *sems(2), across, ctx
            )
            firsts = to_y + [to_x]

            def one():
                for slot in range(2):
                    put(rr, other, slot)
                    to_y[slot].start()

            def two():
                for copy in at_y:
                    copy.wait_recv()
                core[1, rr, mine] = (add(rr, mine, 1) + extra[...].astype(F32)).astype(
                    BF16
                )
                to_x.start()

        else:
            extra = r.two_i
            to_l = [
                remote(core.at[0, give_l, cc], rcv.at[give_l, cc], *sems(4), seq, paired),
                remote(core.at[1, give_l, cc], extra, *sems(9), seq, paired),
            ]
            at_l = [
                remote(core.at[0, keep_l, cc], rcv.at[keep_l, cc], *sems(4), seq, paired),
                remote(core.at[1, keep_l, cc], extra, *sems(9), seq, paired),
            ]
            to_x = remote(
                core.at[1, keep_l, cc], arrived.at[keep_l, cc], *sems(2), across, ctx
            )
            to_y = remote(
                arrived.at[keep_l, other], rcv.at[give_l, other], *sems(3), seq, beside
            )
            at_y = remote(
                arrived.at[keep_l, mine], rcv.at[give_l, mine], *sems(3), seq, beside
            )
            firsts = to_l + [to_x, to_y]

            def one():
                for slot in range(2):
                    put(give_l, cc, slot)
                    to_l[slot].start()

            def two():
                for copy in at_l:
                    copy.wait_recv()
                core[1, keep_l, cc] = (
                    add(keep_l, cc, 1) + extra[...].astype(F32)
                ).astype(BF16)
                to_x.start()

            def three():
                to_x.wait_recv()
                arrived[keep_l, other] = add(keep_l, other, 0, rcv, arrived).astype(BF16)
                to_y.start()
                total[...] = add(keep_l, mine, 0, rcv, arrived)

            def four():
                at_y.wait_recv()
                total[...] += rcv[give_l, mine].astype(F32)
                arrived[give_h, mine] = total[tot_give].astype(BF16)
                to_h.start()

        if first != "z":
            to_l = remote(
                arrived.at[give_l, mine], rcv.at[give_l, other], *sems(4), seq, paired
            )
            at_l = remote(
                arrived.at[keep_l, mine], rcv.at[keep_l, other], *sems(4), seq, paired
            )
            firsts = firsts + [to_l]

            def three():
                (at_y if first == "x" else to_x).wait_recv()
                arrived[give_l, mine] = add(give_l, mine, 0, arrived, rcv).astype(BF16)
                to_l.start()
                total[...] = add(keep_l, mine, 0, arrived, rcv)

            def four():
                at_l.wait_recv()
                arrived[give_h, mine] = (
                    total[tot_give] + rcv[give_h, other].astype(F32)
                ).astype(BF16)
                to_h.start()
                total[tot_keep] += rcv[keep_h, other].astype(F32)

        def step_one():
            cores_in()
            one()

        def step_two():
            if first == "x":
                to_x.wait_recv()
            two()

        def step_five():
            to_h.wait_recv()
            fin[keep_h, mine] = (
                total[tot_keep] + rcv[spot_h, other].astype(F32)
            ).astype(BF16)
            spread(keep_h, mine, 6, mirror).start()

        if first == "z":
            last = [(keep_l, other, 7, beside), (keep_l, cc, 8, paired)]
            ends = [(give_l, cc)]
            middle = (keep_l, mine)
        else:
            last = [(give_l, mine, 7, paired), (rr, mine, 8, beside)]
            ends = [(rr, other)]
            middle = (keep_l, mine)

        def step_six():
            spread(give_h, mine, 6, mirror).wait_recv()
            spread(*middle, 7, last[0][3]).start()

        def step_seven():
            spread(*last[0]).wait_recv()
            spread(*last[1]).start()

        to_out = pltpu.make_async_copy(fin.at[rr, cc], out.at[rr, cc], r.loc.at[10 + k])

        def step_eight():
            spread(*ends[0], 8, last[1][3]).wait_recv()
            to_out.start()

        def end():
            for copy in (
                to_core
                + firsts
                + [
                    to_h,
                    spread(keep_h, mine, 6, mirror),
                    spread(*middle, 7, last[0][3]),
                    spread(*last[1]),
                ]
            ):
                copy.wait_send()
            to_out.wait()

        names = [
            begin,
            step_one,
            step_two,
            three,
            four,
            step_five,
            step_six,
            step_seven,
            step_eight,
            end,
        ]
        for n, step in enumerate(names):
            tasks[f"s{k}_{n}"] = step

    for k in range(5):
        reduce_steps(k, FIRST[k])

    def make_outer(k):
        part = slice(384 * k, 384 * k + 384)
        for owner in (mate, across_mate):
            r.gu[owner, part] = matmul(r.act_t[owner, part], r.d_rows[...]).astype(BF16)
        tasks[f"s{k}_0"]()
        for owner in (across, seq):
            r.gu[owner, part] = matmul(r.act_t[owner, part], r.d_rows[...]).astype(BF16)

    for k in range(2):
        tasks[f"mo{k}"] = functools.partial(make_outer, k)

    def inner_step(n):
        def inner_back(which, unused):
            at = span(which * 128, 128, 128)
            part = (matmul_nt(r.d_rows[at], r.wu_full[n]) * r.slope[n, at]).astype(BF16)
            r.low[at] = part
            tally(8 + n, part.astype(F32))
            r.work[at] += matmul_nt(part, inner_weight(n))
            return unused

        lax.fori_loop(0, 2, inner_back, 0)
        r.gi[:, :, 768 * n : 768 * n + 768] = (
            matmul(r.low_t[...], r.low[...]).astype(BF16).reshape(4, 192, 768)
        )
        if n % 2:
            tasks[f"s{2 + n // 2}_0"]()

    for n in range(4):
        tasks[f"ib{n}"] = functools.partial(inner_step, n)

    own_do = pltpu.make_async_copy(
        r.do_send.at[my_rows, my_lanes], r.do_all.at[:, own_lanes], r.loc.at[15]
    )

    @task("fb")
    def _():
        def first_back(which, unused):
            at = span(which * 128, 128, 128)
            upstream, normed = r.work[at], r.normed[at]
            scaled = upstream * row_vec(4)
            back = r.inverse[at] * (
                scaled
                - jnp.mean(scaled, axis=-1, keepdims=True)
                - normed * jnp.mean(scaled * normed, axis=-1, keepdims=True)
            )
            tally(2, upstream * normed)
            tally(3, upstream)
            r.work[at] = back
            part = back.astype(BF16)
            r.low[at] = part
            tally(0, part.astype(F32))
            return unused

        lax.fori_loop(0, 2, first_back, 0)
        r.do_send[...] = matmul_nt(
            r.wo_full[...].reshape(768, 768), r.low[...]
        ).astype(BF16)
        own_do.start()
        for hop in range(1, 8):
            other = lax.rem(ctx + hop, 8)
            send(
                r.do_send.at[
                    span(lax.rem(other, 4) * 192, 192, 64), span((other // 4) * 128, 128, 128)
                ],
                r.do_all.at[:, own_lanes],
                r.do_ss.at[hop],
                r.do_rs.at[hop],
                seq,
                other,
            )

    @task("dwo")
    def _():
        r.go[...] = matmul(r.ctx_t[...], r.low[...]).astype(BF16).reshape(4, 192, 768)
        tasks["s4_0"]()
        for owner in range(4):
            start = 192 * owner - 64 * (owner % 2)
            r.v_own[owner, 0:8] = r.v_rows[0:8, start : start + 256]
            for part in range(3):
                r.v_own[owner, 8 + part : 9 + part] = r.v_rows[
                    8 + owner : 9 + owner, 256 * part : 256 * part + 256
                ]
            r.v_own[owner, 11:16] = jnp.zeros((5, 256), F32)
        for hop in range(1, 4):
            other = lax.rem(seq + hop, 4)
            send(
                r.v_own.at[other],
                r.v_recv.at[seq],
                r.v_ss.at[0, hop],
                r.v_rs.at[0, hop],
                other,
                ctx,
            )

    @task("v1")
    def _():
        for hop in range(1, 4):
            spot = r.v_recv.at[lax.rem(seq + 4 - hop, 4)]
            landed(spot, r.v_ss.at[0, hop], r.v_rs.at[0, hop])
        r.v_recv[seq] = r.v_own[seq]
        r.v_all[ctx] = r.v_recv[0] + r.v_recv[1] + r.v_recv[2] + r.v_recv[3]
        for hop in range(1, 8):
            send(
                r.v_all.at[ctx],
                r.v_all.at[ctx],
                r.v_ss.at[1, hop],
                r.v_rs.at[1, hop],
                seq,
                lax.rem(ctx + hop, 8),
            )

    def attend_back_head(head):
        if head == 0:
            own_do.wait()
            for hop in range(1, 8):
                spot = r.do_all.at[:, span(lax.rem(ctx + 8 - hop, 8) * 128, 128, 128)]
                landed(spot, r.do_ss.at[hop], r.do_rs.at[hop])
        at = span(inside + 64 * head, 64, 64)
        total = r.sums[head]
        d_out = r.do_all[64 * head : 64 * head + 64].astype(F32)
        r.du[...] = (d_out / total).astype(BF16)
        r.c_row[...] = jnp.sum(d_out * r.ot[head], axis=0, keepdims=True) / total
        r.key_rows[...] = r.ka[head].T
        r.value_rows[...] = r.vt[head].T
        r.dk_acc[...] = jnp.zeros((64, 1024), F32)
        r.dv_acc[...] = jnp.zeros((64, 1024), F32)

        def attend_back(block, unused):
            lanes = span(block * 256, 256, 256)
            scores = matmul(r.key_rows[...], r.qa[head, :, lanes])
            unnorm = jnp.exp(scores)
            d_prob = matmul(r.value_rows[...], r.du[:, lanes])
            d_score = (unnorm * (d_prob - r.c_row[:, lanes])).astype(BF16)
            d_query = matmul(r.ka[head, 0:64], d_score) * SCORE_SCALE
            r.d_all[0, at, lanes] = d_query.astype(BF16)
            r.dk_acc[...] += matmul_nt(r.qa[head, 0:64, lanes], d_score)
            r.dv_acc[...] += matmul_nt(r.du[:, lanes], unnorm.astype(BF16))
            return unused

        lax.fori_loop(0, 4, attend_back, 0)
        r.d_all[1, at] = r.dk_acc[...].astype(BF16)
        r.d_all[2, at] = r.dv_acc[...].astype(BF16)

    for head in range(3):
        tasks[f"ab{head}"] = functools.partial(attend_back_head, head)

    g_cores = [
        remote(
            r.g_all.at[which, owner],
            r.g_core.at[which, n],
            r.h_ss.at[which, n],
            r.h_rs.at[which, n],
            mate,
            ctx,
        )
        for which in range(3)
        for n, owner in ((0, mate), (1, across_mate))
    ]
    own_bias = pltpu.make_async_copy(
        r.b_send, r.b_recv.at[seq * 2 + side], r.loc.at[16]
    )
    to_owners = [
        remote(
            r.b_send,
            r.b_recv.at[seq * 2 + side],
            r.b_ss.at[hop],
            r.b_rs.at[seq * 2 + side],
            group,
            lax.rem(ctx + hop, 8),
        )
        for hop in range(8)
    ]

    @task("dwq")
    def _():
        ones = jnp.ones((16, 1024), BF16)
        for which in range(3):
            product = matmul(r.d_all[which], r.xs[...].reshape(1024, 768)).astype(BF16)
            r.g_all[which] = product.T.reshape(4, 192, 256)
            if which != 1:
                r.b_send[which // 2] = matmul_nt(ones, r.d_all[which])[0:8]
        for copy in g_cores:
            copy.start()

        @pl.when(group == seq)
        def _():
            own_bias.start()

        @pl.when(group != seq)
        def _():
            to_owners[0].start()

        for copy in to_owners[1:]:
            copy.start()

    @task("dx")
    def _():
        for part in range(4):
            lanes = slice(256 * part, 256 * part + 256)
            share = matmul(r.wg[0].reshape(768, 256), r.d_all[0, :, lanes])
            for which in (1, 2):
                share += matmul(r.wg[which].reshape(768, 256), r.d_all[which, :, lanes])
            r.act_t[part] = share.astype(BF16)

    def dx_half(part, bit):
        return r.act_t.at[part, :, span(bit * 128, 128, 128)]

    dx_to_y = [
        remote(
            dx_half(part, 1 - bit_y),
            r.dx_y.at[part],
            r.dx_ss.at[part],
            r.dx_rs.at[part],
            seq,
            beside,
        )
        for part in range(4)
    ]
    dx_to_l = [
        remote(
            dx_half(2 * n + 1 - bit_l, bit_y),
            r.dx_l.at[n],
            r.dx_ss.at[4 + n],
            r.dx_rs.at[4 + n],
            seq,
            paired,
        )
        for n in range(2)
    ]
    lanes_y = span(bit_y * 128, 128, 128)

    def dx_part(which):
        return 2 * which + bit_l

    dx_to_h = remote(
        dx_half(dx_part(1 - side), bit_y),
        r.dx_h,
        r.dx_ss.at[6],
        r.dx_rs.at[6],
        seq,
        mirror,
    )
    for part in range(4):
        tasks[f"d{part}"] = dx_to_y[part].start

    @task("dxp")
    def _():
        for copy in dx_to_y:
            copy.wait_recv()
        for n in range(2):
            part = 2 * n + 1 - bit_l
            r.act_t[part, :, lanes_y] = (
                r.act_t[part, :, lanes_y].astype(F32) + r.dx_y[part].astype(F32)
            ).astype(BF16)
            dx_to_l[n].start()

    def dx_total(which):
        part = dx_part(which)
        return (
            r.act_t[part, :, lanes_y].astype(F32)
            + r.dx_y[part].astype(F32)
            + r.dx_l[which].astype(F32)
        )

    @task("dxm")
    def _():
        for copy in dx_to_l:
            copy.wait_recv()
        r.act_t[dx_part(1 - side), :, lanes_y] = dx_total(1 - side).astype(BF16)
        dx_to_h.start()
        r.grad[side] = dx_total(side).T + r.work[span(side * 128, 128)]

    @task("dxe")
    def _():
        dx_to_h.wait_recv()
        r.grad[1 - side] = (
            r.dx_h[...].astype(F32).T + r.work[span((1 - side) * 128, 128)]
        )

    g_x = remote(r.g_xs, r.g_xr, r.h_ss.at[3, 0], r.h_rs.at[3, 0], across, ctx)
    keep, give = span(side * 96, 96, 32), span((1 - side) * 96, 96, 32)
    g_m = remote(
        r.g_half.at[:, give], r.g_mir, r.h_ss.at[3, 1], r.h_rs.at[3, 1], seq, mirror
    )

    @task("gx")
    def _():
        for copy in g_cores:
            copy.wait_recv()
        for which in range(3):
            r.g_xs[which] = (
                r.g_all[which, across].astype(F32) + r.g_core[which, 1].astype(F32)
            ).astype(BF16)
        g_x.start()

    @task("gm")
    def _():
        g_x.wait_recv()
        for which in range(3):
            r.g_half[which] = (
                r.g_all[which, seq].astype(F32)
                + r.g_core[which, 0].astype(F32)
                + r.g_xr[which].astype(F32)
            ).astype(BF16)
        g_m.start()

    @task("ga")
    def _():
        g_m.wait_recv()
        for which in range(3):
            r.fg[group, which, keep] = (
                r.g_half[which, keep].astype(F32) + r.g_mir[which].astype(F32)
            ).astype(BF16)
        spot = r.fg.at[group, :, keep]
        send(spot, spot, r.h_ss.at[4, 0], r.h_rs.at[4, 0], seq, mirror)
        for n, other in enumerate(square):
            send(spot, spot, r.h_ss.at[5, n], r.h_rs.at[5, n], seq, other)

    @task("gb")
    def _():
        theirs = r.fg.at[group, :, give]
        landed(theirs, r.h_ss.at[4, 0], r.h_rs.at[4, 0])
        for n, other in enumerate(square):
            send(theirs, theirs, r.h_ss.at[6, n], r.h_rs.at[6, n], seq, other)

    @task("v2")
    def _():
        for hop in range(1, 8):
            spot = r.v_all.at[lax.rem(ctx + 8 - hop, 8)]
            landed(spot, r.v_ss.at[1, hop], r.v_rs.at[1, hop])
        gathered = r.v_all[0]
        for n in range(1, 8):
            gathered += r.v_all[n]
        r.vec_sum[...] = gathered

    @task("be")
    def _():
        for n in range(8):
            spot = r.b_recv.at[n]
            arrival = remote(
                spot, spot, r.b_ss.at[0], r.b_rs.at[n], lax.rem(seq + 1, 4), ctx
            )
            here = (n // 2 == seq) & (n % 2 == side) & (group == seq)

            @pl.when(here)
            def _():
                own_bias.wait()

            @pl.when(jnp.logical_not(here))
            def _(arrival=arrival):
                arrival.wait_recv()

        row_sum = r.b_recv[0]
        for n in range(1, 8):
            row_sum += r.b_recv[n]
        r.bias_sum[...] = row_sum

    @task("ge")
    def _():
        for n in range(3):
            source = lax.rem(group + 3 - n, 4)
            landed(r.fg.at[source, :, keep], r.h_ss.at[5, n], r.h_rs.at[5, n])
            landed(r.fg.at[source, :, give], r.h_ss.at[6, n], r.h_rs.at[6, n])

    for name in ORDER:
        with mark(name):
            tasks[name]()

    with mark("ends"):
        for k in range(5):
            tasks[f"s{k}_9"]()
        for copy in (
            sent + g_cores + [g_x, g_m] + to_owners[1:] + dx_to_y + dx_to_l + [dx_to_h]
        ):
            copy.wait_send()

        @pl.when(group != seq)
        def _():
            to_owners[0].wait_send()

        for k in range(5):
            for leg in range(5):
                w_copy(k, leg).wait_send()


FIRST = ("x", "y", "z", "x", "x")
ORDER = [
    "grp",
    "small",
    "pa0",
    "far",
    "pb0",
    "pa1",
    "qkv",
    "pa2",
    "at0",
    "at1",
    "at2",
    "pa3",
    "pb1",
    "pb2",
    "pa4",
    "fn",
    "fe0",
    "pb3",
    "pb4",
    "fe1",
    "sn",
    "mo0",
    "mo1",
    "ib0",
    "s0_1",
    "ib1",
    "s1_1",
    "ib2",
    "ib3",
    "fb",
    "dwo",
    "s2_1",
    "s3_1",
    "s4_1",
    "s0_2",
    "v1",
    "s1_2",
    "ab0",
    "ab1",
    "s3_2",
    "s0_3",
    "ab2",
    "dwq",
    "s0_4",
    "dx",
    "d0",
    "v2",
    "s2_2",
    "s4_2",
    "gx",
    "s3_3",
    "s0_5",
    "s1_3",
    "s3_4",
    "d1",
    "be",
    "s4_3",
    "s0_6",
    "d2",
    "s1_4",
    "s2_3",
    "s3_5",
    "s4_4",
    "gm",
    "s0_7",
    "s1_5",
    "s2_4",
    "s3_6",
    "s4_5",
    "d3",
    "ga",
    "s0_8",
    "s1_6",
    "s3_7",
    "s2_5",
    "dxp",
    "s4_6",
    "gb",
    "s1_7",
    "s2_6",
    "s3_8",
    "dxm",
    "s4_7",
    "s1_8",
    "ge",
    "s2_7",
    "s4_8",
    "dxe",
    "s2_8",
]


def run_layer(*operands):
    vmem = pl.BlockSpec(memory_space=pltpu.VMEM)
    anywhere = pl.BlockSpec(memory_space=pl.ANY)
    shape = jax.ShapeDtypeStruct
    return pl.pallas_call(
        layer_kernel,
        name="layer_kernel",
        out_shape=(
            shape((2, 128, 768), BF16),
            shape((2, 128, 768), F32),
            shape((768, 768), BF16),
            shape((192, 3072), BF16),
            shape((192, 768), BF16),
            shape((4, 3, 192, 256), BF16),
            shape((16, 256), F32),
            shape((2, 8, 256), F32),
        ),
        in_specs=[vmem] * 12 + [anywhere] * 6,
        out_specs=(vmem,) * 2 + (anywhere,) * 3 + (vmem,) * 3,
        scratch_shapes=[pltpu.VMEM(*spec) for spec in SCRATCH.values()]
        + [pltpu.SemaphoreType.DMA(count) for count in SEMAPHORES.values()],
        compiler_params=pltpu.CompilerParams(
            collective_id=1, has_side_effects=True, vmem_limit_bytes=67043328
        ),
    )(*operands)


def fast_body(
    tokens,
    segment_ids,
    w_query,
    w_key,
    w_value,
    w_output,
    w_inner,
    w_outer,
    b_query,
    b_value,
    b_output,
    b_inner,
    b_outer,
    gain_first,
    shift_first,
    gain_second,
    shift_second,
    cotangent,
):
    layer, grad, fu, fi, fo, fg, vec_sum, bias_sum = run_layer(
        jnp.transpose(tokens, (1, 0, 2)),
        jnp.transpose(cotangent, (1, 0, 2)),
        segment_ids,
        b_query,
        b_value,
        b_output,
        b_outer,
        gain_first,
        shift_first,
        gain_second,
        shift_second,
        b_inner,
        w_query,
        w_key,
        w_value,
        w_output,
        w_inner,
        w_outer,
    )

    def widen(part):
        tiles = part.astype(F32)
        return jnp.concatenate(
            [
                tiles[0, :, 0:128],
                tiles[0, :, 128:256] + tiles[1, :, 0:128],
                tiles[1, :, 128:256],
                tiles[2, :, 0:128],
                tiles[2, :, 128:256] + tiles[3, :, 0:128],
                tiles[3, :, 128:256],
            ],
            axis=1,
        )

    odd = lax.rem(lax.axis_index("seq"), 2) == 1

    def owned(row):
        return jnp.where(odd, row[64:256], row[0:192])

    return (
        jnp.transpose(layer, (1, 0, 2)),
        jnp.transpose(grad, (1, 0, 2)),
        widen(fg[:, 0]),
        widen(fg[:, 1]),
        widen(fg[:, 2]),
        fo.astype(F32),
        fi.astype(F32),
        fu.astype(F32),
        owned(bias_sum[0, 0]),
        owned(bias_sum[1, 0]),
        owned(vec_sum[0]),
        vec_sum[8:11].reshape(768),
        owned(vec_sum[1]),
        owned(vec_sum[2]),
        owned(vec_sum[3]),
        owned(vec_sum[4]),
        owned(vec_sum[5]),
    )


def solution(mesh):
    in_specs = (
        P("ctx", "seq", None),
        P("seq", "ctx"),
        P("seq", None),
        P("seq", None),
        P("seq", None),
        P("seq", None),
        P("seq", None),
        P("seq", None),
        P("seq"),
        P("seq"),
        P("seq"),
        P("seq"),
        P("seq"),
        P("seq"),
        P("seq"),
        P("seq"),
        P("seq"),
        P("ctx", "seq", None),
    )
    out_specs = (
        P("ctx", "seq", None),
        P("ctx", "seq", None),
        P("seq", None),
        P("seq", None),
        P("seq", None),
        P("seq", None),
        P("seq", None),
        P("seq", None),
        P("seq"),
        P("seq"),
        P("seq"),
        P("seq"),
        P("seq"),
        P("seq"),
        P("seq"),
        P("seq"),
        P("seq"),
    )
    small = mesh.shape["seq"] == 4 and mesh.shape["ctx"] == 8
    step = fast_body if small else body
    return jax.shard_map(step, mesh=mesh, in_specs=in_specs, out_specs=out_specs, check_vma=False)
```

```python
import functools
import math
import types

import jax
import jax.numpy as jnp
from jax import lax
from jax.experimental import pallas as pl
from jax.experimental.pallas import tpu as pltpu
from jax.sharding import PartitionSpec as P

H = 12
DH = 64


EPSILON = 1e-12
SCORE_SCALE = 0.125


def matmul(first_op, second_op):
    return jnp.dot(first_op, second_op, preferred_element_type=jnp.float32)


def matmul_tn(first_op, second_op):
    return lax.dot_general(
        first_op, second_op, (((0,), (0,)), ((), ())), preferred_element_type=jnp.float32
    )


def matmul_nt(first_op, second_op):
    return lax.dot_general(
        first_op, second_op, (((1,), (1,)), ((), ())), preferred_element_type=jnp.float32
    )


def norm_forward(values, gain_vec, shift_vec):
    center = values - jnp.mean(values, axis=-1, keepdims=True)
    inverse = lax.rsqrt(jnp.mean(center * center, axis=-1, keepdims=True) + EPSILON)
    normed = center * inverse
    return (normed * gain_vec + shift_vec, normed, inverse)


def norm_backward(upstream, normed, inverse, gain_vec):
    scaled = upstream * gain_vec
    back_grad = inverse * (
        scaled
        - jnp.mean(scaled, axis=-1, keepdims=True)
        - normed * jnp.mean(scaled * normed, axis=-1, keepdims=True)
    )
    return (back_grad, jnp.sum(upstream * normed, axis=0), jnp.sum(upstream, axis=0))


def gelu_parts(values):
    cumulative = 0.5 * (1.0 + lax.erf(values * 0.7071067811865476))
    return (
        values * cumulative,
        cumulative + values * jnp.exp(-0.5 * values * values) * 0.3989422804014327,
    )


def block_scores(query_heads, key_heads, seg_query, seg_key):
    raw_scores = (
        jnp.einsum("ishd,jshd->shij", query_heads, key_heads, preferred_element_type=jnp.float32)
        * SCORE_SCALE
    )
    allowed = (jnp.transpose(seg_query)[:, :, None] == jnp.transpose(seg_key)[:, None, :])[:, None]
    return jnp.where(allowed, jnp.exp(raw_scores), 0.0)


def attend_keys(query_heads, seg_query, carry_in, piece_rows):
    key_piece, value_piece, seg_piece = piece_rows
    row_count, seq_count, feature_count = key_piece.shape
    heads, head_size = (query_heads.shape[2], query_heads.shape[3])
    step_rows = math.gcd(row_count, 1024)
    block_count = row_count // step_rows
    key_blocks = key_piece.reshape(block_count, step_rows, seq_count, heads, head_size)
    value_blocks = value_piece.reshape(block_count, step_rows, seq_count, heads, head_size)
    seg_blocks = seg_piece.reshape(block_count, step_rows, seq_count)

    def attend_visit_block(running, element):
        key_block, value_block, seg_block = element
        unnorm = block_scores(query_heads, key_block, seg_query, seg_block)
        totals = running[0] + jnp.sum(unnorm, axis=-1)
        mixture = running[1] + jnp.einsum(
            "shij,jshd->ishd",
            unnorm.astype(jnp.bfloat16),
            value_block,
            preferred_element_type=jnp.float32,
        )
        return ((totals, mixture), None)

    result, unused = lax.scan(attend_visit_block, carry_in, (key_blocks, value_blocks, seg_blocks))
    return result


def key_side(query_heads, d_mixture, correction, seg_query, key_all, value_all, seg_all):
    row_count, seq_count, feature_count = key_all.shape
    heads, head_size = (query_heads.shape[2], query_heads.shape[3])
    step_rows = math.gcd(row_count, 1024)
    block_count = row_count // step_rows
    corr_cols = jnp.transpose(correction, (1, 2, 0))[..., None]
    key_blocks = key_all.reshape(block_count, step_rows, seq_count, heads, head_size)
    value_blocks = value_all.reshape(block_count, step_rows, seq_count, heads, head_size)
    seg_blocks = seg_all.reshape(block_count, step_rows, seq_count)

    def key_visit_block(dq_acc, element):
        key_block, value_block, seg_block = element
        unnorm = block_scores(query_heads, key_block, seg_query, seg_block)
        d_prob = jnp.einsum(
            "ishd,jshd->shij", d_mixture, value_block, preferred_element_type=jnp.float32
        )
        d_score = (unnorm * (d_prob - corr_cols)).astype(jnp.bfloat16)
        dq_acc = dq_acc + jnp.einsum(
            "shij,jshd->ishd", d_score, key_block, preferred_element_type=jnp.float32
        )
        d_key = (
            jnp.einsum("shij,ishd->jshd", d_score, query_heads, preferred_element_type=jnp.float32)
            * SCORE_SCALE
        )
        d_value = jnp.einsum(
            "shij,ishd->jshd",
            unnorm.astype(jnp.bfloat16),
            d_mixture,
            preferred_element_type=jnp.float32,
        )
        stacked = jnp.concatenate(
            [
                d_key.reshape(step_rows, seq_count, feature_count),
                d_value.reshape(step_rows, seq_count, feature_count),
            ],
            axis=-1,
        )
        return (dq_acc, stacked)

    dq_sum, stacked_all = lax.scan(
        key_visit_block,
        jnp.zeros(query_heads.shape, jnp.float32),
        (key_blocks, value_blocks, seg_blocks),
    )
    return (dq_sum, stacked_all.reshape(row_count, seq_count, 2 * feature_count))


def body(
    tokens,
    segment_ids,
    w_query,
    w_key,
    w_value,
    w_output,
    w_inner,
    w_outer,
    b_query,
    b_value,
    b_output,
    b_inner,
    b_outer,
    gain_first,
    shift_first,
    gain_second,
    shift_second,
    cotangent,
):
    tok_rows, seq_count, feature_count = tokens.shape
    rows_total = tok_rows * seq_count
    gathered = (
        lax.all_gather(w_query, "seq", axis=0, tiled=True),
        lax.all_gather(w_key, "seq", axis=0, tiled=True),
        lax.all_gather(w_value, "seq", axis=0, tiled=True),
        lax.all_gather(w_output, "seq", axis=0, tiled=True),
        lax.all_gather(w_inner, "seq", axis=0, tiled=True),
        lax.all_gather(w_outer, "seq", axis=0, tiled=True),
        lax.all_gather(b_query, "seq", axis=0, tiled=True),
        lax.all_gather(b_value, "seq", axis=0, tiled=True),
        lax.all_gather(b_output, "seq", axis=0, tiled=True),
        lax.all_gather(b_inner, "seq", axis=0, tiled=True),
        lax.all_gather(b_outer, "seq", axis=0, tiled=True),
        lax.all_gather(gain_first, "seq", axis=0, tiled=True),
        lax.all_gather(shift_first, "seq", axis=0, tiled=True),
        lax.all_gather(gain_second, "seq", axis=0, tiled=True),
        lax.all_gather(shift_second, "seq", axis=0, tiled=True),
    )
    query_weight, key_weight, value_weight, output_weight, inner_weight, outer_weight = gathered[:6]
    (
        query_bias,
        value_bias,
        output_bias,
        inner_bias,
        outer_bias,
        gain_one,
        shift_one,
        gain_two,
        shift_two,
    ) = [vector.astype(jnp.float32) for vector in gathered[6:]]
    flat_rows = tokens.reshape(rows_total, feature_count)
    flat_float = flat_rows.astype(jnp.float32)
    seg_local = jnp.transpose(segment_ids)
    queries = (matmul(flat_rows, query_weight) + query_bias).astype(jnp.bfloat16)
    key_rows = matmul(flat_rows, key_weight).astype(jnp.bfloat16)
    value_rows = (matmul(flat_rows, value_weight) + value_bias).astype(jnp.bfloat16)
    query_heads = queries.reshape(tok_rows, seq_count, H, DH)
    key_block_rows = key_rows.reshape(tok_rows, seq_count, feature_count)
    value_block_rows = value_rows.reshape(tok_rows, seq_count, feature_count)
    initial = (
        jnp.zeros((seq_count, H, tok_rows), jnp.float32),
        jnp.zeros((tok_rows, seq_count, H, DH), jnp.float32),
    )
    totals, mixture = attend_keys(
        query_heads,
        seg_local,
        initial,
        (
            lax.all_gather(key_block_rows, "ctx", axis=0, tiled=True),
            lax.all_gather(value_block_rows, "ctx", axis=0, tiled=True),
            lax.all_gather(seg_local, "ctx", axis=0, tiled=True),
        ),
    )
    denominator = jnp.transpose(totals, (2, 0, 1))[..., None]
    attended = mixture / denominator
    context = attended.astype(jnp.bfloat16).reshape(rows_total, feature_count)
    first_in = matmul(context, output_weight) + output_bias + flat_float
    hidden, normed_one, inverse_one = norm_forward(first_in, gain_one, shift_one)
    hidden_low = hidden.astype(jnp.bfloat16)
    inner_pre = matmul(hidden_low, inner_weight) + inner_bias
    activated, gelu_slope = gelu_parts(inner_pre)
    act_low = activated.astype(jnp.bfloat16)
    second_in = matmul(act_low, outer_weight) + outer_bias + hidden
    result, normed_two, inverse_two = norm_forward(second_in, gain_two, shift_two)
    layer_out = result.astype(jnp.bfloat16).reshape(tok_rows, seq_count, feature_count)
    upstream = cotangent.astype(jnp.float32).reshape(rows_total, feature_count)
    d_second, dgain_second, dshift_second = norm_backward(
        upstream, normed_two, inverse_two, gain_two
    )
    d_outer = d_second.astype(jnp.bfloat16)
    dbias_outer = jnp.sum(d_outer.astype(jnp.float32), axis=0)
    dweight_outer = matmul_tn(act_low, d_outer)
    d_inner = (matmul_nt(d_outer, outer_weight) * gelu_slope).astype(jnp.bfloat16)
    dbias_inner = jnp.sum(d_inner.astype(jnp.float32), axis=0)
    dweight_inner = matmul_tn(hidden_low, d_inner)
    d_hidden = matmul_nt(d_inner, inner_weight) + d_second
    d_first, dgain_first, dshift_first = norm_backward(d_hidden, normed_one, inverse_one, gain_one)
    d_branch = d_first.astype(jnp.bfloat16)
    dbias_output = jnp.sum(d_branch.astype(jnp.float32), axis=0)
    dweight_output = matmul_tn(context, d_branch)
    d_context = (
        matmul_nt(d_branch, output_weight).astype(jnp.bfloat16).reshape(tok_rows, seq_count, H, DH)
    )
    d_float = d_context.astype(jnp.float32)
    d_mixture = (d_float / denominator).astype(jnp.bfloat16)
    correction = jnp.sum(d_float * attended, axis=-1) / denominator[..., 0]
    key_all, value_all, seg_all = (
        lax.all_gather(key_block_rows, "ctx", axis=0, tiled=True),
        lax.all_gather(value_block_rows, "ctx", axis=0, tiled=True),
        lax.all_gather(seg_local, "ctx", axis=0, tiled=True),
    )
    dq_sum, term_rows = key_side(
        query_heads, d_mixture, correction, seg_local, key_all, value_all, seg_all
    )
    summed = lax.psum_scatter(term_rows, "ctx", scatter_dimension=0, tiled=True)
    d_query = (dq_sum * SCORE_SCALE).astype(jnp.bfloat16)
    d_key = summed[..., :feature_count].astype(jnp.bfloat16)
    d_value = summed[..., feature_count:].astype(jnp.bfloat16)
    dq_flat = d_query.reshape(rows_total, feature_count)
    dk_flat = d_key.reshape(rows_total, feature_count)
    dv_flat = d_value.reshape(rows_total, feature_count)
    dweight_query = matmul_tn(flat_rows, dq_flat)
    dweight_key = matmul_tn(flat_rows, dk_flat)
    dweight_value = matmul_tn(flat_rows, dv_flat)
    dbias_query = jnp.sum(dq_flat.astype(jnp.float32), axis=0)
    dbias_value = jnp.sum(dv_flat.astype(jnp.float32), axis=0)
    grad_tokens = (
        matmul_nt(dq_flat, query_weight)
        + matmul_nt(dk_flat, key_weight)
        + matmul_nt(dv_flat, value_weight)
        + d_first
    )
    shards = (
        lax.psum_scatter(
            dweight_query.astype(jnp.bfloat16), "seq", scatter_dimension=0, tiled=True
        ).astype(jnp.float32),
        lax.psum_scatter(
            dweight_key.astype(jnp.bfloat16), "seq", scatter_dimension=0, tiled=True
        ).astype(jnp.float32),
        lax.psum_scatter(
            dweight_value.astype(jnp.bfloat16), "seq", scatter_dimension=0, tiled=True
        ).astype(jnp.float32),
        lax.psum_scatter(
            dweight_output.astype(jnp.bfloat16), "seq", scatter_dimension=0, tiled=True
        ).astype(jnp.float32),
        lax.psum_scatter(
            dweight_inner.astype(jnp.bfloat16), "seq", scatter_dimension=0, tiled=True
        ).astype(jnp.float32),
        lax.psum_scatter(
            dweight_outer.astype(jnp.bfloat16), "seq", scatter_dimension=0, tiled=True
        ).astype(jnp.float32),
        lax.psum_scatter(
            dbias_query.astype(jnp.bfloat16), "seq", scatter_dimension=0, tiled=True
        ).astype(jnp.float32),
        lax.psum_scatter(
            dbias_value.astype(jnp.bfloat16), "seq", scatter_dimension=0, tiled=True
        ).astype(jnp.float32),
        lax.psum_scatter(
            dbias_output.astype(jnp.bfloat16), "seq", scatter_dimension=0, tiled=True
        ).astype(jnp.float32),
        lax.psum_scatter(
            dbias_inner.astype(jnp.bfloat16), "seq", scatter_dimension=0, tiled=True
        ).astype(jnp.float32),
        lax.psum_scatter(
            dbias_outer.astype(jnp.bfloat16), "seq", scatter_dimension=0, tiled=True
        ).astype(jnp.float32),
        lax.psum_scatter(
            dgain_first.astype(jnp.bfloat16), "seq", scatter_dimension=0, tiled=True
        ).astype(jnp.float32),
        lax.psum_scatter(
            dshift_first.astype(jnp.bfloat16), "seq", scatter_dimension=0, tiled=True
        ).astype(jnp.float32),
        lax.psum_scatter(
            dgain_second.astype(jnp.bfloat16), "seq", scatter_dimension=0, tiled=True
        ).astype(jnp.float32),
        lax.psum_scatter(
            dshift_second.astype(jnp.bfloat16), "seq", scatter_dimension=0, tiled=True
        ).astype(jnp.float32),
    )
    finals = lax.psum(
        (
            shards[0],
            shards[1],
            shards[2],
            shards[3],
            shards[4],
            shards[5],
            shards[6],
            shards[7],
            shards[8],
            shards[9],
            shards[10],
            shards[11],
            shards[12],
            shards[13],
            shards[14],
        ),
        "ctx",
    )
    return (
        layer_out,
        grad_tokens.reshape(tok_rows, seq_count, feature_count),
        finals[0],
        finals[1],
        finals[2],
        finals[3],
        finals[4],
        finals[5],
        finals[6],
        finals[7],
        finals[8],
        finals[9],
        finals[10],
        finals[11],
        finals[12],
        finals[13],
        finals[14],
    )


MESH = pl.DeviceIdType.MESH
BIG = 1e30
F32, BF16 = jnp.float32, jnp.bfloat16


def remote(src, dst, send_sem, recv_sem, seq, ctx):
    return pltpu.make_async_remote_copy(
        src_ref=src,
        dst_ref=dst,
        send_sem=send_sem,
        recv_sem=recv_sem,
        device_id=(seq, ctx),
        device_id_type=MESH,
    )


def greet(seq, ctx):
    barrier = pltpu.get_barrier_semaphore()
    for hop in range(1, 8):
        pl.semaphore_signal(
            barrier, inc=1, device_id=(seq, lax.rem(ctx + hop, 8)), device_id_type=MESH
        )
    for hop in range(1, 4):
        pl.semaphore_signal(
            barrier, inc=1, device_id=(lax.rem(seq + hop, 4), ctx), device_id_type=MESH
        )
    pl.semaphore_wait(barrier, 10)


def flip(index, bit):
    low = lax.rem(index // bit, 2)
    return index + bit - 2 * bit * low


def head_window(group):
    start = group * 192
    inside = lax.rem(group, 2) * 64
    return pl.multiple_of(start - inside, 128), pl.multiple_of(inside, 64)


def span(start, size, unit=16):
    return pl.ds(pl.multiple_of(start, unit), size)


VECTORS = list(
    dict(
        b_query=0,
        b_value=0,
        b_output=0,
        b_outer=0,
        gain_one=0,
        shift_one=0,
        gain_two=0,
        shift_two=0,
    )
)
INPUTS = [
    *dict(x=0, cot=0, seg=0),
    *VECTORS,
    *dict(b_inner=0, wq=0, wk=0, wv=0, wo=0, wi=0, wu=0),
]
OUTPUTS = list(dict(layer=0, grad=0, fu=0, fi=0, fo=0, fg=0, vec_sum=0, bias_sum=0))
SCRATCH = dict(
    seg_own=((2, 8, 128), jnp.int32),
    seg_all=((8, 8, 128), jnp.int32),
    pack_own=((16, 768), BF16),
    pack_all=((4, 16, 768), BF16),
    rows=((8, 768), F32),
    wo_full=((4, 192, 768), BF16),
    wi_full=((4, 192, 3072), BF16),
    wu_full=((4, 768, 768), BF16),
    xs=((8, 128, 768), BF16),
    wg=((3, 4, 192, 256), BF16),
    qa=((3, 128, 1024), BF16),
    ka=((3, 128, 1024), BF16),
    vt=((3, 64, 1024), BF16),
    ot=((3, 64, 1024), F32),
    sums=((3, 1, 1024), F32),
    key_rows=((1024, 128), BF16),
    o_send=((192, 1024), BF16),
    ctx_t=((768, 256), BF16),
    normed=((256, 768), F32),
    inverse=((256, 1), F32),
    low=((256, 768), BF16),
    low_t=((768, 256), BF16),
    act_t=((4, 768, 256), BF16),
    slope=((4, 256, 768), F32),
    work=((256, 768), F32),
    d_rows=((256, 768), BF16),
    v_rows=((16, 768), F32),
    gu=((4, 768, 768), BF16),
    gi=((4, 192, 3072), BF16),
    go=((4, 192, 768), BF16),
    core_u=((2, 768, 768), BF16),
    core_i=((2, 192, 3072), BF16),
    core_o=((2, 192, 768), BF16),
    xr_u=((768, 768), BF16),
    xr_i=((192, 3072), BF16),
    xr_o=((192, 768), BF16),
    rcv_u=((768, 768), BF16),
    rcv_i=((192, 3072), BF16),
    rcv_o=((192, 768), BF16),
    fin_u=((768, 768), BF16),
    fin_i=((192, 3072), BF16),
    fin_o=((192, 768), BF16),
    tot_0=((192, 384), F32),
    tot_1=((192, 384), F32),
    tot_2=((96, 768), F32),
    tot_3=((96, 768), F32),
    tot_4=((96, 384), F32),
    do_send=((768, 256), BF16),
    do_all=((192, 1024), BF16),
    du=((64, 1024), BF16),
    c_row=((1, 1024), F32),
    value_rows=((1024, 64), BF16),
    dk_acc=((64, 1024), F32),
    dv_acc=((64, 1024), F32),
    d_all=((3, 256, 1024), BF16),
    g_all=((3, 4, 192, 256), BF16),
    g_core=((3, 2, 192, 256), BF16),
    g_xs=((3, 192, 256), BF16),
    g_xr=((3, 192, 256), BF16),
    g_half=((3, 192, 256), BF16),
    g_mir=((3, 96, 256), BF16),
    dx_y=((4, 768, 128), BF16),
    dx_l=((2, 768, 128), BF16),
    dx_h=((768, 128), BF16),
    two_u=((384, 384), BF16),
    two_i=((96, 1536), BF16),
    v_own=((4, 16, 256), F32),
    v_recv=((4, 16, 256), F32),
    v_all=((8, 16, 256), F32),
    b_send=((2, 8, 256), F32),
    b_recv=((8, 2, 8, 256), F32),
)
SEMAPHORES = dict(
    loc=(24,),
    w_ss=(7, 5),
    w_rs=(7, 5),
    x_ss=(11,),
    x_rs=(11,),
    s_ss=(8,),
    s_rs=(8,),
    p_ss=(4,),
    p_rs=(4,),
    g_ss=(3, 3),
    g_rs=(3, 3),
    o_ss=(3, 8),
    o_rs=(3, 8),
    r_ss=(5, 10),
    r_rs=(5, 10),
    do_ss=(3, 8),
    do_rs=(3, 8),
    dx_ss=(7,),
    dx_rs=(7,),
    v_ss=(2, 8),
    v_rs=(2, 8),
    b_ss=(8,),
    b_rs=(8,),
    h_ss=(7, 3),
    h_rs=(7, 3),
)


def layer_kernel(*refs):
    r = types.SimpleNamespace(
        **dict(zip(INPUTS + OUTPUTS + list(SCRATCH) + list(SEMAPHORES), refs))
    )
    seq, ctx = lax.axis_index("seq"), lax.axis_index("ctx")
    plane = seq // 2
    mate, across = flip(seq, 1), flip(seq, 2)
    across_mate = flip(mate, 2)
    beside, paired, mirror = flip(ctx, 1), flip(ctx, 2), flip(ctx, 4)
    bit_y, bit_l, bit_h = lax.rem(ctx, 2), lax.rem(ctx // 2, 2), ctx // 4
    side, group = ctx // 4, lax.rem(ctx, 4)
    window, inside = head_window(group)
    own_lanes = span(ctx * 128, 128, 128)
    sent = []

    def wi_cut(k, where):
        which = where if k == 1 else 1 - where
        return span(which * 1536, 1536, 128)

    def w_views(k, where):
        if k == 0:
            return r.wo, lambda owner: r.wo_full.at[owner], 96
        if k in (1, 2):
            cols = wi_cut(k, where)
            return r.wi.at[:, cols], lambda owner: r.wi_full.at[owner, :, cols], 96
        part = slice(192 * (k - 3), 192 * (k - 2))
        return r.wu.at[part], lambda owner: r.wu_full.at[owner, part], 96

    beside_of = [
        (beside, bit_y) if over_y else (paired, bit_l) for over_y in OVER_Y
    ]

    def half(view, rows, which):
        return view.at[span(which * rows, rows, 32)]

    def w_copy(k, leg):
        sems = r.w_ss.at[k, leg], r.w_rs.at[k, leg]
        shard, full, rows = w_views(k, 1 - plane if leg == 1 else plane)
        partner, bit = beside_of[k]
        if leg == 0:
            return remote(shard, full(seq), *sems, mate, ctx)
        if leg == 1:
            return remote(
                half(shard, rows, bit), half(full(seq), rows, bit), *sems, across, ctx
            )
        which = bit if leg in (2, 3) else 1 - bit
        came = half(full(across), rows, which)
        return remote(came, came, *sems, *((seq, partner) if leg == 2 else (mate, ctx)))

    def w_wait(k, leg):
        shard, full, rows = w_views(k, plane)
        bit = beside_of[k][1]
        spots = (
            lambda: full(mate),
            lambda: half(full(across), rows, bit),
            lambda: half(full(across), rows, 1 - bit),
            lambda: half(full(across_mate), rows, bit),
            lambda: half(full(across_mate), rows, 1 - bit),
        )
        spot = spots[leg]()
        remote(spot, spot, r.w_ss.at[k, leg], r.w_rs.at[k, leg], mate, ctx).wait_recv()

    def pass_across(k):
        w_wait(k, 1)
        w_copy(k, 2).start()
        w_copy(k, 3).start()

    def pass_beside(k):
        w_wait(k, 2)
        w_copy(k, 4).start()

    def w_done(k):
        for leg in (0, 3, 4):
            w_wait(k, leg)

    group_refs = (r.wq, r.wk, r.wv)
    g_local, w_local = [], []
    for which in range(3):
        g_local.append(
            pltpu.make_async_copy(
                group_refs[which].at[:, pl.ds(window, 256)],
                r.wg.at[which, seq],
                r.loc.at[which],
            )
        )
    for n, (ref, full) in enumerate(
        ((r.wo, r.wo_full), (r.wi, r.wi_full), (r.wu, r.wu_full))
    ):
        w_local.append(pltpu.make_async_copy(ref, full.at[seq], r.loc.at[3 + n]))
    own_block = pltpu.make_async_copy(r.x.at[side], r.xs.at[ctx], r.loc.at[6])
    for which in range(2):
        r.seg_own[which] = jnp.broadcast_to(r.seg[which : which + 1], (8, 128))
    r.pack_own[...] = jnp.zeros((16, 768), BF16)
    for n, name in enumerate(VECTORS):
        r.pack_own[n : n + 1, 0:192] = getattr(r, name)[...].reshape(1, 192)
    r.pack_own[8:9] = r.b_inner[...].reshape(1, 768)
    own_seg = pltpu.make_async_copy(r.seg_own.at[side], r.seg_all.at[ctx], r.loc.at[7])
    own_pack = pltpu.make_async_copy(r.pack_own, r.pack_all.at[seq], r.loc.at[8])
    for copy in g_local + [own_block, own_seg, own_pack] + w_local:
        copy.start()
    r.v_rows[...] = jnp.zeros((16, 768), F32)
    for which in range(3):
        r.d_all[which] = jnp.zeros((256, 1024), BF16)

    greet(seq, ctx)

    def send(*args):
        copy = remote(*args)
        copy.start()
        sent.append(copy)

    def landed(spot, send_sem, recv_sem):
        remote(spot, spot, send_sem, recv_sem, seq, beside).wait_recv()

    for hop in range(1, 8):
        other = lax.rem(ctx + hop, 8)
        send(
            r.seg_own.at[other // 4],
            r.seg_all.at[ctx],
            r.s_ss.at[hop],
            r.s_rs.at[hop],
            seq,
            other,
        )
    for hop in range(1, 4):
        other = lax.rem(seq + hop, 4)
        send(r.pack_own, r.pack_all.at[seq], r.p_ss.at[hop], r.p_rs.at[hop], other, ctx)
    for n in range(2):
        part = slice(64 * n, 64 * n + 64)
        send(
            r.x.at[1 - side, part],
            r.xs.at[ctx, part],
            r.x_ss.at[n],
            r.x_rs.at[n],
            seq,
            mirror,
        )
    square = [side * 4 + lax.rem(group + hop, 4) for hop in range(1, 4)]
    for hop in range(1, 4):
        send(
            r.x.at[side],
            r.xs.at[ctx],
            r.x_ss.at[1 + hop],
            r.x_rs.at[1 + hop],
            seq,
            square[hop - 1],
        )
    for which in range(3):
        for n, other in enumerate((mate, across)):
            send(
                group_refs[which].at[:, pl.ds(window, 256)],
                r.wg.at[which, seq],
                r.g_ss.at[which, n],
                r.g_rs.at[which, n],
                other,
                ctx,
            )
    for k in range(7):
        w_copy(k, 0).start()
        w_copy(k, 1).start()

    t = types.SimpleNamespace()

    def task(run):
        setattr(t, run.__name__, run)

    t.pa = [functools.partial(pass_across, k) for k in range(7)]
    t.pb = [functools.partial(pass_beside, k) for k in range(7)]

    @task
    def grp():
        for which in range(3):
            spot = r.wg.at[which, across]
            landed(spot, r.g_ss.at[which, 1], r.g_rs.at[which, 1])
            send(spot, spot, r.g_ss.at[which, 2], r.g_rs.at[which, 2], mate, ctx)

    def far_half(half):
        spot = r.xs.at[mirror, 64 * half : 64 * half + 64]
        landed(spot, r.x_ss.at[half], r.x_rs.at[half])
        for n, other in enumerate(square):
            send(
                spot,
                spot,
                r.x_ss.at[5 + 3 * half + n],
                r.x_rs.at[5 + 3 * half + n],
                seq,
                other,
            )

    t.far = [functools.partial(far_half, half) for half in range(2)]

    @task
    def small():
        for which in range(3):
            g_local[which].wait()
            for n, owner in ((0, mate), (2, across_mate)):
                landed(
                    r.wg.at[which, owner], r.g_ss.at[which, n], r.g_rs.at[which, n]
                )
        own_pack.wait()
        for hop in range(1, 4):
            landed(
                r.pack_all.at[lax.rem(seq + 4 - hop, 4)], r.p_ss.at[hop], r.p_rs.at[hop]
            )
        own_seg.wait()
        for hop in range(1, 8):
            landed(
                r.seg_all.at[lax.rem(ctx + 8 - hop, 8)], r.s_ss.at[hop], r.s_rs.at[hop]
            )
        lane = lax.broadcasted_iota(jnp.int32, (256, 768), 1)
        at = lax.broadcasted_iota(jnp.int32, (256, 768), 0)
        rows = jnp.zeros((8, 768), F32)
        for owner in range(4):
            chosen = ((lane == at + 192 * owner) & (at < 192)).astype(BF16)
            rows += matmul(r.pack_all[owner, 0:8, 0:256], chosen)
        r.rows[...] = rows

    @task
    def qkv():
        own_block.wait()
        for hop in range(1, 4):
            spot = r.xs.at[side * 4 + lax.rem(group + 4 - hop, 4)]
            landed(spot, r.x_ss.at[1 + hop], r.x_rs.at[1 + hop])
        for half in range(2):
            for n in range(3):
                spot = r.xs.at[
                    (1 - side) * 4 + lax.rem(group + 3 - n, 4), 64 * half : 64 * half + 64
                ]
                landed(spot, r.x_ss.at[5 + 3 * half + n], r.x_rs.at[5 + 3 * half + n])
        tokens = r.xs[...].reshape(1024, 768)
        own_rows = r.pack_all[group]
        qkv = []
        for which in range(3):
            weight = r.wg[which].reshape(768, 256)
            product = matmul_nt(weight.T, tokens)
            if which != 1:
                bias = own_rows[which // 2 : which // 2 + 1, 0:256].astype(F32)
                column = jnp.broadcast_to(bias, (128, 256)).T
                shifted = jnp.where(inside == 0, column, pltpu.roll(column, 64, 0))
                product = product + jnp.concatenate([shifted] * 8, axis=1)
            part = product.astype(BF16)
            if which == 0:
                part = part * jnp.bfloat16(SCORE_SCALE)
            qkv.append(part)
        number = jnp.concatenate(
            [r.seg_all[block, 0:1] for block in range(8)], axis=1
        )
        hot = lax.broadcasted_iota(jnp.int32, (16, 1024), 0) == number
        query_marks = jnp.where(hot, 1.0, 0.0).astype(BF16)
        key_marks = jnp.where(hot, 0.0, -BIG).astype(BF16)
        blank = jnp.zeros((48, 1024), BF16)
        for head in range(3):
            parts = [
                jnp.where(
                    inside != 0,
                    part[64 * head + 64 : 64 * head + 128],
                    part[64 * head : 64 * head + 64],
                )
                for part in qkv
            ]
            r.qa[head] = jnp.concatenate([parts[0], query_marks, blank], axis=0)
            r.ka[head] = jnp.concatenate([parts[1], key_marks, blank], axis=0)
            r.vt[head] = parts[2]

    my_rows = span(group * 192, 192, 64)
    my_lanes = span(side * 128, 128, 128)
    own_o = pltpu.make_async_copy(
        r.o_send.at[:, own_lanes], r.ctx_t.at[my_rows, my_lanes], r.loc.at[9]
    )

    def attend_head(head):
        r.key_rows[...] = r.ka[head].T

        def attend(block, unused):
            lanes = span(block * 256, 256, 256)
            scores = matmul(r.key_rows[...], r.qa[head, :, lanes])
            unnorm = jnp.exp(scores)
            total = jnp.sum(unnorm, axis=0, keepdims=True)
            attended = matmul(r.vt[head], unnorm.astype(BF16)) / total
            r.ot[head, :, lanes] = attended
            r.sums[head, :, lanes] = total
            r.o_send[64 * head : 64 * head + 64, lanes] = attended.astype(BF16)
            return unused

        lax.fori_loop(0, 4, attend, 0)
        if head == 2:
            own_o.start()
        part = slice(64 * head, 64 * head + 64)
        for hop in range(1, 8):
            other = lax.rem(ctx + hop, 8)
            send(
                r.o_send.at[part, span(other * 128, 128, 128)],
                r.ctx_t.at[span(group * 192 + 64 * head, 64, 64), my_lanes],
                r.o_ss.at[head, hop],
                r.o_rs.at[head, hop],
                seq,
                other,
            )

    t.at = [functools.partial(attend_head, head) for head in range(3)]

    def row_vec(n):
        return r.rows[n : n + 1]

    @task
    def fn():
        own_o.wait()
        for head in range(3):
            for hop in range(1, 8):
                other = lax.rem(ctx + 8 - hop, 8)
                spot = r.ctx_t.at[
                    span(lax.rem(other, 4) * 192 + 64 * head, 64, 64),
                    span((other // 4) * 128, 128, 128),
                ]
                landed(spot, r.o_ss.at[head, hop], r.o_rs.at[head, hop])
        w_local[0].wait()
        w_done(0)

        def first_norm(which, unused):
            at, lanes = span(which * 128, 128, 128), span(which * 128, 128, 128)
            value = (
                matmul(r.ctx_t[:, lanes].T, r.wo_full[...].reshape(768, 768))
                + row_vec(2)
                + r.x[which].astype(F32)
            )
            hidden, normed, inverse = norm_forward(value, row_vec(4), row_vec(5))
            r.normed[at] = normed
            r.inverse[at] = inverse
            part = hidden.astype(BF16)
            r.low[at] = part
            r.low_t[:, lanes] = part.T
            r.work[at] = hidden + row_vec(3)
            return unused

        lax.fori_loop(0, 2, first_norm, 0)

    def inner_weight(n):
        return r.wi_full[:, :, span(n * 768, 768, 128)].reshape(768, 768)

    def feed(where):
        def visit(step, unused):
            n, which = where * 2 + step // 2, lax.rem(step, 2)
            at = span(which * 128, 128, 128)
            value = matmul(r.low[at], inner_weight(n)) + r.pack_all[n, 8:9].astype(F32)
            act, slope = gelu_parts(value)
            part = act.astype(BF16)
            r.slope[n, at] = slope
            r.act_t[n, :, at] = part.T
            r.work[at] += matmul(part, r.wu_full[n])
            return unused

        lax.fori_loop(0, 4, visit, 0)

    @task
    def fe0():
        w_local[1].wait()
        w_local[2].wait()
        w_done(1)
        for k in range(3, 7):
            w_wait(k, 0)
        feed(plane)

    @task
    def fe1():
        w_done(2)
        for k in range(3, 7):
            w_wait(k, 3)
            w_wait(k, 4)
        feed(1 - plane)

    def tally(n, value):
        r.v_rows[n : n + 1] += jnp.sum(value, axis=0, keepdims=True)

    @task
    def sn():
        def second_norm(which, unused):
            at = span(which * 128, 128, 128)
            result, normed, inverse = norm_forward(r.work[at], row_vec(6), row_vec(7))
            r.layer[which] = result.astype(BF16)
            upstream = r.cot[which].astype(F32)
            scaled = upstream * row_vec(6)
            back = inverse * (
                scaled
                - jnp.mean(scaled, axis=-1, keepdims=True)
                - normed * jnp.mean(scaled * normed, axis=-1, keepdims=True)
            )
            tally(4, upstream * normed)
            tally(5, upstream)
            r.work[at] = back
            part = back.astype(BF16)
            r.d_rows[at] = part
            tally(1, part.astype(F32))
            return unused

        lax.fori_loop(0, 2, second_norm, 0)

    chunks = [
        (r.gu, r.fu, r.core_u, r.xr_u, r.rcv_u, r.fin_u, r.tot_0, 0, 384, 0, 768),
        (r.gu, r.fu, r.core_u, r.xr_u, r.rcv_u, r.fin_u, r.tot_1, 384, 384, 0, 768),
        (r.gi, r.fi, r.core_i, r.xr_i, r.rcv_i, r.fin_i, r.tot_2, 0, 192, 0, 1536),
        (r.gi, r.fi, r.core_i, r.xr_i, r.rcv_i, r.fin_i, r.tot_3, 0, 192, 1536, 1536),
        (r.go, r.fo, r.core_o, r.xr_o, r.rcv_o, r.fin_o, r.tot_4, 0, 192, 0, 768),
    ]

    def reduce_steps(k, first):
        grad, out, core, arrived, rcv, fin, total, row, rows, col, cols = chunks[k]
        rr, cc = pl.ds(row, rows), pl.ds(col, cols)
        wide = cols // 2
        mine = span(col + bit_y * wide, wide, 128)
        other = span(col + (1 - bit_y) * wide, wide, 128)
        keep_l = span(row + bit_l * (rows // 2), rows // 2)
        give_l = span(row + (1 - bit_l) * (rows // 2), rows // 2)
        keep_h = span(row + bit_l * (rows // 2) + bit_h * (rows // 4), rows // 4)
        give_h = span(row + bit_l * (rows // 2) + (1 - bit_h) * (rows // 4), rows // 4)
        spot_h = span(row + (1 - bit_l) * (rows // 2), rows // 4)
        tot_keep, tot_give = (
            span(bit_h * (rows // 4), rows // 4),
            span((1 - bit_h) * (rows // 4), rows // 4),
        )
        owner = (seq, across)

        def sems(leg):
            return r.r_ss.at[k, leg], r.r_rs.at[k, leg]

        to_core = [
            remote(grad.at[mate, rr, cc], core.at[0, rr, cc], *sems(0), mate, ctx),
            remote(
                grad.at[across_mate, rr, cc], core.at[1, rr, cc], *sems(1), mate, ctx
            ),
        ]

        def add(at, lanes, slot, *more):
            value = grad[owner[slot], at, lanes].astype(F32) + core[
                slot, at, lanes
            ].astype(F32)
            for ref in more:
                value += ref[at, lanes].astype(F32)
            return value

        def put(at, lanes, slot, *more):
            core[slot, at, lanes] = add(at, lanes, slot, *more).astype(BF16)

        def spread(at, lanes, leg, target):
            spot = fin.at[at, lanes]
            return remote(spot, spot, *sems(leg), seq, target)

        to_h = remote(
            arrived.at[give_h, mine], rcv.at[spot_h, other], *sems(5), seq, mirror
        )

        def begin():
            for copy in to_core:
                copy.start()

        def cores_in():
            for copy in to_core:
                copy.wait_recv()

        if first == "x":
            to_x = remote(core.at[1, rr, cc], arrived.at[rr, cc], *sems(2), across, ctx)
            to_y = remote(arrived.at[rr, other], rcv.at[rr, other], *sems(3), seq, beside)
            at_y = remote(arrived.at[rr, mine], rcv.at[rr, mine], *sems(3), seq, beside)
            firsts = [to_x, to_y]

            def one():
                put(rr, cc, 1)
                to_x.start()

            def two():
                arrived[rr, other] = add(rr, other, 0, arrived).astype(BF16)
                to_y.start()

        elif first == "y":
            extra = r.two_u
            to_y = [
                remote(
                    core.at[0, rr, other], rcv.at[rr, other], *sems(3), seq, beside
                ),
                remote(core.at[1, rr, other], extra, *sems(9), seq, beside),
            ]
            at_y = [
                remote(core.at[0, rr, mine], rcv.at[rr, mine], *sems(3), seq, beside),
                remote(core.at[1, rr, mine], extra, *sems(9), seq, beside),
            ]
            to_x = remote(
                core.at[1, rr, mine], arrived.at[rr, mine], *sems(2), across, ctx
            )
            firsts = to_y + [to_x]

            def one():
                for slot in range(2):
                    put(rr, other, slot)
                    to_y[slot].start()

            def two():
                for copy in at_y:
                    copy.wait_recv()
                core[1, rr, mine] = (add(rr, mine, 1) + extra[...].astype(F32)).astype(
                    BF16
                )
                to_x.start()

        else:
            extra = r.two_i
            to_l = [
                remote(core.at[0, give_l, cc], rcv.at[give_l, cc], *sems(4), seq, paired),
                remote(core.at[1, give_l, cc], extra, *sems(9), seq, paired),
            ]
            at_l = [
                remote(core.at[0, keep_l, cc], rcv.at[keep_l, cc], *sems(4), seq, paired),
                remote(core.at[1, keep_l, cc], extra, *sems(9), seq, paired),
            ]
            to_x = remote(
                core.at[1, keep_l, cc], arrived.at[keep_l, cc], *sems(2), across, ctx
            )
            to_y = remote(
                arrived.at[keep_l, other], rcv.at[give_l, other], *sems(3), seq, beside
            )
            at_y = remote(
                arrived.at[keep_l, mine], rcv.at[give_l, mine], *sems(3), seq, beside
            )
            firsts = to_l + [to_x, to_y]

            def one():
                for slot in range(2):
                    put(give_l, cc, slot)
                    to_l[slot].start()

            def two():
                for copy in at_l:
                    copy.wait_recv()
                core[1, keep_l, cc] = (
                    add(keep_l, cc, 1) + extra[...].astype(F32)
                ).astype(BF16)
                to_x.start()

            def three():
                to_x.wait_recv()
                arrived[keep_l, other] = add(keep_l, other, 0, rcv, arrived).astype(BF16)
                to_y.start()
                total[...] = add(keep_l, mine, 0, rcv, arrived)

            def four():
                at_y.wait_recv()
                total[...] += rcv[give_l, mine].astype(F32)
                arrived[give_h, mine] = total[tot_give].astype(BF16)
                to_h.start()

        if first != "z":
            to_l = remote(
                arrived.at[give_l, mine], rcv.at[give_l, other], *sems(4), seq, paired
            )
            at_l = remote(
                arrived.at[keep_l, mine], rcv.at[keep_l, other], *sems(4), seq, paired
            )
            firsts = firsts + [to_l]

            def three():
                (at_y if first == "x" else to_x).wait_recv()
                arrived[give_l, mine] = add(give_l, mine, 0, arrived, rcv).astype(BF16)
                to_l.start()
                total[...] = add(keep_l, mine, 0, arrived, rcv)

            def four():
                at_l.wait_recv()
                arrived[give_h, mine] = (
                    total[tot_give] + rcv[give_h, other].astype(F32)
                ).astype(BF16)
                to_h.start()
                total[tot_keep] += rcv[keep_h, other].astype(F32)

        def step_one():
            cores_in()
            one()

        def step_two():
            if first == "x":
                to_x.wait_recv()
            two()

        def step_five():
            to_h.wait_recv()
            fin[keep_h, mine] = (
                total[tot_keep] + rcv[spot_h, other].astype(F32)
            ).astype(BF16)
            spread(keep_h, mine, 6, mirror).start()

        if first == "z":
            last = [(keep_l, other, 7, beside), (keep_l, cc, 8, paired)]
            ends = [(give_l, cc)]
            middle = (keep_l, mine)
        else:
            last = [(give_l, mine, 7, paired), (rr, mine, 8, beside)]
            ends = [(rr, other)]
            middle = (keep_l, mine)

        def step_six():
            spread(give_h, mine, 6, mirror).wait_recv()
            spread(*middle, 7, last[0][3]).start()

        def step_seven():
            spread(*last[0]).wait_recv()
            spread(*last[1]).start()

        to_out = pltpu.make_async_copy(fin.at[rr, cc], out.at[rr, cc], r.loc.at[10 + k])

        def step_eight():
            spread(*ends[0], 8, last[1][3]).wait_recv()
            to_out.start()

        def end():
            for copy in (
                to_core
                + firsts
                + [
                    to_h,
                    spread(keep_h, mine, 6, mirror),
                    spread(*middle, 7, last[0][3]),
                    spread(*last[1]),
                ]
            ):
                copy.wait_send()
            to_out.wait()

        names = [
            begin,
            step_one,
            step_two,
            three,
            four,
            step_five,
            step_six,
            step_seven,
            step_eight,
            end,
        ]
        return names

    t.s = [reduce_steps(k, FIRST[k]) for k in range(5)]

    def make_outer(k):
        part = slice(384 * k, 384 * k + 384)
        for owner in (mate, across_mate):
            r.gu[owner, part] = matmul(r.act_t[owner, part], r.d_rows[...]).astype(BF16)
        t.s[k][0]()
        for owner in (across, seq):
            r.gu[owner, part] = matmul(r.act_t[owner, part], r.d_rows[...]).astype(BF16)

    t.mo = [functools.partial(make_outer, k) for k in range(2)]

    def inner_step(n):
        def inner_back(which, unused):
            at = span(which * 128, 128, 128)
            part = (matmul_nt(r.d_rows[at], r.wu_full[n]) * r.slope[n, at]).astype(BF16)
            r.low[at] = part
            tally(8 + n, part.astype(F32))
            r.work[at] += matmul_nt(part, inner_weight(n))
            return unused

        lax.fori_loop(0, 2, inner_back, 0)
        r.gi[:, :, 768 * n : 768 * n + 768] = (
            matmul(r.low_t[...], r.low[...]).astype(BF16).reshape(4, 192, 768)
        )
        if n % 2:
            t.s[2 + n // 2][0]()

    t.ib = [functools.partial(inner_step, n) for n in range(4)]

    own_do = pltpu.make_async_copy(
        r.do_send.at[my_rows, my_lanes], r.do_all.at[:, own_lanes], r.loc.at[15]
    )

    @task
    def fb():
        def first_back(which, unused):
            at = span(which * 128, 128, 128)
            upstream, normed = r.work[at], r.normed[at]
            scaled = upstream * row_vec(4)
            back = r.inverse[at] * (
                scaled
                - jnp.mean(scaled, axis=-1, keepdims=True)
                - normed * jnp.mean(scaled * normed, axis=-1, keepdims=True)
            )
            tally(2, upstream * normed)
            tally(3, upstream)
            r.work[at] = back
            part = back.astype(BF16)
            r.low[at] = part
            tally(0, part.astype(F32))
            return unused

        lax.fori_loop(0, 2, first_back, 0)
        r.do_send[...] = matmul_nt(
            r.wo_full[...].reshape(768, 768), r.low[...]
        ).astype(BF16)
        own_do.start()
        for head in range(3):
            for hop in range(1, 8):
                other = lax.rem(ctx + hop, 8)
                send(
                    r.do_send.at[
                        span(lax.rem(other, 4) * 192 + 64 * head, 64, 64),
                        span((other // 4) * 128, 128, 128),
                    ],
                    r.do_all.at[64 * head : 64 * head + 64, own_lanes],
                    r.do_ss.at[head, hop],
                    r.do_rs.at[head, hop],
                    seq,
                    other,
                )

    @task
    def dwo():
        r.go[...] = matmul(r.ctx_t[...], r.low[...]).astype(BF16).reshape(4, 192, 768)
        t.s[4][0]()
        for owner in range(4):
            start = 192 * owner - 64 * (owner % 2)
            r.v_own[owner, 0:8] = r.v_rows[0:8, start : start + 256]
            for part in range(3):
                r.v_own[owner, 8 + part : 9 + part] = r.v_rows[
                    8 + owner : 9 + owner, 256 * part : 256 * part + 256
                ]
            r.v_own[owner, 11:16] = jnp.zeros((5, 256), F32)
        for hop in range(1, 4):
            other = lax.rem(seq + hop, 4)
            send(
                r.v_own.at[other],
                r.v_recv.at[seq],
                r.v_ss.at[0, hop],
                r.v_rs.at[0, hop],
                other,
                ctx,
            )

    @task
    def v1():
        for hop in range(1, 4):
            spot = r.v_recv.at[lax.rem(seq + 4 - hop, 4)]
            landed(spot, r.v_ss.at[0, hop], r.v_rs.at[0, hop])
        r.v_recv[seq] = r.v_own[seq]
        r.v_all[ctx] = r.v_recv[0] + r.v_recv[1] + r.v_recv[2] + r.v_recv[3]
        for hop in range(1, 8):
            send(
                r.v_all.at[ctx],
                r.v_all.at[ctx],
                r.v_ss.at[1, hop],
                r.v_rs.at[1, hop],
                seq,
                lax.rem(ctx + hop, 8),
            )

    def attend_back_head(head):
        if head == 0:
            own_do.wait()
        for hop in range(1, 8):
            spot = r.do_all.at[
                64 * head : 64 * head + 64, span(lax.rem(ctx + 8 - hop, 8) * 128, 128, 128)
            ]
            landed(spot, r.do_ss.at[head, hop], r.do_rs.at[head, hop])
        at = span(inside + 64 * head, 64, 64)
        total = r.sums[head]
        d_out = r.do_all[64 * head : 64 * head + 64].astype(F32)
        r.du[...] = (d_out / total).astype(BF16)
        r.c_row[...] = jnp.sum(d_out * r.ot[head], axis=0, keepdims=True) / total
        r.key_rows[...] = r.ka[head].T
        r.value_rows[...] = r.vt[head].T
        r.dk_acc[...] = jnp.zeros((64, 1024), F32)
        r.dv_acc[...] = jnp.zeros((64, 1024), F32)

        def attend_back(block, unused):
            lanes = span(block * 256, 256, 256)
            scores = matmul(r.key_rows[...], r.qa[head, :, lanes])
            unnorm = jnp.exp(scores)
            d_prob = matmul(r.value_rows[...], r.du[:, lanes])
            d_score = (unnorm * (d_prob - r.c_row[:, lanes])).astype(BF16)
            d_query = matmul(r.ka[head, 0:64], d_score) * SCORE_SCALE
            r.d_all[0, at, lanes] = d_query.astype(BF16)
            r.dk_acc[...] += matmul_nt(r.qa[head, 0:64, lanes], d_score)
            r.dv_acc[...] += matmul_nt(r.du[:, lanes], unnorm.astype(BF16))
            return unused

        lax.fori_loop(0, 4, attend_back, 0)
        r.d_all[1, at] = r.dk_acc[...].astype(BF16)
        r.d_all[2, at] = r.dv_acc[...].astype(BF16)

    t.ab = [functools.partial(attend_back_head, head) for head in range(3)]

    g_cores = [
        remote(
            r.g_all.at[which, owner],
            r.g_core.at[which, n],
            r.h_ss.at[which, n],
            r.h_rs.at[which, n],
            mate,
            ctx,
        )
        for which in range(3)
        for n, owner in ((0, mate), (1, across_mate))
    ]
    own_bias = pltpu.make_async_copy(
        r.b_send, r.b_recv.at[seq * 2 + side], r.loc.at[16]
    )
    to_owners = [
        remote(
            r.b_send,
            r.b_recv.at[seq * 2 + side],
            r.b_ss.at[hop],
            r.b_rs.at[seq * 2 + side],
            group,
            lax.rem(ctx + hop, 8),
        )
        for hop in range(8)
    ]

    @task
    def dwq():
        ones = jnp.ones((16, 1024), BF16)
        for which in range(3):
            product = matmul(r.d_all[which], r.xs[...].reshape(1024, 768)).astype(BF16)
            r.g_all[which] = product.T.reshape(4, 192, 256)
            if which != 1:
                r.b_send[which // 2] = matmul_nt(ones, r.d_all[which])[0:8]
        for copy in g_cores:
            copy.start()

        @pl.when(group == seq)
        def _():
            own_bias.start()

        @pl.when(group != seq)
        def _():
            to_owners[0].start()

        for copy in to_owners[1:]:
            copy.start()

    @task
    def dx():
        for part in range(4):
            lanes = slice(256 * part, 256 * part + 256)
            share = matmul(r.wg[0].reshape(768, 256), r.d_all[0, :, lanes])
            for which in (1, 2):
                share += matmul(r.wg[which].reshape(768, 256), r.d_all[which, :, lanes])
            r.act_t[part] = share.astype(BF16)

    def dx_half(part, bit):
        return r.act_t.at[part, :, span(bit * 128, 128, 128)]

    dx_to_y = [
        remote(
            dx_half(part, 1 - bit_y),
            r.dx_y.at[part],
            r.dx_ss.at[part],
            r.dx_rs.at[part],
            seq,
            beside,
        )
        for part in range(4)
    ]
    dx_to_l = [
        remote(
            dx_half(2 * n + 1 - bit_l, bit_y),
            r.dx_l.at[n],
            r.dx_ss.at[4 + n],
            r.dx_rs.at[4 + n],
            seq,
            paired,
        )
        for n in range(2)
    ]
    lanes_y = span(bit_y * 128, 128, 128)

    def dx_part(which):
        return 2 * which + bit_l

    dx_to_h = remote(
        dx_half(dx_part(1 - side), bit_y),
        r.dx_h,
        r.dx_ss.at[6],
        r.dx_rs.at[6],
        seq,
        mirror,
    )
    t.d = [copy.start for copy in dx_to_y]

    @task
    def dxp():
        for copy in dx_to_y:
            copy.wait_recv()
        for n in range(2):
            part = 2 * n + 1 - bit_l
            r.act_t[part, :, lanes_y] = (
                r.act_t[part, :, lanes_y].astype(F32) + r.dx_y[part].astype(F32)
            ).astype(BF16)
            dx_to_l[n].start()

    def dx_total(which):
        part = dx_part(which)
        return (
            r.act_t[part, :, lanes_y].astype(F32)
            + r.dx_y[part].astype(F32)
            + r.dx_l[which].astype(F32)
        )

    @task
    def dxm():
        for copy in dx_to_l:
            copy.wait_recv()
        r.act_t[dx_part(1 - side), :, lanes_y] = dx_total(1 - side).astype(BF16)
        dx_to_h.start()
        r.grad[side] = dx_total(side).T + r.work[span(side * 128, 128)]

    @task
    def dxe():
        dx_to_h.wait_recv()
        r.grad[1 - side] = (
            r.dx_h[...].astype(F32).T + r.work[span((1 - side) * 128, 128)]
        )

    g_x = remote(r.g_xs, r.g_xr, r.h_ss.at[3, 0], r.h_rs.at[3, 0], across, ctx)
    keep, give = span(side * 96, 96, 32), span((1 - side) * 96, 96, 32)
    g_m = remote(
        r.g_half.at[:, give], r.g_mir, r.h_ss.at[3, 1], r.h_rs.at[3, 1], seq, mirror
    )

    @task
    def gx():
        for copy in g_cores:
            copy.wait_recv()
        for which in range(3):
            r.g_xs[which] = (
                r.g_all[which, across].astype(F32) + r.g_core[which, 1].astype(F32)
            ).astype(BF16)
        g_x.start()

    @task
    def gm():
        g_x.wait_recv()
        for which in range(3):
            r.g_half[which] = (
                r.g_all[which, seq].astype(F32)
                + r.g_core[which, 0].astype(F32)
                + r.g_xr[which].astype(F32)
            ).astype(BF16)
        g_m.start()

    @task
    def ga():
        g_m.wait_recv()
        for which in range(3):
            r.fg[group, which, keep] = (
                r.g_half[which, keep].astype(F32) + r.g_mir[which].astype(F32)
            ).astype(BF16)
        spot = r.fg.at[group, :, keep]
        send(spot, spot, r.h_ss.at[4, 0], r.h_rs.at[4, 0], seq, mirror)
        for n, other in enumerate(square):
            send(spot, spot, r.h_ss.at[5, n], r.h_rs.at[5, n], seq, other)

    @task
    def gb():
        theirs = r.fg.at[group, :, give]
        landed(theirs, r.h_ss.at[4, 0], r.h_rs.at[4, 0])
        for n, other in enumerate(square):
            send(theirs, theirs, r.h_ss.at[6, n], r.h_rs.at[6, n], seq, other)

    @task
    def v2():
        for hop in range(1, 8):
            spot = r.v_all.at[lax.rem(ctx + 8 - hop, 8)]
            landed(spot, r.v_ss.at[1, hop], r.v_rs.at[1, hop])
        gathered = r.v_all[0]
        for n in range(1, 8):
            gathered += r.v_all[n]
        r.vec_sum[...] = gathered

    @task
    def be():
        for n in range(8):
            spot = r.b_recv.at[n]
            arrival = remote(
                spot, spot, r.b_ss.at[0], r.b_rs.at[n], lax.rem(seq + 1, 4), ctx
            )
            here = (n // 2 == seq) & (n % 2 == side) & (group == seq)

            @pl.when(here)
            def _():
                own_bias.wait()

            @pl.when(jnp.logical_not(here))
            def _(arrival=arrival):
                arrival.wait_recv()

        row_sum = r.b_recv[0]
        for n in range(1, 8):
            row_sum += r.b_recv[n]
        r.bias_sum[...] = row_sum

    @task
    def ge():
        for n in range(3):
            source = lax.rem(group + 3 - n, 4)
            landed(r.fg.at[source, :, keep], r.h_ss.at[5, n], r.h_rs.at[5, n])
            landed(r.fg.at[source, :, give], r.h_ss.at[6, n], r.h_rs.at[6, n])

    for step in in_order(t):
        step()

    for k in range(5):
        t.s[k][9]()
    for copy in (
        sent + g_cores + [g_x, g_m] + to_owners[1:] + dx_to_y + dx_to_l + [dx_to_h]
    ):
        copy.wait_send()

    @pl.when(group != seq)
    def _():
        to_owners[0].wait_send()

    for k in range(7):
        for leg in range(5):
            w_copy(k, leg).wait_send()


FIRST = "xyzxx"
OVER_Y = (1, 0, 1, 0, 1, 0, 1)


def in_order(t):
    return (
        t.grp,
        t.far[0],
        t.small,
        t.pa[0],
        t.far[1],
        t.pa[1],
        t.pb[0],
        t.pa[2],
        t.qkv,
        t.at[0],
        t.at[1],
        t.at[2],
        t.pb[2],
        t.pa[5],
        t.pb[1],
        t.pa[3],
        t.pa[4],
        t.pa[6],
        t.pb[4],
        t.fn,
        t.pb[5],
        t.fe0,
        t.pb[6],
        t.pb[3],
        t.fe1,
        t.sn,
        t.mo[0],
        t.mo[1],
        t.ib[0],
        t.s[0][1],
        t.ib[1],
        t.s[1][1],
        t.ib[2],
        t.ib[3],
        t.s[2][1],
        t.fb,
        t.dwo,
        t.s[3][1],
        t.s[4][1],
        t.s[0][2],
        t.v1,
        t.s[1][2],
        t.s[2][2],
        t.ab[0],
        t.s[0][3],
        t.s[3][2],
        t.ab[1],
        t.ab[2],
        t.s[0][4],
        t.dx,
        t.d[0],
        t.s[4][2],
        t.s[3][3],
        t.dwq,
        t.v2,
        t.s[1][3],
        t.gx,
        t.s[0][5],
        t.s[3][4],
        t.d[1],
        t.s[2][3],
        t.s[1][4],
        t.s[4][3],
        t.be,
        t.s[0][6],
        t.d[2],
        t.s[3][5],
        t.s[4][4],
        t.gm,
        t.s[2][4],
        t.s[1][5],
        t.d[3],
        t.s[0][7],
        t.s[3][6],
        t.s[4][5],
        t.dxp,
        t.ga,
        t.s[3][7],
        t.s[0][8],
        t.s[2][5],
        t.s[1][6],
        t.s[4][6],
        t.dxm,
        t.s[3][8],
        t.gb,
        t.s[2][6],
        t.s[1][7],
        t.s[4][7],
        t.dxe,
        t.s[2][7],
        t.ge,
        t.s[1][8],
        t.s[4][8],
        t.s[2][8],
    )


def run_layer(*operands):
    vmem = pl.BlockSpec(memory_space=pltpu.VMEM)
    anywhere = pl.BlockSpec(memory_space=pl.ANY)
    shape = jax.ShapeDtypeStruct
    return pl.pallas_call(
        layer_kernel,
        name="layer_kernel",
        out_shape=(
            shape((2, 128, 768), BF16),
            shape((2, 128, 768), F32),
            shape((768, 768), BF16),
            shape((192, 3072), BF16),
            shape((192, 768), BF16),
            shape((4, 3, 192, 256), BF16),
            shape((16, 256), F32),
            shape((2, 8, 256), F32),
        ),
        in_specs=[vmem] * 12 + [anywhere] * 6,
        out_specs=(vmem,) * 2 + (anywhere,) * 3 + (vmem,) * 3,
        scratch_shapes=[pltpu.VMEM(*spec) for spec in SCRATCH.values()]
        + [pltpu.SemaphoreType.DMA(count) for count in SEMAPHORES.values()],
        compiler_params=pltpu.CompilerParams(
            collective_id=1, has_side_effects=True, vmem_limit_bytes=67043328
        ),
    )(*operands)


def finish_kernel(*refs):
    ins, outs, bufs = refs[:8], refs[8:25], refs[25:]
    low, wide, load, store = bufs[:8], bufs[8:17], bufs[17], bufs[18]
    grad, layer, low_u, low_i, low_o, low_g, vec, bias = low
    wide_t, wide_l, out_l, wide_u, wide_i, wide_o, wide_q, wide_k, wide_v = wide
    loads = [
        pltpu.make_async_copy(source, target, load.at[n])
        for n, (source, target) in enumerate(zip(ins, low))
    ]
    for copy in loads:
        copy.start()
    stores = []

    def put(source, target):
        copy = pltpu.make_async_copy(source, target, store.at[len(stores)])
        copy.start()
        stores.append(copy)

    loads[2].wait()
    for part in (slice(0, 384), slice(384, 768)):
        wide_u[part] = low_u[part].astype(F32)
        put(wide_u.at[part], outs[7].at[part])
    loads[3].wait()
    for part in (slice(0, 96), slice(96, 192)):
        wide_i[part] = low_i[part].astype(F32)
        put(wide_i.at[part], outs[6].at[part])
    loads[0].wait()
    for which in range(2):
        wide_t[:, which, :] = grad[which]
    put(wide_t, outs[1])
    loads[1].wait()
    for which in range(2):
        wide_l[:, which, :] = layer[which].astype(F32)
    out_l[...] = wide_l[...].astype(BF16)
    put(out_l, outs[0])
    loads[4].wait()
    wide_o[...] = low_o[...].astype(F32)
    put(wide_o, outs[5])
    loads[5].wait()
    for which, target in enumerate((wide_q, wide_k, wide_v)):
        for pair in range(2):
            left = low_g[2 * pair, which].astype(F32)
            right = low_g[2 * pair + 1, which].astype(F32)
            at = 384 * pair
            target[:, at : at + 128] = left[:, 0:128]
            target[:, at + 128 : at + 256] = left[:, 128:256] + right[:, 0:128]
            target[:, at + 256 : at + 384] = right[:, 128:256]
        put(target, outs[2 + which])
    odd = lax.rem(lax.axis_index("seq"), 2) == 1

    def owned(row):
        return jnp.where(odd, row[:, 64:256], row[:, 0:192]).reshape(192)

    loads[6].wait()
    loads[7].wait()
    outs[8][...] = owned(bias[0, 0:1])
    outs[9][...] = owned(bias[1, 0:1])
    outs[10][...] = owned(vec[0:1])
    outs[11][...] = jnp.concatenate([vec[n : n + 1] for n in (8, 9, 10)], axis=1).reshape(
        768
    )
    for n in range(1, 6):
        outs[11 + n][...] = owned(vec[n : n + 1])
    for copy in stores:
        copy.wait()


def run_finish(*operands):
    vmem = pl.BlockSpec(memory_space=pltpu.VMEM)
    anywhere = pl.BlockSpec(memory_space=pl.ANY)
    shape = jax.ShapeDtypeStruct
    large = [(192, 768)] * 4 + [(192, 3072), (768, 768)]
    small = [(192,)] * 3 + [(768,)] + [(192,)] * 5
    return pl.pallas_call(
        finish_kernel,
        name="finish_kernel",
        out_shape=[shape((128, 2, 768), BF16), shape((128, 2, 768), F32)]
        + [shape(size, F32) for size in large + small],
        in_specs=[anywhere] * 8,
        out_specs=[anywhere] * 8 + [vmem] * 9,
        scratch_shapes=[
            pltpu.VMEM((2, 128, 768), F32),
            pltpu.VMEM((2, 128, 768), BF16),
            pltpu.VMEM((768, 768), BF16),
            pltpu.VMEM((192, 3072), BF16),
            pltpu.VMEM((192, 768), BF16),
            pltpu.VMEM((4, 3, 192, 256), BF16),
            pltpu.VMEM((16, 256), F32),
            pltpu.VMEM((2, 8, 256), F32),
            pltpu.VMEM((128, 2, 768), F32),
            pltpu.VMEM((128, 2, 768), F32),
            pltpu.VMEM((128, 2, 768), BF16),
            pltpu.VMEM((768, 768), F32),
            pltpu.VMEM((192, 3072), F32),
            pltpu.VMEM((192, 768), F32),
            pltpu.VMEM((192, 768), F32),
            pltpu.VMEM((192, 768), F32),
            pltpu.VMEM((192, 768), F32),
            pltpu.SemaphoreType.DMA((8,)),
            pltpu.SemaphoreType.DMA((10,)),
        ],
        compiler_params=pltpu.CompilerParams(vmem_limit_bytes=67043328),
    )(*operands)


def fast_body(
    tokens,
    segment_ids,
    w_query,
    w_key,
    w_value,
    w_output,
    w_inner,
    w_outer,
    b_query,
    b_value,
    b_output,
    b_inner,
    b_outer,
    gain_first,
    shift_first,
    gain_second,
    shift_second,
    cotangent,
):
    layer, grad, fu, fi, fo, fg, vec_sum, bias_sum = run_layer(
        jnp.transpose(tokens, (1, 0, 2)),
        jnp.transpose(cotangent, (1, 0, 2)),
        segment_ids,
        b_query,
        b_value,
        b_output,
        b_outer,
        gain_first,
        shift_first,
        gain_second,
        shift_second,
        b_inner,
        w_query,
        w_key,
        w_value,
        w_output,
        w_inner,
        w_outer,
    )

    return tuple(run_finish(grad, layer, fu, fi, fo, fg, vec_sum, bias_sum))


def solution(mesh):
    in_specs = (
        P("ctx", "seq", None),
        P("seq", "ctx"),
        P("seq", None),
        P("seq", None),
        P("seq", None),
        P("seq", None),
        P("seq", None),
        P("seq", None),
        P("seq"),
        P("seq"),
        P("seq"),
        P("seq"),
        P("seq"),
        P("seq"),
        P("seq"),
        P("seq"),
        P("seq"),
        P("ctx", "seq", None),
    )
    out_specs = (
        P("ctx", "seq", None),
        P("ctx", "seq", None),
        P("seq", None),
        P("seq", None),
        P("seq", None),
        P("seq", None),
        P("seq", None),
        P("seq", None),
        P("seq"),
        P("seq"),
        P("seq"),
        P("seq"),
        P("seq"),
        P("seq"),
        P("seq"),
        P("seq"),
        P("seq"),
    )
    small = mesh.shape["seq"] == 4 and mesh.shape["ctx"] == 8
    step = fast_body if small else body
    return jax.shard_map(step, mesh=mesh, in_specs=in_specs, out_specs=out_specs, check_vma=False)
```

```python
import functools
import math
import types

import jax
import jax.numpy as jnp
from jax import lax
from jax.experimental import pallas as pl
from jax.experimental.pallas import tpu as pltpu
from jax.sharding import PartitionSpec as P

H = 12
DH = 64


EPSILON = 1e-12
SCORE_SCALE = 0.125


def matmul(first_op, second_op):
    return jnp.dot(first_op, second_op, preferred_element_type=jnp.float32)


def matmul_tn(first_op, second_op):
    return lax.dot_general(
        first_op, second_op, (((0,), (0,)), ((), ())), preferred_element_type=jnp.float32
    )


def matmul_nt(first_op, second_op):
    return lax.dot_general(
        first_op, second_op, (((1,), (1,)), ((), ())), preferred_element_type=jnp.float32
    )


def norm_forward(values, gain_vec, shift_vec):
    center = values - jnp.mean(values, axis=-1, keepdims=True)
    inverse = lax.rsqrt(jnp.mean(center * center, axis=-1, keepdims=True) + EPSILON)
    normed = center * inverse
    return (normed * gain_vec + shift_vec, normed, inverse)


def norm_backward(upstream, normed, inverse, gain_vec):
    scaled = upstream * gain_vec
    back_grad = inverse * (
        scaled
        - jnp.mean(scaled, axis=-1, keepdims=True)
        - normed * jnp.mean(scaled * normed, axis=-1, keepdims=True)
    )
    return (back_grad, jnp.sum(upstream * normed, axis=0), jnp.sum(upstream, axis=0))


def gelu_parts(values):
    cumulative = 0.5 * (1.0 + lax.erf(values * 0.7071067811865476))
    return (
        values * cumulative,
        cumulative + values * jnp.exp(-0.5 * values * values) * 0.3989422804014327,
    )


def block_scores(query_heads, key_heads, seg_query, seg_key):
    raw_scores = (
        jnp.einsum("ishd,jshd->shij", query_heads, key_heads, preferred_element_type=jnp.float32)
        * SCORE_SCALE
    )
    allowed = (jnp.transpose(seg_query)[:, :, None] == jnp.transpose(seg_key)[:, None, :])[:, None]
    return jnp.where(allowed, jnp.exp(raw_scores), 0.0)


def attend_keys(query_heads, seg_query, carry_in, piece_rows):
    key_piece, value_piece, seg_piece = piece_rows
    row_count, seq_count, feature_count = key_piece.shape
    heads, head_size = (query_heads.shape[2], query_heads.shape[3])
    step_rows = math.gcd(row_count, 1024)
    block_count = row_count // step_rows
    key_blocks = key_piece.reshape(block_count, step_rows, seq_count, heads, head_size)
    value_blocks = value_piece.reshape(block_count, step_rows, seq_count, heads, head_size)
    seg_blocks = seg_piece.reshape(block_count, step_rows, seq_count)

    def attend_visit_block(running, element):
        key_block, value_block, seg_block = element
        unnorm = block_scores(query_heads, key_block, seg_query, seg_block)
        totals = running[0] + jnp.sum(unnorm, axis=-1)
        mixture = running[1] + jnp.einsum(
            "shij,jshd->ishd",
            unnorm.astype(jnp.bfloat16),
            value_block,
            preferred_element_type=jnp.float32,
        )
        return ((totals, mixture), None)

    result, unused = lax.scan(attend_visit_block, carry_in, (key_blocks, value_blocks, seg_blocks))
    return result


def key_side(query_heads, d_mixture, correction, seg_query, key_all, value_all, seg_all):
    row_count, seq_count, feature_count = key_all.shape
    heads, head_size = (query_heads.shape[2], query_heads.shape[3])
    step_rows = math.gcd(row_count, 1024)
    block_count = row_count // step_rows
    corr_cols = jnp.transpose(correction, (1, 2, 0))[..., None]
    key_blocks = key_all.reshape(block_count, step_rows, seq_count, heads, head_size)
    value_blocks = value_all.reshape(block_count, step_rows, seq_count, heads, head_size)
    seg_blocks = seg_all.reshape(block_count, step_rows, seq_count)

    def key_visit_block(dq_acc, element):
        key_block, value_block, seg_block = element
        unnorm = block_scores(query_heads, key_block, seg_query, seg_block)
        d_prob = jnp.einsum(
            "ishd,jshd->shij", d_mixture, value_block, preferred_element_type=jnp.float32
        )
        d_score = (unnorm * (d_prob - corr_cols)).astype(jnp.bfloat16)
        dq_acc = dq_acc + jnp.einsum(
            "shij,jshd->ishd", d_score, key_block, preferred_element_type=jnp.float32
        )
        d_key = (
            jnp.einsum("shij,ishd->jshd", d_score, query_heads, preferred_element_type=jnp.float32)
            * SCORE_SCALE
        )
        d_value = jnp.einsum(
            "shij,ishd->jshd",
            unnorm.astype(jnp.bfloat16),
            d_mixture,
            preferred_element_type=jnp.float32,
        )
        stacked = jnp.concatenate(
            [
                d_key.reshape(step_rows, seq_count, feature_count),
                d_value.reshape(step_rows, seq_count, feature_count),
            ],
            axis=-1,
        )
        return (dq_acc, stacked)

    dq_sum, stacked_all = lax.scan(
        key_visit_block,
        jnp.zeros(query_heads.shape, jnp.float32),
        (key_blocks, value_blocks, seg_blocks),
    )
    return (dq_sum, stacked_all.reshape(row_count, seq_count, 2 * feature_count))


def body(
    tokens,
    segment_ids,
    w_query,
    w_key,
    w_value,
    w_output,
    w_inner,
    w_outer,
    b_query,
    b_value,
    b_output,
    b_inner,
    b_outer,
    gain_first,
    shift_first,
    gain_second,
    shift_second,
    cotangent,
):
    tok_rows, seq_count, feature_count = tokens.shape
    rows_total = tok_rows * seq_count
    gathered = (
        lax.all_gather(w_query, "seq", axis=0, tiled=True),
        lax.all_gather(w_key, "seq", axis=0, tiled=True),
        lax.all_gather(w_value, "seq", axis=0, tiled=True),
        lax.all_gather(w_output, "seq", axis=0, tiled=True),
        lax.all_gather(w_inner, "seq", axis=0, tiled=True),
        lax.all_gather(w_outer, "seq", axis=0, tiled=True),
        lax.all_gather(b_query, "seq", axis=0, tiled=True),
        lax.all_gather(b_value, "seq", axis=0, tiled=True),
        lax.all_gather(b_output, "seq", axis=0, tiled=True),
        lax.all_gather(b_inner, "seq", axis=0, tiled=True),
        lax.all_gather(b_outer, "seq", axis=0, tiled=True),
        lax.all_gather(gain_first, "seq", axis=0, tiled=True),
        lax.all_gather(shift_first, "seq", axis=0, tiled=True),
        lax.all_gather(gain_second, "seq", axis=0, tiled=True),
        lax.all_gather(shift_second, "seq", axis=0, tiled=True),
    )
    query_weight, key_weight, value_weight, output_weight, inner_weight, outer_weight = gathered[:6]
    (
        query_bias,
        value_bias,
        output_bias,
        inner_bias,
        outer_bias,
        gain_one,
        shift_one,
        gain_two,
        shift_two,
    ) = [vector.astype(jnp.float32) for vector in gathered[6:]]
    flat_rows = tokens.reshape(rows_total, feature_count)
    flat_float = flat_rows.astype(jnp.float32)
    seg_local = jnp.transpose(segment_ids)
    queries = (matmul(flat_rows, query_weight) + query_bias).astype(jnp.bfloat16)
    key_rows = matmul(flat_rows, key_weight).astype(jnp.bfloat16)
    value_rows = (matmul(flat_rows, value_weight) + value_bias).astype(jnp.bfloat16)
    query_heads = queries.reshape(tok_rows, seq_count, H, DH)
    key_block_rows = key_rows.reshape(tok_rows, seq_count, feature_count)
    value_block_rows = value_rows.reshape(tok_rows, seq_count, feature_count)
    initial = (
        jnp.zeros((seq_count, H, tok_rows), jnp.float32),
        jnp.zeros((tok_rows, seq_count, H, DH), jnp.float32),
    )
    totals, mixture = attend_keys(
        query_heads,
        seg_local,
        initial,
        (
            lax.all_gather(key_block_rows, "ctx", axis=0, tiled=True),
            lax.all_gather(value_block_rows, "ctx", axis=0, tiled=True),
            lax.all_gather(seg_local, "ctx", axis=0, tiled=True),
        ),
    )
    denominator = jnp.transpose(totals, (2, 0, 1))[..., None]
    attended = mixture / denominator
    context = attended.astype(jnp.bfloat16).reshape(rows_total, feature_count)
    first_in = matmul(context, output_weight) + output_bias + flat_float
    hidden, normed_one, inverse_one = norm_forward(first_in, gain_one, shift_one)
    hidden_low = hidden.astype(jnp.bfloat16)
    inner_pre = matmul(hidden_low, inner_weight) + inner_bias
    activated, gelu_slope = gelu_parts(inner_pre)
    act_low = activated.astype(jnp.bfloat16)
    second_in = matmul(act_low, outer_weight) + outer_bias + hidden
    result, normed_two, inverse_two = norm_forward(second_in, gain_two, shift_two)
    layer_out = result.astype(jnp.bfloat16).reshape(tok_rows, seq_count, feature_count)
    upstream = cotangent.astype(jnp.float32).reshape(rows_total, feature_count)
    d_second, dgain_second, dshift_second = norm_backward(
        upstream, normed_two, inverse_two, gain_two
    )
    d_outer = d_second.astype(jnp.bfloat16)
    dbias_outer = jnp.sum(d_outer.astype(jnp.float32), axis=0)
    dweight_outer = matmul_tn(act_low, d_outer)
    d_inner = (matmul_nt(d_outer, outer_weight) * gelu_slope).astype(jnp.bfloat16)
    dbias_inner = jnp.sum(d_inner.astype(jnp.float32), axis=0)
    dweight_inner = matmul_tn(hidden_low, d_inner)
    d_hidden = matmul_nt(d_inner, inner_weight) + d_second
    d_first, dgain_first, dshift_first = norm_backward(d_hidden, normed_one, inverse_one, gain_one)
    d_branch = d_first.astype(jnp.bfloat16)
    dbias_output = jnp.sum(d_branch.astype(jnp.float32), axis=0)
    dweight_output = matmul_tn(context, d_branch)
    d_context = (
        matmul_nt(d_branch, output_weight).astype(jnp.bfloat16).reshape(tok_rows, seq_count, H, DH)
    )
    d_float = d_context.astype(jnp.float32)
    d_mixture = (d_float / denominator).astype(jnp.bfloat16)
    correction = jnp.sum(d_float * attended, axis=-1) / denominator[..., 0]
    key_all, value_all, seg_all = (
        lax.all_gather(key_block_rows, "ctx", axis=0, tiled=True),
        lax.all_gather(value_block_rows, "ctx", axis=0, tiled=True),
        lax.all_gather(seg_local, "ctx", axis=0, tiled=True),
    )
    dq_sum, term_rows = key_side(
        query_heads, d_mixture, correction, seg_local, key_all, value_all, seg_all
    )
    summed = lax.psum_scatter(term_rows, "ctx", scatter_dimension=0, tiled=True)
    d_query = (dq_sum * SCORE_SCALE).astype(jnp.bfloat16)
    d_key = summed[..., :feature_count].astype(jnp.bfloat16)
    d_value = summed[..., feature_count:].astype(jnp.bfloat16)
    dq_flat = d_query.reshape(rows_total, feature_count)
    dk_flat = d_key.reshape(rows_total, feature_count)
    dv_flat = d_value.reshape(rows_total, feature_count)
    dweight_query = matmul_tn(flat_rows, dq_flat)
    dweight_key = matmul_tn(flat_rows, dk_flat)
    dweight_value = matmul_tn(flat_rows, dv_flat)
    dbias_query = jnp.sum(dq_flat.astype(jnp.float32), axis=0)
    dbias_value = jnp.sum(dv_flat.astype(jnp.float32), axis=0)
    grad_tokens = (
        matmul_nt(dq_flat, query_weight)
        + matmul_nt(dk_flat, key_weight)
        + matmul_nt(dv_flat, value_weight)
        + d_first
    )
    shards = (
        lax.psum_scatter(
            dweight_query.astype(jnp.bfloat16), "seq", scatter_dimension=0, tiled=True
        ).astype(jnp.float32),
        lax.psum_scatter(
            dweight_key.astype(jnp.bfloat16), "seq", scatter_dimension=0, tiled=True
        ).astype(jnp.float32),
        lax.psum_scatter(
            dweight_value.astype(jnp.bfloat16), "seq", scatter_dimension=0, tiled=True
        ).astype(jnp.float32),
        lax.psum_scatter(
            dweight_output.astype(jnp.bfloat16), "seq", scatter_dimension=0, tiled=True
        ).astype(jnp.float32),
        lax.psum_scatter(
            dweight_inner.astype(jnp.bfloat16), "seq", scatter_dimension=0, tiled=True
        ).astype(jnp.float32),
        lax.psum_scatter(
            dweight_outer.astype(jnp.bfloat16), "seq", scatter_dimension=0, tiled=True
        ).astype(jnp.float32),
        lax.psum_scatter(
            dbias_query.astype(jnp.bfloat16), "seq", scatter_dimension=0, tiled=True
        ).astype(jnp.float32),
        lax.psum_scatter(
            dbias_value.astype(jnp.bfloat16), "seq", scatter_dimension=0, tiled=True
        ).astype(jnp.float32),
        lax.psum_scatter(
            dbias_output.astype(jnp.bfloat16), "seq", scatter_dimension=0, tiled=True
        ).astype(jnp.float32),
        lax.psum_scatter(
            dbias_inner.astype(jnp.bfloat16), "seq", scatter_dimension=0, tiled=True
        ).astype(jnp.float32),
        lax.psum_scatter(
            dbias_outer.astype(jnp.bfloat16), "seq", scatter_dimension=0, tiled=True
        ).astype(jnp.float32),
        lax.psum_scatter(
            dgain_first.astype(jnp.bfloat16), "seq", scatter_dimension=0, tiled=True
        ).astype(jnp.float32),
        lax.psum_scatter(
            dshift_first.astype(jnp.bfloat16), "seq", scatter_dimension=0, tiled=True
        ).astype(jnp.float32),
        lax.psum_scatter(
            dgain_second.astype(jnp.bfloat16), "seq", scatter_dimension=0, tiled=True
        ).astype(jnp.float32),
        lax.psum_scatter(
            dshift_second.astype(jnp.bfloat16), "seq", scatter_dimension=0, tiled=True
        ).astype(jnp.float32),
    )
    finals = lax.psum(
        (
            shards[0],
            shards[1],
            shards[2],
            shards[3],
            shards[4],
            shards[5],
            shards[6],
            shards[7],
            shards[8],
            shards[9],
            shards[10],
            shards[11],
            shards[12],
            shards[13],
            shards[14],
        ),
        "ctx",
    )
    return (
        layer_out,
        grad_tokens.reshape(tok_rows, seq_count, feature_count),
        finals[0],
        finals[1],
        finals[2],
        finals[3],
        finals[4],
        finals[5],
        finals[6],
        finals[7],
        finals[8],
        finals[9],
        finals[10],
        finals[11],
        finals[12],
        finals[13],
        finals[14],
    )


MESH = pl.DeviceIdType.MESH
BIG = 1e30
F32, BF16 = jnp.float32, jnp.bfloat16


def remote(src, dst, send_sem, recv_sem, seq, ctx):
    return pltpu.make_async_remote_copy(
        src_ref=src,
        dst_ref=dst,
        send_sem=send_sem,
        recv_sem=recv_sem,
        device_id=(seq, ctx),
        device_id_type=MESH,
    )


def greet(seq, ctx):
    barrier = pltpu.get_barrier_semaphore()
    for hop in range(1, 8):
        pl.semaphore_signal(
            barrier, inc=1, device_id=(seq, lax.rem(ctx + hop, 8)), device_id_type=MESH
        )
    for hop in range(1, 4):
        pl.semaphore_signal(
            barrier, inc=1, device_id=(lax.rem(seq + hop, 4), ctx), device_id_type=MESH
        )
    pl.semaphore_wait(barrier, 10)


def flip(index, bit):
    low = lax.rem(index // bit, 2)
    return index + bit - 2 * bit * low


def head_window(group):
    start = group * 192
    inside = lax.rem(group, 2) * 64
    return pl.multiple_of(start - inside, 128), pl.multiple_of(inside, 64)


def span(start, size, unit=16):
    return pl.ds(pl.multiple_of(start, unit), size)


VECTORS = list(
    dict(
        b_query=0,
        b_value=0,
        b_output=0,
        b_outer=0,
        gain_one=0,
        shift_one=0,
        gain_two=0,
        shift_two=0,
    )
)
INPUTS = [
    *dict(x=0, cot=0, seg=0),
    *VECTORS,
    *dict(b_inner=0, wq=0, wk=0, wv=0, wo=0, wi=0, wu=0),
]
OUTPUTS = list(dict(layer=0, grad=0, fu=0, fi=0, fo=0, fg=0, vec_sum=0, bias_sum=0))
SCRATCH = dict(
    seg_own=((2, 8, 128), jnp.int32),
    seg_all=((8, 8, 128), jnp.int32),
    pack_own=((16, 768), BF16),
    pack_all=((4, 16, 768), BF16),
    rows=((8, 768), F32),
    wo_full=((4, 192, 768), BF16),
    wi_full=((4, 192, 3072), BF16),
    wu_full=((4, 768, 768), BF16),
    xs=((8, 128, 768), BF16),
    wg=((3, 4, 192, 256), BF16),
    qa=((3, 128, 1024), BF16),
    ka=((3, 128, 1024), BF16),
    vt=((3, 64, 1024), BF16),
    ot=((3, 64, 1024), F32),
    sums=((3, 1, 1024), F32),
    key_rows=((1024, 128), BF16),
    o_send=((192, 1024), BF16),
    ctx_t=((768, 256), BF16),
    normed=((256, 768), F32),
    inverse=((256, 1), F32),
    low=((256, 768), BF16),
    low_t=((768, 256), BF16),
    act_t=((4, 768, 256), BF16),
    slope=((4, 256, 768), F32),
    work=((256, 768), F32),
    d_rows=((256, 768), BF16),
    v_rows=((16, 768), F32),
    gu=((4, 768, 768), BF16),
    gi=((4, 192, 3072), BF16),
    go=((4, 192, 768), BF16),
    core_u=((2, 768, 768), BF16),
    core_i=((2, 192, 3072), BF16),
    core_o=((2, 192, 768), BF16),
    xr_u=((768, 768), BF16),
    xr_i=((192, 3072), BF16),
    xr_o=((192, 768), BF16),
    rcv_u=((768, 768), BF16),
    rcv_i=((192, 3072), BF16),
    rcv_o=((192, 768), BF16),
    fin_u=((768, 768), BF16),
    fin_i=((192, 3072), BF16),
    fin_o=((192, 768), BF16),
    tot_u=((4, 96, 384), F32),
    tot_i=((2, 96, 768), F32),
    tot_o=((96, 384), F32),
    do_send=((768, 256), BF16),
    do_all=((192, 1024), BF16),
    du=((64, 1024), BF16),
    c_row=((1, 1024), F32),
    value_rows=((1024, 64), BF16),
    dk_acc=((64, 1024), F32),
    dv_acc=((64, 1024), F32),
    d_all=((3, 256, 1024), BF16),
    g_all=((3, 4, 192, 256), BF16),
    g_core=((3, 2, 192, 256), BF16),
    g_xs=((3, 192, 256), BF16),
    g_xr=((3, 192, 256), BF16),
    g_half=((3, 192, 256), BF16),
    g_mir=((3, 96, 256), BF16),
    dx_y=((4, 768, 128), BF16),
    dx_l=((2, 768, 128), BF16),
    dx_h=((768, 128), BF16),
    two_u=((2, 192, 384), BF16),
    two_i=((96, 1536), BF16),
    v_own=((4, 16, 256), F32),
    v_recv=((4, 16, 256), F32),
    v_all=((8, 16, 256), F32),
    b_send=((2, 8, 256), F32),
    b_recv=((8, 2, 8, 256), F32),
)
SEMAPHORES = dict(
    loc=(24,),
    w_ss=(7, 5),
    w_rs=(7, 5),
    x_ss=(12,),
    x_rs=(12,),
    s_ss=(8,),
    s_rs=(8,),
    p_ss=(4,),
    p_rs=(4,),
    g_ss=(3, 3),
    g_rs=(3, 3),
    o_ss=(3, 8),
    o_rs=(3, 8),
    r_ss=(7, 10),
    r_rs=(7, 10),
    do_ss=(3, 8),
    do_rs=(3, 8),
    dx_ss=(7,),
    dx_rs=(7,),
    v_ss=(2, 8),
    v_rs=(2, 8),
    b_ss=(8,),
    b_rs=(8,),
    h_ss=(7, 3),
    h_rs=(7, 3),
)


def layer_kernel(*refs):
    r = types.SimpleNamespace(
        **dict(zip(INPUTS + OUTPUTS + list(SCRATCH) + list(SEMAPHORES), refs))
    )
    seq, ctx = lax.axis_index("seq"), lax.axis_index("ctx")
    plane = seq // 2
    mate, across = flip(seq, 1), flip(seq, 2)
    across_mate = flip(mate, 2)
    beside, paired, mirror = flip(ctx, 1), flip(ctx, 2), flip(ctx, 4)
    bit_y, bit_l, bit_h = lax.rem(ctx, 2), lax.rem(ctx // 2, 2), ctx // 4
    side, group = ctx // 4, lax.rem(ctx, 4)
    window, inside = head_window(group)
    own_lanes = span(ctx * 128, 128, 128)
    sent = []

    def wi_cut(k, where):
        which = where if k == 1 else 1 - where
        return span(which * 1536, 1536, 128)

    def w_views(k, where):
        if k == 0:
            return r.wo, lambda owner: r.wo_full.at[owner], 96
        if k in (1, 2):
            cols = wi_cut(k, where)
            return r.wi.at[:, cols], lambda owner: r.wi_full.at[owner, :, cols], 96
        part = slice(192 * (k - 3), 192 * (k - 2))
        return r.wu.at[part], lambda owner: r.wu_full.at[owner, part], 96

    beside_of = [
        (beside, bit_y) if over_y else (paired, bit_l) for over_y in OVER_Y
    ]

    def half(view, rows, which):
        return view.at[span(which * rows, rows, 32)]

    def w_copy(k, leg):
        sems = r.w_ss.at[k, leg], r.w_rs.at[k, leg]
        shard, full, rows = w_views(k, 1 - plane if leg == 1 else plane)
        partner, bit = beside_of[k]
        if leg == 0:
            return remote(shard, full(seq), *sems, mate, ctx)
        if leg == 1:
            return remote(
                half(shard, rows, bit), half(full(seq), rows, bit), *sems, across, ctx
            )
        which = bit if leg in (2, 3) else 1 - bit
        came = half(full(across), rows, which)
        return remote(came, came, *sems, *((seq, partner) if leg == 2 else (mate, ctx)))

    def w_wait(k, leg):
        shard, full, rows = w_views(k, plane)
        bit = beside_of[k][1]
        spots = (
            lambda: full(mate),
            lambda: half(full(across), rows, bit),
            lambda: half(full(across), rows, 1 - bit),
            lambda: half(full(across_mate), rows, bit),
            lambda: half(full(across_mate), rows, 1 - bit),
        )
        spot = spots[leg]()
        remote(spot, spot, r.w_ss.at[k, leg], r.w_rs.at[k, leg], mate, ctx).wait_recv()

    def pass_across(k):
        w_wait(k, 1)
        w_copy(k, 2).start()
        w_copy(k, 3).start()

    def pass_beside(k):
        w_wait(k, 2)
        w_copy(k, 4).start()

    def w_done(k):
        for leg in (0, 3, 4):
            w_wait(k, leg)

    group_refs = (r.wq, r.wk, r.wv)
    g_local, w_local = [], []
    for which in range(3):
        g_local.append(
            pltpu.make_async_copy(
                group_refs[which].at[:, pl.ds(window, 256)],
                r.wg.at[which, seq],
                r.loc.at[which],
            )
        )
    for n, (ref, full) in enumerate(
        ((r.wo, r.wo_full), (r.wi, r.wi_full), (r.wu, r.wu_full))
    ):
        w_local.append(pltpu.make_async_copy(ref, full.at[seq], r.loc.at[3 + n]))
    own_block = pltpu.make_async_copy(r.x.at[side], r.xs.at[ctx], r.loc.at[6])
    for which in range(2):
        r.seg_own[which] = jnp.broadcast_to(r.seg[which : which + 1], (8, 128))
    r.pack_own[...] = jnp.zeros((16, 768), BF16)
    for n, name in enumerate(VECTORS):
        r.pack_own[n : n + 1, 0:192] = getattr(r, name)[...].reshape(1, 192)
    r.pack_own[8:9] = r.b_inner[...].reshape(1, 768)
    own_seg = pltpu.make_async_copy(r.seg_own.at[side], r.seg_all.at[ctx], r.loc.at[7])
    own_pack = pltpu.make_async_copy(r.pack_own, r.pack_all.at[seq], r.loc.at[8])
    for copy in g_local + [own_block, own_seg, own_pack] + w_local:
        copy.start()
    r.v_rows[...] = jnp.zeros((16, 768), F32)
    for which in range(3):
        r.d_all[which] = jnp.zeros((256, 1024), BF16)

    greet(seq, ctx)

    def send(*args):
        copy = remote(*args)
        copy.start()
        sent.append(copy)

    def landed(spot, send_sem, recv_sem):
        remote(spot, spot, send_sem, recv_sem, seq, beside).wait_recv()

    for hop in range(1, 8):
        other = lax.rem(ctx + hop, 8)
        send(
            r.seg_own.at[other // 4],
            r.seg_all.at[ctx],
            r.s_ss.at[hop],
            r.s_rs.at[hop],
            seq,
            other,
        )
    for hop in range(1, 4):
        other = lax.rem(seq + hop, 4)
        send(r.pack_own, r.pack_all.at[seq], r.p_ss.at[hop], r.p_rs.at[hop], other, ctx)
    for n in range(2):
        part = slice(64 * n, 64 * n + 64)
        send(
            r.x.at[1 - side, part],
            r.xs.at[ctx, part],
            r.x_ss.at[n],
            r.x_rs.at[n],
            seq,
            mirror,
        )
    for n, other in enumerate((beside, paired)):
        send(
            r.x.at[side], r.xs.at[ctx], r.x_ss.at[2 + n], r.x_rs.at[2 + n], seq, other
        )
    for which in range(3):
        for n, other in enumerate((mate, across)):
            send(
                group_refs[which].at[:, pl.ds(window, 256)],
                r.wg.at[which, seq],
                r.g_ss.at[which, n],
                r.g_rs.at[which, n],
                other,
                ctx,
            )
    for k in range(7):
        w_copy(k, 0).start()
        w_copy(k, 1).start()

    t = types.SimpleNamespace()

    def task(run):
        setattr(t, run.__name__, run)

    t.pa = [functools.partial(pass_across, k) for k in range(7)]
    t.pb = [functools.partial(pass_beside, k) for k in range(7)]

    @task
    def grp():
        for which in range(3):
            spot = r.wg.at[which, across]
            landed(spot, r.g_ss.at[which, 1], r.g_rs.at[which, 1])
            send(spot, spot, r.g_ss.at[which, 2], r.g_rs.at[which, 2], mate, ctx)

    diagonal = flip(beside, 2)

    def pass_on(source, half, arrived_by, leg, other):
        spot = r.xs.at[source, 64 * half : 64 * half + 64]
        if arrived_by is not None:
            landed(spot, r.x_ss.at[arrived_by], r.x_rs.at[arrived_by])
        send(spot, spot, r.x_ss.at[leg], r.x_rs.at[leg], seq, other)

    @task
    def nf():
        for n, other in enumerate((beside, paired)):
            landed(r.xs.at[other], r.x_ss.at[2 + n], r.x_rs.at[2 + n])
        pass_on(beside, 0, None, 4, paired)
        pass_on(paired, 1, None, 5, beside)

    def far_half(half):
        pass_on(mirror, half, half, 6 + 2 * half, beside)
        pass_on(mirror, half, None, 7 + 2 * half, paired)

    t.far = [functools.partial(far_half, half) for half in range(2)]
    t.ff = [
        functools.partial(pass_on, flip(beside, 4), 0, 6, 10, paired),
        functools.partial(pass_on, flip(paired, 4), 1, 9, 11, beside),
    ]

    @task
    def small():
        for which in range(3):
            g_local[which].wait()
            for n, owner in ((0, mate), (2, across_mate)):
                landed(
                    r.wg.at[which, owner], r.g_ss.at[which, n], r.g_rs.at[which, n]
                )
        own_pack.wait()
        for hop in range(1, 4):
            landed(
                r.pack_all.at[lax.rem(seq + 4 - hop, 4)], r.p_ss.at[hop], r.p_rs.at[hop]
            )
        own_seg.wait()
        for hop in range(1, 8):
            landed(
                r.seg_all.at[lax.rem(ctx + 8 - hop, 8)], r.s_ss.at[hop], r.s_rs.at[hop]
            )
        lane = lax.broadcasted_iota(jnp.int32, (256, 768), 1)
        at = lax.broadcasted_iota(jnp.int32, (256, 768), 0)
        rows = jnp.zeros((8, 768), F32)
        for owner in range(4):
            chosen = ((lane == at + 192 * owner) & (at < 192)).astype(BF16)
            rows += matmul(r.pack_all[owner, 0:8, 0:256], chosen)
        r.rows[...] = rows

    @task
    def qkv():
        own_block.wait()
        for source, half, leg in (
            (diagonal, 0, 4),
            (diagonal, 1, 5),
            (flip(paired, 4), 0, 7),
            (flip(beside, 4), 1, 8),
            (flip(diagonal, 4), 0, 10),
            (flip(diagonal, 4), 1, 11),
        ):
            spot = r.xs.at[source, 64 * half : 64 * half + 64]
            landed(spot, r.x_ss.at[leg], r.x_rs.at[leg])
        tokens = r.xs[...].reshape(1024, 768)
        own_rows = r.pack_all[group]
        qkv = []
        for which in range(3):
            weight = r.wg[which].reshape(768, 256)
            product = matmul_nt(weight.T, tokens)
            if which != 1:
                bias = own_rows[which // 2 : which // 2 + 1, 0:256].astype(F32)
                column = jnp.broadcast_to(bias, (128, 256)).T
                shifted = jnp.where(inside == 0, column, pltpu.roll(column, 64, 0))
                product = product + jnp.concatenate([shifted] * 8, axis=1)
            part = product.astype(BF16)
            if which == 0:
                part = part * jnp.bfloat16(SCORE_SCALE)
            qkv.append(part)
        number = jnp.concatenate(
            [r.seg_all[block, 0:1] for block in range(8)], axis=1
        )
        hot = lax.broadcasted_iota(jnp.int32, (16, 1024), 0) == number
        query_marks = jnp.where(hot, 1.0, 0.0).astype(BF16)
        key_marks = jnp.where(hot, 0.0, -BIG).astype(BF16)
        blank = jnp.zeros((48, 1024), BF16)
        for head in range(3):
            parts = [
                jnp.where(
                    inside != 0,
                    part[64 * head + 64 : 64 * head + 128],
                    part[64 * head : 64 * head + 64],
                )
                for part in qkv
            ]
            r.qa[head] = jnp.concatenate([parts[0], query_marks, blank], axis=0)
            r.ka[head] = jnp.concatenate([parts[1], key_marks, blank], axis=0)
            r.vt[head] = parts[2]

    my_rows = span(group * 192, 192, 64)
    my_lanes = span(side * 128, 128, 128)
    own_o = pltpu.make_async_copy(
        r.o_send.at[:, own_lanes], r.ctx_t.at[my_rows, my_lanes], r.loc.at[9]
    )

    def attend_head(head):
        r.key_rows[...] = r.ka[head].T

        def attend(block, unused):
            lanes = span(block * 256, 256, 256)
            scores = matmul(r.key_rows[...], r.qa[head, :, lanes])
            unnorm = jnp.exp(scores)
            total = jnp.sum(unnorm, axis=0, keepdims=True)
            attended = matmul(r.vt[head], unnorm.astype(BF16)) / total
            r.ot[head, :, lanes] = attended
            r.sums[head, :, lanes] = total
            r.o_send[64 * head : 64 * head + 64, lanes] = attended.astype(BF16)
            return unused

        lax.fori_loop(0, 4, attend, 0)
        if head == 2:
            own_o.start()
        part = slice(64 * head, 64 * head + 64)
        for hop in range(1, 8):
            other = lax.rem(ctx + hop, 8)
            send(
                r.o_send.at[part, span(other * 128, 128, 128)],
                r.ctx_t.at[span(group * 192 + 64 * head, 64, 64), my_lanes],
                r.o_ss.at[head, hop],
                r.o_rs.at[head, hop],
                seq,
                other,
            )

    t.at = [functools.partial(attend_head, head) for head in range(3)]

    def row_vec(n):
        return r.rows[n : n + 1]

    @task
    def fn():
        own_o.wait()
        for head in range(3):
            for hop in range(1, 8):
                other = lax.rem(ctx + 8 - hop, 8)
                spot = r.ctx_t.at[
                    span(lax.rem(other, 4) * 192 + 64 * head, 64, 64),
                    span((other // 4) * 128, 128, 128),
                ]
                landed(spot, r.o_ss.at[head, hop], r.o_rs.at[head, hop])
        w_local[0].wait()
        w_done(0)

        def first_norm(which, unused):
            at, lanes = span(which * 128, 128, 128), span(which * 128, 128, 128)
            value = (
                matmul(r.ctx_t[:, lanes].T, r.wo_full[...].reshape(768, 768))
                + row_vec(2)
                + r.x[which].astype(F32)
            )
            hidden, normed, inverse = norm_forward(value, row_vec(4), row_vec(5))
            r.normed[at] = normed
            r.inverse[at] = inverse
            part = hidden.astype(BF16)
            r.low[at] = part
            r.low_t[:, lanes] = part.T
            r.work[at] = hidden + row_vec(3)
            return unused

        lax.fori_loop(0, 2, first_norm, 0)

    def inner_weight(n):
        return r.wi_full[:, :, span(n * 768, 768, 128)].reshape(768, 768)

    def feed(where):
        def visit(step, unused):
            n, which = where * 2 + step // 2, lax.rem(step, 2)
            at = span(which * 128, 128, 128)
            value = matmul(r.low[at], inner_weight(n)) + r.pack_all[n, 8:9].astype(F32)
            act, slope = gelu_parts(value)
            part = act.astype(BF16)
            r.slope[n, at] = slope
            r.act_t[n, :, at] = part.T
            r.work[at] += matmul(part, r.wu_full[n])
            return unused

        lax.fori_loop(0, 4, visit, 0)

    @task
    def fe0():
        w_local[1].wait()
        w_local[2].wait()
        w_done(1)
        for k in range(3, 7):
            w_wait(k, 0)
        feed(plane)

    @task
    def fe1():
        w_done(2)
        for k in range(3, 7):
            w_wait(k, 3)
            w_wait(k, 4)
        feed(1 - plane)

    def tally(n, value):
        r.v_rows[n : n + 1] += jnp.sum(value, axis=0, keepdims=True)

    @task
    def sn():
        def second_norm(which, unused):
            at = span(which * 128, 128, 128)
            result, normed, inverse = norm_forward(r.work[at], row_vec(6), row_vec(7))
            r.layer[which] = result.astype(BF16)
            upstream = r.cot[which].astype(F32)
            scaled = upstream * row_vec(6)
            back = inverse * (
                scaled
                - jnp.mean(scaled, axis=-1, keepdims=True)
                - normed * jnp.mean(scaled * normed, axis=-1, keepdims=True)
            )
            tally(4, upstream * normed)
            tally(5, upstream)
            r.work[at] = back
            part = back.astype(BF16)
            r.d_rows[at] = part
            tally(1, part.astype(F32))
            return unused

        lax.fori_loop(0, 2, second_norm, 0)

    chunks = [
        (r.gu, r.fu, r.core_u, r.xr_u, r.rcv_u, r.fin_u, r.tot_u.at[k], 192 * k, 192, 0, 768)
        for k in range(4)
    ]
    chunks += [
        (r.gi, r.fi, r.core_i, r.xr_i, r.rcv_i, r.fin_i, r.tot_i.at[k], 0, 192, 1536 * k, 1536)
        for k in range(2)
    ]
    chunks += [
        (r.go, r.fo, r.core_o, r.xr_o, r.rcv_o, r.fin_o, r.tot_o, 0, 192, 0, 768),
    ]

    def reduce_steps(k, first):
        grad, out, core, arrived, rcv, fin, total, row, rows, col, cols = chunks[k]
        rr, cc = pl.ds(row, rows), pl.ds(col, cols)
        wide = cols // 2
        mine = span(col + bit_y * wide, wide, 128)
        other = span(col + (1 - bit_y) * wide, wide, 128)
        keep_l = span(row + bit_l * (rows // 2), rows // 2)
        give_l = span(row + (1 - bit_l) * (rows // 2), rows // 2)
        keep_h = span(row + bit_l * (rows // 2) + bit_h * (rows // 4), rows // 4)
        give_h = span(row + bit_l * (rows // 2) + (1 - bit_h) * (rows // 4), rows // 4)
        spot_h = span(row + (1 - bit_l) * (rows // 2), rows // 4)
        tot_keep, tot_give = (
            span(bit_h * (rows // 4), rows // 4),
            span((1 - bit_h) * (rows // 4), rows // 4),
        )
        owner = (seq, across)

        def sems(leg):
            return r.r_ss.at[k, leg], r.r_rs.at[k, leg]

        to_core = [
            remote(grad.at[mate, rr, cc], core.at[0, rr, cc], *sems(0), mate, ctx),
            remote(
                grad.at[across_mate, rr, cc], core.at[1, rr, cc], *sems(1), mate, ctx
            ),
        ]

        def add(at, lanes, slot, *more):
            value = grad[owner[slot], at, lanes].astype(F32) + core[
                slot, at, lanes
            ].astype(F32)
            for ref in more:
                value += ref[at, lanes].astype(F32)
            return value

        def put(at, lanes, slot, *more):
            core[slot, at, lanes] = add(at, lanes, slot, *more).astype(BF16)

        def spread(at, lanes, leg, target):
            spot = fin.at[at, lanes]
            return remote(spot, spot, *sems(leg), seq, target)

        to_h = remote(
            arrived.at[give_h, mine], rcv.at[spot_h, other], *sems(5), seq, mirror
        )

        def begin():
            for copy in to_core:
                copy.start()

        def cores_in():
            for copy in to_core:
                copy.wait_recv()

        if first == "x":
            to_x = remote(core.at[1, rr, cc], arrived.at[rr, cc], *sems(2), across, ctx)
            to_y = remote(arrived.at[rr, other], rcv.at[rr, other], *sems(3), seq, beside)
            at_y = remote(arrived.at[rr, mine], rcv.at[rr, mine], *sems(3), seq, beside)
            firsts = [to_x, to_y]

            def one():
                put(rr, cc, 1)
                to_x.start()

            def two():
                arrived[rr, other] = add(rr, other, 0, arrived).astype(BF16)
                to_y.start()

        elif first == "y":
            extra = r.two_u.at[k % 2]
            to_y = [
                remote(
                    core.at[0, rr, other], rcv.at[rr, other], *sems(3), seq, beside
                ),
                remote(core.at[1, rr, other], extra, *sems(9), seq, beside),
            ]
            at_y = [
                remote(core.at[0, rr, mine], rcv.at[rr, mine], *sems(3), seq, beside),
                remote(core.at[1, rr, mine], extra, *sems(9), seq, beside),
            ]
            to_x = remote(
                core.at[1, rr, mine], arrived.at[rr, mine], *sems(2), across, ctx
            )
            firsts = to_y + [to_x]

            def one():
                for slot in range(2):
                    put(rr, other, slot)
                    to_y[slot].start()

            def two():
                for copy in at_y:
                    copy.wait_recv()
                core[1, rr, mine] = (add(rr, mine, 1) + extra[...].astype(F32)).astype(
                    BF16
                )
                to_x.start()

        else:
            extra = r.two_i
            to_l = [
                remote(core.at[0, give_l, cc], rcv.at[give_l, cc], *sems(4), seq, paired),
                remote(core.at[1, give_l, cc], extra, *sems(9), seq, paired),
            ]
            at_l = [
                remote(core.at[0, keep_l, cc], rcv.at[keep_l, cc], *sems(4), seq, paired),
                remote(core.at[1, keep_l, cc], extra, *sems(9), seq, paired),
            ]
            to_x = remote(
                core.at[1, keep_l, cc], arrived.at[keep_l, cc], *sems(2), across, ctx
            )
            to_y = remote(
                arrived.at[keep_l, other], rcv.at[give_l, other], *sems(3), seq, beside
            )
            at_y = remote(
                arrived.at[keep_l, mine], rcv.at[give_l, mine], *sems(3), seq, beside
            )
            firsts = to_l + [to_x, to_y]

            def one():
                for slot in range(2):
                    put(give_l, cc, slot)
                    to_l[slot].start()

            def two():
                for copy in at_l:
                    copy.wait_recv()
                core[1, keep_l, cc] = (
                    add(keep_l, cc, 1) + extra[...].astype(F32)
                ).astype(BF16)
                to_x.start()

            def three():
                to_x.wait_recv()
                arrived[keep_l, other] = add(keep_l, other, 0, rcv, arrived).astype(BF16)
                to_y.start()
                total[...] = add(keep_l, mine, 0, rcv, arrived)

            def four():
                at_y.wait_recv()
                total[...] += rcv[give_l, mine].astype(F32)
                arrived[give_h, mine] = total[tot_give].astype(BF16)
                to_h.start()

        if first != "z":
            to_l = remote(
                arrived.at[give_l, mine], rcv.at[give_l, other], *sems(4), seq, paired
            )
            at_l = remote(
                arrived.at[keep_l, mine], rcv.at[keep_l, other], *sems(4), seq, paired
            )
            firsts = firsts + [to_l]

            def three():
                (at_y if first == "x" else to_x).wait_recv()
                arrived[give_l, mine] = add(give_l, mine, 0, arrived, rcv).astype(BF16)
                to_l.start()
                total[...] = add(keep_l, mine, 0, arrived, rcv)

            def four():
                at_l.wait_recv()
                arrived[give_h, mine] = (
                    total[tot_give] + rcv[give_h, other].astype(F32)
                ).astype(BF16)
                to_h.start()
                total[tot_keep] += rcv[keep_h, other].astype(F32)

        def step_one():
            cores_in()
            one()

        def step_two():
            if first == "x":
                to_x.wait_recv()
            two()

        def step_five():
            to_h.wait_recv()
            fin[keep_h, mine] = (
                total[tot_keep] + rcv[spot_h, other].astype(F32)
            ).astype(BF16)
            spread(keep_h, mine, 6, mirror).start()

        if first == "z":
            last = [(keep_l, other, 7, beside), (keep_l, cc, 8, paired)]
            ends = [(give_l, cc)]
            middle = (keep_l, mine)
        else:
            last = [(give_l, mine, 7, paired), (rr, mine, 8, beside)]
            ends = [(rr, other)]
            middle = (keep_l, mine)

        def step_six():
            spread(give_h, mine, 6, mirror).wait_recv()
            spread(*middle, 7, last[0][3]).start()

        def step_seven():
            spread(*last[0]).wait_recv()
            spread(*last[1]).start()

        to_out = pltpu.make_async_copy(fin.at[rr, cc], out.at[rr, cc], r.loc.at[17 + k])

        def step_eight():
            spread(*ends[0], 8, last[1][3]).wait_recv()
            to_out.start()

        def end():
            for copy in (
                to_core
                + firsts
                + [
                    to_h,
                    spread(keep_h, mine, 6, mirror),
                    spread(*middle, 7, last[0][3]),
                    spread(*last[1]),
                ]
            ):
                copy.wait_send()
            to_out.wait()

        names = [
            begin,
            step_one,
            step_two,
            three,
            four,
            step_five,
            step_six,
            step_seven,
            step_eight,
            end,
        ]
        return names

    t.s = [reduce_steps(k, FIRST[k]) for k in range(7)]

    def make_outer(k):
        part = slice(192 * k, 192 * k + 192)
        for owner in (mate, across_mate):
            r.gu[owner, part] = matmul(r.act_t[owner, part], r.d_rows[...]).astype(BF16)
        t.s[k][0]()
        for owner in (across, seq):
            r.gu[owner, part] = matmul(r.act_t[owner, part], r.d_rows[...]).astype(BF16)

    t.mo = [functools.partial(make_outer, k) for k in range(4)]

    def inner_step(n):
        def inner_back(which, unused):
            at = span(which * 128, 128, 128)
            part = (matmul_nt(r.d_rows[at], r.wu_full[n]) * r.slope[n, at]).astype(BF16)
            r.low[at] = part
            tally(8 + n, part.astype(F32))
            r.work[at] += matmul_nt(part, inner_weight(n))
            return unused

        lax.fori_loop(0, 2, inner_back, 0)
        r.gi[:, :, 768 * n : 768 * n + 768] = (
            matmul(r.low_t[...], r.low[...]).astype(BF16).reshape(4, 192, 768)
        )
        if n % 2:
            t.s[4 + n // 2][0]()

    t.ib = [functools.partial(inner_step, n) for n in range(4)]

    own_do = pltpu.make_async_copy(
        r.do_send.at[my_rows, my_lanes], r.do_all.at[:, own_lanes], r.loc.at[15]
    )

    @task
    def fb():
        def first_back(which, unused):
            at = span(which * 128, 128, 128)
            upstream, normed = r.work[at], r.normed[at]
            scaled = upstream * row_vec(4)
            back = r.inverse[at] * (
                scaled
                - jnp.mean(scaled, axis=-1, keepdims=True)
                - normed * jnp.mean(scaled * normed, axis=-1, keepdims=True)
            )
            tally(2, upstream * normed)
            tally(3, upstream)
            r.work[at] = back
            part = back.astype(BF16)
            r.low[at] = part
            tally(0, part.astype(F32))
            return unused

        lax.fori_loop(0, 2, first_back, 0)
        r.do_send[...] = matmul_nt(
            r.wo_full[...].reshape(768, 768), r.low[...]
        ).astype(BF16)
        own_do.start()
        for head in range(3):
            for hop in range(1, 8):
                other = lax.rem(ctx + hop, 8)
                send(
                    r.do_send.at[
                        span(lax.rem(other, 4) * 192 + 64 * head, 64, 64),
                        span((other // 4) * 128, 128, 128),
                    ],
                    r.do_all.at[64 * head : 64 * head + 64, own_lanes],
                    r.do_ss.at[head, hop],
                    r.do_rs.at[head, hop],
                    seq,
                    other,
                )

    @task
    def dwo():
        r.go[...] = matmul(r.ctx_t[...], r.low[...]).astype(BF16).reshape(4, 192, 768)
        t.s[6][0]()
        for owner in range(4):
            start = 192 * owner - 64 * (owner % 2)
            r.v_own[owner, 0:8] = r.v_rows[0:8, start : start + 256]
            for part in range(3):
                r.v_own[owner, 8 + part : 9 + part] = r.v_rows[
                    8 + owner : 9 + owner, 256 * part : 256 * part + 256
                ]
            r.v_own[owner, 11:16] = jnp.zeros((5, 256), F32)
        for hop in range(1, 4):
            other = lax.rem(seq + hop, 4)
            send(
                r.v_own.at[other],
                r.v_recv.at[seq],
                r.v_ss.at[0, hop],
                r.v_rs.at[0, hop],
                other,
                ctx,
            )

    @task
    def v1():
        for hop in range(1, 4):
            spot = r.v_recv.at[lax.rem(seq + 4 - hop, 4)]
            landed(spot, r.v_ss.at[0, hop], r.v_rs.at[0, hop])
        r.v_recv[seq] = r.v_own[seq]
        r.v_all[ctx] = r.v_recv[0] + r.v_recv[1] + r.v_recv[2] + r.v_recv[3]
        for hop in range(1, 8):
            send(
                r.v_all.at[ctx],
                r.v_all.at[ctx],
                r.v_ss.at[1, hop],
                r.v_rs.at[1, hop],
                seq,
                lax.rem(ctx + hop, 8),
            )

    def attend_back_head(head):
        if head == 0:
            own_do.wait()
        for hop in range(1, 8):
            spot = r.do_all.at[
                64 * head : 64 * head + 64, span(lax.rem(ctx + 8 - hop, 8) * 128, 128, 128)
            ]
            landed(spot, r.do_ss.at[head, hop], r.do_rs.at[head, hop])
        at = span(inside + 64 * head, 64, 64)
        total = r.sums[head]
        d_out = r.do_all[64 * head : 64 * head + 64].astype(F32)
        r.du[...] = (d_out / total).astype(BF16)
        r.c_row[...] = jnp.sum(d_out * r.ot[head], axis=0, keepdims=True) / total
        r.key_rows[...] = r.ka[head].T
        r.value_rows[...] = r.vt[head].T
        r.dk_acc[...] = jnp.zeros((64, 1024), F32)
        r.dv_acc[...] = jnp.zeros((64, 1024), F32)

        def attend_back(block, unused):
            lanes = span(block * 256, 256, 256)
            scores = matmul(r.key_rows[...], r.qa[head, :, lanes])
            unnorm = jnp.exp(scores)
            d_prob = matmul(r.value_rows[...], r.du[:, lanes])
            d_score = (unnorm * (d_prob - r.c_row[:, lanes])).astype(BF16)
            d_query = matmul(r.ka[head, 0:64], d_score) * SCORE_SCALE
            r.d_all[0, at, lanes] = d_query.astype(BF16)
            r.dk_acc[...] += matmul_nt(r.qa[head, 0:64, lanes], d_score)
            r.dv_acc[...] += matmul_nt(r.du[:, lanes], unnorm.astype(BF16))
            return unused

        lax.fori_loop(0, 4, attend_back, 0)
        r.d_all[1, at] = r.dk_acc[...].astype(BF16)
        r.d_all[2, at] = r.dv_acc[...].astype(BF16)

    t.ab = [functools.partial(attend_back_head, head) for head in range(3)]

    g_cores = [
        remote(
            r.g_all.at[which, owner],
            r.g_core.at[which, n],
            r.h_ss.at[which, n],
            r.h_rs.at[which, n],
            mate,
            ctx,
        )
        for which in range(3)
        for n, owner in ((0, mate), (1, across_mate))
    ]
    own_bias = pltpu.make_async_copy(
        r.b_send, r.b_recv.at[seq * 2 + side], r.loc.at[16]
    )
    to_owners = [
        remote(
            r.b_send,
            r.b_recv.at[seq * 2 + side],
            r.b_ss.at[hop],
            r.b_rs.at[seq * 2 + side],
            group,
            lax.rem(ctx + hop, 8),
        )
        for hop in range(8)
    ]

    @task
    def dwq():
        ones = jnp.ones((16, 1024), BF16)
        for which in range(3):
            product = matmul(r.d_all[which], r.xs[...].reshape(1024, 768)).astype(BF16)
            r.g_all[which] = product.T.reshape(4, 192, 256)
            if which != 1:
                r.b_send[which // 2] = matmul_nt(ones, r.d_all[which])[0:8]
        for copy in g_cores:
            copy.start()

        @pl.when(group == seq)
        def _():
            own_bias.start()

        @pl.when(group != seq)
        def _():
            to_owners[0].start()

        for copy in to_owners[1:]:
            copy.start()

    @task
    def dx():
        for part in range(4):
            lanes = slice(256 * part, 256 * part + 256)
            share = matmul(r.wg[0].reshape(768, 256), r.d_all[0, :, lanes])
            for which in (1, 2):
                share += matmul(r.wg[which].reshape(768, 256), r.d_all[which, :, lanes])
            r.act_t[part] = share.astype(BF16)

    def dx_half(part, bit):
        return r.act_t.at[part, :, span(bit * 128, 128, 128)]

    dx_to_y = [
        remote(
            dx_half(part, 1 - bit_y),
            r.dx_y.at[part],
            r.dx_ss.at[part],
            r.dx_rs.at[part],
            seq,
            beside,
        )
        for part in range(4)
    ]
    dx_to_l = [
        remote(
            dx_half(2 * n + 1 - bit_l, bit_y),
            r.dx_l.at[n],
            r.dx_ss.at[4 + n],
            r.dx_rs.at[4 + n],
            seq,
            paired,
        )
        for n in range(2)
    ]
    lanes_y = span(bit_y * 128, 128, 128)

    def dx_part(which):
        return 2 * which + bit_l

    dx_to_h = remote(
        dx_half(dx_part(1 - side), bit_y),
        r.dx_h,
        r.dx_ss.at[6],
        r.dx_rs.at[6],
        seq,
        mirror,
    )
    t.d = [copy.start for copy in dx_to_y]

    @task
    def dxp():
        for copy in dx_to_y:
            copy.wait_recv()
        for n in range(2):
            part = 2 * n + 1 - bit_l
            r.act_t[part, :, lanes_y] = (
                r.act_t[part, :, lanes_y].astype(F32) + r.dx_y[part].astype(F32)
            ).astype(BF16)
            dx_to_l[n].start()

    def dx_total(which):
        part = dx_part(which)
        return (
            r.act_t[part, :, lanes_y].astype(F32)
            + r.dx_y[part].astype(F32)
            + r.dx_l[which].astype(F32)
        )

    @task
    def dxm():
        for copy in dx_to_l:
            copy.wait_recv()
        r.act_t[dx_part(1 - side), :, lanes_y] = dx_total(1 - side).astype(BF16)
        dx_to_h.start()
        r.grad[side] = dx_total(side).T + r.work[span(side * 128, 128)]

    @task
    def dxe():
        dx_to_h.wait_recv()
        r.grad[1 - side] = (
            r.dx_h[...].astype(F32).T + r.work[span((1 - side) * 128, 128)]
        )

    g_x = remote(r.g_xs, r.g_xr, r.h_ss.at[3, 0], r.h_rs.at[3, 0], across, ctx)
    keep, give = span(side * 96, 96, 32), span((1 - side) * 96, 96, 32)
    g_m = remote(
        r.g_half.at[:, give], r.g_mir, r.h_ss.at[3, 1], r.h_rs.at[3, 1], seq, mirror
    )

    @task
    def gx():
        for copy in g_cores:
            copy.wait_recv()
        for which in range(3):
            r.g_xs[which] = (
                r.g_all[which, across].astype(F32) + r.g_core[which, 1].astype(F32)
            ).astype(BF16)
        g_x.start()

    @task
    def gm():
        g_x.wait_recv()
        for which in range(3):
            r.g_half[which] = (
                r.g_all[which, seq].astype(F32)
                + r.g_core[which, 0].astype(F32)
                + r.g_xr[which].astype(F32)
            ).astype(BF16)
        g_m.start()

    @task
    def ga():
        g_m.wait_recv()
        for which in range(3):
            r.fg[group, which, keep] = (
                r.g_half[which, keep].astype(F32) + r.g_mir[which].astype(F32)
            ).astype(BF16)
        spot = r.fg.at[group, :, keep]
        send(spot, spot, r.h_ss.at[4, 0], r.h_rs.at[4, 0], seq, mirror)
        for n, other in enumerate((beside, paired)):
            send(spot, spot, r.h_ss.at[5, n], r.h_rs.at[5, n], seq, other)

    @task
    def gb():
        theirs = r.fg.at[group, :, give]
        landed(theirs, r.h_ss.at[4, 0], r.h_rs.at[4, 0])
        for n, other in enumerate((beside, paired)):
            send(theirs, theirs, r.h_ss.at[6, n], r.h_rs.at[6, n], seq, other)

    def of_group(other, rows):
        return r.fg.at[lax.rem(other, 4), :, rows]

    @task
    def gc():
        spot = of_group(beside, keep)
        landed(spot, r.h_ss.at[5, 0], r.h_rs.at[5, 0])
        send(spot, spot, r.h_ss.at[5, 2], r.h_rs.at[5, 2], seq, paired)

    @task
    def gd():
        spot = of_group(paired, give)
        landed(spot, r.h_ss.at[6, 1], r.h_rs.at[6, 1])
        send(spot, spot, r.h_ss.at[6, 2], r.h_rs.at[6, 2], seq, beside)

    @task
    def v2():
        for hop in range(1, 8):
            spot = r.v_all.at[lax.rem(ctx + 8 - hop, 8)]
            landed(spot, r.v_ss.at[1, hop], r.v_rs.at[1, hop])
        gathered = r.v_all[0]
        for n in range(1, 8):
            gathered += r.v_all[n]
        r.vec_sum[...] = gathered

    @task
    def be():
        for n in range(8):
            spot = r.b_recv.at[n]
            arrival = remote(
                spot, spot, r.b_ss.at[0], r.b_rs.at[n], lax.rem(seq + 1, 4), ctx
            )
            here = (n // 2 == seq) & (n % 2 == side) & (group == seq)

            @pl.when(here)
            def _():
                own_bias.wait()

            @pl.when(jnp.logical_not(here))
            def _(arrival=arrival):
                arrival.wait_recv()

        row_sum = r.b_recv[0]
        for n in range(1, 8):
            row_sum += r.b_recv[n]
        r.bias_sum[...] = row_sum

    @task
    def ge():
        landed(of_group(paired, keep), r.h_ss.at[5, 1], r.h_rs.at[5, 1])
        landed(of_group(beside, give), r.h_ss.at[6, 0], r.h_rs.at[6, 0])
        landed(of_group(diagonal, keep), r.h_ss.at[5, 2], r.h_rs.at[5, 2])
        landed(of_group(diagonal, give), r.h_ss.at[6, 2], r.h_rs.at[6, 2])

    for step in in_order(t):
        step()

    for k in range(7):
        t.s[k][9]()
    for copy in (
        sent + g_cores + [g_x, g_m] + to_owners[1:] + dx_to_y + dx_to_l + [dx_to_h]
    ):
        copy.wait_send()

    @pl.when(group != seq)
    def _():
        to_owners[0].wait_send()

    for k in range(7):
        for leg in range(5):
            w_copy(k, leg).wait_send()


FIRST = "xxyyxzx"
OVER_Y = (1, 0, 1, 0, 1, 0, 1)


def in_order(t):
    return (
        t.far[0],
        t.grp,
        t.far[1],
        t.nf,
        t.ff[0],
        t.ff[1],
        t.pa[0],
        t.pa[1],
        t.small,
        t.qkv,
        t.pa[2],
        t.at[0],
        t.at[1],
        t.pb[1],
        t.at[2],
        t.pa[4],
        t.pa[5],
        t.pa[3],
        t.pb[0],
        t.pa[6],
        t.fn,
        t.pb[5],
        t.pb[2],
        t.pb[4],
        t.fe0,
        t.pb[3],
        t.pb[6],
        t.fe1,
        t.sn,
        t.mo[0],
        t.mo[1],
        t.mo[2],
        t.mo[3],
        t.ib[0],
        t.s[0][1],
        t.s[1][1],
        t.ib[1],
        t.s[2][1],
        t.ib[2],
        t.ib[3],
        t.fb,
        t.s[3][1],
        t.s[5][1],
        t.dwo,
        t.s[4][1],
        t.s[0][2],
        t.ab[0],
        t.ab[1],
        t.s[2][2],
        t.s[1][2],
        t.v1,
        t.s[3][2],
        t.ab[2],
        t.dx,
        t.s[4][2],
        t.s[0][3],
        t.s[1][3],
        t.dwq,
        t.s[6][1],
        t.s[2][3],
        t.v2,
        t.s[0][4],
        t.d[0],
        t.s[1][4],
        t.s[3][3],
        t.s[2][4],
        t.d[1],
        t.s[4][3],
        t.s[0][5],
        t.s[5][2],
        t.be,
        t.s[3][4],
        t.s[1][5],
        t.s[6][2],
        t.s[2][5],
        t.s[4][4],
        t.s[0][6],
        t.s[1][6],
        t.s[5][3],
        t.s[3][5],
        t.s[6][3],
        t.gx,
        t.s[0][7],
        t.s[2][6],
        t.s[4][5],
        t.s[6][4],
        t.s[1][7],
        t.s[3][6],
        t.d[2],
        t.s[5][4],
        t.s[0][8],
        t.s[4][6],
        t.s[1][8],
        t.s[6][5],
        t.d[3],
        t.gm,
        t.s[3][7],
        t.s[5][5],
        t.s[6][6],
        t.s[2][7],
        t.dxp,
        t.s[3][8],
        t.s[6][7],
        t.s[4][7],
        t.ga,
        t.s[2][8],
        t.s[6][8],
        t.dxm,
        t.s[5][6],
        t.s[4][8],
        t.gb,
        t.s[5][7],
        t.dxe,
        t.gd,
        t.gc,
        t.s[5][8],
        t.ge,
    )


def run_layer(*operands):
    vmem = pl.BlockSpec(memory_space=pltpu.VMEM)
    anywhere = pl.BlockSpec(memory_space=pl.ANY)
    shape = jax.ShapeDtypeStruct
    return pl.pallas_call(
        layer_kernel,
        name="layer_kernel",
        out_shape=(
            shape((2, 128, 768), BF16),
            shape((2, 128, 768), F32),
            shape((768, 768), BF16),
            shape((192, 3072), BF16),
            shape((192, 768), BF16),
            shape((4, 3, 192, 256), BF16),
            shape((16, 256), F32),
            shape((2, 8, 256), F32),
        ),
        in_specs=[vmem] * 12 + [anywhere] * 6,
        out_specs=(vmem,) * 2 + (anywhere,) * 3 + (vmem,) * 3,
        scratch_shapes=[pltpu.VMEM(*spec) for spec in SCRATCH.values()]
        + [pltpu.SemaphoreType.DMA(count) for count in SEMAPHORES.values()],
        compiler_params=pltpu.CompilerParams(
            collective_id=1, has_side_effects=True, vmem_limit_bytes=67043328
        ),
    )(*operands)


def finish_kernel(*refs):
    ins, outs, bufs = refs[:8], refs[8:25], refs[25:]
    low, wide, load, store = bufs[:8], bufs[8:17], bufs[17], bufs[18]
    grad, layer, low_u, low_i, low_o, low_g, vec, bias = low
    wide_t, wide_l, out_l, wide_u, wide_i, wide_o, wide_q, wide_k, wide_v = wide
    loads = [
        pltpu.make_async_copy(source, target, load.at[n])
        for n, (source, target) in enumerate(zip(ins, low))
    ]
    for copy in loads:
        copy.start()
    stores = []

    def put(source, target):
        copy = pltpu.make_async_copy(source, target, store.at[len(stores)])
        copy.start()
        stores.append(copy)

    loads[2].wait()
    for part in (slice(0, 384), slice(384, 768)):
        wide_u[part] = low_u[part].astype(F32)
        put(wide_u.at[part], outs[7].at[part])
    loads[3].wait()
    for part in (slice(0, 96), slice(96, 192)):
        wide_i[part] = low_i[part].astype(F32)
        put(wide_i.at[part], outs[6].at[part])
    loads[0].wait()
    for which in range(2):
        wide_t[:, which, :] = grad[which]
    put(wide_t, outs[1])
    loads[1].wait()
    for which in range(2):
        wide_l[:, which, :] = layer[which].astype(F32)
    out_l[...] = wide_l[...].astype(BF16)
    put(out_l, outs[0])
    loads[4].wait()
    wide_o[...] = low_o[...].astype(F32)
    put(wide_o, outs[5])
    loads[5].wait()
    for which, target in enumerate((wide_q, wide_k, wide_v)):
        for pair in range(2):
            left = low_g[2 * pair, which].astype(F32)
            right = low_g[2 * pair + 1, which].astype(F32)
            at = 384 * pair
            target[:, at : at + 128] = left[:, 0:128]
            target[:, at + 128 : at + 256] = left[:, 128:256] + right[:, 0:128]
            target[:, at + 256 : at + 384] = right[:, 128:256]
        put(target, outs[2 + which])
    odd = lax.rem(lax.axis_index("seq"), 2) == 1

    def owned(row):
        return jnp.where(odd, row[:, 64:256], row[:, 0:192]).reshape(192)

    loads[6].wait()
    loads[7].wait()
    outs[8][...] = owned(bias[0, 0:1])
    outs[9][...] = owned(bias[1, 0:1])
    outs[10][...] = owned(vec[0:1])
    outs[11][...] = jnp.concatenate([vec[n : n + 1] for n in (8, 9, 10)], axis=1).reshape(
        768
    )
    for n in range(1, 6):
        outs[11 + n][...] = owned(vec[n : n + 1])
    for copy in stores:
        copy.wait()


def run_finish(*operands):
    vmem = pl.BlockSpec(memory_space=pltpu.VMEM)
    anywhere = pl.BlockSpec(memory_space=pl.ANY)
    shape = jax.ShapeDtypeStruct
    large = [(192, 768)] * 4 + [(192, 3072), (768, 768)]
    small = [(192,)] * 3 + [(768,)] + [(192,)] * 5
    return pl.pallas_call(
        finish_kernel,
        name="finish_kernel",
        out_shape=[shape((128, 2, 768), BF16), shape((128, 2, 768), F32)]
        + [shape(size, F32) for size in large + small],
        in_specs=[anywhere] * 8,
        out_specs=[anywhere] * 8 + [vmem] * 9,
        scratch_shapes=[
            pltpu.VMEM((2, 128, 768), F32),
            pltpu.VMEM((2, 128, 768), BF16),
            pltpu.VMEM((768, 768), BF16),
            pltpu.VMEM((192, 3072), BF16),
            pltpu.VMEM((192, 768), BF16),
            pltpu.VMEM((4, 3, 192, 256), BF16),
            pltpu.VMEM((16, 256), F32),
            pltpu.VMEM((2, 8, 256), F32),
            pltpu.VMEM((128, 2, 768), F32),
            pltpu.VMEM((128, 2, 768), F32),
            pltpu.VMEM((128, 2, 768), BF16),
            pltpu.VMEM((768, 768), F32),
            pltpu.VMEM((192, 3072), F32),
            pltpu.VMEM((192, 768), F32),
            pltpu.VMEM((192, 768), F32),
            pltpu.VMEM((192, 768), F32),
            pltpu.VMEM((192, 768), F32),
            pltpu.SemaphoreType.DMA((8,)),
            pltpu.SemaphoreType.DMA((10,)),
        ],
        compiler_params=pltpu.CompilerParams(vmem_limit_bytes=67043328),
    )(*operands)


def fast_body(
    tokens,
    segment_ids,
    w_query,
    w_key,
    w_value,
    w_output,
    w_inner,
    w_outer,
    b_query,
    b_value,
    b_output,
    b_inner,
    b_outer,
    gain_first,
    shift_first,
    gain_second,
    shift_second,
    cotangent,
):
    layer, grad, fu, fi, fo, fg, vec_sum, bias_sum = run_layer(
        jnp.transpose(tokens, (1, 0, 2)),
        jnp.transpose(cotangent, (1, 0, 2)),
        segment_ids,
        b_query,
        b_value,
        b_output,
        b_outer,
        gain_first,
        shift_first,
        gain_second,
        shift_second,
        b_inner,
        w_query,
        w_key,
        w_value,
        w_output,
        w_inner,
        w_outer,
    )

    return tuple(run_finish(grad, layer, fu, fi, fo, fg, vec_sum, bias_sum))


def solution(mesh):
    in_specs = (
        P("ctx", "seq", None),
        P("seq", "ctx"),
        P("seq", None),
        P("seq", None),
        P("seq", None),
        P("seq", None),
        P("seq", None),
        P("seq", None),
        P("seq"),
        P("seq"),
        P("seq"),
        P("seq"),
        P("seq"),
        P("seq"),
        P("seq"),
        P("seq"),
        P("seq"),
        P("ctx", "seq", None),
    )
    out_specs = (
        P("ctx", "seq", None),
        P("ctx", "seq", None),
        P("seq", None),
        P("seq", None),
        P("seq", None),
        P("seq", None),
        P("seq", None),
        P("seq", None),
        P("seq"),
        P("seq"),
        P("seq"),
        P("seq"),
        P("seq"),
        P("seq"),
        P("seq"),
        P("seq"),
        P("seq"),
    )
    small = mesh.shape["seq"] == 4 and mesh.shape["ctx"] == 8
    step = fast_body if small else body
    return jax.shard_map(step, mesh=mesh, in_specs=in_specs, out_specs=out_specs, check_vma=False)
```

```python
import functools
import math
import types

import jax
import jax.numpy as jnp
from jax import lax
from jax.experimental import pallas as pl
from jax.experimental.pallas import tpu as pltpu
from jax.sharding import PartitionSpec as P

H = 12
DH = 64


EPSILON = 1e-12
SCORE_SCALE = 0.125


def matmul(first_op, second_op):
    return jnp.dot(first_op, second_op, preferred_element_type=jnp.float32)


def matmul_tn(first_op, second_op):
    return lax.dot_general(
        first_op, second_op, (((0,), (0,)), ((), ())), preferred_element_type=jnp.float32
    )


def matmul_nt(first_op, second_op):
    return lax.dot_general(
        first_op, second_op, (((1,), (1,)), ((), ())), preferred_element_type=jnp.float32
    )


def norm_forward(values, gain_vec, shift_vec):
    center = values - jnp.mean(values, axis=-1, keepdims=True)
    inverse = lax.rsqrt(jnp.mean(center * center, axis=-1, keepdims=True) + EPSILON)
    normed = center * inverse
    return (normed * gain_vec + shift_vec, normed, inverse)


def norm_backward(upstream, normed, inverse, gain_vec):
    scaled = upstream * gain_vec
    back_grad = inverse * (
        scaled
        - jnp.mean(scaled, axis=-1, keepdims=True)
        - normed * jnp.mean(scaled * normed, axis=-1, keepdims=True)
    )
    return (back_grad, jnp.sum(upstream * normed, axis=0), jnp.sum(upstream, axis=0))


def gelu_parts(values):
    cumulative = 0.5 * (1.0 + lax.erf(values * 0.7071067811865476))
    return (
        values * cumulative,
        cumulative + values * jnp.exp(-0.5 * values * values) * 0.3989422804014327,
    )


def block_scores(query_heads, key_heads, seg_query, seg_key):
    raw_scores = (
        jnp.einsum("ishd,jshd->shij", query_heads, key_heads, preferred_element_type=jnp.float32)
        * SCORE_SCALE
    )
    allowed = (jnp.transpose(seg_query)[:, :, None] == jnp.transpose(seg_key)[:, None, :])[:, None]
    return jnp.where(allowed, jnp.exp(raw_scores), 0.0)


def attend_keys(query_heads, seg_query, carry_in, piece_rows):
    key_piece, value_piece, seg_piece = piece_rows
    row_count, seq_count, feature_count = key_piece.shape
    heads, head_size = (query_heads.shape[2], query_heads.shape[3])
    step_rows = math.gcd(row_count, 1024)
    block_count = row_count // step_rows
    key_blocks = key_piece.reshape(block_count, step_rows, seq_count, heads, head_size)
    value_blocks = value_piece.reshape(block_count, step_rows, seq_count, heads, head_size)
    seg_blocks = seg_piece.reshape(block_count, step_rows, seq_count)

    def attend_visit_block(running, element):
        key_block, value_block, seg_block = element
        unnorm = block_scores(query_heads, key_block, seg_query, seg_block)
        totals = running[0] + jnp.sum(unnorm, axis=-1)
        mixture = running[1] + jnp.einsum(
            "shij,jshd->ishd",
            unnorm.astype(jnp.bfloat16),
            value_block,
            preferred_element_type=jnp.float32,
        )
        return ((totals, mixture), None)

    result, unused = lax.scan(attend_visit_block, carry_in, (key_blocks, value_blocks, seg_blocks))
    return result


def key_side(query_heads, d_mixture, correction, seg_query, key_all, value_all, seg_all):
    row_count, seq_count, feature_count = key_all.shape
    heads, head_size = (query_heads.shape[2], query_heads.shape[3])
    step_rows = math.gcd(row_count, 1024)
    block_count = row_count // step_rows
    corr_cols = jnp.transpose(correction, (1, 2, 0))[..., None]
    key_blocks = key_all.reshape(block_count, step_rows, seq_count, heads, head_size)
    value_blocks = value_all.reshape(block_count, step_rows, seq_count, heads, head_size)
    seg_blocks = seg_all.reshape(block_count, step_rows, seq_count)

    def key_visit_block(dq_acc, element):
        key_block, value_block, seg_block = element
        unnorm = block_scores(query_heads, key_block, seg_query, seg_block)
        d_prob = jnp.einsum(
            "ishd,jshd->shij", d_mixture, value_block, preferred_element_type=jnp.float32
        )
        d_score = (unnorm * (d_prob - corr_cols)).astype(jnp.bfloat16)
        dq_acc = dq_acc + jnp.einsum(
            "shij,jshd->ishd", d_score, key_block, preferred_element_type=jnp.float32
        )
        d_key = (
            jnp.einsum("shij,ishd->jshd", d_score, query_heads, preferred_element_type=jnp.float32)
            * SCORE_SCALE
        )
        d_value = jnp.einsum(
            "shij,ishd->jshd",
            unnorm.astype(jnp.bfloat16),
            d_mixture,
            preferred_element_type=jnp.float32,
        )
        stacked = jnp.concatenate(
            [
                d_key.reshape(step_rows, seq_count, feature_count),
                d_value.reshape(step_rows, seq_count, feature_count),
            ],
            axis=-1,
        )
        return (dq_acc, stacked)

    dq_sum, stacked_all = lax.scan(
        key_visit_block,
        jnp.zeros(query_heads.shape, jnp.float32),
        (key_blocks, value_blocks, seg_blocks),
    )
    return (dq_sum, stacked_all.reshape(row_count, seq_count, 2 * feature_count))


def body(
    tokens,
    segment_ids,
    w_query,
    w_key,
    w_value,
    w_output,
    w_inner,
    w_outer,
    b_query,
    b_value,
    b_output,
    b_inner,
    b_outer,
    gain_first,
    shift_first,
    gain_second,
    shift_second,
    cotangent,
):
    tok_rows, seq_count, feature_count = tokens.shape
    rows_total = tok_rows * seq_count
    gathered = (
        lax.all_gather(w_query, "seq", axis=0, tiled=True),
        lax.all_gather(w_key, "seq", axis=0, tiled=True),
        lax.all_gather(w_value, "seq", axis=0, tiled=True),
        lax.all_gather(w_output, "seq", axis=0, tiled=True),
        lax.all_gather(w_inner, "seq", axis=0, tiled=True),
        lax.all_gather(w_outer, "seq", axis=0, tiled=True),
        lax.all_gather(b_query, "seq", axis=0, tiled=True),
        lax.all_gather(b_value, "seq", axis=0, tiled=True),
        lax.all_gather(b_output, "seq", axis=0, tiled=True),
        lax.all_gather(b_inner, "seq", axis=0, tiled=True),
        lax.all_gather(b_outer, "seq", axis=0, tiled=True),
        lax.all_gather(gain_first, "seq", axis=0, tiled=True),
        lax.all_gather(shift_first, "seq", axis=0, tiled=True),
        lax.all_gather(gain_second, "seq", axis=0, tiled=True),
        lax.all_gather(shift_second, "seq", axis=0, tiled=True),
    )
    query_weight, key_weight, value_weight, output_weight, inner_weight, outer_weight = gathered[:6]
    (
        query_bias,
        value_bias,
        output_bias,
        inner_bias,
        outer_bias,
        gain_one,
        shift_one,
        gain_two,
        shift_two,
    ) = [vector.astype(jnp.float32) for vector in gathered[6:]]
    flat_rows = tokens.reshape(rows_total, feature_count)
    flat_float = flat_rows.astype(jnp.float32)
    seg_local = jnp.transpose(segment_ids)
    queries = (matmul(flat_rows, query_weight) + query_bias).astype(jnp.bfloat16)
    key_rows = matmul(flat_rows, key_weight).astype(jnp.bfloat16)
    value_rows = (matmul(flat_rows, value_weight) + value_bias).astype(jnp.bfloat16)
    query_heads = queries.reshape(tok_rows, seq_count, H, DH)
    key_block_rows = key_rows.reshape(tok_rows, seq_count, feature_count)
    value_block_rows = value_rows.reshape(tok_rows, seq_count, feature_count)
    initial = (
        jnp.zeros((seq_count, H, tok_rows), jnp.float32),
        jnp.zeros((tok_rows, seq_count, H, DH), jnp.float32),
    )
    totals, mixture = attend_keys(
        query_heads,
        seg_local,
        initial,
        (
            lax.all_gather(key_block_rows, "ctx", axis=0, tiled=True),
            lax.all_gather(value_block_rows, "ctx", axis=0, tiled=True),
            lax.all_gather(seg_local, "ctx", axis=0, tiled=True),
        ),
    )
    denominator = jnp.transpose(totals, (2, 0, 1))[..., None]
    attended = mixture / denominator
    context = attended.astype(jnp.bfloat16).reshape(rows_total, feature_count)
    first_in = matmul(context, output_weight) + output_bias + flat_float
    hidden, normed_one, inverse_one = norm_forward(first_in, gain_one, shift_one)
    hidden_low = hidden.astype(jnp.bfloat16)
    inner_pre = matmul(hidden_low, inner_weight) + inner_bias
    activated, gelu_slope = gelu_parts(inner_pre)
    act_low = activated.astype(jnp.bfloat16)
    second_in = matmul(act_low, outer_weight) + outer_bias + hidden
    result, normed_two, inverse_two = norm_forward(second_in, gain_two, shift_two)
    layer_out = result.astype(jnp.bfloat16).reshape(tok_rows, seq_count, feature_count)
    upstream = cotangent.astype(jnp.float32).reshape(rows_total, feature_count)
    d_second, dgain_second, dshift_second = norm_backward(
        upstream, normed_two, inverse_two, gain_two
    )
    d_outer = d_second.astype(jnp.bfloat16)
    dbias_outer = jnp.sum(d_outer.astype(jnp.float32), axis=0)
    dweight_outer = matmul_tn(act_low, d_outer)
    d_inner = (matmul_nt(d_outer, outer_weight) * gelu_slope).astype(jnp.bfloat16)
    dbias_inner = jnp.sum(d_inner.astype(jnp.float32), axis=0)
    dweight_inner = matmul_tn(hidden_low, d_inner)
    d_hidden = matmul_nt(d_inner, inner_weight) + d_second
    d_first, dgain_first, dshift_first = norm_backward(d_hidden, normed_one, inverse_one, gain_one)
    d_branch = d_first.astype(jnp.bfloat16)
    dbias_output = jnp.sum(d_branch.astype(jnp.float32), axis=0)
    dweight_output = matmul_tn(context, d_branch)
    d_context = (
        matmul_nt(d_branch, output_weight).astype(jnp.bfloat16).reshape(tok_rows, seq_count, H, DH)
    )
    d_float = d_context.astype(jnp.float32)
    d_mixture = (d_float / denominator).astype(jnp.bfloat16)
    correction = jnp.sum(d_float * attended, axis=-1) / denominator[..., 0]
    key_all, value_all, seg_all = (
        lax.all_gather(key_block_rows, "ctx", axis=0, tiled=True),
        lax.all_gather(value_block_rows, "ctx", axis=0, tiled=True),
        lax.all_gather(seg_local, "ctx", axis=0, tiled=True),
    )
    dq_sum, term_rows = key_side(
        query_heads, d_mixture, correction, seg_local, key_all, value_all, seg_all
    )
    summed = lax.psum_scatter(term_rows, "ctx", scatter_dimension=0, tiled=True)
    d_query = (dq_sum * SCORE_SCALE).astype(jnp.bfloat16)
    d_key = summed[..., :feature_count].astype(jnp.bfloat16)
    d_value = summed[..., feature_count:].astype(jnp.bfloat16)
    dq_flat = d_query.reshape(rows_total, feature_count)
    dk_flat = d_key.reshape(rows_total, feature_count)
    dv_flat = d_value.reshape(rows_total, feature_count)
    dweight_query = matmul_tn(flat_rows, dq_flat)
    dweight_key = matmul_tn(flat_rows, dk_flat)
    dweight_value = matmul_tn(flat_rows, dv_flat)
    dbias_query = jnp.sum(dq_flat.astype(jnp.float32), axis=0)
    dbias_value = jnp.sum(dv_flat.astype(jnp.float32), axis=0)
    grad_tokens = (
        matmul_nt(dq_flat, query_weight)
        + matmul_nt(dk_flat, key_weight)
        + matmul_nt(dv_flat, value_weight)
        + d_first
    )
    shards = (
        lax.psum_scatter(
            dweight_query.astype(jnp.bfloat16), "seq", scatter_dimension=0, tiled=True
        ).astype(jnp.float32),
        lax.psum_scatter(
            dweight_key.astype(jnp.bfloat16), "seq", scatter_dimension=0, tiled=True
        ).astype(jnp.float32),
        lax.psum_scatter(
            dweight_value.astype(jnp.bfloat16), "seq", scatter_dimension=0, tiled=True
        ).astype(jnp.float32),
        lax.psum_scatter(
            dweight_output.astype(jnp.bfloat16), "seq", scatter_dimension=0, tiled=True
        ).astype(jnp.float32),
        lax.psum_scatter(
            dweight_inner.astype(jnp.bfloat16), "seq", scatter_dimension=0, tiled=True
        ).astype(jnp.float32),
        lax.psum_scatter(
            dweight_outer.astype(jnp.bfloat16), "seq", scatter_dimension=0, tiled=True
        ).astype(jnp.float32),
        lax.psum_scatter(
            dbias_query.astype(jnp.bfloat16), "seq", scatter_dimension=0, tiled=True
        ).astype(jnp.float32),
        lax.psum_scatter(
            dbias_value.astype(jnp.bfloat16), "seq", scatter_dimension=0, tiled=True
        ).astype(jnp.float32),
        lax.psum_scatter(
            dbias_output.astype(jnp.bfloat16), "seq", scatter_dimension=0, tiled=True
        ).astype(jnp.float32),
        lax.psum_scatter(
            dbias_inner.astype(jnp.bfloat16), "seq", scatter_dimension=0, tiled=True
        ).astype(jnp.float32),
        lax.psum_scatter(
            dbias_outer.astype(jnp.bfloat16), "seq", scatter_dimension=0, tiled=True
        ).astype(jnp.float32),
        lax.psum_scatter(
            dgain_first.astype(jnp.bfloat16), "seq", scatter_dimension=0, tiled=True
        ).astype(jnp.float32),
        lax.psum_scatter(
            dshift_first.astype(jnp.bfloat16), "seq", scatter_dimension=0, tiled=True
        ).astype(jnp.float32),
        lax.psum_scatter(
            dgain_second.astype(jnp.bfloat16), "seq", scatter_dimension=0, tiled=True
        ).astype(jnp.float32),
        lax.psum_scatter(
            dshift_second.astype(jnp.bfloat16), "seq", scatter_dimension=0, tiled=True
        ).astype(jnp.float32),
    )
    finals = lax.psum(
        (
            shards[0],
            shards[1],
            shards[2],
            shards[3],
            shards[4],
            shards[5],
            shards[6],
            shards[7],
            shards[8],
            shards[9],
            shards[10],
            shards[11],
            shards[12],
            shards[13],
            shards[14],
        ),
        "ctx",
    )
    return (
        layer_out,
        grad_tokens.reshape(tok_rows, seq_count, feature_count),
        finals[0],
        finals[1],
        finals[2],
        finals[3],
        finals[4],
        finals[5],
        finals[6],
        finals[7],
        finals[8],
        finals[9],
        finals[10],
        finals[11],
        finals[12],
        finals[13],
        finals[14],
    )


MESH = pl.DeviceIdType.MESH
BIG = 1e30
F32, BF16 = jnp.float32, jnp.bfloat16


def remote(src, dst, send_sem, recv_sem, seq, ctx):
    return pltpu.make_async_remote_copy(
        src_ref=src,
        dst_ref=dst,
        send_sem=send_sem,
        recv_sem=recv_sem,
        device_id=(seq, ctx),
        device_id_type=MESH,
    )


def greet(seq, ctx):
    barrier = pltpu.get_barrier_semaphore()
    for hop in range(1, 8):
        pl.semaphore_signal(
            barrier, inc=1, device_id=(seq, lax.rem(ctx + hop, 8)), device_id_type=MESH
        )
    for hop in range(1, 4):
        pl.semaphore_signal(
            barrier, inc=1, device_id=(lax.rem(seq + hop, 4), ctx), device_id_type=MESH
        )
    pl.semaphore_wait(barrier, 10)


def flip(index, bit):
    low = lax.rem(index // bit, 2)
    return index + bit - 2 * bit * low


def head_window(group):
    start = group * 192
    inside = lax.rem(group, 2) * 64
    return pl.multiple_of(start - inside, 128), pl.multiple_of(inside, 64)


def span(start, size, unit=16):
    return pl.ds(pl.multiple_of(start, unit), size)


VECTORS = list(
    dict(
        b_query=0,
        b_value=0,
        b_output=0,
        b_outer=0,
        gain_one=0,
        shift_one=0,
        gain_two=0,
        shift_two=0,
    )
)
INPUTS = [
    *dict(x=0, cot=0, seg=0),
    *VECTORS,
    *dict(b_inner=0, wq=0, wk=0, wv=0, wo=0, wi=0, wu=0),
]
OUTPUTS = list(dict(layer=0, grad=0, fu=0, fi=0, fo=0, fg=0, vec_sum=0, bias_sum=0))
FIRST = "xxyyxzxzx"
OVER_Y = (1, 0, 1, 0, 1, 0, 1)

SCRATCH = dict(
    x_rows=((2, 128, 768), BF16),
    cot_rows=((2, 128, 768), BF16),
    layer_rows=((2, 128, 768), BF16),
    grad_rows=((2, 128, 768), F32),
    fg_all=((4, 3, 192, 256), BF16),
    seg_own=((2, 8, 128), jnp.int32),
    seg_all=((8, 8, 128), jnp.int32),
    pack_own=((16, 768), BF16),
    pack_all=((4, 16, 768), BF16),
    rows=((8, 768), F32),
    wo_full=((4, 192, 768), BF16),
    wi_full=((4, 192, 3072), BF16),
    wu_full=((4, 768, 768), BF16),
    xs=((8, 128, 768), BF16),
    wg=((3, 4, 192, 256), BF16),
    qa=((3, 128, 1024), BF16),
    ka=((3, 128, 1024), BF16),
    vt=((3, 64, 1024), BF16),
    ot=((3, 64, 1024), F32),
    sums=((3, 1, 1024), F32),
    key_rows=((1024, 128), BF16),
    o_send=((192, 1024), BF16),
    ctx_t=((768, 256), BF16),
    normed=((256, 768), F32),
    inverse=((256, 1), F32),
    low=((256, 768), BF16),
    low_t=((768, 256), BF16),
    act_t=((4, 768, 256), BF16),
    slope=((4, 256, 768), F32),
    work=((256, 768), F32),
    d_rows=((256, 768), BF16),
    v_rows=((16, 768), F32),
    gu=((4, 768, 768), BF16),
    gi=((4, 192, 3072), BF16),
    go=((4, 192, 768), BF16),
    core_u=((2, 768, 768), BF16),
    core_i=((2, 192, 3072), BF16),
    core_o=((2, 192, 768), BF16),
    xr_u=((768, 768), BF16),
    xr_i=((192, 3072), BF16),
    xr_o=((192, 768), BF16),
    rcv_u=((768, 768), BF16),
    rcv_i=((192, 3072), BF16),
    rcv_o=((192, 768), BF16),
    fin_u=((768, 768), BF16),
    fin_i=((192, 3072), BF16),
    fin_o=((192, 768), BF16),
    tot_u=((4, 96, 384), F32),
    tot_i=((4, 96, 384), F32),
    tot_o=((96, 384), F32),
    do_send=((768, 256), BF16),
    do_all=((192, 1024), BF16),
    du=((64, 1024), BF16),
    c_row=((1, 1024), F32),
    value_rows=((1024, 64), BF16),
    dk_acc=((64, 1024), F32),
    dv_acc=((64, 1024), F32),
    d_all=((3, 256, 1024), BF16),
    g_all=((3, 4, 192, 256), BF16),
    g_core=((3, 2, 192, 256), BF16),
    g_xs=((3, 192, 256), BF16),
    g_xr=((3, 192, 256), BF16),
    g_half=((3, 192, 256), BF16),
    g_mir=((3, 96, 256), BF16),
    dx_y=((4, 768, 128), BF16),
    dx_l=((2, 768, 128), BF16),
    dx_h=((768, 128), BF16),
    two_y=((max(1, FIRST.count("y")), 192, 384), BF16),
    two_z=((max(1, FIRST.count("z")), 96, 768), BF16),
    v_own=((4, 16, 256), F32),
    v_recv=((4, 16, 256), F32),
    v_all=((8, 16, 256), F32),
    b_send=((2, 8, 256), F32),
    b_recv=((8, 2, 8, 256), F32),
)
SEMAPHORES = dict(
    loc=(36,),
    w_ss=(7, 5),
    w_rs=(7, 5),
    x_ss=(12,),
    x_rs=(12,),
    s_ss=(8,),
    s_rs=(8,),
    p_ss=(4,),
    p_rs=(4,),
    g_ss=(3, 3),
    g_rs=(3, 3),
    o_ss=(3, 8),
    o_rs=(3, 8),
    r_ss=(9, 10),
    r_rs=(9, 10),
    do_ss=(3, 8),
    do_rs=(3, 8),
    dx_ss=(7,),
    dx_rs=(7,),
    v_ss=(2, 8),
    v_rs=(2, 8),
    b_ss=(8,),
    b_rs=(8,),
    h_ss=(7, 3),
    h_rs=(7, 3),
)


def layer_kernel(*refs):
    r = types.SimpleNamespace(
        **dict(zip(INPUTS + OUTPUTS + list(SCRATCH) + list(SEMAPHORES), refs))
    )
    seq, ctx = lax.axis_index("seq"), lax.axis_index("ctx")
    plane = seq // 2
    mate, across = flip(seq, 1), flip(seq, 2)
    across_mate = flip(mate, 2)
    beside, paired, mirror = flip(ctx, 1), flip(ctx, 2), flip(ctx, 4)
    bit_y, bit_l, bit_h = lax.rem(ctx, 2), lax.rem(ctx // 2, 2), ctx // 4
    side, group = ctx // 4, lax.rem(ctx, 4)
    window, inside = head_window(group)
    own_lanes = span(ctx * 128, 128, 128)
    sent = []

    def wi_cut(k, where):
        which = where if k == 1 else 1 - where
        return span(which * 1536, 1536, 128)

    def w_views(k, where):
        if k == 0:
            return r.wo, lambda owner: r.wo_full.at[owner], 96
        if k in (1, 2):
            cols = wi_cut(k, where)
            return r.wi.at[:, cols], lambda owner: r.wi_full.at[owner, :, cols], 96
        part = slice(192 * (k - 3), 192 * (k - 2))
        return r.wu.at[part], lambda owner: r.wu_full.at[owner, part], 96

    beside_of = [
        (beside, bit_y) if over_y else (paired, bit_l) for over_y in OVER_Y
    ]

    def half(view, rows, which):
        return view.at[span(which * rows, rows, 32)]

    def w_copy(k, leg):
        sems = r.w_ss.at[k, leg], r.w_rs.at[k, leg]
        shard, full, rows = w_views(k, 1 - plane if leg == 1 else plane)
        partner, bit = beside_of[k]
        if leg == 0:
            return remote(shard, full(seq), *sems, mate, ctx)
        if leg == 1:
            return remote(
                half(shard, rows, bit), half(full(seq), rows, bit), *sems, across, ctx
            )
        which = bit if leg in (2, 3) else 1 - bit
        came = half(full(across), rows, which)
        return remote(came, came, *sems, *((seq, partner) if leg == 2 else (mate, ctx)))

    def w_wait(k, leg):
        shard, full, rows = w_views(k, plane)
        bit = beside_of[k][1]
        spots = (
            lambda: full(mate),
            lambda: half(full(across), rows, bit),
            lambda: half(full(across), rows, 1 - bit),
            lambda: half(full(across_mate), rows, bit),
            lambda: half(full(across_mate), rows, 1 - bit),
        )
        spot = spots[leg]()
        remote(spot, spot, r.w_ss.at[k, leg], r.w_rs.at[k, leg], mate, ctx).wait_recv()

    def pass_across(k):
        w_wait(k, 1)
        w_copy(k, 2).start()
        w_copy(k, 3).start()

    def pass_beside(k):
        w_wait(k, 2)
        w_copy(k, 4).start()

    def w_done(k):
        for leg in (0, 3, 4):
            w_wait(k, leg)

    group_refs = (r.wq, r.wk, r.wv)
    g_local, w_local = [], []
    for which in range(3):
        g_local.append(
            pltpu.make_async_copy(
                group_refs[which].at[:, pl.ds(window, 256)],
                r.wg.at[which, seq],
                r.loc.at[which],
            )
        )
    for n, (ref, full) in enumerate(
        ((r.wo, r.wo_full), (r.wi, r.wi_full), (r.wu, r.wu_full))
    ):
        w_local.append(pltpu.make_async_copy(ref, full.at[seq], r.loc.at[3 + n]))
    own_block = pltpu.make_async_copy(r.x.at[side], r.xs.at[ctx], r.loc.at[6])
    for which in range(2):
        r.seg_own[which] = jnp.broadcast_to(r.seg[which : which + 1], (8, 128))
    r.pack_own[...] = jnp.zeros((16, 768), BF16)
    for n, name in enumerate(VECTORS):
        r.pack_own[n : n + 1, 0:192] = getattr(r, name)[...].reshape(1, 192)
    r.pack_own[8:9] = r.b_inner[...].reshape(1, 768)
    x_local = pltpu.make_async_copy(r.x, r.x_rows, r.loc.at[26])
    cot_local = pltpu.make_async_copy(r.cot, r.cot_rows, r.loc.at[27])
    own_seg = pltpu.make_async_copy(r.seg_own.at[side], r.seg_all.at[ctx], r.loc.at[7])
    own_pack = pltpu.make_async_copy(r.pack_own, r.pack_all.at[seq], r.loc.at[8])
    for copy in g_local + [own_block, own_seg, own_pack, x_local, cot_local] + w_local:
        copy.start()
    r.v_rows[...] = jnp.zeros((16, 768), F32)
    for which in range(3):
        r.d_all[which] = jnp.zeros((256, 1024), BF16)

    greet(seq, ctx)

    def send(*args):
        copy = remote(*args)
        copy.start()
        sent.append(copy)

    def landed(spot, send_sem, recv_sem):
        remote(spot, spot, send_sem, recv_sem, seq, beside).wait_recv()

    for hop in range(1, 8):
        other = lax.rem(ctx + hop, 8)
        send(
            r.seg_own.at[other // 4],
            r.seg_all.at[ctx],
            r.s_ss.at[hop],
            r.s_rs.at[hop],
            seq,
            other,
        )
    for hop in range(1, 4):
        other = lax.rem(seq + hop, 4)
        send(r.pack_own, r.pack_all.at[seq], r.p_ss.at[hop], r.p_rs.at[hop], other, ctx)
    for n in range(2):
        part = slice(64 * n, 64 * n + 64)
        send(
            r.x.at[1 - side, part],
            r.xs.at[ctx, part],
            r.x_ss.at[n],
            r.x_rs.at[n],
            seq,
            mirror,
        )
    for n, other in enumerate((beside, paired)):
        send(
            r.x.at[side], r.xs.at[ctx], r.x_ss.at[2 + n], r.x_rs.at[2 + n], seq, other
        )
    for which in range(3):
        for n, other in enumerate((mate, across)):
            send(
                group_refs[which].at[:, pl.ds(window, 256)],
                r.wg.at[which, seq],
                r.g_ss.at[which, n],
                r.g_rs.at[which, n],
                other,
                ctx,
            )
    for k in range(7):
        w_copy(k, 0).start()
        w_copy(k, 1).start()

    t = types.SimpleNamespace()
    to_hbm_all = []
    early = []

    def to_hbm(source, target):
        copy = pltpu.make_async_copy(source, target, r.loc.at[28 + len(to_hbm_all)])
        copy.start()
        to_hbm_all.append(copy)

    def task(run):
        setattr(t, run.__name__, run)

    t.pa = [functools.partial(pass_across, k) for k in range(7)]
    t.pb = [functools.partial(pass_beside, k) for k in range(7)]

    @task
    def grp():
        for which in range(3):
            spot = r.wg.at[which, across]
            landed(spot, r.g_ss.at[which, 1], r.g_rs.at[which, 1])
            send(spot, spot, r.g_ss.at[which, 2], r.g_rs.at[which, 2], mate, ctx)

    diagonal = flip(beside, 2)

    def pass_on(source, half, arrived_by, leg, other):
        spot = r.xs.at[source, 64 * half : 64 * half + 64]
        if arrived_by is not None:
            landed(spot, r.x_ss.at[arrived_by], r.x_rs.at[arrived_by])
        send(spot, spot, r.x_ss.at[leg], r.x_rs.at[leg], seq, other)

    @task
    def nf():
        for n, other in enumerate((beside, paired)):
            landed(r.xs.at[other], r.x_ss.at[2 + n], r.x_rs.at[2 + n])
        pass_on(beside, 0, None, 4, paired)
        pass_on(paired, 1, None, 5, beside)

    def far_half(half):
        pass_on(mirror, half, half, 6 + 2 * half, beside)
        pass_on(mirror, half, None, 7 + 2 * half, paired)

    t.far = [functools.partial(far_half, half) for half in range(2)]
    t.ff = [
        functools.partial(pass_on, flip(beside, 4), 0, 6, 10, paired),
        functools.partial(pass_on, flip(paired, 4), 1, 9, 11, beside),
    ]

    @task
    def small():
        for which in range(3):
            g_local[which].wait()
            for n, owner in ((0, mate), (2, across_mate)):
                landed(
                    r.wg.at[which, owner], r.g_ss.at[which, n], r.g_rs.at[which, n]
                )
        own_pack.wait()
        for hop in range(1, 4):
            landed(
                r.pack_all.at[lax.rem(seq + 4 - hop, 4)], r.p_ss.at[hop], r.p_rs.at[hop]
            )
        own_seg.wait()
        for hop in range(1, 8):
            landed(
                r.seg_all.at[lax.rem(ctx + 8 - hop, 8)], r.s_ss.at[hop], r.s_rs.at[hop]
            )
        lane = lax.broadcasted_iota(jnp.int32, (256, 768), 1)
        at = lax.broadcasted_iota(jnp.int32, (256, 768), 0)
        rows = jnp.zeros((8, 768), F32)
        for owner in range(4):
            chosen = ((lane == at + 192 * owner) & (at < 192)).astype(BF16)
            rows += matmul(r.pack_all[owner, 0:8, 0:256], chosen)
        r.rows[...] = rows

    @task
    def qkv():
        own_block.wait()
        for source, half, leg in (
            (diagonal, 0, 4),
            (diagonal, 1, 5),
            (flip(paired, 4), 0, 7),
            (flip(beside, 4), 1, 8),
            (flip(diagonal, 4), 0, 10),
            (flip(diagonal, 4), 1, 11),
        ):
            spot = r.xs.at[source, 64 * half : 64 * half + 64]
            landed(spot, r.x_ss.at[leg], r.x_rs.at[leg])
        tokens = r.xs[...].reshape(1024, 768)
        own_rows = r.pack_all[group]
        qkv = []
        for which in range(3):
            weight = r.wg[which].reshape(768, 256)
            product = matmul_nt(weight.T, tokens)
            if which != 1:
                bias = own_rows[which // 2 : which // 2 + 1, 0:256].astype(F32)
                column = jnp.broadcast_to(bias, (128, 256)).T
                shifted = jnp.where(inside == 0, column, pltpu.roll(column, 64, 0))
                product = product + jnp.concatenate([shifted] * 8, axis=1)
            part = product.astype(BF16)
            if which == 0:
                part = part * jnp.bfloat16(SCORE_SCALE)
            qkv.append(part)
        number = jnp.concatenate(
            [r.seg_all[block, 0:1] for block in range(8)], axis=1
        )
        hot = lax.broadcasted_iota(jnp.int32, (16, 1024), 0) == number
        query_marks = jnp.where(hot, 1.0, 0.0).astype(BF16)
        key_marks = jnp.where(hot, 0.0, -BIG).astype(BF16)
        blank = jnp.zeros((48, 1024), BF16)
        for head in range(3):
            parts = [
                jnp.where(
                    inside != 0,
                    part[64 * head + 64 : 64 * head + 128],
                    part[64 * head : 64 * head + 64],
                )
                for part in qkv
            ]
            r.qa[head] = jnp.concatenate([parts[0], query_marks, blank], axis=0)
            r.ka[head] = jnp.concatenate([parts[1], key_marks, blank], axis=0)
            r.vt[head] = parts[2]

    my_rows = span(group * 192, 192, 64)
    my_lanes = span(side * 128, 128, 128)
    own_o = pltpu.make_async_copy(
        r.o_send.at[:, own_lanes], r.ctx_t.at[my_rows, my_lanes], r.loc.at[9]
    )

    def attend_head(head):
        r.key_rows[...] = r.ka[head].T

        def attend(block, unused):
            lanes = span(block * 256, 256, 256)
            scores = matmul(r.key_rows[...], r.qa[head, :, lanes])
            unnorm = jnp.exp(scores)
            total = jnp.sum(unnorm, axis=0, keepdims=True)
            attended = matmul(r.vt[head], unnorm.astype(BF16)) / total
            r.ot[head, :, lanes] = attended
            r.sums[head, :, lanes] = total
            r.o_send[64 * head : 64 * head + 64, lanes] = attended.astype(BF16)
            return unused

        lax.fori_loop(0, 4, attend, 0)
        if head == 2:
            own_o.start()
        part = slice(64 * head, 64 * head + 64)
        for hop in range(1, 8):
            other = lax.rem(ctx + hop, 8)
            send(
                r.o_send.at[part, span(other * 128, 128, 128)],
                r.ctx_t.at[span(group * 192 + 64 * head, 64, 64), my_lanes],
                r.o_ss.at[head, hop],
                r.o_rs.at[head, hop],
                seq,
                other,
            )

    t.at = [functools.partial(attend_head, head) for head in range(3)]

    def row_vec(n):
        return r.rows[n : n + 1]

    @task
    def fn():
        own_o.wait()
        for head in range(3):
            for hop in range(1, 8):
                other = lax.rem(ctx + 8 - hop, 8)
                spot = r.ctx_t.at[
                    span(lax.rem(other, 4) * 192 + 64 * head, 64, 64),
                    span((other // 4) * 128, 128, 128),
                ]
                landed(spot, r.o_ss.at[head, hop], r.o_rs.at[head, hop])
        w_local[0].wait()
        x_local.wait()
        w_done(0)

        def first_norm(which, unused):
            at, lanes = span(which * 128, 128, 128), span(which * 128, 128, 128)
            value = (
                matmul(r.ctx_t[:, lanes].T, r.wo_full[...].reshape(768, 768))
                + row_vec(2)
                + r.x_rows[which].astype(F32)
            )
            hidden, normed, inverse = norm_forward(value, row_vec(4), row_vec(5))
            r.normed[at] = normed
            r.inverse[at] = inverse
            part = hidden.astype(BF16)
            r.low[at] = part
            r.low_t[:, lanes] = part.T
            r.work[at] = hidden + row_vec(3)
            return unused

        lax.fori_loop(0, 2, first_norm, 0)

    def inner_weight(n):
        return r.wi_full[:, :, span(n * 768, 768, 128)].reshape(768, 768)

    def feed(where):
        def visit(step, unused):
            n, which = where * 2 + step // 2, lax.rem(step, 2)
            at = span(which * 128, 128, 128)
            value = matmul(r.low[at], inner_weight(n)) + r.pack_all[n, 8:9].astype(F32)
            act, slope = gelu_parts(value)
            part = act.astype(BF16)
            r.slope[n, at] = slope
            r.act_t[n, :, at] = part.T
            r.work[at] += matmul(part, r.wu_full[n])
            return unused

        lax.fori_loop(0, 4, visit, 0)

    @task
    def fe0():
        w_local[1].wait()
        w_local[2].wait()
        w_done(1)
        for k in range(3, 7):
            w_wait(k, 0)
        feed(plane)

    @task
    def fe1():
        w_done(2)
        for k in range(3, 7):
            w_wait(k, 3)
            w_wait(k, 4)
        feed(1 - plane)

    def tally(n, value):
        r.v_rows[n : n + 1] += jnp.sum(value, axis=0, keepdims=True)

    @task
    def sn():
        def second_norm(which, unused):
            at = span(which * 128, 128, 128)
            result, normed, inverse = norm_forward(r.work[at], row_vec(6), row_vec(7))
            r.layer_rows[which] = result.astype(BF16)
            upstream = r.cot_rows[which].astype(F32)
            scaled = upstream * row_vec(6)
            back = inverse * (
                scaled
                - jnp.mean(scaled, axis=-1, keepdims=True)
                - normed * jnp.mean(scaled * normed, axis=-1, keepdims=True)
            )
            tally(4, upstream * normed)
            tally(5, upstream)
            r.work[at] = back
            part = back.astype(BF16)
            r.d_rows[at] = part
            tally(1, part.astype(F32))
            return unused

        cot_local.wait()
        lax.fori_loop(0, 2, second_norm, 0)
        to_hbm(r.layer_rows, r.layer)
        early.append(len(sent))

    chunks = [
        (r.gu, r.fu, r.core_u, r.xr_u, r.rcv_u, r.fin_u, r.tot_u.at[k], 192 * k, 192, 0, 768)
        for k in range(4)
    ]
    chunks += [
        (r.gi, r.fi, r.core_i, r.xr_i, r.rcv_i, r.fin_i, r.tot_i.at[k], 0, 192, 768 * k, 768)
        for k in range(4)
    ]
    chunks += [
        (r.go, r.fo, r.core_o, r.xr_o, r.rcv_o, r.fin_o, r.tot_o, 0, 192, 0, 768),
    ]

    def reduce_steps(k, first):
        grad, out, core, arrived, rcv, fin, total, row, rows, col, cols = chunks[k]
        rr, cc = pl.ds(row, rows), pl.ds(col, cols)
        wide = cols // 2
        mine = span(col + bit_y * wide, wide, 128)
        other = span(col + (1 - bit_y) * wide, wide, 128)
        keep_l = span(row + bit_l * (rows // 2), rows // 2)
        give_l = span(row + (1 - bit_l) * (rows // 2), rows // 2)
        keep_h = span(row + bit_l * (rows // 2) + bit_h * (rows // 4), rows // 4)
        give_h = span(row + bit_l * (rows // 2) + (1 - bit_h) * (rows // 4), rows // 4)
        spot_h = span(row + (1 - bit_l) * (rows // 2), rows // 4)
        tot_keep, tot_give = (
            span(bit_h * (rows // 4), rows // 4),
            span((1 - bit_h) * (rows // 4), rows // 4),
        )
        owner = (seq, across)

        def sems(leg):
            return r.r_ss.at[k, leg], r.r_rs.at[k, leg]

        to_core = [
            remote(grad.at[mate, rr, cc], core.at[0, rr, cc], *sems(0), mate, ctx),
            remote(
                grad.at[across_mate, rr, cc], core.at[1, rr, cc], *sems(1), mate, ctx
            ),
        ]

        def add(at, lanes, slot, *more):
            value = grad[owner[slot], at, lanes].astype(F32) + core[
                slot, at, lanes
            ].astype(F32)
            for ref in more:
                value += ref[at, lanes].astype(F32)
            return value

        def put(at, lanes, slot, *more):
            core[slot, at, lanes] = add(at, lanes, slot, *more).astype(BF16)

        def spread(at, lanes, leg, target):
            spot = fin.at[at, lanes]
            return remote(spot, spot, *sems(leg), seq, target)

        to_h = remote(
            arrived.at[give_h, mine], rcv.at[spot_h, other], *sems(5), seq, mirror
        )

        def begin():
            for copy in to_core:
                copy.start()

        def cores_in():
            for copy in to_core:
                copy.wait_recv()

        if first == "x":
            to_x = remote(core.at[1, rr, cc], arrived.at[rr, cc], *sems(2), across, ctx)
            to_y = remote(arrived.at[rr, other], rcv.at[rr, other], *sems(3), seq, beside)
            at_y = remote(arrived.at[rr, mine], rcv.at[rr, mine], *sems(3), seq, beside)
            firsts = [to_x, to_y]

            def one():
                put(rr, cc, 1)
                to_x.start()

            def two():
                arrived[rr, other] = add(rr, other, 0, arrived).astype(BF16)
                to_y.start()

        elif first == "y":
            extra = r.two_y.at[FIRST[:k].count("y")]
            to_y = [
                remote(
                    core.at[0, rr, other], rcv.at[rr, other], *sems(3), seq, beside
                ),
                remote(core.at[1, rr, other], extra, *sems(9), seq, beside),
            ]
            at_y = [
                remote(core.at[0, rr, mine], rcv.at[rr, mine], *sems(3), seq, beside),
                remote(core.at[1, rr, mine], extra, *sems(9), seq, beside),
            ]
            to_x = remote(
                core.at[1, rr, mine], arrived.at[rr, mine], *sems(2), across, ctx
            )
            firsts = to_y + [to_x]

            def one():
                for slot in range(2):
                    put(rr, other, slot)
                    to_y[slot].start()

            def two():
                for copy in at_y:
                    copy.wait_recv()
                core[1, rr, mine] = (add(rr, mine, 1) + extra[...].astype(F32)).astype(
                    BF16
                )
                to_x.start()

        elif first == "w":
            to_x = remote(core.at[1, rr, cc], arrived.at[rr, cc], *sems(2), across, ctx)
            to_l = remote(
                arrived.at[give_l, cc], rcv.at[give_l, cc], *sems(4), seq, paired
            )
            at_l = [
                remote(arrived.at[keep_l, cc], rcv.at[keep_l, cc], *sems(4), seq, paired)
            ]
            firsts = [to_x, to_l]

            def one():
                put(rr, cc, 1)
                to_x.start()

            def two():
                arrived[give_l, cc] = add(give_l, cc, 0, arrived).astype(BF16)
                to_l.start()

        else:
            extra = r.two_z.at[FIRST[:k].count("z")]
            to_l = [
                remote(core.at[0, give_l, cc], rcv.at[give_l, cc], *sems(4), seq, paired),
                remote(core.at[1, give_l, cc], extra, *sems(9), seq, paired),
            ]
            at_l = [
                remote(core.at[0, keep_l, cc], rcv.at[keep_l, cc], *sems(4), seq, paired),
                remote(core.at[1, keep_l, cc], extra, *sems(9), seq, paired),
            ]
            to_x = remote(
                core.at[1, keep_l, cc], arrived.at[keep_l, cc], *sems(2), across, ctx
            )
            firsts = to_l + [to_x]

            def one():
                for slot in range(2):
                    put(give_l, cc, slot)
                    to_l[slot].start()

            def two():
                for copy in at_l:
                    copy.wait_recv()
                core[1, keep_l, cc] = (
                    add(keep_l, cc, 1) + extra[...].astype(F32)
                ).astype(BF16)
                to_x.start()

        if first in "zw":
            to_y = remote(
                arrived.at[keep_l, other], rcv.at[give_l, other], *sems(3), seq, beside
            )
            at_y = remote(
                arrived.at[keep_l, mine], rcv.at[give_l, mine], *sems(3), seq, beside
            )
            firsts = firsts + [to_y]

            def three():
                for copy in at_l if first == "w" else [to_x]:
                    copy.wait_recv()
                arrived[keep_l, other] = add(keep_l, other, 0, rcv, arrived).astype(BF16)
                to_y.start()
                total[...] = add(keep_l, mine, 0, rcv, arrived)

            def four():
                at_y.wait_recv()
                total[...] += rcv[give_l, mine].astype(F32)
                arrived[give_h, mine] = total[tot_give].astype(BF16)
                to_h.start()

        else:
            to_l = remote(
                arrived.at[give_l, mine], rcv.at[give_l, other], *sems(4), seq, paired
            )
            at_l = remote(
                arrived.at[keep_l, mine], rcv.at[keep_l, other], *sems(4), seq, paired
            )
            firsts = firsts + [to_l]

            def three():
                (at_y if first == "x" else to_x).wait_recv()
                arrived[give_l, mine] = add(give_l, mine, 0, arrived, rcv).astype(BF16)
                to_l.start()
                total[...] = add(keep_l, mine, 0, arrived, rcv)

            def four():
                at_l.wait_recv()
                arrived[give_h, mine] = (
                    total[tot_give] + rcv[give_h, other].astype(F32)
                ).astype(BF16)
                to_h.start()
                total[tot_keep] += rcv[keep_h, other].astype(F32)

        def step_one():
            cores_in()
            one()

        def step_two():
            if first in "xw":
                to_x.wait_recv()
            two()

        def step_five():
            to_h.wait_recv()
            fin[keep_h, mine] = (
                total[tot_keep] + rcv[spot_h, other].astype(F32)
            ).astype(BF16)
            spread(keep_h, mine, 6, mirror).start()

        if first in "zw":
            last = [(keep_l, other, 7, beside), (keep_l, cc, 8, paired)]
            ends = [(give_l, cc)]
            middle = (keep_l, mine)
        else:
            last = [(give_l, mine, 7, paired), (rr, mine, 8, beside)]
            ends = [(rr, other)]
            middle = (keep_l, mine)

        def step_six():
            spread(give_h, mine, 6, mirror).wait_recv()
            spread(*middle, 7, last[0][3]).start()

        def step_seven():
            spread(*last[0]).wait_recv()
            spread(*last[1]).start()

        to_out = pltpu.make_async_copy(fin.at[rr, cc], out.at[rr, cc], r.loc.at[17 + k])

        def step_eight():
            spread(*ends[0], 8, last[1][3]).wait_recv()
            to_out.start()

        def end():
            for copy in (
                to_core
                + firsts
                + [
                    to_h,
                    spread(keep_h, mine, 6, mirror),
                    spread(*middle, 7, last[0][3]),
                    spread(*last[1]),
                ]
            ):
                copy.wait_send()
            to_out.wait()

        names = [
            begin,
            step_one,
            step_two,
            three,
            four,
            step_five,
            step_six,
            step_seven,
            step_eight,
            end,
        ]
        return names

    t.s = [reduce_steps(k, FIRST[k]) for k in range(9)]

    def make_outer(k):
        part = slice(192 * k, 192 * k + 192)
        for owner in (mate, across_mate):
            r.gu[owner, part] = matmul(r.act_t[owner, part], r.d_rows[...]).astype(BF16)
        t.s[k][0]()
        for owner in (across, seq):
            r.gu[owner, part] = matmul(r.act_t[owner, part], r.d_rows[...]).astype(BF16)

    t.mo = [functools.partial(make_outer, k) for k in range(4)]

    def inner_step(n):
        def inner_back(which, unused):
            at = span(which * 128, 128, 128)
            part = (matmul_nt(r.d_rows[at], r.wu_full[n]) * r.slope[n, at]).astype(BF16)
            r.low[at] = part
            tally(8 + n, part.astype(F32))
            r.work[at] += matmul_nt(part, inner_weight(n))
            return unused

        lax.fori_loop(0, 2, inner_back, 0)
        r.gi[:, :, 768 * n : 768 * n + 768] = (
            matmul(r.low_t[...], r.low[...]).astype(BF16).reshape(4, 192, 768)
        )
        t.s[4 + n][0]()

    t.ib = [functools.partial(inner_step, n) for n in range(4)]

    own_do = pltpu.make_async_copy(
        r.do_send.at[my_rows, my_lanes], r.do_all.at[:, own_lanes], r.loc.at[15]
    )

    @task
    def fb():
        def first_back(which, unused):
            at = span(which * 128, 128, 128)
            upstream, normed = r.work[at], r.normed[at]
            scaled = upstream * row_vec(4)
            back = r.inverse[at] * (
                scaled
                - jnp.mean(scaled, axis=-1, keepdims=True)
                - normed * jnp.mean(scaled * normed, axis=-1, keepdims=True)
            )
            tally(2, upstream * normed)
            tally(3, upstream)
            r.work[at] = back
            part = back.astype(BF16)
            r.low[at] = part
            tally(0, part.astype(F32))
            return unused

        lax.fori_loop(0, 2, first_back, 0)
        r.do_send[...] = matmul_nt(
            r.wo_full[...].reshape(768, 768), r.low[...]
        ).astype(BF16)
        own_do.start()
        for head in range(3):
            for hop in range(1, 8):
                other = lax.rem(ctx + hop, 8)
                send(
                    r.do_send.at[
                        span(lax.rem(other, 4) * 192 + 64 * head, 64, 64),
                        span((other // 4) * 128, 128, 128),
                    ],
                    r.do_all.at[64 * head : 64 * head + 64, own_lanes],
                    r.do_ss.at[head, hop],
                    r.do_rs.at[head, hop],
                    seq,
                    other,
                )

    @task
    def dwo():
        r.go[...] = matmul(r.ctx_t[...], r.low[...]).astype(BF16).reshape(4, 192, 768)
        t.s[8][0]()
        for owner in range(4):
            start = 192 * owner - 64 * (owner % 2)
            r.v_own[owner, 0:8] = r.v_rows[0:8, start : start + 256]
            for part in range(3):
                r.v_own[owner, 8 + part : 9 + part] = r.v_rows[
                    8 + owner : 9 + owner, 256 * part : 256 * part + 256
                ]
            r.v_own[owner, 11:16] = jnp.zeros((5, 256), F32)
        for hop in range(1, 4):
            other = lax.rem(seq + hop, 4)
            send(
                r.v_own.at[other],
                r.v_recv.at[seq],
                r.v_ss.at[0, hop],
                r.v_rs.at[0, hop],
                other,
                ctx,
            )

    @task
    def v1():
        for hop in range(1, 4):
            spot = r.v_recv.at[lax.rem(seq + 4 - hop, 4)]
            landed(spot, r.v_ss.at[0, hop], r.v_rs.at[0, hop])
        r.v_recv[seq] = r.v_own[seq]
        r.v_all[ctx] = r.v_recv[0] + r.v_recv[1] + r.v_recv[2] + r.v_recv[3]
        for hop in range(1, 8):
            send(
                r.v_all.at[ctx],
                r.v_all.at[ctx],
                r.v_ss.at[1, hop],
                r.v_rs.at[1, hop],
                seq,
                lax.rem(ctx + hop, 8),
            )

    def attend_back_head(head):
        if head == 0:
            own_do.wait()
        for hop in range(1, 8):
            spot = r.do_all.at[
                64 * head : 64 * head + 64, span(lax.rem(ctx + 8 - hop, 8) * 128, 128, 128)
            ]
            landed(spot, r.do_ss.at[head, hop], r.do_rs.at[head, hop])
        at = span(inside + 64 * head, 64, 64)
        total = r.sums[head]
        d_out = r.do_all[64 * head : 64 * head + 64].astype(F32)
        r.du[...] = (d_out / total).astype(BF16)
        r.c_row[...] = jnp.sum(d_out * r.ot[head], axis=0, keepdims=True) / total
        r.key_rows[...] = r.ka[head].T
        r.value_rows[...] = r.vt[head].T
        r.dk_acc[...] = jnp.zeros((64, 1024), F32)
        r.dv_acc[...] = jnp.zeros((64, 1024), F32)

        def attend_back(block, unused):
            lanes = span(block * 256, 256, 256)
            scores = matmul(r.key_rows[...], r.qa[head, :, lanes])
            unnorm = jnp.exp(scores)
            d_prob = matmul(r.value_rows[...], r.du[:, lanes])
            d_score = (unnorm * (d_prob - r.c_row[:, lanes])).astype(BF16)
            d_query = matmul(r.ka[head, 0:64], d_score) * SCORE_SCALE
            r.d_all[0, at, lanes] = d_query.astype(BF16)
            r.dk_acc[...] += matmul_nt(r.qa[head, 0:64, lanes], d_score)
            r.dv_acc[...] += matmul_nt(r.du[:, lanes], unnorm.astype(BF16))
            return unused

        lax.fori_loop(0, 4, attend_back, 0)
        r.d_all[1, at] = r.dk_acc[...].astype(BF16)
        r.d_all[2, at] = r.dv_acc[...].astype(BF16)

    t.ab = [functools.partial(attend_back_head, head) for head in range(3)]

    g_cores = [
        remote(
            r.g_all.at[which, owner],
            r.g_core.at[which, n],
            r.h_ss.at[which, n],
            r.h_rs.at[which, n],
            mate,
            ctx,
        )
        for which in range(3)
        for n, owner in ((0, mate), (1, across_mate))
    ]
    own_bias = pltpu.make_async_copy(
        r.b_send, r.b_recv.at[seq * 2 + side], r.loc.at[16]
    )
    to_owners = [
        remote(
            r.b_send,
            r.b_recv.at[seq * 2 + side],
            r.b_ss.at[hop],
            r.b_rs.at[seq * 2 + side],
            group,
            lax.rem(ctx + hop, 8),
        )
        for hop in range(8)
    ]

    @task
    def dwq():
        ones = jnp.ones((16, 1024), BF16)
        for which in range(3):
            product = matmul(r.d_all[which], r.xs[...].reshape(1024, 768)).astype(BF16)
            r.g_all[which] = product.T.reshape(4, 192, 256)
            if which != 1:
                r.b_send[which // 2] = matmul_nt(ones, r.d_all[which])[0:8]
        for copy in g_cores:
            copy.start()

        @pl.when(group == seq)
        def _():
            own_bias.start()

        @pl.when(group != seq)
        def _():
            to_owners[0].start()

        for copy in to_owners[1:]:
            copy.start()

    @task
    def dx():
        for part in range(4):
            lanes = slice(256 * part, 256 * part + 256)
            share = matmul(r.wg[0].reshape(768, 256), r.d_all[0, :, lanes])
            for which in (1, 2):
                share += matmul(r.wg[which].reshape(768, 256), r.d_all[which, :, lanes])
            r.act_t[part] = share.astype(BF16)

    def dx_half(part, bit):
        return r.act_t.at[part, :, span(bit * 128, 128, 128)]

    dx_to_y = [
        remote(
            dx_half(part, 1 - bit_y),
            r.dx_y.at[part],
            r.dx_ss.at[part],
            r.dx_rs.at[part],
            seq,
            beside,
        )
        for part in range(4)
    ]
    dx_to_l = [
        remote(
            dx_half(2 * n + 1 - bit_l, bit_y),
            r.dx_l.at[n],
            r.dx_ss.at[4 + n],
            r.dx_rs.at[4 + n],
            seq,
            paired,
        )
        for n in range(2)
    ]
    lanes_y = span(bit_y * 128, 128, 128)

    def dx_part(which):
        return 2 * which + bit_l

    dx_to_h = remote(
        dx_half(dx_part(1 - side), bit_y),
        r.dx_h,
        r.dx_ss.at[6],
        r.dx_rs.at[6],
        seq,
        mirror,
    )
    t.d = [copy.start for copy in dx_to_y]

    @task
    def dxp():
        for copy in dx_to_y:
            copy.wait_recv()
        for n in range(2):
            part = 2 * n + 1 - bit_l
            r.act_t[part, :, lanes_y] = (
                r.act_t[part, :, lanes_y].astype(F32) + r.dx_y[part].astype(F32)
            ).astype(BF16)
            dx_to_l[n].start()

    def dx_total(which):
        part = dx_part(which)
        return (
            r.act_t[part, :, lanes_y].astype(F32)
            + r.dx_y[part].astype(F32)
            + r.dx_l[which].astype(F32)
        )

    @task
    def dxm():
        for copy in dx_to_l:
            copy.wait_recv()
        r.act_t[dx_part(1 - side), :, lanes_y] = dx_total(1 - side).astype(BF16)
        dx_to_h.start()
        r.grad_rows[side] = dx_total(side).T + r.work[span(side * 128, 128)]
        to_hbm(r.grad_rows.at[side], r.grad.at[side])

    @task
    def dxe():
        dx_to_h.wait_recv()
        r.grad_rows[1 - side] = (
            r.dx_h[...].astype(F32).T + r.work[span((1 - side) * 128, 128)]
        )
        to_hbm(r.grad_rows.at[1 - side], r.grad.at[1 - side])

    g_x = remote(r.g_xs, r.g_xr, r.h_ss.at[3, 0], r.h_rs.at[3, 0], across, ctx)
    keep, give = span(side * 96, 96, 32), span((1 - side) * 96, 96, 32)
    g_m = remote(
        r.g_half.at[:, give], r.g_mir, r.h_ss.at[3, 1], r.h_rs.at[3, 1], seq, mirror
    )

    @task
    def gx():
        for copy in g_cores:
            copy.wait_recv()
        for which in range(3):
            r.g_xs[which] = (
                r.g_all[which, across].astype(F32) + r.g_core[which, 1].astype(F32)
            ).astype(BF16)
        g_x.start()

    @task
    def gm():
        g_x.wait_recv()
        for which in range(3):
            r.g_half[which] = (
                r.g_all[which, seq].astype(F32)
                + r.g_core[which, 0].astype(F32)
                + r.g_xr[which].astype(F32)
            ).astype(BF16)
        g_m.start()

    @task
    def ga():
        g_m.wait_recv()
        for which in range(3):
            r.fg_all[group, which, keep] = (
                r.g_half[which, keep].astype(F32) + r.g_mir[which].astype(F32)
            ).astype(BF16)
        spot = r.fg_all.at[group, :, keep]
        send(spot, spot, r.h_ss.at[4, 0], r.h_rs.at[4, 0], seq, mirror)
        for n, other in enumerate((beside, paired)):
            send(spot, spot, r.h_ss.at[5, n], r.h_rs.at[5, n], seq, other)

    @task
    def gb():
        theirs = r.fg_all.at[group, :, give]
        landed(theirs, r.h_ss.at[4, 0], r.h_rs.at[4, 0])
        for n, other in enumerate((beside, paired)):
            send(theirs, theirs, r.h_ss.at[6, n], r.h_rs.at[6, n], seq, other)
        to_hbm(r.fg_all.at[group], r.fg.at[group])

    def of_group(other, rows):
        return r.fg_all.at[lax.rem(other, 4), :, rows]

    @task
    def gc():
        spot = of_group(beside, keep)
        landed(spot, r.h_ss.at[5, 0], r.h_rs.at[5, 0])
        send(spot, spot, r.h_ss.at[5, 2], r.h_rs.at[5, 2], seq, paired)

    @task
    def gd():
        spot = of_group(paired, give)
        landed(spot, r.h_ss.at[6, 1], r.h_rs.at[6, 1])
        send(spot, spot, r.h_ss.at[6, 2], r.h_rs.at[6, 2], seq, beside)

    @task
    def v2():
        for hop in range(1, 8):
            spot = r.v_all.at[lax.rem(ctx + 8 - hop, 8)]
            landed(spot, r.v_ss.at[1, hop], r.v_rs.at[1, hop])
        gathered = r.v_all[0]
        for n in range(1, 8):
            gathered += r.v_all[n]
        r.vec_sum[...] = gathered

    @task
    def be():
        for n in range(8):
            spot = r.b_recv.at[n]
            arrival = remote(
                spot, spot, r.b_ss.at[0], r.b_rs.at[n], lax.rem(seq + 1, 4), ctx
            )
            here = (n // 2 == seq) & (n % 2 == side) & (group == seq)

            @pl.when(here)
            def _():
                own_bias.wait()

            @pl.when(jnp.logical_not(here))
            def _(arrival=arrival):
                arrival.wait_recv()

        row_sum = r.b_recv[0]
        for n in range(1, 8):
            row_sum += r.b_recv[n]
        r.bias_sum[...] = row_sum

    @task
    def ge():
        landed(of_group(paired, keep), r.h_ss.at[5, 1], r.h_rs.at[5, 1])
        landed(of_group(beside, give), r.h_ss.at[6, 0], r.h_rs.at[6, 0])
        landed(of_group(diagonal, keep), r.h_ss.at[5, 2], r.h_rs.at[5, 2])
        landed(of_group(diagonal, give), r.h_ss.at[6, 2], r.h_rs.at[6, 2])
        for other in (beside, paired, diagonal):
            part = lax.rem(other, 4)
            to_hbm(r.fg_all.at[part], r.fg.at[part])

    @task
    def left():
        for copy in sent[: early[0]]:
            copy.wait_send()
        for k in range(7):
            for leg in range(5):
                w_copy(k, leg).wait_send()

    for step in in_order(t):
        step()

    for k in range(9):
        t.s[k][9]()
    for copy in (
        sent[early[0] :]
        + g_cores
        + [g_x, g_m]
        + to_owners[1:]
        + dx_to_y
        + dx_to_l
        + [dx_to_h]
    ):
        copy.wait_send()

    @pl.when(group != seq)
    def _():
        to_owners[0].wait_send()

    for copy in to_hbm_all:
        copy.wait()


def in_order(t):
    return (
        t.far[0],
        t.far[1],
        t.ff[0],
        t.grp,
        t.nf,
        t.ff[1],
        t.pa[0],
        t.pa[1],
        t.small,
        t.qkv,
        t.pa[2],
        t.at[0],
        t.at[1],
        t.at[2],
        t.pa[5],
        t.pb[1],
        t.pb[0],
        t.pa[4],
        t.pa[6],
        t.pb[2],
        t.pa[3],
        t.fn,
        t.pb[4],
        t.pb[5],
        t.fe0,
        t.pb[3],
        t.pb[6],
        t.fe1,
        t.sn,
        t.mo[0],
        t.mo[1],
        t.mo[2],
        t.mo[3],
        t.ib[0],
        t.s[0][1],
        t.ib[1],
        t.s[2][1],
        t.ib[2],
        t.s[5][1],
        t.s[1][1],
        t.ib[3],
        t.s[0][2],
        t.fb,
        t.s[2][2],
        t.s[4][1],
        t.dwo,
        t.s[0][3],
        t.s[8][1],
        t.s[7][1],
        t.s[1][2],
        t.s[3][1],
        t.ab[0],
        t.ab[1],
        t.s[0][4],
        t.s[2][3],
        t.s[1][3],
        t.s[4][2],
        t.ab[2],
        t.v1,
        t.s[3][2],
        t.dwq,
        t.s[2][4],
        t.s[7][2],
        t.s[0][5],
        t.s[8][2],
        t.s[6][1],
        t.s[4][3],
        t.s[1][4],
        t.dx,
        t.d[0],
        t.v2,
        t.d[1],
        t.s[3][3],
        t.s[2][5],
        t.be,
        t.s[4][4],
        t.s[8][3],
        t.s[1][5],
        t.gx,
        t.s[3][4],
        t.s[2][6],
        t.s[8][4],
        t.s[7][3],
        t.s[4][5],
        t.s[1][6],
        t.s[5][2],
        t.s[2][7],
        t.s[6][2],
        t.s[0][6],
        t.s[3][5],
        t.s[7][4],
        t.s[8][5],
        t.s[4][6],
        t.d[2],
        t.s[2][8],
        t.gm,
        t.s[6][3],
        t.s[8][6],
        t.s[5][3],
        t.s[0][7],
        t.d[3],
        t.s[3][6],
        t.s[7][5],
        t.s[4][7],
        t.s[6][4],
        t.s[5][4],
        t.s[1][7],
        t.ga,
        t.s[0][8],
        t.s[5][5],
        t.s[6][5],
        t.left,
        t.dxp,
        t.s[4][8],
        t.s[1][8],
        t.s[7][6],
        t.s[5][6],
        t.s[6][6],
        t.s[3][7],
        t.s[7][7],
        t.s[8][7],
        t.s[5][7],
        t.s[6][7],
        t.s[3][8],
        t.gb,
        t.dxm,
        t.s[7][8],
        t.s[8][8],
        t.gc,
        t.s[5][8],
        t.s[6][8],
        t.gd,
        t.dxe,
        t.ge,
    )


def run_layer(*operands):
    vmem = pl.BlockSpec(memory_space=pltpu.VMEM)
    anywhere = pl.BlockSpec(memory_space=pl.ANY)
    shape = jax.ShapeDtypeStruct
    return pl.pallas_call(
        layer_kernel,
        name="layer_kernel",
        out_shape=(
            shape((2, 128, 768), BF16),
            shape((2, 128, 768), F32),
            shape((768, 768), BF16),
            shape((192, 3072), BF16),
            shape((192, 768), BF16),
            shape((4, 3, 192, 256), BF16),
            shape((16, 256), F32),
            shape((2, 8, 256), F32),
        ),
        in_specs=[anywhere] * 2 + [vmem] * 10 + [anywhere] * 6,
        out_specs=(anywhere,) * 6 + (vmem,) * 2,
        scratch_shapes=[pltpu.VMEM(*spec) for spec in SCRATCH.values()]
        + [pltpu.SemaphoreType.DMA(count) for count in SEMAPHORES.values()],
        compiler_params=pltpu.CompilerParams(
            collective_id=1, has_side_effects=True, vmem_limit_bytes=67043328
        ),
    )(*operands)


def finish_kernel(*refs):
    ins, outs, bufs = refs[:8], refs[8:25], refs[25:]
    low, wide, load, store = bufs[:8], bufs[8:17], bufs[17], bufs[18]
    grad, layer, low_u, low_i, low_o, low_g, vec, bias = low
    wide_t, wide_l, out_l, wide_u, wide_i, wide_o, wide_q, wide_k, wide_v = wide
    loads = [
        pltpu.make_async_copy(source, target, load.at[n])
        for n, (source, target) in enumerate(zip(ins, low))
    ]
    for copy in loads:
        copy.start()
    stores = []

    def put(source, target):
        copy = pltpu.make_async_copy(source, target, store.at[len(stores)])
        copy.start()
        stores.append(copy)

    loads[2].wait()
    for part in (slice(0, 384), slice(384, 768)):
        wide_u[part] = low_u[part].astype(F32)
        put(wide_u.at[part], outs[7].at[part])
    loads[3].wait()
    for part in (slice(0, 96), slice(96, 192)):
        wide_i[part] = low_i[part].astype(F32)
        put(wide_i.at[part], outs[6].at[part])
    loads[0].wait()
    for which in range(2):
        wide_t[:, which, :] = grad[which]
    put(wide_t, outs[1])
    loads[1].wait()
    for which in range(2):
        wide_l[:, which, :] = layer[which].astype(F32)
    out_l[...] = wide_l[...].astype(BF16)
    put(out_l, outs[0])
    loads[4].wait()
    wide_o[...] = low_o[...].astype(F32)
    put(wide_o, outs[5])
    loads[5].wait()
    for which, target in enumerate((wide_q, wide_k, wide_v)):
        for pair in range(2):
            left = low_g[2 * pair, which].astype(F32)
            right = low_g[2 * pair + 1, which].astype(F32)
            at = 384 * pair
            target[:, at : at + 128] = left[:, 0:128]
            target[:, at + 128 : at + 256] = left[:, 128:256] + right[:, 0:128]
            target[:, at + 256 : at + 384] = right[:, 128:256]
        put(target, outs[2 + which])
    odd = lax.rem(lax.axis_index("seq"), 2) == 1

    def owned(row):
        return jnp.where(odd, row[:, 64:256], row[:, 0:192]).reshape(192)

    loads[6].wait()
    loads[7].wait()
    outs[8][...] = owned(bias[0, 0:1])
    outs[9][...] = owned(bias[1, 0:1])
    outs[10][...] = owned(vec[0:1])
    outs[11][...] = jnp.concatenate([vec[n : n + 1] for n in (8, 9, 10)], axis=1).reshape(
        768
    )
    for n in range(1, 6):
        outs[11 + n][...] = owned(vec[n : n + 1])
    for copy in stores:
        copy.wait()


def run_finish(*operands):
    vmem = pl.BlockSpec(memory_space=pltpu.VMEM)
    anywhere = pl.BlockSpec(memory_space=pl.ANY)
    shape = jax.ShapeDtypeStruct
    large = [(192, 768)] * 4 + [(192, 3072), (768, 768)]
    small = [(192,)] * 3 + [(768,)] + [(192,)] * 5
    return pl.pallas_call(
        finish_kernel,
        name="finish_kernel",
        out_shape=[shape((128, 2, 768), BF16), shape((128, 2, 768), F32)]
        + [shape(size, F32) for size in large + small],
        in_specs=[anywhere] * 8,
        out_specs=[anywhere] * 8 + [vmem] * 9,
        scratch_shapes=[
            pltpu.VMEM((2, 128, 768), F32),
            pltpu.VMEM((2, 128, 768), BF16),
            pltpu.VMEM((768, 768), BF16),
            pltpu.VMEM((192, 3072), BF16),
            pltpu.VMEM((192, 768), BF16),
            pltpu.VMEM((4, 3, 192, 256), BF16),
            pltpu.VMEM((16, 256), F32),
            pltpu.VMEM((2, 8, 256), F32),
            pltpu.VMEM((128, 2, 768), F32),
            pltpu.VMEM((128, 2, 768), F32),
            pltpu.VMEM((128, 2, 768), BF16),
            pltpu.VMEM((768, 768), F32),
            pltpu.VMEM((192, 3072), F32),
            pltpu.VMEM((192, 768), F32),
            pltpu.VMEM((192, 768), F32),
            pltpu.VMEM((192, 768), F32),
            pltpu.VMEM((192, 768), F32),
            pltpu.SemaphoreType.DMA((8,)),
            pltpu.SemaphoreType.DMA((10,)),
        ],
        compiler_params=pltpu.CompilerParams(vmem_limit_bytes=67043328),
    )(*operands)


def fast_body(
    tokens,
    segment_ids,
    w_query,
    w_key,
    w_value,
    w_output,
    w_inner,
    w_outer,
    b_query,
    b_value,
    b_output,
    b_inner,
    b_outer,
    gain_first,
    shift_first,
    gain_second,
    shift_second,
    cotangent,
):
    layer, grad, fu, fi, fo, fg, vec_sum, bias_sum = run_layer(
        jnp.transpose(tokens, (1, 0, 2)),
        jnp.transpose(cotangent, (1, 0, 2)),
        segment_ids,
        b_query,
        b_value,
        b_output,
        b_outer,
        gain_first,
        shift_first,
        gain_second,
        shift_second,
        b_inner,
        w_query,
        w_key,
        w_value,
        w_output,
        w_inner,
        w_outer,
    )

    return tuple(run_finish(grad, layer, fu, fi, fo, fg, vec_sum, bias_sum))


def solution(mesh):
    in_specs = (
        P("ctx", "seq", None),
        P("seq", "ctx"),
        P("seq", None),
        P("seq", None),
        P("seq", None),
        P("seq", None),
        P("seq", None),
        P("seq", None),
        P("seq"),
        P("seq"),
        P("seq"),
        P("seq"),
        P("seq"),
        P("seq"),
        P("seq"),
        P("seq"),
        P("seq"),
        P("ctx", "seq", None),
    )
    out_specs = (
        P("ctx", "seq", None),
        P("ctx", "seq", None),
        P("seq", None),
        P("seq", None),
        P("seq", None),
        P("seq", None),
        P("seq", None),
        P("seq", None),
        P("seq"),
        P("seq"),
        P("seq"),
        P("seq"),
        P("seq"),
        P("seq"),
        P("seq"),
        P("seq"),
        P("seq"),
    )
    small = mesh.shape["seq"] == 4 and mesh.shape["ctx"] == 8
    step = fast_body if small else body
    return jax.shard_map(step, mesh=mesh, in_specs=in_specs, out_specs=out_specs, check_vma=False)
```

```python
import functools
import math
import types

import jax
import jax.numpy as jnp
from jax import lax
from jax.experimental import pallas as pl
from jax.experimental.pallas import tpu as pltpu
from jax.sharding import PartitionSpec as P

H = 12
DH = 64


EPSILON = 1e-12
SCORE_SCALE = 0.125


def matmul(first_op, second_op):
    return jnp.dot(first_op, second_op, preferred_element_type=jnp.float32)


def matmul_tn(first_op, second_op):
    return lax.dot_general(
        first_op, second_op, (((0,), (0,)), ((), ())), preferred_element_type=jnp.float32
    )


def matmul_nt(first_op, second_op):
    return lax.dot_general(
        first_op, second_op, (((1,), (1,)), ((), ())), preferred_element_type=jnp.float32
    )


def norm_forward(values, gain_vec, shift_vec):
    center = values - jnp.mean(values, axis=-1, keepdims=True)
    inverse = lax.rsqrt(jnp.mean(center * center, axis=-1, keepdims=True) + EPSILON)
    normed = center * inverse
    return (normed * gain_vec + shift_vec, normed, inverse)


def norm_backward(upstream, normed, inverse, gain_vec):
    scaled = upstream * gain_vec
    back_grad = inverse * (
        scaled
        - jnp.mean(scaled, axis=-1, keepdims=True)
        - normed * jnp.mean(scaled * normed, axis=-1, keepdims=True)
    )
    return (back_grad, jnp.sum(upstream * normed, axis=0), jnp.sum(upstream, axis=0))


def gelu_parts(values):
    cumulative = 0.5 * (1.0 + lax.erf(values * 0.7071067811865476))
    return (
        values * cumulative,
        cumulative + values * jnp.exp(-0.5 * values * values) * 0.3989422804014327,
    )


def block_scores(query_heads, key_heads, seg_query, seg_key):
    raw_scores = (
        jnp.einsum("ishd,jshd->shij", query_heads, key_heads, preferred_element_type=jnp.float32)
        * SCORE_SCALE
    )
    allowed = (jnp.transpose(seg_query)[:, :, None] == jnp.transpose(seg_key)[:, None, :])[:, None]
    return jnp.where(allowed, jnp.exp(raw_scores), 0.0)


def attend_keys(query_heads, seg_query, carry_in, piece_rows):
    key_piece, value_piece, seg_piece = piece_rows
    row_count, seq_count, feature_count = key_piece.shape
    heads, head_size = (query_heads.shape[2], query_heads.shape[3])
    step_rows = math.gcd(row_count, 1024)
    block_count = row_count // step_rows
    key_blocks = key_piece.reshape(block_count, step_rows, seq_count, heads, head_size)
    value_blocks = value_piece.reshape(block_count, step_rows, seq_count, heads, head_size)
    seg_blocks = seg_piece.reshape(block_count, step_rows, seq_count)

    def attend_visit_block(running, element):
        key_block, value_block, seg_block = element
        unnorm = block_scores(query_heads, key_block, seg_query, seg_block)
        totals = running[0] + jnp.sum(unnorm, axis=-1)
        mixture = running[1] + jnp.einsum(
            "shij,jshd->ishd",
            unnorm.astype(jnp.bfloat16),
            value_block,
            preferred_element_type=jnp.float32,
        )
        return ((totals, mixture), None)

    result, unused = lax.scan(attend_visit_block, carry_in, (key_blocks, value_blocks, seg_blocks))
    return result


def key_side(query_heads, d_mixture, correction, seg_query, key_all, value_all, seg_all):
    row_count, seq_count, feature_count = key_all.shape
    heads, head_size = (query_heads.shape[2], query_heads.shape[3])
    step_rows = math.gcd(row_count, 1024)
    block_count = row_count // step_rows
    corr_cols = jnp.transpose(correction, (1, 2, 0))[..., None]
    key_blocks = key_all.reshape(block_count, step_rows, seq_count, heads, head_size)
    value_blocks = value_all.reshape(block_count, step_rows, seq_count, heads, head_size)
    seg_blocks = seg_all.reshape(block_count, step_rows, seq_count)

    def key_visit_block(dq_acc, element):
        key_block, value_block, seg_block = element
        unnorm = block_scores(query_heads, key_block, seg_query, seg_block)
        d_prob = jnp.einsum(
            "ishd,jshd->shij", d_mixture, value_block, preferred_element_type=jnp.float32
        )
        d_score = (unnorm * (d_prob - corr_cols)).astype(jnp.bfloat16)
        dq_acc = dq_acc + jnp.einsum(
            "shij,jshd->ishd", d_score, key_block, preferred_element_type=jnp.float32
        )
        d_key = (
            jnp.einsum("shij,ishd->jshd", d_score, query_heads, preferred_element_type=jnp.float32)
            * SCORE_SCALE
        )
        d_value = jnp.einsum(
            "shij,ishd->jshd",
            unnorm.astype(jnp.bfloat16),
            d_mixture,
            preferred_element_type=jnp.float32,
        )
        stacked = jnp.concatenate(
            [
                d_key.reshape(step_rows, seq_count, feature_count),
                d_value.reshape(step_rows, seq_count, feature_count),
            ],
            axis=-1,
        )
        return (dq_acc, stacked)

    dq_sum, stacked_all = lax.scan(
        key_visit_block,
        jnp.zeros(query_heads.shape, jnp.float32),
        (key_blocks, value_blocks, seg_blocks),
    )
    return (dq_sum, stacked_all.reshape(row_count, seq_count, 2 * feature_count))


def body(
    tokens,
    segment_ids,
    w_query,
    w_key,
    w_value,
    w_output,
    w_inner,
    w_outer,
    b_query,
    b_value,
    b_output,
    b_inner,
    b_outer,
    gain_first,
    shift_first,
    gain_second,
    shift_second,
    cotangent,
):
    tok_rows, seq_count, feature_count = tokens.shape
    rows_total = tok_rows * seq_count
    gathered = (
        lax.all_gather(w_query, "seq", axis=0, tiled=True),
        lax.all_gather(w_key, "seq", axis=0, tiled=True),
        lax.all_gather(w_value, "seq", axis=0, tiled=True),
        lax.all_gather(w_output, "seq", axis=0, tiled=True),
        lax.all_gather(w_inner, "seq", axis=0, tiled=True),
        lax.all_gather(w_outer, "seq", axis=0, tiled=True),
        lax.all_gather(b_query, "seq", axis=0, tiled=True),
        lax.all_gather(b_value, "seq", axis=0, tiled=True),
        lax.all_gather(b_output, "seq", axis=0, tiled=True),
        lax.all_gather(b_inner, "seq", axis=0, tiled=True),
        lax.all_gather(b_outer, "seq", axis=0, tiled=True),
        lax.all_gather(gain_first, "seq", axis=0, tiled=True),
        lax.all_gather(shift_first, "seq", axis=0, tiled=True),
        lax.all_gather(gain_second, "seq", axis=0, tiled=True),
        lax.all_gather(shift_second, "seq", axis=0, tiled=True),
    )
    query_weight, key_weight, value_weight, output_weight, inner_weight, outer_weight = gathered[:6]
    (
        query_bias,
        value_bias,
        output_bias,
        inner_bias,
        outer_bias,
        gain_one,
        shift_one,
        gain_two,
        shift_two,
    ) = [vector.astype(jnp.float32) for vector in gathered[6:]]
    flat_rows = tokens.reshape(rows_total, feature_count)
    flat_float = flat_rows.astype(jnp.float32)
    seg_local = jnp.transpose(segment_ids)
    queries = (matmul(flat_rows, query_weight) + query_bias).astype(jnp.bfloat16)
    key_rows = matmul(flat_rows, key_weight).astype(jnp.bfloat16)
    value_rows = (matmul(flat_rows, value_weight) + value_bias).astype(jnp.bfloat16)
    query_heads = queries.reshape(tok_rows, seq_count, H, DH)
    key_block_rows = key_rows.reshape(tok_rows, seq_count, feature_count)
    value_block_rows = value_rows.reshape(tok_rows, seq_count, feature_count)
    initial = (
        jnp.zeros((seq_count, H, tok_rows), jnp.float32),
        jnp.zeros((tok_rows, seq_count, H, DH), jnp.float32),
    )
    totals, mixture = attend_keys(
        query_heads,
        seg_local,
        initial,
        (
            lax.all_gather(key_block_rows, "ctx", axis=0, tiled=True),
            lax.all_gather(value_block_rows, "ctx", axis=0, tiled=True),
            lax.all_gather(seg_local, "ctx", axis=0, tiled=True),
        ),
    )
    denominator = jnp.transpose(totals, (2, 0, 1))[..., None]
    attended = mixture / denominator
    context = attended.astype(jnp.bfloat16).reshape(rows_total, feature_count)
    first_in = matmul(context, output_weight) + output_bias + flat_float
    hidden, normed_one, inverse_one = norm_forward(first_in, gain_one, shift_one)
    hidden_low = hidden.astype(jnp.bfloat16)
    inner_pre = matmul(hidden_low, inner_weight) + inner_bias
    activated, gelu_slope = gelu_parts(inner_pre)
    act_low = activated.astype(jnp.bfloat16)
    second_in = matmul(act_low, outer_weight) + outer_bias + hidden
    result, normed_two, inverse_two = norm_forward(second_in, gain_two, shift_two)
    layer_out = result.astype(jnp.bfloat16).reshape(tok_rows, seq_count, feature_count)
    upstream = cotangent.astype(jnp.float32).reshape(rows_total, feature_count)
    d_second, dgain_second, dshift_second = norm_backward(
        upstream, normed_two, inverse_two, gain_two
    )
    d_outer = d_second.astype(jnp.bfloat16)
    dbias_outer = jnp.sum(d_outer.astype(jnp.float32), axis=0)
    dweight_outer = matmul_tn(act_low, d_outer)
    d_inner = (matmul_nt(d_outer, outer_weight) * gelu_slope).astype(jnp.bfloat16)
    dbias_inner = jnp.sum(d_inner.astype(jnp.float32), axis=0)
    dweight_inner = matmul_tn(hidden_low, d_inner)
    d_hidden = matmul_nt(d_inner, inner_weight) + d_second
    d_first, dgain_first, dshift_first = norm_backward(d_hidden, normed_one, inverse_one, gain_one)
    d_branch = d_first.astype(jnp.bfloat16)
    dbias_output = jnp.sum(d_branch.astype(jnp.float32), axis=0)
    dweight_output = matmul_tn(context, d_branch)
    d_context = (
        matmul_nt(d_branch, output_weight).astype(jnp.bfloat16).reshape(tok_rows, seq_count, H, DH)
    )
    d_float = d_context.astype(jnp.float32)
    d_mixture = (d_float / denominator).astype(jnp.bfloat16)
    correction = jnp.sum(d_float * attended, axis=-1) / denominator[..., 0]
    key_all, value_all, seg_all = (
        lax.all_gather(key_block_rows, "ctx", axis=0, tiled=True),
        lax.all_gather(value_block_rows, "ctx", axis=0, tiled=True),
        lax.all_gather(seg_local, "ctx", axis=0, tiled=True),
    )
    dq_sum, term_rows = key_side(
        query_heads, d_mixture, correction, seg_local, key_all, value_all, seg_all
    )
    summed = lax.psum_scatter(term_rows, "ctx", scatter_dimension=0, tiled=True)
    d_query = (dq_sum * SCORE_SCALE).astype(jnp.bfloat16)
    d_key = summed[..., :feature_count].astype(jnp.bfloat16)
    d_value = summed[..., feature_count:].astype(jnp.bfloat16)
    dq_flat = d_query.reshape(rows_total, feature_count)
    dk_flat = d_key.reshape(rows_total, feature_count)
    dv_flat = d_value.reshape(rows_total, feature_count)
    dweight_query = matmul_tn(flat_rows, dq_flat)
    dweight_key = matmul_tn(flat_rows, dk_flat)
    dweight_value = matmul_tn(flat_rows, dv_flat)
    dbias_query = jnp.sum(dq_flat.astype(jnp.float32), axis=0)
    dbias_value = jnp.sum(dv_flat.astype(jnp.float32), axis=0)
    grad_tokens = (
        matmul_nt(dq_flat, query_weight)
        + matmul_nt(dk_flat, key_weight)
        + matmul_nt(dv_flat, value_weight)
        + d_first
    )
    shards = (
        lax.psum_scatter(
            dweight_query.astype(jnp.bfloat16), "seq", scatter_dimension=0, tiled=True
        ).astype(jnp.float32),
        lax.psum_scatter(
            dweight_key.astype(jnp.bfloat16), "seq", scatter_dimension=0, tiled=True
        ).astype(jnp.float32),
        lax.psum_scatter(
            dweight_value.astype(jnp.bfloat16), "seq", scatter_dimension=0, tiled=True
        ).astype(jnp.float32),
        lax.psum_scatter(
            dweight_output.astype(jnp.bfloat16), "seq", scatter_dimension=0, tiled=True
        ).astype(jnp.float32),
        lax.psum_scatter(
            dweight_inner.astype(jnp.bfloat16), "seq", scatter_dimension=0, tiled=True
        ).astype(jnp.float32),
        lax.psum_scatter(
            dweight_outer.astype(jnp.bfloat16), "seq", scatter_dimension=0, tiled=True
        ).astype(jnp.float32),
        lax.psum_scatter(
            dbias_query.astype(jnp.bfloat16), "seq", scatter_dimension=0, tiled=True
        ).astype(jnp.float32),
        lax.psum_scatter(
            dbias_value.astype(jnp.bfloat16), "seq", scatter_dimension=0, tiled=True
        ).astype(jnp.float32),
        lax.psum_scatter(
            dbias_output.astype(jnp.bfloat16), "seq", scatter_dimension=0, tiled=True
        ).astype(jnp.float32),
        lax.psum_scatter(
            dbias_inner.astype(jnp.bfloat16), "seq", scatter_dimension=0, tiled=True
        ).astype(jnp.float32),
        lax.psum_scatter(
            dbias_outer.astype(jnp.bfloat16), "seq", scatter_dimension=0, tiled=True
        ).astype(jnp.float32),
        lax.psum_scatter(
            dgain_first.astype(jnp.bfloat16), "seq", scatter_dimension=0, tiled=True
        ).astype(jnp.float32),
        lax.psum_scatter(
            dshift_first.astype(jnp.bfloat16), "seq", scatter_dimension=0, tiled=True
        ).astype(jnp.float32),
        lax.psum_scatter(
            dgain_second.astype(jnp.bfloat16), "seq", scatter_dimension=0, tiled=True
        ).astype(jnp.float32),
        lax.psum_scatter(
            dshift_second.astype(jnp.bfloat16), "seq", scatter_dimension=0, tiled=True
        ).astype(jnp.float32),
    )
    finals = lax.psum(
        (
            shards[0],
            shards[1],
            shards[2],
            shards[3],
            shards[4],
            shards[5],
            shards[6],
            shards[7],
            shards[8],
            shards[9],
            shards[10],
            shards[11],
            shards[12],
            shards[13],
            shards[14],
        ),
        "ctx",
    )
    return (
        layer_out,
        grad_tokens.reshape(tok_rows, seq_count, feature_count),
        finals[0],
        finals[1],
        finals[2],
        finals[3],
        finals[4],
        finals[5],
        finals[6],
        finals[7],
        finals[8],
        finals[9],
        finals[10],
        finals[11],
        finals[12],
        finals[13],
        finals[14],
    )


MESH = pl.DeviceIdType.MESH
BIG = 1e30
F32, BF16 = jnp.float32, jnp.bfloat16


def remote(src, dst, send_sem, recv_sem, seq, ctx):
    return pltpu.make_async_remote_copy(
        src_ref=src,
        dst_ref=dst,
        send_sem=send_sem,
        recv_sem=recv_sem,
        device_id=(seq, ctx),
        device_id_type=MESH,
    )


def greet(seq, ctx):
    barrier = pltpu.get_barrier_semaphore()
    for hop in range(1, 8):
        pl.semaphore_signal(
            barrier, inc=1, device_id=(seq, lax.rem(ctx + hop, 8)), device_id_type=MESH
        )
    for hop in range(1, 4):
        pl.semaphore_signal(
            barrier, inc=1, device_id=(lax.rem(seq + hop, 4), ctx), device_id_type=MESH
        )
    pl.semaphore_wait(barrier, 10)


def flip(index, bit):
    low = lax.rem(index // bit, 2)
    return index + bit - 2 * bit * low


def head_window(group):
    start = group * 192
    inside = lax.rem(group, 2) * 64
    return pl.multiple_of(start - inside, 128), pl.multiple_of(inside, 64)


def span(start, size, unit=16):
    return pl.ds(pl.multiple_of(start, unit), size)


VECTORS = list(
    dict(
        b_query=0,
        b_value=0,
        b_output=0,
        b_outer=0,
        gain_one=0,
        shift_one=0,
        gain_two=0,
        shift_two=0,
    )
)
INPUTS = [
    *dict(x=0, cot=0, seg=0),
    *VECTORS,
    *dict(b_inner=0, wq=0, wk=0, wv=0, wo=0, wi=0, wu=0),
]
OUTPUTS = list(dict(layer=0, grad=0, fu=0, fi=0, fo=0, fg=0, vec_sum=0, bias_sum=0))
FIRST = "yxyyxzxxx"
OVER_Y = (1, 0, 1, 0, 1, 0, 1)

SCRATCH = dict(
    x_rows=((2, 128, 768), BF16),
    cot_rows=((2, 128, 768), BF16),
    layer_rows=((2, 128, 768), BF16),
    grad_rows=((2, 128, 768), F32),
    fg_all=((4, 3, 192, 256), BF16),
    seg_own=((2, 8, 128), jnp.int32),
    seg_all=((8, 8, 128), jnp.int32),
    pack_own=((16, 768), BF16),
    pack_all=((4, 16, 768), BF16),
    rows=((8, 768), F32),
    wo_full=((4, 192, 768), BF16),
    wi_full=((4, 192, 3072), BF16),
    wu_full=((4, 768, 768), BF16),
    xs=((8, 128, 768), BF16),
    wg=((3, 4, 192, 256), BF16),
    qa=((3, 128, 1024), BF16),
    ka=((3, 128, 1024), BF16),
    vt=((3, 64, 1024), BF16),
    ot=((3, 64, 1024), F32),
    sums=((3, 1, 1024), F32),
    key_rows=((1024, 128), BF16),
    o_send=((192, 1024), BF16),
    ctx_t=((768, 256), BF16),
    normed=((256, 768), F32),
    inverse=((256, 1), F32),
    low=((256, 768), BF16),
    low_t=((768, 256), BF16),
    act_t=((4, 768, 256), BF16),
    slope=((4, 256, 768), F32),
    work=((256, 768), F32),
    d_rows=((256, 768), BF16),
    v_rows=((16, 768), F32),
    gu=((4, 768, 768), BF16),
    gi=((4, 192, 3072), BF16),
    go=((4, 192, 768), BF16),
    core_u=((2, 768, 768), BF16),
    core_i=((2, 192, 3072), BF16),
    core_o=((2, 192, 768), BF16),
    xr_u=((768, 768), BF16),
    xr_i=((192, 3072), BF16),
    xr_o=((192, 768), BF16),
    rcv_u=((768, 768), BF16),
    rcv_i=((192, 3072), BF16),
    rcv_o=((192, 768), BF16),
    fin_u=((768, 768), BF16),
    fin_i=((192, 3072), BF16),
    fin_o=((192, 768), BF16),
    tot_u=((4, 96, 384), F32),
    tot_i=((4, 96, 384), F32),
    tot_o=((96, 384), F32),
    do_send=((768, 256), BF16),
    do_all=((192, 1024), BF16),
    du=((64, 1024), BF16),
    c_row=((1, 1024), F32),
    value_rows=((1024, 64), BF16),
    dk_acc=((64, 1024), F32),
    dv_acc=((64, 1024), F32),
    d_all=((3, 256, 1024), BF16),
    g_all=((3, 4, 192, 256), BF16),
    g_core=((3, 2, 192, 256), BF16),
    g_xs=((3, 192, 256), BF16),
    g_xr=((3, 192, 256), BF16),
    g_half=((3, 192, 256), BF16),
    g_mir=((3, 96, 256), BF16),
    dx_y=((4, 768, 128), BF16),
    dx_l=((2, 768, 128), BF16),
    dx_h=((768, 128), BF16),
    two_y=((max(1, FIRST.count("y")), 192, 384), BF16),
    two_z=((max(1, FIRST.count("z")), 96, 768), BF16),
    v_own=((4, 16, 256), F32),
    v_recv=((4, 16, 256), F32),
    v_all=((8, 16, 256), F32),
    b_send=((2, 8, 256), F32),
    b_recv=((8, 2, 8, 256), F32),
)
SEMAPHORES = dict(
    loc=(36,),
    w_ss=(7, 5),
    w_rs=(7, 5),
    x_ss=(12,),
    x_rs=(12,),
    s_ss=(8,),
    s_rs=(8,),
    p_ss=(4,),
    p_rs=(4,),
    g_ss=(3, 3),
    g_rs=(3, 3),
    o_ss=(3, 8),
    o_rs=(3, 8),
    r_ss=(9, 10),
    r_rs=(9, 10),
    do_ss=(3, 8),
    do_rs=(3, 8),
    dx_ss=(7,),
    dx_rs=(7,),
    v_ss=(2, 8),
    v_rs=(2, 8),
    b_ss=(8,),
    b_rs=(8,),
    h_ss=(7, 3),
    h_rs=(7, 3),
)


def layer_kernel(*refs):
    r = types.SimpleNamespace(
        **dict(zip(INPUTS + OUTPUTS + list(SCRATCH) + list(SEMAPHORES), refs))
    )
    seq, ctx = lax.axis_index("seq"), lax.axis_index("ctx")
    plane = seq // 2
    mate, across = flip(seq, 1), flip(seq, 2)
    across_mate = flip(mate, 2)
    beside, paired, mirror = flip(ctx, 1), flip(ctx, 2), flip(ctx, 4)
    bit_y, bit_l, bit_h = lax.rem(ctx, 2), lax.rem(ctx // 2, 2), ctx // 4
    side, group = ctx // 4, lax.rem(ctx, 4)
    window, inside = head_window(group)
    own_lanes = span(ctx * 128, 128, 128)
    sent = []

    def wi_cut(k, where):
        which = where if k == 1 else 1 - where
        return span(which * 1536, 1536, 128)

    def w_views(k, where):
        if k == 0:
            return r.wo, lambda owner: r.wo_full.at[owner], 96
        if k in (1, 2):
            cols = wi_cut(k, where)
            return r.wi.at[:, cols], lambda owner: r.wi_full.at[owner, :, cols], 96
        part = slice(192 * (k - 3), 192 * (k - 2))
        return r.wu.at[part], lambda owner: r.wu_full.at[owner, part], 96

    beside_of = [
        (beside, bit_y) if over_y else (paired, bit_l) for over_y in OVER_Y
    ]

    def half(view, rows, which):
        return view.at[span(which * rows, rows, 32)]

    def w_copy(k, leg):
        sems = r.w_ss.at[k, leg], r.w_rs.at[k, leg]
        shard, full, rows = w_views(k, 1 - plane if leg == 1 else plane)
        partner, bit = beside_of[k]
        if leg == 0:
            return remote(shard, full(seq), *sems, mate, ctx)
        if leg == 1:
            return remote(
                half(shard, rows, bit), half(full(seq), rows, bit), *sems, across, ctx
            )
        which = bit if leg in (2, 3) else 1 - bit
        came = half(full(across), rows, which)
        return remote(came, came, *sems, *((seq, partner) if leg == 2 else (mate, ctx)))

    def w_wait(k, leg):
        shard, full, rows = w_views(k, plane)
        bit = beside_of[k][1]
        spots = (
            lambda: full(mate),
            lambda: half(full(across), rows, bit),
            lambda: half(full(across), rows, 1 - bit),
            lambda: half(full(across_mate), rows, bit),
            lambda: half(full(across_mate), rows, 1 - bit),
        )
        spot = spots[leg]()
        remote(spot, spot, r.w_ss.at[k, leg], r.w_rs.at[k, leg], mate, ctx).wait_recv()

    def pass_across(k):
        w_wait(k, 1)
        w_copy(k, 2).start()
        w_copy(k, 3).start()

    def pass_beside(k):
        w_wait(k, 2)
        w_copy(k, 4).start()

    def w_done(k):
        for leg in (0, 3, 4):
            w_wait(k, leg)

    group_refs = (r.wq, r.wk, r.wv)
    g_local, w_local = [], []
    for which in range(3):
        g_local.append(
            pltpu.make_async_copy(
                group_refs[which].at[:, pl.ds(window, 256)],
                r.wg.at[which, seq],
                r.loc.at[which],
            )
        )
    for n, (ref, full) in enumerate(
        ((r.wo, r.wo_full), (r.wi, r.wi_full), (r.wu, r.wu_full))
    ):
        w_local.append(pltpu.make_async_copy(ref, full.at[seq], r.loc.at[3 + n]))
    own_block = pltpu.make_async_copy(r.x.at[side], r.xs.at[ctx], r.loc.at[6])
    for which in range(2):
        r.seg_own[which] = jnp.broadcast_to(r.seg[which : which + 1], (8, 128))
    r.pack_own[...] = jnp.zeros((16, 768), BF16)
    for n, name in enumerate(VECTORS):
        r.pack_own[n : n + 1, 0:192] = getattr(r, name)[...].reshape(1, 192)
    r.pack_own[8:9] = r.b_inner[...].reshape(1, 768)
    x_local = pltpu.make_async_copy(r.x, r.x_rows, r.loc.at[26])
    cot_local = pltpu.make_async_copy(r.cot, r.cot_rows, r.loc.at[27])
    own_seg = pltpu.make_async_copy(r.seg_own.at[side], r.seg_all.at[ctx], r.loc.at[7])
    own_pack = pltpu.make_async_copy(r.pack_own, r.pack_all.at[seq], r.loc.at[8])
    for copy in g_local + [own_block, own_seg, own_pack, x_local, cot_local] + w_local:
        copy.start()
    r.v_rows[...] = jnp.zeros((16, 768), F32)
    for which in range(3):
        r.d_all[which] = jnp.zeros((256, 1024), BF16)

    greet(seq, ctx)

    def send(*args):
        copy = remote(*args)
        copy.start()
        sent.append(copy)

    def landed(spot, send_sem, recv_sem):
        remote(spot, spot, send_sem, recv_sem, seq, beside).wait_recv()

    for hop in range(1, 8):
        other = lax.rem(ctx + hop, 8)
        send(
            r.seg_own.at[other // 4],
            r.seg_all.at[ctx],
            r.s_ss.at[hop],
            r.s_rs.at[hop],
            seq,
            other,
        )
    for hop in range(1, 4):
        other = lax.rem(seq + hop, 4)
        send(r.pack_own, r.pack_all.at[seq], r.p_ss.at[hop], r.p_rs.at[hop], other, ctx)
    for n in range(2):
        part = slice(64 * n, 64 * n + 64)
        send(
            r.x.at[1 - side, part],
            r.xs.at[ctx, part],
            r.x_ss.at[n],
            r.x_rs.at[n],
            seq,
            mirror,
        )
    for n, other in enumerate((beside, paired)):
        send(
            r.x.at[side], r.xs.at[ctx], r.x_ss.at[2 + n], r.x_rs.at[2 + n], seq, other
        )
    for which in range(3):
        for n, other in enumerate((mate, across)):
            send(
                group_refs[which].at[:, pl.ds(window, 256)],
                r.wg.at[which, seq],
                r.g_ss.at[which, n],
                r.g_rs.at[which, n],
                other,
                ctx,
            )
    for k in range(7):
        w_copy(k, 0).start()
        w_copy(k, 1).start()

    t = types.SimpleNamespace()
    to_hbm_all = []
    early = []

    def to_hbm(source, target):
        copy = pltpu.make_async_copy(source, target, r.loc.at[28 + len(to_hbm_all)])
        copy.start()
        to_hbm_all.append(copy)

    def task(run):
        setattr(t, run.__name__, run)

    t.pa = [functools.partial(pass_across, k) for k in range(7)]
    t.pb = [functools.partial(pass_beside, k) for k in range(7)]

    @task
    def grp():
        for which in range(3):
            spot = r.wg.at[which, across]
            landed(spot, r.g_ss.at[which, 1], r.g_rs.at[which, 1])
            send(spot, spot, r.g_ss.at[which, 2], r.g_rs.at[which, 2], mate, ctx)

    diagonal = flip(beside, 2)

    def pass_on(source, half, arrived_by, leg, other):
        spot = r.xs.at[source, 64 * half : 64 * half + 64]
        if arrived_by is not None:
            landed(spot, r.x_ss.at[arrived_by], r.x_rs.at[arrived_by])
        send(spot, spot, r.x_ss.at[leg], r.x_rs.at[leg], seq, other)

    @task
    def nf():
        for n, other in enumerate((beside, paired)):
            landed(r.xs.at[other], r.x_ss.at[2 + n], r.x_rs.at[2 + n])
        pass_on(beside, 0, None, 4, paired)
        pass_on(paired, 1, None, 5, beside)

    def far_half(half):
        pass_on(mirror, half, half, 6 + 2 * half, beside)
        pass_on(mirror, half, None, 7 + 2 * half, paired)

    t.far = [functools.partial(far_half, half) for half in range(2)]
    t.ff = [
        functools.partial(pass_on, flip(beside, 4), 0, 6, 10, paired),
        functools.partial(pass_on, flip(paired, 4), 1, 9, 11, beside),
    ]

    @task
    def small():
        for which in range(3):
            g_local[which].wait()
            for n, owner in ((0, mate), (2, across_mate)):
                landed(
                    r.wg.at[which, owner], r.g_ss.at[which, n], r.g_rs.at[which, n]
                )
        own_pack.wait()
        for hop in range(1, 4):
            landed(
                r.pack_all.at[lax.rem(seq + 4 - hop, 4)], r.p_ss.at[hop], r.p_rs.at[hop]
            )
        own_seg.wait()
        for hop in range(1, 8):
            landed(
                r.seg_all.at[lax.rem(ctx + 8 - hop, 8)], r.s_ss.at[hop], r.s_rs.at[hop]
            )
        lane = lax.broadcasted_iota(jnp.int32, (256, 768), 1)
        at = lax.broadcasted_iota(jnp.int32, (256, 768), 0)
        rows = jnp.zeros((8, 768), F32)
        for owner in range(4):
            chosen = ((lane == at + 192 * owner) & (at < 192)).astype(BF16)
            rows += matmul(r.pack_all[owner, 0:8, 0:256], chosen)
        r.rows[...] = rows

    @task
    def qkv():
        own_block.wait()
        for source, half, leg in (
            (diagonal, 0, 4),
            (diagonal, 1, 5),
            (flip(paired, 4), 0, 7),
            (flip(beside, 4), 1, 8),
            (flip(diagonal, 4), 0, 10),
            (flip(diagonal, 4), 1, 11),
        ):
            spot = r.xs.at[source, 64 * half : 64 * half + 64]
            landed(spot, r.x_ss.at[leg], r.x_rs.at[leg])
        tokens = r.xs[...].reshape(1024, 768)
        own_rows = r.pack_all[group]
        qkv = []
        for which in range(3):
            weight = r.wg[which].reshape(768, 256)
            product = matmul_nt(weight.T, tokens)
            if which != 1:
                bias = own_rows[which // 2 : which // 2 + 1, 0:256].astype(F32)
                column = jnp.broadcast_to(bias, (128, 256)).T
                shifted = jnp.where(inside == 0, column, pltpu.roll(column, 64, 0))
                product = product + jnp.concatenate([shifted] * 8, axis=1)
            part = product.astype(BF16)
            if which == 0:
                part = part * jnp.bfloat16(SCORE_SCALE)
            qkv.append(part)
        number = jnp.concatenate(
            [r.seg_all[block, 0:1] for block in range(8)], axis=1
        )
        hot = lax.broadcasted_iota(jnp.int32, (16, 1024), 0) == number
        query_marks = jnp.where(hot, 1.0, 0.0).astype(BF16)
        key_marks = jnp.where(hot, 0.0, -BIG).astype(BF16)
        blank = jnp.zeros((48, 1024), BF16)
        for head in range(3):
            parts = [
                jnp.where(
                    inside != 0,
                    part[64 * head + 64 : 64 * head + 128],
                    part[64 * head : 64 * head + 64],
                )
                for part in qkv
            ]
            r.qa[head] = jnp.concatenate([parts[0], query_marks, blank], axis=0)
            r.ka[head] = jnp.concatenate([parts[1], key_marks, blank], axis=0)
            r.vt[head] = parts[2]

    my_rows = span(group * 192, 192, 64)
    my_lanes = span(side * 128, 128, 128)
    own_o = pltpu.make_async_copy(
        r.o_send.at[:, own_lanes], r.ctx_t.at[my_rows, my_lanes], r.loc.at[9]
    )

    def attend_head(head):
        r.key_rows[...] = r.ka[head].T

        def attend(block, unused):
            lanes = span(block * 256, 256, 256)
            scores = matmul(r.key_rows[...], r.qa[head, :, lanes])
            unnorm = jnp.exp(scores)
            total = jnp.sum(unnorm, axis=0, keepdims=True)
            attended = matmul(r.vt[head], unnorm.astype(BF16)) / total
            r.ot[head, :, lanes] = attended
            r.sums[head, :, lanes] = total
            r.o_send[64 * head : 64 * head + 64, lanes] = attended.astype(BF16)
            return unused

        lax.fori_loop(0, 4, attend, 0)
        if head == 2:
            own_o.start()
        part = slice(64 * head, 64 * head + 64)
        for hop in range(1, 8):
            other = lax.rem(ctx + hop, 8)
            send(
                r.o_send.at[part, span(other * 128, 128, 128)],
                r.ctx_t.at[span(group * 192 + 64 * head, 64, 64), my_lanes],
                r.o_ss.at[head, hop],
                r.o_rs.at[head, hop],
                seq,
                other,
            )

    t.at = [functools.partial(attend_head, head) for head in range(3)]

    def row_vec(n):
        return r.rows[n : n + 1]

    @task
    def fn():
        own_o.wait()
        for head in range(3):
            for hop in range(1, 8):
                other = lax.rem(ctx + 8 - hop, 8)
                spot = r.ctx_t.at[
                    span(lax.rem(other, 4) * 192 + 64 * head, 64, 64),
                    span((other // 4) * 128, 128, 128),
                ]
                landed(spot, r.o_ss.at[head, hop], r.o_rs.at[head, hop])
        w_local[0].wait()
        x_local.wait()
        w_done(0)

        def first_norm(which, unused):
            at, lanes = span(which * 128, 128, 128), span(which * 128, 128, 128)
            value = (
                matmul(r.ctx_t[:, lanes].T, r.wo_full[...].reshape(768, 768))
                + row_vec(2)
                + r.x_rows[which].astype(F32)
            )
            hidden, normed, inverse = norm_forward(value, row_vec(4), row_vec(5))
            r.normed[at] = normed
            r.inverse[at] = inverse
            part = hidden.astype(BF16)
            r.low[at] = part
            r.low_t[:, lanes] = part.T
            r.work[at] = hidden + row_vec(3)
            return unused

        lax.fori_loop(0, 2, first_norm, 0)

    def inner_weight(n):
        return r.wi_full[:, :, span(n * 768, 768, 128)].reshape(768, 768)

    def feed(where):
        def visit(step, unused):
            n, which = where * 2 + step // 2, lax.rem(step, 2)
            at = span(which * 128, 128, 128)
            value = matmul(r.low[at], inner_weight(n)) + r.pack_all[n, 8:9].astype(F32)
            act, slope = gelu_parts(value)
            part = act.astype(BF16)
            r.slope[n, at] = slope
            r.act_t[n, :, at] = part.T
            r.work[at] += matmul(part, r.wu_full[n])
            return unused

        lax.fori_loop(0, 4, visit, 0)

    @task
    def fe0():
        w_local[1].wait()
        w_local[2].wait()
        w_done(1)
        for k in range(3, 7):
            w_wait(k, 0)
        feed(plane)

    @task
    def fe1():
        w_done(2)
        for k in range(3, 7):
            w_wait(k, 3)
            w_wait(k, 4)
        feed(1 - plane)

    def tally(n, value):
        r.v_rows[n : n + 1] += jnp.sum(value, axis=0, keepdims=True)

    @task
    def sn():
        def second_norm(which, unused):
            at = span(which * 128, 128, 128)
            result, normed, inverse = norm_forward(r.work[at], row_vec(6), row_vec(7))
            r.layer_rows[which] = result.astype(BF16)
            upstream = r.cot_rows[which].astype(F32)
            scaled = upstream * row_vec(6)
            back = inverse * (
                scaled
                - jnp.mean(scaled, axis=-1, keepdims=True)
                - normed * jnp.mean(scaled * normed, axis=-1, keepdims=True)
            )
            tally(4, upstream * normed)
            tally(5, upstream)
            r.work[at] = back
            part = back.astype(BF16)
            r.d_rows[at] = part
            tally(1, part.astype(F32))
            return unused

        cot_local.wait()
        lax.fori_loop(0, 2, second_norm, 0)
        to_hbm(r.layer_rows, r.layer)
        early.append(len(sent))

    chunks = [
        (r.gu, r.fu, r.core_u, r.xr_u, r.rcv_u, r.fin_u, r.tot_u.at[k], 192 * k, 192, 0, 768)
        for k in range(4)
    ]
    chunks += [
        (r.gi, r.fi, r.core_i, r.xr_i, r.rcv_i, r.fin_i, r.tot_i.at[k], 0, 192, 768 * k, 768)
        for k in range(4)
    ]
    chunks += [
        (r.go, r.fo, r.core_o, r.xr_o, r.rcv_o, r.fin_o, r.tot_o, 0, 192, 0, 768),
    ]

    def reduce_steps(k, first):
        grad, out, core, arrived, rcv, fin, total, row, rows, col, cols = chunks[k]
        rr, cc = pl.ds(row, rows), pl.ds(col, cols)
        wide = cols // 2
        mine = span(col + bit_y * wide, wide, 128)
        other = span(col + (1 - bit_y) * wide, wide, 128)
        keep_l = span(row + bit_l * (rows // 2), rows // 2)
        give_l = span(row + (1 - bit_l) * (rows // 2), rows // 2)
        keep_h = span(row + bit_l * (rows // 2) + bit_h * (rows // 4), rows // 4)
        give_h = span(row + bit_l * (rows // 2) + (1 - bit_h) * (rows // 4), rows // 4)
        spot_h = span(row + (1 - bit_l) * (rows // 2), rows // 4)
        tot_keep, tot_give = (
            span(bit_h * (rows // 4), rows // 4),
            span((1 - bit_h) * (rows // 4), rows // 4),
        )
        owner = (seq, across)

        def sems(leg):
            return r.r_ss.at[k, leg], r.r_rs.at[k, leg]

        to_core = [
            remote(grad.at[mate, rr, cc], core.at[0, rr, cc], *sems(0), mate, ctx),
            remote(
                grad.at[across_mate, rr, cc], core.at[1, rr, cc], *sems(1), mate, ctx
            ),
        ]

        def add(at, lanes, slot, *more):
            value = grad[owner[slot], at, lanes].astype(F32) + core[
                slot, at, lanes
            ].astype(F32)
            for ref in more:
                value += ref[at, lanes].astype(F32)
            return value

        def put(at, lanes, slot, *more):
            core[slot, at, lanes] = add(at, lanes, slot, *more).astype(BF16)

        def spread(at, lanes, leg, target):
            spot = fin.at[at, lanes]
            return remote(spot, spot, *sems(leg), seq, target)

        to_h = remote(
            arrived.at[give_h, mine], rcv.at[spot_h, other], *sems(5), seq, mirror
        )

        def begin():
            for copy in to_core:
                copy.start()

        def cores_in():
            for copy in to_core:
                copy.wait_recv()

        if first == "x":
            to_x = remote(core.at[1, rr, cc], arrived.at[rr, cc], *sems(2), across, ctx)
            to_y = remote(arrived.at[rr, other], rcv.at[rr, other], *sems(3), seq, beside)
            at_y = remote(arrived.at[rr, mine], rcv.at[rr, mine], *sems(3), seq, beside)
            firsts = [to_x, to_y]

            def one():
                put(rr, cc, 1)
                to_x.start()

            def two():
                arrived[rr, other] = add(rr, other, 0, arrived).astype(BF16)
                to_y.start()

        elif first == "y":
            extra = r.two_y.at[FIRST[:k].count("y")]
            to_y = [
                remote(
                    core.at[0, rr, other], rcv.at[rr, other], *sems(3), seq, beside
                ),
                remote(core.at[1, rr, other], extra, *sems(9), seq, beside),
            ]
            at_y = [
                remote(core.at[0, rr, mine], rcv.at[rr, mine], *sems(3), seq, beside),
                remote(core.at[1, rr, mine], extra, *sems(9), seq, beside),
            ]
            to_x = remote(
                core.at[1, rr, mine], arrived.at[rr, mine], *sems(2), across, ctx
            )
            firsts = to_y + [to_x]

            def one():
                for slot in range(2):
                    put(rr, other, slot)
                    to_y[slot].start()

            def two():
                for copy in at_y:
                    copy.wait_recv()
                core[1, rr, mine] = (add(rr, mine, 1) + extra[...].astype(F32)).astype(
                    BF16
                )
                to_x.start()

        elif first == "w":
            to_x = remote(core.at[1, rr, cc], arrived.at[rr, cc], *sems(2), across, ctx)
            to_l = remote(
                arrived.at[give_l, cc], rcv.at[give_l, cc], *sems(4), seq, paired
            )
            at_l = [
                remote(arrived.at[keep_l, cc], rcv.at[keep_l, cc], *sems(4), seq, paired)
            ]
            firsts = [to_x, to_l]

            def one():
                put(rr, cc, 1)
                to_x.start()

            def two():
                arrived[give_l, cc] = add(give_l, cc, 0, arrived).astype(BF16)
                to_l.start()

        else:
            extra = r.two_z.at[FIRST[:k].count("z")]
            to_l = [
                remote(core.at[0, give_l, cc], rcv.at[give_l, cc], *sems(4), seq, paired),
                remote(core.at[1, give_l, cc], extra, *sems(9), seq, paired),
            ]
            at_l = [
                remote(core.at[0, keep_l, cc], rcv.at[keep_l, cc], *sems(4), seq, paired),
                remote(core.at[1, keep_l, cc], extra, *sems(9), seq, paired),
            ]
            to_x = remote(
                core.at[1, keep_l, cc], arrived.at[keep_l, cc], *sems(2), across, ctx
            )
            firsts = to_l + [to_x]

            def one():
                for slot in range(2):
                    put(give_l, cc, slot)
                    to_l[slot].start()

            def two():
                for copy in at_l:
                    copy.wait_recv()
                core[1, keep_l, cc] = (
                    add(keep_l, cc, 1) + extra[...].astype(F32)
                ).astype(BF16)
                to_x.start()

        if first in "zw":
            to_y = remote(
                arrived.at[keep_l, other], rcv.at[give_l, other], *sems(3), seq, beside
            )
            at_y = remote(
                arrived.at[keep_l, mine], rcv.at[give_l, mine], *sems(3), seq, beside
            )
            firsts = firsts + [to_y]

            def three():
                for copy in at_l if first == "w" else [to_x]:
                    copy.wait_recv()
                arrived[keep_l, other] = add(keep_l, other, 0, rcv, arrived).astype(BF16)
                to_y.start()
                total[...] = add(keep_l, mine, 0, rcv, arrived)

            def four():
                at_y.wait_recv()
                total[...] += rcv[give_l, mine].astype(F32)
                arrived[give_h, mine] = total[tot_give].astype(BF16)
                to_h.start()

        else:
            to_l = remote(
                arrived.at[give_l, mine], rcv.at[give_l, other], *sems(4), seq, paired
            )
            at_l = remote(
                arrived.at[keep_l, mine], rcv.at[keep_l, other], *sems(4), seq, paired
            )
            firsts = firsts + [to_l]

            def three():
                (at_y if first == "x" else to_x).wait_recv()
                arrived[give_l, mine] = add(give_l, mine, 0, arrived, rcv).astype(BF16)
                to_l.start()
                total[...] = add(keep_l, mine, 0, arrived, rcv)

            def four():
                at_l.wait_recv()
                arrived[give_h, mine] = (
                    total[tot_give] + rcv[give_h, other].astype(F32)
                ).astype(BF16)
                to_h.start()
                total[tot_keep] += rcv[keep_h, other].astype(F32)

        def step_one():
            cores_in()
            one()

        def step_two():
            if first in "xw":
                to_x.wait_recv()
            two()

        def step_five():
            to_h.wait_recv()
            fin[keep_h, mine] = (
                total[tot_keep] + rcv[spot_h, other].astype(F32)
            ).astype(BF16)
            spread(keep_h, mine, 6, mirror).start()

        if first in "zw":
            last = [(keep_l, other, 7, beside), (keep_l, cc, 8, paired)]
            ends = [(give_l, cc)]
            middle = (keep_l, mine)
        else:
            last = [(give_l, mine, 7, paired), (rr, mine, 8, beside)]
            ends = [(rr, other)]
            middle = (keep_l, mine)

        def step_six():
            spread(give_h, mine, 6, mirror).wait_recv()
            spread(*middle, 7, last[0][3]).start()

        def step_seven():
            spread(*last[0]).wait_recv()
            spread(*last[1]).start()

        to_out = pltpu.make_async_copy(fin.at[rr, cc], out.at[rr, cc], r.loc.at[17 + k])

        def step_eight():
            spread(*ends[0], 8, last[1][3]).wait_recv()
            to_out.start()

        def end():
            for copy in (
                to_core
                + firsts
                + [
                    to_h,
                    spread(keep_h, mine, 6, mirror),
                    spread(*middle, 7, last[0][3]),
                    spread(*last[1]),
                ]
            ):
                copy.wait_send()
            to_out.wait()

        names = [
            begin,
            step_one,
            step_two,
            three,
            four,
            step_five,
            step_six,
            step_seven,
            step_eight,
            end,
        ]
        return names

    t.s = [reduce_steps(k, FIRST[k]) for k in range(9)]

    def make_outer(k):
        part = slice(192 * k, 192 * k + 192)
        for owner in (mate, across_mate):
            r.gu[owner, part] = matmul(r.act_t[owner, part], r.d_rows[...]).astype(BF16)
        t.s[k][0]()
        for owner in (across, seq):
            r.gu[owner, part] = matmul(r.act_t[owner, part], r.d_rows[...]).astype(BF16)

    t.mo = [functools.partial(make_outer, k) for k in range(4)]

    def inner_step(n):
        def inner_back(which, unused):
            at = span(which * 128, 128, 128)
            part = (matmul_nt(r.d_rows[at], r.wu_full[n]) * r.slope[n, at]).astype(BF16)
            r.low[at] = part
            tally(8 + n, part.astype(F32))
            r.work[at] += matmul_nt(part, inner_weight(n))
            return unused

        lax.fori_loop(0, 2, inner_back, 0)
        r.gi[:, :, 768 * n : 768 * n + 768] = (
            matmul(r.low_t[...], r.low[...]).astype(BF16).reshape(4, 192, 768)
        )
        t.s[4 + n][0]()

    t.ib = [functools.partial(inner_step, n) for n in range(4)]

    own_do = pltpu.make_async_copy(
        r.do_send.at[my_rows, my_lanes], r.do_all.at[:, own_lanes], r.loc.at[15]
    )

    @task
    def fb():
        def first_back(which, unused):
            at = span(which * 128, 128, 128)
            upstream, normed = r.work[at], r.normed[at]
            scaled = upstream * row_vec(4)
            back = r.inverse[at] * (
                scaled
                - jnp.mean(scaled, axis=-1, keepdims=True)
                - normed * jnp.mean(scaled * normed, axis=-1, keepdims=True)
            )
            tally(2, upstream * normed)
            tally(3, upstream)
            r.work[at] = back
            part = back.astype(BF16)
            r.low[at] = part
            tally(0, part.astype(F32))
            return unused

        lax.fori_loop(0, 2, first_back, 0)
        r.do_send[...] = matmul_nt(
            r.wo_full[...].reshape(768, 768), r.low[...]
        ).astype(BF16)
        own_do.start()
        for head in range(3):
            for hop in range(1, 8):
                other = lax.rem(ctx + hop, 8)
                send(
                    r.do_send.at[
                        span(lax.rem(other, 4) * 192 + 64 * head, 64, 64),
                        span((other // 4) * 128, 128, 128),
                    ],
                    r.do_all.at[64 * head : 64 * head + 64, own_lanes],
                    r.do_ss.at[head, hop],
                    r.do_rs.at[head, hop],
                    seq,
                    other,
                )

    @task
    def dwo():
        r.go[...] = matmul(r.ctx_t[...], r.low[...]).astype(BF16).reshape(4, 192, 768)
        t.s[8][0]()
        for owner in range(4):
            start = 192 * owner - 64 * (owner % 2)
            r.v_own[owner, 0:8] = r.v_rows[0:8, start : start + 256]
            for part in range(3):
                r.v_own[owner, 8 + part : 9 + part] = r.v_rows[
                    8 + owner : 9 + owner, 256 * part : 256 * part + 256
                ]
            r.v_own[owner, 11:16] = jnp.zeros((5, 256), F32)
        for hop in range(1, 4):
            other = lax.rem(seq + hop, 4)
            send(
                r.v_own.at[other],
                r.v_recv.at[seq],
                r.v_ss.at[0, hop],
                r.v_rs.at[0, hop],
                other,
                ctx,
            )

    @task
    def v1():
        for hop in range(1, 4):
            spot = r.v_recv.at[lax.rem(seq + 4 - hop, 4)]
            landed(spot, r.v_ss.at[0, hop], r.v_rs.at[0, hop])
        r.v_recv[seq] = r.v_own[seq]
        r.v_all[ctx] = r.v_recv[0] + r.v_recv[1] + r.v_recv[2] + r.v_recv[3]
        for hop in range(1, 8):
            send(
                r.v_all.at[ctx],
                r.v_all.at[ctx],
                r.v_ss.at[1, hop],
                r.v_rs.at[1, hop],
                seq,
                lax.rem(ctx + hop, 8),
            )

    def attend_back_head(head):
        if head == 0:
            own_do.wait()
        for hop in range(1, 8):
            spot = r.do_all.at[
                64 * head : 64 * head + 64, span(lax.rem(ctx + 8 - hop, 8) * 128, 128, 128)
            ]
            landed(spot, r.do_ss.at[head, hop], r.do_rs.at[head, hop])
        at = span(inside + 64 * head, 64, 64)
        total = r.sums[head]
        d_out = r.do_all[64 * head : 64 * head + 64].astype(F32)
        r.du[...] = (d_out / total).astype(BF16)
        r.c_row[...] = jnp.sum(d_out * r.ot[head], axis=0, keepdims=True) / total
        r.key_rows[...] = r.ka[head].T
        r.value_rows[...] = r.vt[head].T
        r.dk_acc[...] = jnp.zeros((64, 1024), F32)
        r.dv_acc[...] = jnp.zeros((64, 1024), F32)

        def attend_back(block, unused):
            lanes = span(block * 256, 256, 256)
            scores = matmul(r.key_rows[...], r.qa[head, :, lanes])
            unnorm = jnp.exp(scores)
            d_prob = matmul(r.value_rows[...], r.du[:, lanes])
            d_score = (unnorm * (d_prob - r.c_row[:, lanes])).astype(BF16)
            d_query = matmul(r.ka[head, 0:64], d_score) * SCORE_SCALE
            r.d_all[0, at, lanes] = d_query.astype(BF16)
            r.dk_acc[...] += matmul_nt(r.qa[head, 0:64, lanes], d_score)
            r.dv_acc[...] += matmul_nt(r.du[:, lanes], unnorm.astype(BF16))
            return unused

        lax.fori_loop(0, 4, attend_back, 0)
        r.d_all[1, at] = r.dk_acc[...].astype(BF16)
        r.d_all[2, at] = r.dv_acc[...].astype(BF16)

    t.ab = [functools.partial(attend_back_head, head) for head in range(3)]

    g_cores = [
        remote(
            r.g_all.at[which, owner],
            r.g_core.at[which, n],
            r.h_ss.at[which, n],
            r.h_rs.at[which, n],
            mate,
            ctx,
        )
        for which in range(3)
        for n, owner in ((0, mate), (1, across_mate))
    ]
    own_bias = pltpu.make_async_copy(
        r.b_send, r.b_recv.at[seq * 2 + side], r.loc.at[16]
    )
    to_owners = [
        remote(
            r.b_send,
            r.b_recv.at[seq * 2 + side],
            r.b_ss.at[hop],
            r.b_rs.at[seq * 2 + side],
            group,
            lax.rem(ctx + hop, 8),
        )
        for hop in range(8)
    ]

    @task
    def dwq():
        ones = jnp.ones((16, 1024), BF16)
        for which in range(3):
            product = matmul(r.d_all[which], r.xs[...].reshape(1024, 768)).astype(BF16)
            r.g_all[which] = product.T.reshape(4, 192, 256)
            if which != 1:
                r.b_send[which // 2] = matmul_nt(ones, r.d_all[which])[0:8]
        for copy in g_cores:
            copy.start()

        @pl.when(group == seq)
        def _():
            own_bias.start()

        @pl.when(group != seq)
        def _():
            to_owners[0].start()

        for copy in to_owners[1:]:
            copy.start()

    @task
    def dx():
        for part in range(4):
            lanes = slice(256 * part, 256 * part + 256)
            share = matmul(r.wg[0].reshape(768, 256), r.d_all[0, :, lanes])
            for which in (1, 2):
                share += matmul(r.wg[which].reshape(768, 256), r.d_all[which, :, lanes])
            r.act_t[part] = share.astype(BF16)

    def dx_half(part, bit):
        return r.act_t.at[part, :, span(bit * 128, 128, 128)]

    dx_to_y = [
        remote(
            dx_half(part, 1 - bit_y),
            r.dx_y.at[part],
            r.dx_ss.at[part],
            r.dx_rs.at[part],
            seq,
            beside,
        )
        for part in range(4)
    ]
    dx_to_l = [
        remote(
            dx_half(2 * n + 1 - bit_l, bit_y),
            r.dx_l.at[n],
            r.dx_ss.at[4 + n],
            r.dx_rs.at[4 + n],
            seq,
            paired,
        )
        for n in range(2)
    ]
    lanes_y = span(bit_y * 128, 128, 128)

    def dx_part(which):
        return 2 * which + bit_l

    dx_to_h = remote(
        dx_half(dx_part(1 - side), bit_y),
        r.dx_h,
        r.dx_ss.at[6],
        r.dx_rs.at[6],
        seq,
        mirror,
    )
    t.d = [copy.start for copy in dx_to_y]

    @task
    def dxp():
        for copy in dx_to_y:
            copy.wait_recv()
        for n in range(2):
            part = 2 * n + 1 - bit_l
            r.act_t[part, :, lanes_y] = (
                r.act_t[part, :, lanes_y].astype(F32) + r.dx_y[part].astype(F32)
            ).astype(BF16)
            dx_to_l[n].start()

    def dx_total(which):
        part = dx_part(which)
        return (
            r.act_t[part, :, lanes_y].astype(F32)
            + r.dx_y[part].astype(F32)
            + r.dx_l[which].astype(F32)
        )

    @task
    def dxm():
        for copy in dx_to_l:
            copy.wait_recv()
        r.act_t[dx_part(1 - side), :, lanes_y] = dx_total(1 - side).astype(BF16)
        dx_to_h.start()
        r.grad_rows[side] = dx_total(side).T + r.work[span(side * 128, 128)]
        to_hbm(r.grad_rows.at[side], r.grad.at[side])

    @task
    def dxe():
        dx_to_h.wait_recv()
        r.grad_rows[1 - side] = (
            r.dx_h[...].astype(F32).T + r.work[span((1 - side) * 128, 128)]
        )
        to_hbm(r.grad_rows.at[1 - side], r.grad.at[1 - side])

    g_x = remote(r.g_xs, r.g_xr, r.h_ss.at[3, 0], r.h_rs.at[3, 0], across, ctx)
    keep, give = span(side * 96, 96, 32), span((1 - side) * 96, 96, 32)
    g_m = remote(
        r.g_half.at[:, give], r.g_mir, r.h_ss.at[3, 1], r.h_rs.at[3, 1], seq, mirror
    )

    @task
    def gx():
        for copy in g_cores:
            copy.wait_recv()
        for which in range(3):
            r.g_xs[which] = (
                r.g_all[which, across].astype(F32) + r.g_core[which, 1].astype(F32)
            ).astype(BF16)
        g_x.start()

    @task
    def gm():
        g_x.wait_recv()
        for which in range(3):
            r.g_half[which] = (
                r.g_all[which, seq].astype(F32)
                + r.g_core[which, 0].astype(F32)
                + r.g_xr[which].astype(F32)
            ).astype(BF16)
        g_m.start()

    @task
    def ga():
        g_m.wait_recv()
        for which in range(3):
            r.fg_all[group, which, keep] = (
                r.g_half[which, keep].astype(F32) + r.g_mir[which].astype(F32)
            ).astype(BF16)
        spot = r.fg_all.at[group, :, keep]
        send(spot, spot, r.h_ss.at[4, 0], r.h_rs.at[4, 0], seq, mirror)
        for n, other in enumerate((beside, paired)):
            send(spot, spot, r.h_ss.at[5, n], r.h_rs.at[5, n], seq, other)

    @task
    def gb():
        theirs = r.fg_all.at[group, :, give]
        landed(theirs, r.h_ss.at[4, 0], r.h_rs.at[4, 0])
        for n, other in enumerate((beside, paired)):
            send(theirs, theirs, r.h_ss.at[6, n], r.h_rs.at[6, n], seq, other)
        to_hbm(r.fg_all.at[group], r.fg.at[group])

    def of_group(other, rows):
        return r.fg_all.at[lax.rem(other, 4), :, rows]

    @task
    def gc():
        spot = of_group(beside, keep)
        landed(spot, r.h_ss.at[5, 0], r.h_rs.at[5, 0])
        send(spot, spot, r.h_ss.at[5, 2], r.h_rs.at[5, 2], seq, paired)

    @task
    def gd():
        spot = of_group(paired, give)
        landed(spot, r.h_ss.at[6, 1], r.h_rs.at[6, 1])
        send(spot, spot, r.h_ss.at[6, 2], r.h_rs.at[6, 2], seq, beside)

    @task
    def v2():
        for hop in range(1, 8):
            spot = r.v_all.at[lax.rem(ctx + 8 - hop, 8)]
            landed(spot, r.v_ss.at[1, hop], r.v_rs.at[1, hop])
        gathered = r.v_all[0]
        for n in range(1, 8):
            gathered += r.v_all[n]
        r.vec_sum[...] = gathered

    @task
    def be():
        for n in range(8):
            spot = r.b_recv.at[n]
            arrival = remote(
                spot, spot, r.b_ss.at[0], r.b_rs.at[n], lax.rem(seq + 1, 4), ctx
            )
            here = (n // 2 == seq) & (n % 2 == side) & (group == seq)

            @pl.when(here)
            def _():
                own_bias.wait()

            @pl.when(jnp.logical_not(here))
            def _(arrival=arrival):
                arrival.wait_recv()

        row_sum = r.b_recv[0]
        for n in range(1, 8):
            row_sum += r.b_recv[n]
        r.bias_sum[...] = row_sum

    @task
    def ge():
        landed(of_group(paired, keep), r.h_ss.at[5, 1], r.h_rs.at[5, 1])
        landed(of_group(beside, give), r.h_ss.at[6, 0], r.h_rs.at[6, 0])
        landed(of_group(diagonal, keep), r.h_ss.at[5, 2], r.h_rs.at[5, 2])
        landed(of_group(diagonal, give), r.h_ss.at[6, 2], r.h_rs.at[6, 2])
        for other in (beside, paired, diagonal):
            part = lax.rem(other, 4)
            to_hbm(r.fg_all.at[part], r.fg.at[part])

    @task
    def left():
        for copy in sent[: early[0]]:
            copy.wait_send()
        for k in range(7):
            for leg in range(5):
                w_copy(k, leg).wait_send()

    for step in in_order(t):
        step()

    for k in range(9):
        t.s[k][9]()
    for copy in (
        sent[early[0] :]
        + g_cores
        + [g_x, g_m]
        + to_owners[1:]
        + dx_to_y
        + dx_to_l
        + [dx_to_h]
    ):
        copy.wait_send()

    @pl.when(group != seq)
    def _():
        to_owners[0].wait_send()

    for copy in to_hbm_all:
        copy.wait()


def in_order(t):
    return (
        t.far[0],
        t.grp,
        t.small,
        t.far[1],
        t.nf,
        t.ff[1],
        t.ff[0],
        t.pa[1],
        t.pa[0],
        t.qkv,
        t.pa[2],
        t.at[0],
        t.at[1],
        t.at[2],
        t.pb[0],
        t.pa[4],
        t.pa[3],
        t.pa[5],
        t.pb[1],
        t.pa[6],
        t.fn,
        t.pb[2],
        t.pb[3],
        t.pb[4],
        t.fe0,
        t.pb[5],
        t.pb[6],
        t.fe1,
        t.sn,
        t.mo[0],
        t.mo[1],
        t.mo[2],
        t.s[0][1],
        t.mo[3],
        t.s[1][1],
        t.ib[0],
        t.s[2][1],
        t.ib[1],
        t.s[4][1],
        t.ib[2],
        t.s[5][1],
        t.ib[3],
        t.s[0][2],
        t.s[1][2],
        t.fb,
        t.dwo,
        t.s[2][2],
        t.s[4][2],
        t.v1,
        t.s[6][1],
        t.s[0][3],
        t.s[8][1],
        t.s[1][3],
        t.s[3][1],
        t.ab[0],
        t.s[2][3],
        t.ab[1],
        t.v2,
        t.s[1][4],
        t.s[4][3],
        t.s[0][4],
        t.s[7][1],
        t.s[2][4],
        t.s[6][2],
        t.ab[2],
        t.s[1][5],
        t.s[4][4],
        t.dwq,
        t.s[0][5],
        t.s[8][2],
        t.s[6][3],
        t.dx,
        t.s[3][2],
        t.s[2][5],
        t.d[0],
        t.s[5][2],
        t.s[1][6],
        t.s[6][4],
        t.s[8][3],
        t.s[0][6],
        t.s[7][2],
        t.be,
        t.s[4][5],
        t.d[1],
        t.s[3][3],
        t.d[2],
        t.gx,
        t.s[8][4],
        t.s[6][5],
        t.s[2][6],
        t.s[3][4],
        t.s[5][3],
        t.s[7][3],
        t.s[8][5],
        t.s[6][6],
        t.s[4][6],
        t.s[3][5],
        t.d[3],
        t.s[7][4],
        t.s[0][7],
        t.gm,
        t.s[8][6],
        t.s[5][4],
        t.s[7][5],
        t.s[3][6],
        t.s[6][7],
        t.left,
        t.dxp,
        t.s[4][7],
        t.s[0][8],
        t.s[1][7],
        t.s[2][7],
        t.s[8][7],
        t.s[3][7],
        t.s[6][8],
        t.s[5][5],
        t.s[4][8],
        t.ga,
        t.s[1][8],
        t.dxm,
        t.s[5][6],
        t.s[2][8],
        t.s[8][8],
        t.s[7][6],
        t.s[3][8],
        t.gb,
        t.s[5][7],
        t.s[7][7],
        t.gc,
        t.dxe,
        t.gd,
        t.s[7][8],
        t.s[5][8],
        t.ge,
    )


def run_layer(*operands):
    vmem = pl.BlockSpec(memory_space=pltpu.VMEM)
    anywhere = pl.BlockSpec(memory_space=pl.ANY)
    shape = jax.ShapeDtypeStruct
    return pl.pallas_call(
        layer_kernel,
        name="layer_kernel",
        out_shape=(
            shape((2, 128, 768), BF16),
            shape((2, 128, 768), F32),
            shape((768, 768), BF16),
            shape((192, 3072), BF16),
            shape((192, 768), BF16),
            shape((4, 3, 192, 256), BF16),
            shape((16, 256), F32),
            shape((2, 8, 256), F32),
        ),
        in_specs=[anywhere] * 2 + [vmem] * 10 + [anywhere] * 6,
        out_specs=(anywhere,) * 6 + (vmem,) * 2,
        scratch_shapes=[pltpu.VMEM(*spec) for spec in SCRATCH.values()]
        + [pltpu.SemaphoreType.DMA(count) for count in SEMAPHORES.values()],
        compiler_params=pltpu.CompilerParams(
            collective_id=1, has_side_effects=True, vmem_limit_bytes=67043328
        ),
    )(*operands)


def finish_kernel(*refs):
    ins, outs, bufs = refs[:8], refs[8:25], refs[25:]
    low, wide, load, store = bufs[:8], bufs[8:17], bufs[17], bufs[18]
    grad, layer, low_u, low_i, low_o, low_g, vec, bias = low
    wide_t, wide_l, out_l, wide_u, wide_i, wide_o, wide_q, wide_k, wide_v = wide
    loads = [
        pltpu.make_async_copy(source, target, load.at[n])
        for n, (source, target) in enumerate(zip(ins, low))
    ]
    for copy in loads:
        copy.start()
    stores = []

    def put(source, target):
        copy = pltpu.make_async_copy(source, target, store.at[len(stores)])
        copy.start()
        stores.append(copy)

    loads[2].wait()
    for part in (slice(0, 384), slice(384, 768)):
        wide_u[part] = low_u[part].astype(F32)
        put(wide_u.at[part], outs[7].at[part])
    loads[3].wait()
    for part in (slice(0, 96), slice(96, 192)):
        wide_i[part] = low_i[part].astype(F32)
        put(wide_i.at[part], outs[6].at[part])
    loads[0].wait()
    for which in range(2):
        wide_t[:, which, :] = grad[which]
    put(wide_t, outs[1])
    loads[1].wait()
    for which in range(2):
        wide_l[:, which, :] = layer[which].astype(F32)
    out_l[...] = wide_l[...].astype(BF16)
    put(out_l, outs[0])
    loads[4].wait()
    wide_o[...] = low_o[...].astype(F32)
    put(wide_o, outs[5])
    loads[5].wait()
    for which, target in enumerate((wide_q, wide_k, wide_v)):
        for pair in range(2):
            left = low_g[2 * pair, which].astype(F32)
            right = low_g[2 * pair + 1, which].astype(F32)
            at = 384 * pair
            target[:, at : at + 128] = left[:, 0:128]
            target[:, at + 128 : at + 256] = left[:, 128:256] + right[:, 0:128]
            target[:, at + 256 : at + 384] = right[:, 128:256]
        put(target, outs[2 + which])
    odd = lax.rem(lax.axis_index("seq"), 2) == 1

    def owned(row):
        return jnp.where(odd, row[:, 64:256], row[:, 0:192]).reshape(192)

    loads[6].wait()
    loads[7].wait()
    outs[8][...] = owned(bias[0, 0:1])
    outs[9][...] = owned(bias[1, 0:1])
    outs[10][...] = owned(vec[0:1])
    outs[11][...] = jnp.concatenate([vec[n : n + 1] for n in (8, 9, 10)], axis=1).reshape(
        768
    )
    for n in range(1, 6):
        outs[11 + n][...] = owned(vec[n : n + 1])
    for copy in stores:
        copy.wait()


def run_finish(*operands):
    vmem = pl.BlockSpec(memory_space=pltpu.VMEM)
    anywhere = pl.BlockSpec(memory_space=pl.ANY)
    shape = jax.ShapeDtypeStruct
    large = [(192, 768)] * 4 + [(192, 3072), (768, 768)]
    small = [(192,)] * 3 + [(768,)] + [(192,)] * 5
    return pl.pallas_call(
        finish_kernel,
        name="finish_kernel",
        out_shape=[shape((128, 2, 768), BF16), shape((128, 2, 768), F32)]
        + [shape(size, F32) for size in large + small],
        in_specs=[anywhere] * 8,
        out_specs=[anywhere] * 8 + [vmem] * 9,
        scratch_shapes=[
            pltpu.VMEM((2, 128, 768), F32),
            pltpu.VMEM((2, 128, 768), BF16),
            pltpu.VMEM((768, 768), BF16),
            pltpu.VMEM((192, 3072), BF16),
            pltpu.VMEM((192, 768), BF16),
            pltpu.VMEM((4, 3, 192, 256), BF16),
            pltpu.VMEM((16, 256), F32),
            pltpu.VMEM((2, 8, 256), F32),
            pltpu.VMEM((128, 2, 768), F32),
            pltpu.VMEM((128, 2, 768), F32),
            pltpu.VMEM((128, 2, 768), BF16),
            pltpu.VMEM((768, 768), F32),
            pltpu.VMEM((192, 3072), F32),
            pltpu.VMEM((192, 768), F32),
            pltpu.VMEM((192, 768), F32),
            pltpu.VMEM((192, 768), F32),
            pltpu.VMEM((192, 768), F32),
            pltpu.SemaphoreType.DMA((8,)),
            pltpu.SemaphoreType.DMA((10,)),
        ],
        compiler_params=pltpu.CompilerParams(vmem_limit_bytes=67043328),
    )(*operands)


def fast_body(
    tokens,
    segment_ids,
    w_query,
    w_key,
    w_value,
    w_output,
    w_inner,
    w_outer,
    b_query,
    b_value,
    b_output,
    b_inner,
    b_outer,
    gain_first,
    shift_first,
    gain_second,
    shift_second,
    cotangent,
):
    layer, grad, fu, fi, fo, fg, vec_sum, bias_sum = run_layer(
        jnp.transpose(tokens, (1, 0, 2)),
        jnp.transpose(cotangent, (1, 0, 2)),
        segment_ids,
        b_query,
        b_value,
        b_output,
        b_outer,
        gain_first,
        shift_first,
        gain_second,
        shift_second,
        b_inner,
        w_query,
        w_key,
        w_value,
        w_output,
        w_inner,
        w_outer,
    )

    return tuple(run_finish(grad, layer, fu, fi, fo, fg, vec_sum, bias_sum))


def solution(mesh):
    in_specs = (
        P("ctx", "seq", None),
        P("seq", "ctx"),
        P("seq", None),
        P("seq", None),
        P("seq", None),
        P("seq", None),
        P("seq", None),
        P("seq", None),
        P("seq"),
        P("seq"),
        P("seq"),
        P("seq"),
        P("seq"),
        P("seq"),
        P("seq"),
        P("seq"),
        P("seq"),
        P("ctx", "seq", None),
    )
    out_specs = (
        P("ctx", "seq", None),
        P("ctx", "seq", None),
        P("seq", None),
        P("seq", None),
        P("seq", None),
        P("seq", None),
        P("seq", None),
        P("seq", None),
        P("seq"),
        P("seq"),
        P("seq"),
        P("seq"),
        P("seq"),
        P("seq"),
        P("seq"),
        P("seq"),
        P("seq"),
    )
    small = mesh.shape["seq"] == 4 and mesh.shape["ctx"] == 8
    step = fast_body if small else body
    return jax.shard_map(step, mesh=mesh, in_specs=in_specs, out_specs=out_specs, check_vma=False)
```
